32 devices in a mesh: dp: 4 (over z), fsdp: 8 (over y, x, core).
Axes of the slice: x: 2, y: 2, z: 4, core: 2. Of those that a mesh axis runs over, the one named last changes fastest.
Arguments:
- tokens: bfloat16 [16384, 768], P(('dp', 'fsdp')), may hold values from -6 to 6
- condition: bfloat16 [64, 768], P(('dp', 'fsdp')), may hold values from -6 to 6
- ada_weight: bfloat16 [768, 4608], P('fsdp', 'dp'), may hold values from -0.21875 to 0.21875
- qkv_weight: bfloat16 [768, 2304], P('fsdp', 'dp'), may hold values from -0.21875 to 0.21875
- out_weight: bfloat16 [768, 768], P('fsdp', 'dp'), may hold values from -2 to 2
- shared_up: bfloat16 [768, 3072], P('fsdp', 'dp'), may hold values from -0.21875 to 0.21875
- shared_down: bfloat16 [3072, 768], P('fsdp', 'dp'), may hold values from -0.109375 to 0.109375
- router_weight: bfloat16 [768, 8], P('fsdp', 'dp'), may hold values from -0.21875 to 0.21875
- expert_up: bfloat16 [8, 768, 3072], P('dp', 'fsdp'), may hold values from -0.21875 to 0.21875
- expert_down: bfloat16 [8, 3072, 768], P('dp', 'fsdp'), may hold values from -0.109375 to 0.109375
- routes: int32 [16384, 2], P(('dp', 'fsdp')), may hold values from 0 to 7, all different within a row; in each aligned block of 512 rows (0 to 511, 512 to 1023, ...) at most 144 rows name the same one
- image_sizes: int32 [64], P(('dp', 'fsdp')), may hold values from 0 to 512, as said below
- cotangent: bfloat16 [16384, 768], P(('dp', 'fsdp')), may hold values from -6 to 6
Outputs:
- output: bfloat16 [16384, 768], P(('dp', 'fsdp'))
- tokens_grad: float32 [16384, 768], P(('dp', 'fsdp'))
- condition_grad: float32 [64, 768], P(('dp', 'fsdp'))
- ada_grad: float32 [768, 4608], P('fsdp', 'dp')
- qkv_grad: float32 [768, 2304], P('fsdp', 'dp')
- out_grad: float32 [768, 768], P('fsdp', 'dp')
- shared_up_grad: float32 [768, 3072], P('fsdp', 'dp')
- shared_down_grad: float32 [3072, 768], P('fsdp', 'dp')
- router_grad: float32 [768, 8], P('fsdp', 'dp')
- expert_up_grad: float32 [8, 768, 3072], P('dp', 'fsdp')
- expert_down_grad: float32 [8, 3072, 768], P('dp', 'fsdp')
- expert_counts: int32 [8], replicated
The draws below stay inside these ranges and needn't reach their ends.
Inputs may be any that keep to these rules, and one draw needn't show every extreme that they name: `routes`: each row names two different experts; in the rows of one device no expert is named by more than 144 rows, and in every draw some expert is named by exactly 144 rows of some device. `image_sizes`: each aligned group of 2 entries is either one image of 512 patches followed by zeros, or k images of 256 patches followed by zeros, k from 1 to 2; in every draw some group holds one image of 512 and another holds 2 images of 256.
All inputs are finite; a program needn't handle non-finite values.
Results may differ from the reference program's by a relative error of at most 0.015.
The reference program's roundings to bfloat16 on the way count: a program that leaves them out, or rounds other values in their place, can miss the bound.
Values may be sent and summed in bfloat16 or wider, within the bound.
A program may use at most 512 MiB of HBM per device.

```python
import math
import jax
import jax.numpy as jnp
import numpy as np
from jax import lax

D = 768
HEADS = 12
FF = 3072
EXPERTS = 8
CAP = 144
SHORT = 256
IMG_DEV = 2
LONG = 512
TOKENS = 16384
IMAGES = 64


def draw_image_sizes(key, part):
    device_count = IMAGES // IMG_DEV
    pattern_key, long_key, short_key = jax.random.split(key, 3)
    pattern = jax.random.randint(pattern_key, (device_count,), 0, IMG_DEV + 1)
    long_at = jax.random.randint(long_key, (), 0, device_count)
    short_at = (long_at + 1 + jax.random.randint(short_key, (), 0, device_count - 1)) % device_count
    pattern = pattern.at[long_at].set(0).at[short_at].set(IMG_DEV)
    slot_ids = jnp.arange(IMG_DEV)
    lengths = jnp.where(pattern[:, None] == 0, jnp.where(slot_ids[None, :] == 0, LONG, 0), jnp.where(slot_ids[None, :] < pattern[:, None], SHORT, 0))
    return lengths.reshape(-1).astype(jnp.int32)


def shard_levels(rng, dims, cuts, least, top_value):
    def one(axis_at, parts):
        steps = jax.random.uniform(jax.random.fold_in(jax.random.fold_in(rng, 6), axis_at), (parts,), jnp.float32, least / len(cuts), top_value / len(cuts))
        return jnp.repeat(jnp.exp(steps), dims[axis_at] // parts).reshape((-1,) + (1,) * (len(dims) - axis_at - 1))

    factor_of = one(*cuts[0])
    for cut in cuts[1:]:
        factor_of = factor_of * one(*cut)
    return factor_of


def routed_block(own_key, own, number, rows, count, top, bound, slope):
    ranking = jax.random.permutation(own_key, count)
    crowded, ordinary = shares(count, rows * top, bound, slope, True), shares(count, rows * top, bound, slope, False)
    places = jnp.arange(count)

    def named(sizes, rotation):
        used = int((sizes > 0).sum())
        fixed = max(1, used // 4)
        passed = fixed + (places - fixed + rotation * (used - fixed)) % max(1, count - fixed)
        return jnp.zeros((count,), jnp.int32).at[ranking[jnp.where(places < fixed, places, passed)]].set(jnp.asarray(sizes, jnp.int32))

    sizes = jnp.where(number % 4 == 0, named(crowded, number // 4), named(ordinary, number - number // 4 - 1))
    mixed = jax.random.permutation(jax.random.fold_in(own, 3), count)
    giver, taker = mixed[0:count // 2 * 2:2], mixed[1:count // 2 * 2:2]
    slack = jnp.minimum(sizes[giver] - 1, bound - sizes[taker]) // 2
    slack = jnp.where((giver == ranking[0]) | (taker == ranking[0]) | (sizes[taker] == 0), 0, jnp.maximum(slack, 0))
    passed = jax.random.randint(jax.random.fold_in(own, 4), (count // 2,), 0, 1 << 20) % (slack + 1)
    sizes = sizes.at[giver].add(-passed).at[taker].add(passed)
    members = jnp.searchsorted(jnp.cumsum(sizes), jnp.arange(rows * top), side="right").astype(jnp.int32)
    table = members.reshape(top, rows).T
    table = table[jax.random.permutation(jax.random.fold_in(own, 1), rows)]
    rotation = jax.random.randint(jax.random.fold_in(own, 2), (rows, 1), 0, top)
    return jnp.take_along_axis(table, (jnp.arange(top)[None, :] + rotation) % top, axis=1)


def shares(amount, total, bound, slope, full):
    portions = [(1 << 20) // math.isqrt(standing ** slope) + 1 for standing in range(1, amount + 1)]
    largest = bound if full else min(bound, max(-(-total // amount), total * portions[0] // sum(portions)))
    least = 1 if total - largest >= amount - 1 else 0
    holding, spare = [largest] + [least] * (amount - 1), total - largest - least * (amount - 1)
    while spare > 0:
        candidates = [i for i in range(1, amount) if holding[i] < largest] or [i for i in range(1, amount) if holding[i] < bound]
        whole, left = sum([portions[i] for i in candidates]), spare
        for i in candidates:
            extra = min(bound - holding[i], max(1, left * portions[i] // whole), spare)
            holding[i] = holding[i] + extra
            spare = spare - extra
    return np.array(holding)


def scatter_about(rng, dims, width, bound, cuts=(), kind=jnp.bfloat16):
    entries = jax.random.normal(rng, dims, jnp.float32) * width
    if len(cuts) > 0:
        entries = shard_levels(rng, dims, cuts, -0.22, 0.18) * entries
    return jnp.clip(entries, min=-bound, max=bound).astype(kind)


def setup_inputs(seed: int = 0) -> dict:
    arg_keys = jax.random.split(jax.random.key(seed), 14)
    tokens = scatter_about(arg_keys[0], (TOKENS, D), 1.0, 6.0, ((0, 32),))
    condition = scatter_about(arg_keys[1], (IMAGES, D), 1.0, 6.0, ((0, 32),))
    ada_weight = scatter_about(arg_keys[2], (D, 6 * D), D ** -0.5, 0.21875, ((0, 8), (1, 4)))
    qkv_weight = scatter_about(arg_keys[3], (D, 3 * D), D ** -0.5, 0.21875, ((0, 8), (1, 4)))
    out_weight = scatter_about(arg_keys[4], (D, D), (max(D // 96, 1)) ** -0.5, 2.0, ((0, 8), (1, 4)))
    shared_up = scatter_about(arg_keys[5], (D, FF), D ** -0.5, 0.21875, ((0, 8), (1, 4)))
    shared_down = scatter_about(arg_keys[6], (FF, D), FF ** -0.5, 0.109375, ((0, 8), (1, 4)))
    router_weight = scatter_about(arg_keys[7], (D, EXPERTS), D ** -0.5, 0.21875, ((0, 8), (1, 4)))
    expert_up = scatter_about(arg_keys[8], (EXPERTS, D, FF), D ** -0.5, 0.21875, ((0, 4), (1, 8)))
    expert_down = scatter_about(arg_keys[9], (EXPERTS, FF, D), FF ** -0.5, 0.109375, ((0, 4), (1, 8)))
    routes_keys = jax.random.split(jax.random.fold_in(arg_keys[10], 1), TOKENS // LONG)
    routes_turns = jax.random.permutation(jax.random.fold_in(arg_keys[10], 3), TOKENS // LONG)
    routes = jax.vmap(lambda own, number: routed_block(jax.random.fold_in(arg_keys[10], 2), own, number, LONG, EXPERTS, 2, CAP, 1))(routes_keys, routes_turns).reshape((TOKENS, 2))
    image_sizes = draw_image_sizes(jax.random.fold_in(arg_keys[13], 71), 0)
    cotangent = scatter_about(arg_keys[12], (TOKENS, D), 1.0, 6.0, ((0, 32),))
    return dict(tokens=tokens, condition=condition, ada_weight=ada_weight, qkv_weight=qkv_weight, out_weight=out_weight, shared_up=shared_up, shared_down=shared_down, router_weight=router_weight, expert_up=expert_up, expert_down=expert_down, routes=routes, image_sizes=image_sizes, cotangent=cotangent)


@jax.custom_vjp
def low(v):
    return lax.optimization_barrier(v.astype(jnp.bfloat16)).astype(jnp.float32)

@jax.custom_vjp
def low_back(v):
    return v

def low_keep(v):
    return (low(v), None)

def low_pass(kept, grad):
    return (grad,)

def back_keep(v):
    return (v, None)

def back_low(kept, grad):
    return (low(grad),)
low.defvjp(low_keep, low_pass)
low_back.defvjp(back_keep, back_low)

def matmul(left, right):
    return jnp.dot(left, right, precision=lax.Precision.HIGHEST, preferred_element_type=jnp.float32)

def layer_norm(values_in):
    centred = values_in - lax.optimization_barrier(jnp.mean(values_in, axis=-1, keepdims=True))
    variance = lax.optimization_barrier(jnp.mean(centred * centred, axis=-1, keepdims=True))
    return centred * lax.rsqrt(variance + 1e-06)

def owners(image_sizes):
    sizes_int = image_sizes.astype(jnp.int32)
    starts = (jnp.cumsum(sizes_int) - sizes_int).astype(jnp.int32)
    position = jnp.arange(LONG, dtype=jnp.int32)[:, None]
    inside = (position >= starts[None, :]) & (position < (starts + sizes_int)[None, :])
    slot_ids = jnp.arange(IMG_DEV, dtype=jnp.int32)
    segment = lax.optimization_barrier(jnp.sum(jnp.where(inside, slot_ids[None, :], 0), axis=1)) + jnp.where(jnp.any(inside, axis=1), 0, IMG_DEV)
    return (inside.astype(jnp.float32), segment.astype(jnp.int32))

def dispatch_plan(routes):
    flat = routes.reshape(-1).astype(jnp.int32)
    onehot = (flat[:, None] == jnp.arange(EXPERTS, dtype=jnp.int32)[None, :]).astype(jnp.int32)
    before = (jnp.cumsum(onehot, axis=0) - onehot).astype(jnp.int32)
    position = lax.optimization_barrier(jnp.sum(before * onehot, axis=1)).astype(jnp.int32)
    target = (flat * CAP + position).astype(jnp.int32)
    assignment = jnp.arange(2 * LONG, dtype=jnp.int32)
    source = jnp.zeros((EXPERTS * CAP,), jnp.int32).at[target].set(assignment)
    filled = jnp.zeros((EXPERTS * CAP,), jnp.int32).at[target].set(1)
    return (target, source, filled)

def attention(queries, keys, values, segment):
    row_count, head_count, head_size = queries.shape
    block_rows = min(512, LONG)
    block_count = row_count // block_rows
    score_scale = head_size ** (-0.5)

    def one_block(pieces):
        query_part, segment_part = pieces
        scores = jnp.einsum('qhd,khd->hqk', query_part, keys, precision=lax.Precision.HIGHEST) * score_scale
        scores = low_back(scores)
        allowed = (segment_part[:, None] == segment[None, :])[None]
        scores = jnp.where(allowed, scores, -1e+30)
        row_max = lax.optimization_barrier(jnp.max(scores, axis=-1, keepdims=True))
        weight = jnp.exp(scores - row_max)
        probability = weight / lax.optimization_barrier(jnp.sum(weight, axis=-1, keepdims=True))
        return jnp.einsum('hqk,khd->qhd', low(probability), values, precision=lax.Precision.HIGHEST)
    attended = lax.map(jax.checkpoint(one_block), (queries.reshape(block_count, block_rows, head_count, head_size), segment.reshape(block_count, block_rows)))
    return attended.reshape(row_count, head_count * head_size)

def forward(token_in, cond_in, params, route_hot, inside, segment, target, source):
    ada_full, qkv_full, out_full, shared_first, shared_second, router_full, expert_first, expert_second = params
    model_width = token_in.shape[1]
    head_size = model_width // HEADS
    activated = low(jax.nn.silu(cond_in))
    modulation = low_back(matmul(activated, ada_full))
    per_row = matmul(inside, modulation)
    shift_one, scale_one, gate_one, shift_two, scale_two, gate_two = jnp.split(per_row, 6, axis=1)
    first_input = low(layer_norm(token_in) * (1.0 + scale_one) + shift_one)
    qkv_rows = low_back(low(matmul(first_input, qkv_full)))
    queries = qkv_rows[:, :model_width].reshape(-1, HEADS, head_size)
    keys_all = qkv_rows[:, model_width:2 * model_width].reshape(-1, HEADS, head_size)
    values_all = qkv_rows[:, 2 * model_width:].reshape(-1, HEADS, head_size)
    attended = low_back(low(attention(queries, keys_all, values_all, segment)))
    projected = low_back(matmul(attended, out_full))
    residual_one = token_in + gate_one * projected
    second_input = low(layer_norm(residual_one) * (1.0 + scale_two) + shift_two)
    shared_pre = low_back(matmul(second_input, shared_first))
    shared_act = low(jax.nn.gelu(shared_pre, approximate=True))
    shared_out = low_back(matmul(shared_act, shared_second))
    logits = low_back(matmul(second_input, router_full))
    chosen = lax.optimization_barrier(jnp.sum(logits[:, None, :] * route_hot, axis=-1))
    gate_share = jax.nn.softmax(chosen, axis=-1)
    buffer_rows = low_back(jnp.take(second_input, source // 2, axis=0)).reshape(EXPERTS, CAP, model_width)
    expert_pre = low_back(jnp.einsum('ecd,edf->ecf', buffer_rows, expert_first, precision=lax.Precision.HIGHEST))
    expert_act = low(jax.nn.gelu(expert_pre, approximate=True))
    expert_out = low_back(low(jnp.einsum('ecf,efd->ecd', expert_act, expert_second, precision=lax.Precision.HIGHEST)))
    picked = jnp.take(expert_out.reshape(EXPERTS * CAP, model_width), target, axis=0).reshape(-1, 2, model_width)
    mixed = shared_out + lax.optimization_barrier(jnp.sum(gate_share[:, :, None] * picked, axis=1))
    return residual_one + gate_two * mixed

def reference(tokens, condition, ada_weight, qkv_weight, out_weight, shared_up, shared_down, router_weight, expert_up, expert_down, routes, image_sizes, cotangent):
    weights = tuple((matrix.astype(jnp.float32) for matrix in (ada_weight, qkv_weight, out_weight, shared_up, shared_down, router_weight, expert_up, expert_down)))
    model_width = tokens.shape[1]
    device_count = tokens.shape[0] // LONG
    stacked = (tokens.astype(jnp.float32).reshape(device_count, LONG, model_width), condition.astype(jnp.float32).reshape(device_count, IMG_DEV, model_width), routes.reshape(device_count, LONG, 2), image_sizes.reshape(device_count, IMG_DEV), cotangent.astype(jnp.float32).reshape(device_count, LONG, model_width))

    def one_device(running, pieces):
        token_part, cond_part, route_part, size_part, cot_part = pieces
        inside, segment = owners(size_part)
        target, source, filled = dispatch_plan(route_part)
        route_hot = (route_part[:, :, None] == jnp.arange(EXPERTS, dtype=jnp.int32)[None, None, :]).astype(jnp.float32)

        def local_run(token_in, cond_in, *params):
            return forward(token_in, cond_in, params, route_hot, inside, segment, target, source)
        result, pullback = jax.vjp(local_run, token_part, cond_part, *weights)
        grads = pullback(cot_part)
        live = (segment < IMG_DEV).astype(jnp.int32)
        counted = lax.optimization_barrier(jnp.sum(live[:, None, None] * route_hot.astype(jnp.int32), axis=(0, 1))).astype(jnp.int32)
        running = tuple((earlier + update for earlier, update in zip(running, grads[2:])))
        return (running, (result.astype(jnp.bfloat16), grads[0], grads[1], counted))
    zeros = tuple((jnp.zeros_like(matrix) for matrix in weights))
    totals, (outputs, token_grads, cond_grads, counted_all) = lax.scan(one_device, zeros, stacked)
    return (outputs.reshape(-1, model_width), token_grads.reshape(-1, model_width), cond_grads.reshape(-1, model_width), totals[0], totals[1], totals[2], totals[3], totals[4], totals[5], totals[6], totals[7], lax.optimization_barrier(jnp.sum(counted_all, axis=0)).astype(jnp.int32))
```

```python
import functools

import jax
import jax.numpy as jnp
from jax import lax
from jax.experimental import pallas as pl
from jax.experimental.pallas import tpu as pltpu
from jax.sharding import PartitionSpec as P

HEADS = 12
EXPERTS = 8
CAP = 144
IMG_DEV = 2
LONG = 512
MESH = pl.DeviceIdType.MESH


EXACT = lax.Precision.HIGHEST


def owners(image_sizes):
    starts = jnp.cumsum(image_sizes) - image_sizes
    position = jnp.arange(LONG, dtype=jnp.int32)[:, None]
    inside = (position >= starts[None, :]) & (position < (starts + image_sizes)[None, :])
    slot_ids = jnp.arange(IMG_DEV, dtype=jnp.int32)
    segment = jnp.sum(jnp.where(inside, slot_ids[None, :], 0), axis=1) + jnp.where(
        jnp.any(inside, axis=1), 0, IMG_DEV
    )
    return (inside.astype(jnp.float32), segment)


def dispatch_plan(routes):
    flat = routes.reshape(-1)
    onehot = (flat[:, None] == jnp.arange(EXPERTS, dtype=jnp.int32)[None, :]).astype(jnp.int32)
    before = jnp.cumsum(onehot, axis=0) - onehot
    position = jnp.sum(before * onehot, axis=1)
    target = flat * CAP + position
    assignment = jnp.arange(2 * LONG, dtype=jnp.int32)
    source = jnp.zeros((EXPERTS * CAP,), jnp.int32).at[target].set(assignment)
    filled = jnp.zeros((EXPERTS * CAP,), jnp.int32).at[target].set(1)
    return (target, source, filled)


def layer_norm(values_in):
    centred = values_in - jnp.mean(values_in, axis=-1, keepdims=True)
    inv_std = lax.rsqrt(jnp.mean(centred * centred, axis=-1, keepdims=True) + 1e-06)
    return (centred * inv_std, inv_std)


def norm_back(upstream, normed, inv_std):
    return (
        upstream
        - jnp.mean(upstream, axis=-1, keepdims=True)
        - normed * jnp.mean(upstream * normed, axis=-1, keepdims=True)
    ) * inv_std


def gelu_tanh(values_in):
    return jax.nn.gelu(values_in, approximate=True)


def gelu_back(values_in, upstream):
    return jax.vjp(gelu_tanh, values_in)[1](upstream)[0]


def collect(first, second, third):
    widened = (
        lax.all_gather(first, "dp", axis=1, tiled=True),
        lax.all_gather(second, "dp", axis=1, tiled=True),
        lax.all_gather(third, "dp", axis=1, tiled=True),
    )
    return (
        lax.all_gather(widened[0], "fsdp", axis=0, tiled=True),
        lax.all_gather(widened[1], "fsdp", axis=0, tiled=True),
        lax.all_gather(widened[2], "fsdp", axis=0, tiled=True),
    )


def spread(first, second, third):
    row_sums = (
        lax.psum_scatter(first, "fsdp", scatter_dimension=0, tiled=True),
        lax.psum_scatter(second, "fsdp", scatter_dimension=0, tiled=True),
        lax.psum_scatter(third, "fsdp", scatter_dimension=0, tiled=True),
    )
    return (
        lax.psum_scatter(row_sums[0], "dp", scatter_dimension=1, tiled=True),
        lax.psum_scatter(row_sums[1], "dp", scatter_dimension=1, tiled=True),
        lax.psum_scatter(row_sums[2], "dp", scatter_dimension=1, tiled=True),
    )


def gather_experts(up_shard, down_shard):
    return (
        lax.all_gather(up_shard, "fsdp", axis=1, tiled=True),
        lax.all_gather(down_shard, "fsdp", axis=1, tiled=True),
    )


def expert_forward(buffer_in, up_full, down_full):
    expert_pre = jnp.einsum(
        "secd,edf->secf", buffer_in, up_full, preferred_element_type=jnp.float32
    )
    expert_act = gelu_tanh(expert_pre).astype(jnp.bfloat16)
    expert_out = jnp.einsum(
        "secf,efd->secd", expert_act, down_full, preferred_element_type=jnp.float32
    ).astype(jnp.bfloat16)
    return (expert_pre, expert_act, expert_out)


def expert_backward(buffer_in, expert_pre, expert_act, d_out, up_full, down_full):
    d_act = jnp.einsum("secd,efd->secf", d_out, down_full, preferred_element_type=jnp.float32)
    d_pre = gelu_back(expert_pre, d_act).astype(jnp.bfloat16)
    d_rows = jnp.einsum(
        "secf,edf->secd", d_pre, up_full, preferred_element_type=jnp.float32
    ).astype(jnp.bfloat16)
    down_grad = jnp.einsum("secf,secd->efd", expert_act, d_out, preferred_element_type=jnp.float32)
    up_grad = jnp.einsum("secd,secf->edf", buffer_in, d_pre, preferred_element_type=jnp.float32)
    return (up_grad, down_grad, d_rows)


def attend(queries, keys_all, values_all, segment):
    row_count, head_count, head_size = queries.shape
    block_rows = min(512, row_count)
    block_count = row_count // block_rows
    score_scale = head_size ** (-0.5)

    def one_block(pieces):
        query_part, segment_part = pieces
        allowed = (segment_part[:, None] == segment[None, :])[None]
        scores = (
            jnp.einsum("qhd,khd->hqk", query_part, keys_all, preferred_element_type=jnp.float32)
            * score_scale
        )
        scores = jnp.where(allowed, scores, -1e30)
        row_max = jnp.max(scores, axis=-1, keepdims=True)
        weight = jnp.exp(scores - row_max)
        running = jnp.sum(weight, axis=-1, keepdims=True)
        probability = (weight / running).astype(jnp.bfloat16)
        attended = jnp.einsum(
            "hqk,khd->qhd", probability, values_all, preferred_element_type=jnp.float32
        )
        return (attended.astype(jnp.bfloat16), (row_max + jnp.log(running))[:, :, 0])

    return lax.map(
        one_block,
        (
            queries.reshape(block_count, block_rows, head_count, head_size),
            segment.reshape(block_count, block_rows),
        ),
    )


def attend_back(queries, keys_all, values_all, segment, log_totals, d_attended):
    row_count, head_count, head_size = queries.shape
    block_rows = min(512, row_count)
    block_count = row_count // block_rows
    score_scale = head_size ** (-0.5)

    def one_block(carry, pieces):
        key_sum, value_sum = carry
        query_part, segment_part, total_part, grad_part = pieces
        allowed = (segment_part[:, None] == segment[None, :])[None]
        scores = (
            jnp.einsum("qhd,khd->hqk", query_part, keys_all, preferred_element_type=jnp.float32)
            * score_scale
        )
        scores = jnp.where(allowed, scores, -1e30)
        probability = jnp.exp(scores - total_part[:, :, None])
        d_prob = jnp.einsum(
            "qhd,khd->hqk", grad_part, values_all, preferred_element_type=jnp.float32
        )
        d_scores = (
            probability * (d_prob - jnp.sum(probability * d_prob, axis=-1, keepdims=True))
        ).astype(jnp.bfloat16)
        query_grad = (
            jnp.einsum("hqk,khd->qhd", d_scores, keys_all, preferred_element_type=jnp.float32)
            * score_scale
        )
        key_sum = (
            key_sum
            + jnp.einsum("hqk,qhd->khd", d_scores, query_part, preferred_element_type=jnp.float32)
            * score_scale
        )
        value_sum = value_sum + jnp.einsum(
            "hqk,qhd->khd",
            probability.astype(jnp.bfloat16),
            grad_part,
            preferred_element_type=jnp.float32,
        )
        return ((key_sum, value_sum), query_grad)

    empty = jnp.zeros(keys_all.shape, jnp.float32)
    sums, query_grads = lax.scan(
        one_block,
        (empty, empty),
        (
            queries.reshape(block_count, block_rows, head_count, head_size),
            segment.reshape(block_count, block_rows),
            log_totals,
            d_attended.reshape(block_count, block_rows, head_count, head_size),
        ),
    )
    return (query_grads.reshape(row_count, head_count, head_size), sums[0], sums[1])


def shards(
    tokens,
    condition,
    ada_weight,
    qkv_weight,
    out_weight,
    shared_up,
    shared_down,
    router_weight,
    expert_up,
    expert_down,
    routes,
    image_sizes,
    cotangent,
):
    model_width = tokens.shape[1]
    head_size = model_width // HEADS
    inside, segment = owners(image_sizes)
    target, source, filled = dispatch_plan(routes)
    route_hot = (routes[:, :, None] == jnp.arange(EXPERTS, dtype=jnp.int32)[None, None, :]).astype(
        jnp.float32
    )
    live = (segment < IMG_DEV).astype(jnp.int32)
    local_counts = jnp.sum(live[:, None, None] * route_hot.astype(jnp.int32), axis=(0, 1))
    expert_counts = lax.psum(local_counts, ("dp", "fsdp"))
    ada_full, qkv_full, out_full = collect(ada_weight, qkv_weight, out_weight)
    cond_float = condition.astype(jnp.float32)
    activated = jax.nn.silu(cond_float).astype(jnp.bfloat16)
    modulation = jnp.dot(activated, ada_full, preferred_element_type=jnp.float32)
    per_row = jnp.dot(inside, modulation, precision=EXACT, preferred_element_type=jnp.float32)
    shift_one, scale_one, gate_one, shift_two, scale_two, gate_two = jnp.split(per_row, 6, axis=1)
    token_float = tokens.astype(jnp.float32)
    normed_one, inv_one = layer_norm(token_float)
    first_input = (normed_one * (1.0 + scale_one) + shift_one).astype(jnp.bfloat16)
    qkv_rows = jnp.dot(first_input, qkv_full, preferred_element_type=jnp.float32).astype(
        jnp.bfloat16
    )
    queries = qkv_rows[:, :model_width].reshape(-1, HEADS, head_size)
    keys_all = qkv_rows[:, model_width : 2 * model_width].reshape(-1, HEADS, head_size)
    values_all = qkv_rows[:, 2 * model_width :].reshape(-1, HEADS, head_size)
    attended_blocks, log_totals = attend(queries, keys_all, values_all, segment)
    attended = attended_blocks.reshape(-1, model_width)
    projected = jnp.dot(attended, out_full, preferred_element_type=jnp.float32)
    residual_one = token_float + gate_one * projected
    normed_two, inv_two = layer_norm(residual_one)
    second_input = (normed_two * (1.0 + scale_two) + shift_two).astype(jnp.bfloat16)
    shared_first, shared_second, router_full = collect(shared_up, shared_down, router_weight)
    shared_pre = jnp.dot(second_input, shared_first, preferred_element_type=jnp.float32)
    shared_act = gelu_tanh(shared_pre).astype(jnp.bfloat16)
    shared_out = jnp.dot(shared_act, shared_second, preferred_element_type=jnp.float32)
    logits = jnp.dot(second_input, router_full, preferred_element_type=jnp.float32)
    chosen = jnp.sum(logits[:, None, :] * route_hot, axis=-1)
    gate_share = jax.nn.softmax(chosen, axis=-1)
    buffer_rows = jnp.take(second_input, source // 2, axis=0).reshape(EXPERTS, CAP, model_width)
    up_full, down_full = gather_experts(expert_up, expert_down)
    groups = lax.axis_size("dp")
    expert_in = lax.all_to_all(
        buffer_rows.reshape(groups, EXPERTS // groups, CAP, model_width),
        "dp",
        split_axis=0,
        concat_axis=0,
        tiled=True,
    )
    expert_pre, expert_act, expert_out = expert_forward(expert_in, up_full, down_full)
    returned = lax.all_to_all(expert_out, "dp", split_axis=0, concat_axis=0, tiled=True).reshape(
        EXPERTS, CAP, model_width
    )
    picked = (
        jnp.take(returned.reshape(EXPERTS * CAP, model_width), target, axis=0)
        .reshape(-1, 2, model_width)
        .astype(jnp.float32)
    )
    mixed = shared_out + jnp.sum(gate_share[:, :, None] * picked, axis=1)
    output = (residual_one + gate_two * mixed).astype(jnp.bfloat16)
    upstream = cotangent.astype(jnp.float32)
    d_mixed = gate_two * upstream
    d_gate_two = upstream * mixed
    d_gate_share = jnp.sum(d_mixed[:, None, :] * picked, axis=-1)
    slot_gate = jnp.take(gate_share.reshape(-1), source) * filled.astype(jnp.float32)
    d_buffer = (
        (jnp.take(d_mixed, source // 2, axis=0) * slot_gate[:, None])
        .astype(jnp.bfloat16)
        .reshape(EXPERTS, CAP, model_width)
    )
    shared_first, shared_second, router_full = collect(shared_up, shared_down, router_weight)
    up_full, down_full = gather_experts(expert_up, expert_down)
    arrived = lax.all_to_all(
        d_buffer.reshape(groups, EXPERTS // groups, CAP, model_width),
        "dp",
        split_axis=0,
        concat_axis=0,
        tiled=True,
    )
    up_grad, down_grad, d_rows = expert_backward(
        expert_in, expert_pre, expert_act, arrived, up_full, down_full
    )
    d_returned = lax.all_to_all(d_rows, "dp", split_axis=0, concat_axis=0, tiled=True).reshape(
        EXPERTS, CAP, model_width
    )
    expert_sums = (
        lax.psum_scatter(up_grad, "fsdp", scatter_dimension=1, tiled=True),
        lax.psum_scatter(down_grad, "fsdp", scatter_dimension=1, tiled=True),
    )
    d_shared = d_mixed.astype(jnp.bfloat16)
    shared_second_grad = jnp.einsum(
        "tf,td->fd", shared_act, d_shared, preferred_element_type=jnp.float32
    )
    d_shared_act = jnp.einsum(
        "td,fd->tf", d_shared, shared_second, preferred_element_type=jnp.float32
    )
    d_shared_pre = gelu_back(shared_pre, d_shared_act).astype(jnp.bfloat16)
    shared_first_grad = jnp.einsum(
        "td,tf->df", second_input, d_shared_pre, preferred_element_type=jnp.float32
    )
    d_chosen = gate_share * (
        d_gate_share - jnp.sum(gate_share * d_gate_share, axis=-1, keepdims=True)
    )
    d_logits = jnp.sum(d_chosen[:, :, None] * route_hot, axis=1).astype(jnp.bfloat16)
    router_grad = jnp.einsum(
        "td,te->de", second_input, d_logits, preferred_element_type=jnp.float32
    )
    from_experts = (
        jnp.take(d_returned.reshape(EXPERTS * CAP, model_width), target, axis=0)
        .reshape(-1, 2, model_width)
        .astype(jnp.float32)
    )
    d_second = (
        jnp.einsum("tf,df->td", d_shared_pre, shared_first, preferred_element_type=jnp.float32)
        + jnp.einsum("te,de->td", d_logits, router_full, preferred_element_type=jnp.float32)
        + jnp.sum(from_experts, axis=1)
    )
    mlp_sums = spread(shared_first_grad, shared_second_grad, router_grad)
    d_scale_two = d_second * normed_two
    d_residual = upstream + norm_back(d_second * (1.0 + scale_two), normed_two, inv_two)
    ada_full, qkv_full, out_full = collect(ada_weight, qkv_weight, out_weight)
    d_projected = (gate_one * d_residual).astype(jnp.bfloat16)
    d_gate_one = d_residual * projected
    out_grad = jnp.einsum("td,te->de", attended, d_projected, preferred_element_type=jnp.float32)
    d_attended = jnp.einsum(
        "te,de->td", d_projected, out_full, preferred_element_type=jnp.float32
    ).astype(jnp.bfloat16)
    d_queries, d_keys, d_values = attend_back(
        queries, keys_all, values_all, segment, log_totals, d_attended.reshape(-1, HEADS, head_size)
    )
    d_qkv = jnp.concatenate(
        [
            d_queries.reshape(-1, model_width),
            d_keys.reshape(-1, model_width),
            d_values.reshape(-1, model_width),
        ],
        axis=1,
    ).astype(jnp.bfloat16)
    qkv_grad = jnp.einsum("td,te->de", first_input, d_qkv, preferred_element_type=jnp.float32)
    d_first = jnp.einsum("te,de->td", d_qkv, qkv_full, preferred_element_type=jnp.float32)
    d_scale_one = d_first * normed_one
    tokens_grad = d_residual + norm_back(d_first * (1.0 + scale_one), normed_one, inv_one)
    d_per_row = jnp.concatenate(
        [d_first, d_scale_one, d_gate_one, d_second, d_scale_two, d_gate_two], axis=1
    )
    d_modulation = jnp.einsum(
        "tj,te->je", inside, d_per_row, precision=EXACT, preferred_element_type=jnp.float32
    ).astype(jnp.bfloat16)
    ada_grad = jnp.einsum("jd,je->de", activated, d_modulation, preferred_element_type=jnp.float32)
    d_activated = jnp.einsum(
        "je,de->jd", d_modulation, ada_full, preferred_element_type=jnp.float32
    )
    condition_grad = jax.vjp(jax.nn.silu, cond_float)[1](d_activated)[0]
    attn_sums = spread(ada_grad, qkv_grad, out_grad)
    return (
        output,
        tokens_grad,
        condition_grad,
        attn_sums[0],
        attn_sums[1],
        attn_sums[2],
        mlp_sums[0],
        mlp_sums[1],
        mlp_sums[2],
        expert_sums[0],
        expert_sums[1],
        expert_counts,
    )


def at(d, s, c):
    return (d, 2 * s + c)


def slot(kind, f, d):
    if kind == "cols":
        return (pl.ds(pl.multiple_of(96 * f, 96), 96), pl.ds(pl.multiple_of(768 * d, 768), 768))
    return (pl.ds(pl.multiple_of(192 * d, 192), 192), pl.ds(pl.multiple_of(384 * f, 384), 384))


def half_slot(kind, f, d, h):
    if kind == "cols":
        return (
            pl.ds(pl.multiple_of(96 * f, 96), 96),
            pl.ds(pl.multiple_of(768 * d + 384 * h, 384), 384),
        )
    return (
        pl.ds(pl.multiple_of(192 * d + 96 * h, 96), 96),
        pl.ds(pl.multiple_of(384 * f, 384), 384),
    )


def place():
    d = lax.axis_index("dp")
    f = lax.axis_index("fsdp")
    return d, f // 2, lax.rem(f, 2)


def flip(v, bit):
    return v + bit - 2 * bit * lax.rem(v // bit, 2)


def greet(devices):
    barrier = pltpu.get_barrier_semaphore()
    for device in devices:
        pl.semaphore_signal(barrier, inc=1, device_id=device, device_id_type=MESH)
    pl.semaphore_wait(barrier, len(devices))


def push(src, dst, send_sem, recv_sem, device):
    return pltpu.make_async_remote_copy(
        src_ref=src,
        dst_ref=dst,
        send_sem=send_sem,
        recv_sem=recv_sem,
        device_id=device,
        device_id_type=MESH,
    )


GATHER_SEMS = 3 + 8 + 8 + 20


class Gather:
    def __init__(self, kind, shard, full, ssem, rsem, lsem):
        self.kind, self.shard, self.full = kind, shard, full
        self.ssem, self.rsem, self.lsem = ssem, rsem, lsem
        self.d, self.s, self.c = place()
        self.sent = []

    def f(self, s):
        return 2 * s + self.c

    def go(self, index, where, device, src=None):
        ref = self.full.at[where]
        copy = push(
            ref if src is None else src, ref, self.ssem.at[index], self.rsem.at[index], device
        )
        copy.start()
        self.sent.append(copy)

    def arrived(self, index, where):
        ref = self.full.at[where]
        push(ref, ref, self.ssem.at[index], self.rsem.at[index], at(self.d, self.s, self.c)).wait_recv()

    def start(self):
        d, s, c = self.d, self.s, self.c
        mine = slot(self.kind, self.f(s), d)
        self.own = pltpu.make_async_copy(self.shard, self.full.at[mine], self.lsem)
        self.own.start()
        for k in range(1, 4):
            self.go(k - 1, mine, at(lax.rem(d + k, 4), s, c), self.shard)
        self.go(3, mine, at(d, flip(s, 1), c), self.shard)
        self.go(4, mine, at(d, flip(s, 2), c), self.shard)
        self.go(19, mine, at(d, s, 1 - c), self.shard)

    def spread_z(self, k):
        d, s, c = self.d, self.s, self.c
        source = lax.rem(d + 4 - k, 4)
        block = slot(self.kind, self.f(s), source)
        self.arrived(k - 1, block)
        self.go(3 + 2 * k, block, at(d, flip(s, 1), c))
        self.go(4 + 2 * k, block, at(d, flip(s, 2), c))
        self.go(19 + 5 * k, block, at(d, s, 1 - c))

    def relay(self, k):
        d, s, c = self.d, self.s, self.c
        source = lax.rem(d + 4 - k, 4)
        sx, sy = flip(s, 1), flip(s, 2)
        from_x = slot(self.kind, self.f(sx), source)
        from_y = slot(self.kind, self.f(sy), source)
        self.arrived(3 + 2 * k, from_x)
        self.go(11 + 2 * k, half_slot(self.kind, self.f(sx), source, 0), at(d, sy, c))
        self.go(20 + 5 * k, from_x, at(d, s, 1 - c))
        self.arrived(4 + 2 * k, from_y)
        self.go(12 + 2 * k, half_slot(self.kind, self.f(sy), source, 1), at(d, sx, c))
        self.go(21 + 5 * k, from_y, at(d, s, 1 - c))

    def corner(self, k):
        d, s, c = self.d, self.s, self.c
        source = lax.rem(d + 4 - k, 4)
        sd = flip(flip(s, 1), 2)
        for h in range(2):
            where = half_slot(self.kind, self.f(sd), source, h)
            self.arrived(11 + 2 * k + h, where)
            self.go(22 + 5 * k + h, where, at(d, s, 1 - c))

    def finish(self):
        d, s, c = self.d, self.s, self.c
        sx, sy = flip(s, 1), flip(s, 2)
        sd = flip(sx, 2)
        self.own.wait()
        for k in range(4):
            source = lax.rem(d + 4 - k, 4)
            for j, position in enumerate((s, sx, sy)):
                self.arrived(19 + 5 * k + j, slot(self.kind, 2 * position + 1 - c, source))
            for h in range(2):
                self.arrived(22 + 5 * k + h, half_slot(self.kind, 2 * sd + 1 - c, source, h))
        for copy in self.sent:
            copy.wait_send()


def everyone_else():
    me = lax.axis_index("dp") * 8 + lax.axis_index("fsdp")

    def other(k):
        device = lax.rem(me + k, 32)
        return (device // 8, lax.rem(device, 8))

    return me, other


def open_kernel(
    shard, router, act_ref, ada_ref, full, routers, seen, rows_out,
    heard, part, got, mixed, ssem, rsem, lsem, asem, brsem, rssem, rrsem, tssem, trsem, zssem, zrsem,
):
    me, other = everyone_else()
    d, s, c = place()
    f = 2 * s + c
    barrier = pltpu.get_barrier_semaphore()

    def hello(k, carry):
        pl.semaphore_signal(barrier, inc=1, device_id=other(k), device_id_type=MESH)
        return carry

    lax.fori_loop(1, 32, hello, 0)
    pl.semaphore_wait(barrier, 31)

    def act_copy(k, source):
        device = other(k)
        return push(act_ref.at[device[1]], heard.at[source], asem.at[k], brsem.at[k], device)

    def router_copy(k, source):
        return push(router, routers.at[source], rssem.at[k], rrsem.at[k], other(k))

    def send(k, carry):
        act_copy(k, me).start()
        return carry

    lax.fori_loop(1, 32, send, 0)
    gather = Gather("cols", shard, full, ssem, rsem, lsem.at[0])
    gather.start()
    own_router = pltpu.make_async_copy(router, routers.at[me], lsem.at[1])
    own_router.start()

    def send_router(k, carry):
        router_copy(k, me).start()
        return carry

    lax.fori_loop(1, 32, send_router, 0)
    heard[me] = act_ref[f]

    def take(k, carry):
        copy = act_copy(k, lax.rem(me + 32 - k, 32))
        copy.wait_recv()
        return carry

    lax.fori_loop(1, 32, take, 0)
    everything = heard[...].reshape(256, 128)
    row = lax.broadcasted_iota(jnp.int32, (64, 256), 0)
    column = lax.broadcasted_iota(jnp.int32, (64, 256), 1)
    source = lax.rem(row // 2, 4) * 8 + row // 8
    pick = (column == source * 8 + lax.rem(row, 2)).astype(jnp.bfloat16)
    compact = jnp.dot(
        pick, everything.astype(jnp.bfloat16), preferred_element_type=jnp.float32
    ).astype(jnp.bfloat16)
    seen[...] = jnp.concatenate(
        [compact.astype(jnp.float32), jnp.sum(heard[...], axis=0)], axis=0
    )
    part[...] = jnp.dot(compact, ada_ref[...], preferred_element_type=jnp.float32).reshape(
        8, 8, 1152
    )

    def tile_copy(k):
        target = lax.rem(f + k, 8)
        return push(part.at[target], got.at[k], tssem.at[k], trsem.at[k], (d, target))

    for k in range(1, 8):
        tile_copy(k).start()
    gather.relay(0)
    for k in range(1, 8):
        tile_copy(k).wait_recv()
    total = part[f]
    for k in range(1, 8):
        total = total + got[k]
    mixed[...] = total
    zs = []
    for k in range(1, 4):
        copy = push(mixed, rows_out.at[d], zssem.at[k], zrsem.at[k], at(lax.rem(d + k, 4), s, c))
        copy.start()
        zs.append(copy)
    own_rows = pltpu.make_async_copy(mixed, rows_out.at[d], lsem.at[2])
    own_rows.start()
    gather.corner(0)
    for k in range(1, 4):
        gather.spread_z(k)
    for k in range(1, 4):
        gather.relay(k)
    for k in range(1, 4):
        gather.corner(k)
    gather.finish()
    own_router.wait()
    own_rows.wait()
    for k in range(1, 4):
        push(
            mixed, rows_out.at[lax.rem(d + 4 - k, 4)], zssem.at[k], zrsem.at[k],
            at(lax.rem(d + k, 4), s, c),
        ).wait_recv()
    for copy in zs:
        copy.wait_send()
    for k in range(1, 8):
        tile_copy(k).wait_send()

    def drain(k, carry):
        act_copy(k, me).wait_send()
        copy = router_copy(k, lax.rem(me + 32 - k, 32))
        copy.wait_recv()
        copy.wait_send()
        return carry

    lax.fori_loop(1, 32, drain, 0)


DMA = pltpu.SemaphoreType.DMA
ANYWHERE = pl.BlockSpec(memory_space=pl.ANY)
ONCHIP = pl.BlockSpec(memory_space=pltpu.VMEM)


def opening(shard, router, act, ada):
    return pl.pallas_call(
        open_kernel,
        out_shape=(
            jax.ShapeDtypeStruct((768, 3072), jnp.bfloat16),
            jax.ShapeDtypeStruct((32, 16, 128), jnp.bfloat16),
            jax.ShapeDtypeStruct((72, 128), jnp.float32),
            jax.ShapeDtypeStruct((4, 8, 1152), jnp.float32),
        ),
        in_specs=[ONCHIP] * 4,
        out_specs=(ANYWHERE, ANYWHERE, ONCHIP, ANYWHERE),
        scratch_shapes=[
            pltpu.VMEM((32, 8, 128), jnp.float32),
            pltpu.VMEM((8, 8, 1152), jnp.float32),
            pltpu.VMEM((8, 8, 1152), jnp.float32),
            pltpu.VMEM((8, 1152), jnp.float32),
            DMA((GATHER_SEMS,)), DMA((GATHER_SEMS,)), DMA((3,)),
            DMA((32,)), DMA((32,)), DMA((32,)), DMA((32,)),
            DMA((8,)), DMA((8,)), DMA((4,)), DMA((4,)),
        ],
        compiler_params=pltpu.CompilerParams(collective_id=0, has_side_effects=True),
        name="opening",
    )(shard, router, act, ada)


def group_of(d, s, c):
    return [(j, at(lax.rem(d + j // 2, 4), s, lax.rem(c + j, 2))) for j in range(1, 8)]


class Swap:
    def __init__(self, blocks, out, ssem, rsem, lsem):
        self.blocks, self.out, self.ssem, self.rsem, self.lsem = blocks, out, ssem, rsem, lsem
        self.d, self.s, self.c = place()
        self.me = 2 * self.d + self.c

    def copy(self, j, landing):
        target_d = lax.rem(self.d + j // 2, 4)
        target_c = lax.rem(self.c + j, 2)
        return push(
            self.blocks.at[2 * target_d + target_c],
            self.out.at[landing],
            self.ssem.at[j],
            self.rsem.at[j],
            at(target_d, self.s, target_c),
        )

    def start(self):
        for j in (4, 5, 2, 3, 6, 7, 1):
            self.copy(j, self.me).start()
        self.own = pltpu.make_async_copy(
            self.blocks.at[self.me], self.out.at[self.me], self.lsem
        )
        self.own.start()

    def finish(self):
        self.own.wait()
        for j in range(1, 8):
            source_d = lax.rem(self.d + 4 - j // 2, 4)
            source_c = lax.rem(self.c + j, 2)
            copy = self.copy(j, 2 * source_d + source_c)
            copy.wait_recv()
            copy.wait_send()


def out_kernel(
    rows, grads, up_shard, down_shard, rows_in, grads_in, up_full, down_full,
    s1, r1, s2, r2, ssem, rsem, ssem2, rsem2, lsem,
):
    d, s, c = place()
    greet([device for _, device in group_of(d, s, c)] + [at(d, flip(s, 1), c), at(d, flip(s, 2), c)])
    first = Gather("cols", up_shard, up_full, ssem, rsem, lsem.at[0])
    second = Gather("rows", down_shard, down_full, ssem2, rsem2, lsem.at[1])
    swap_a = Swap(rows, rows_in, s1, r1, lsem.at[2])
    swap_b = Swap(grads, grads_in, s2, r2, lsem.at[3])
    both = (first, second)
    for g in both:
        g.start()
    swap_a.start()
    swap_b.start()
    for g in both:
        g.relay(0)
    for k in range(1, 4):
        for g in both:
            g.spread_z(k)
    for g in both:
        g.corner(0)
    for k in range(1, 4):
        for g in both:
            g.relay(k)
    for k in range(1, 4):
        for g in both:
            g.corner(k)
    for g in both:
        g.finish()
    swap_a.finish()
    swap_b.finish()


def outbound(rows, grads, up_shard, down_shard):
    return pl.pallas_call(
        out_kernel,
        out_shape=(
            jax.ShapeDtypeStruct((8, 144, 768), jnp.bfloat16),
            jax.ShapeDtypeStruct((8, 144, 768), jnp.bfloat16),
            jax.ShapeDtypeStruct((768, 3072), jnp.bfloat16),
            jax.ShapeDtypeStruct((768, 3072), jnp.bfloat16),
        ),
        in_specs=[ONCHIP] * 4,
        out_specs=(ANYWHERE,) * 4,
        scratch_shapes=[DMA((8,))] * 4 + [DMA((GATHER_SEMS,))] * 4 + [DMA((4,))],
        compiler_params=pltpu.CompilerParams(collective_id=1, has_side_effects=True),
        name="outbound",
    )(rows, grads, up_shard, down_shard)


def widened(ref):
    return ref[...].astype(jnp.float32)


class ExpertSum:
    def __init__(self, grad, out, own, near, far, last, outgoing, ssem, rsem, lsem):
        self.grad, self.out, self.own, self.near = grad, out, own, near
        self.far, self.last, self.outgoing = far, last, outgoing
        self.ssem, self.rsem, self.lsem = ssem, rsem, lsem
        self.d, self.s, self.c = place()
        self.sx, self.sy = flip(self.s, 1), flip(self.s, 2)
        self.sd = flip(self.sx, 2)
        self.rows = grad.shape[0] // 8

    def part(self, position, h):
        return self.grad.at[pl.ds(pl.multiple_of((2 * position + h) * self.rows, 32), self.rows)]

    def start(self):
        d, c = self.d, self.c
        self.one = [
            push(self.part(self.sd, 0), self.near.at[0], self.ssem.at[0], self.rsem.at[0], at(d, self.sx, c)),
            push(self.part(self.sd, 1), self.near.at[1], self.ssem.at[1], self.rsem.at[1], at(d, self.sy, c)),
        ]
        self.two = [
            push(self.part(self.sx, 0), self.far.at[0], self.ssem.at[2], self.rsem.at[2], at(d, self.sx, c)),
            push(self.part(self.sy, 1), self.far.at[1], self.ssem.at[3], self.rsem.at[3], at(d, self.sy, c)),
        ]
        for copy in self.one + self.two:
            copy.start()
        self.local = [
            pltpu.make_async_copy(self.part(self.sy, 0), self.own.at[0], self.lsem.at[0]),
            pltpu.make_async_copy(self.part(self.sx, 1), self.own.at[1], self.lsem.at[1]),
            pltpu.make_async_copy(self.part(self.s, 0), self.own.at[2], self.lsem.at[2]),
            pltpu.make_async_copy(self.part(self.s, 1), self.own.at[3], self.lsem.at[3]),
        ]
        for copy in self.local:
            copy.start()

    def join(self):
        d, c = self.d, self.c
        for copy in self.local:
            copy.wait()
        targets = (at(d, self.sy, c), at(d, self.sx, c))
        self.three = []
        for h in range(2):
            self.one[h].wait_recv()
            self.outgoing[h] = (widened(self.own.at[h]) + widened(self.near.at[h])).astype(jnp.bfloat16)
            copy = push(
                self.outgoing.at[h], self.far.at[2 + h], self.ssem.at[4 + h], self.rsem.at[4 + h], targets[h]
            )
            copy.start()
            self.three.append(copy)

    def close(self):
        d, s, c = self.d, self.s, self.c
        for copy in self.two + self.three:
            copy.wait_recv()
        low = (widened(self.own.at[2]) + widened(self.far.at[0])) + widened(self.far.at[2])
        high = (widened(self.own.at[3]) + widened(self.far.at[1])) + widened(self.far.at[3])
        self.outgoing[2] = jnp.where(c == 0, high, low).astype(jnp.bfloat16)
        self.out[c] = jnp.where(c == 0, low, high)
        self.four = push(
            self.outgoing.at[2], self.last, self.ssem.at[6], self.rsem.at[6], at(d, s, 1 - c)
        )
        self.four.start()

    def finish(self):
        self.four.wait_recv()
        self.out[1 - self.c] = widened(self.last)
        for copy in self.one + self.two + self.three + [self.four]:
            copy.wait_send()


def back_kernel(
    rows, grads, up_grad, down_grad, rows_in, grads_in, up_out, down_out,
    uo, un, uf, ul, ug, do, dn, df, dl, dg, s1, r1, s2, r2, s3, r3, s4, r4, lsem, l3, l4,
):
    d, s, c = place()
    greet([device for _, device in group_of(d, s, c)] + [at(d, flip(s, 1), c), at(d, flip(s, 2), c)])
    swap_a = Swap(rows, rows_in, s1, r1, lsem.at[0])
    swap_b = Swap(grads, grads_in, s2, r2, lsem.at[1])
    sums = (
        ExpertSum(up_grad, up_out, uo, un, uf, ul, ug, s3, r3, l3),
        ExpertSum(down_grad, down_out, do, dn, df, dl, dg, s4, r4, l4),
    )
    for each in sums:
        each.start()
    swap_a.start()
    swap_b.start()
    for each in sums:
        each.join()
    for each in sums:
        each.close()
    for each in sums:
        each.finish()
    swap_a.finish()
    swap_b.finish()


def inbound(rows, grads, up_grad, down_grad):
    bf, f32 = jnp.bfloat16, jnp.float32

    def rooms(r, n):
        return [
            pltpu.VMEM((4, r, n), bf),
            pltpu.VMEM((2, r, n), bf),
            pltpu.VMEM((4, r, n), bf),
            pltpu.VMEM((r, n), bf),
            pltpu.VMEM((3, r, n), bf),
        ]

    return pl.pallas_call(
        back_kernel,
        out_shape=(
            jax.ShapeDtypeStruct((8, 144, 768), bf),
            jax.ShapeDtypeStruct((8, 144, 768), bf),
            jax.ShapeDtypeStruct((2, 96, 3072), f32),
            jax.ShapeDtypeStruct((2, 384, 768), f32),
        ),
        in_specs=[ONCHIP, ONCHIP, ANYWHERE, ANYWHERE],
        out_specs=(ANYWHERE, ANYWHERE, ONCHIP, ONCHIP),
        scratch_shapes=rooms(96, 3072)
        + rooms(384, 768)
        + [DMA((8,))] * 8
        + [DMA((2,)), DMA((4,)), DMA((4,))],
        compiler_params=pltpu.CompilerParams(collective_id=2, has_side_effects=True),
        name="inbound",
    )(rows, grads, up_grad, down_grad)


class DenseSum:
    def __init__(self, kind, grad, out, own, mate, near, far, line, ssem, rsem, lsem):
        self.kind, self.grad, self.out = kind, grad, out
        self.own, self.mate, self.near, self.far, self.line = own, mate, near, far, line
        self.ssem, self.rsem, self.lsem = ssem, rsem, lsem
        self.d, self.s, self.c = place()
        self.order = (
            flip(flip(self.s, 1), 2),
            flip(self.s, 1),
            flip(self.s, 2),
            self.s,
        )

    def piece(self, f):
        if self.kind == "cols":
            return self.grad.at[pl.ds(pl.multiple_of(96 * f, 96), 96)]
        return self.grad.at[:, pl.ds(pl.multiple_of(384 * f, 384), 384)]

    def half(self, ref, h):
        if self.kind == "cols":
            return ref.at[:, pl.ds(1536 * h, 1536)]
        return ref.at[pl.ds(384 * h, 384)]

    def quarter(self, ref, q):
        if self.kind == "cols":
            return ref.at[:, pl.ds(pl.multiple_of(768 * q, 768), 768)]
        return ref.at[pl.ds(pl.multiple_of(192 * q, 192), 192)]

    def start(self):
        d, s, c = self.d, self.s, self.c
        self.zero, self.local = [], []
        for j, position in enumerate(self.order):
            copy = push(
                self.piece(2 * position + 1 - c), self.mate.at[j], self.ssem.at[j], self.rsem.at[j], at(d, s, 1 - c)
            )
            copy.start()
            self.zero.append(copy)
            copy = pltpu.make_async_copy(self.piece(2 * position + c), self.own.at[j], self.lsem.at[j])
            copy.start()
            self.local.append(copy)

    def merge(self):
        d, s, c = self.d, self.s, self.c
        sx, sy = flip(s, 1), flip(s, 2)
        self.one = []
        for j in range(4):
            self.zero[j].wait_recv()
            self.local[j].wait()
            self.own[j] = (widened(self.own.at[j]) + widened(self.mate.at[j])).astype(jnp.bfloat16)
            if j == 0:
                for h, target in enumerate((sx, sy)):
                    copy = push(
                        self.half(self.own.at[0], h), self.near.at[h], self.ssem.at[4 + h], self.rsem.at[4 + h],
                        at(d, target, c),
                    )
                    copy.start()
                    self.one.append(copy)

    def join(self):
        d, s, c = self.d, self.s, self.c
        sx, sy = flip(s, 1), flip(s, 2)
        for h, j in ((0, 2), (1, 1)):
            self.one[h].wait_recv()
            where = self.half(self.own.at[j], h)
            where[...] = (widened(where) + widened(self.near.at[h])).astype(jnp.bfloat16)
        self.two = []
        for h, target in enumerate((sx, sy)):
            copy = push(
                self.own.at[1 + h], self.far.at[h], self.ssem.at[6 + h], self.rsem.at[6 + h], at(d, target, c)
            )
            copy.start()
            self.two.append(copy)

    def along(self):
        d, s, c = self.d, self.s, self.c
        for copy in self.two:
            copy.wait_recv()
        self.own[3] = (
            widened(self.own.at[3]) + widened(self.far.at[0]) + widened(self.far.at[1])
        ).astype(jnp.bfloat16)
        self.three = []
        for k in range(1, 4):
            target = lax.rem(d + k, 4)
            copy = push(
                self.quarter(self.own.at[3], target), self.line.at[k - 1], self.ssem.at[7 + k], self.rsem.at[7 + k],
                at(target, s, c),
            )
            copy.start()
            self.three.append(copy)

    def finish(self):
        total = widened(self.quarter(self.own.at[3], self.d))
        for k in range(1, 4):
            self.three[k - 1].wait_recv()
            total = total + widened(self.line.at[k - 1])
        self.out[...] = total
        for copy in self.zero + self.one + self.two + self.three:
            copy.wait_send()


def dense_kernel(kinds, *refs):
    n = len(kinds)
    grads, outs, rest = refs[:n], refs[n : 2 * n], refs[2 * n :]
    d, s, c = place()
    greet(
        [at(lax.rem(d + k, 4), s, c) for k in range(1, 4)]
        + [at(d, s, 1 - c), at(d, flip(s, 1), c), at(d, flip(s, 2), c)]
    )
    sums = [
        DenseSum(kinds[i], grads[i], outs[i], *rest[8 * i : 8 * i + 8]) for i in range(n)
    ]
    for each in sums:
        each.start()
    for each in sums:
        each.merge()
    for each in sums:
        each.join()
    for each in sums:
        each.along()
    for each in sums:
        each.finish()


def dense_sums(kinds, grads, collective_id):
    bf = jnp.bfloat16
    outs, scratch = [], []
    for kind in kinds:
        if kind == "cols":
            piece, half, quarter = (96, 3072), (96, 1536), (96, 768)
        else:
            piece, half, quarter = (768, 384), (384, 384), (192, 384)
        outs.append(jax.ShapeDtypeStruct(quarter, jnp.float32))
        scratch += [
            pltpu.VMEM((4,) + piece, bf),
            pltpu.VMEM((4,) + piece, bf),
            pltpu.VMEM((2,) + half, bf),
            pltpu.VMEM((2,) + piece, bf),
            pltpu.VMEM((3,) + quarter, bf),
            DMA((11,)),
            DMA((11,)),
            DMA((4,)),
        ]
    return pl.pallas_call(
        functools.partial(dense_kernel, kinds),
        out_shape=tuple(outs),
        in_specs=[ANYWHERE] * len(kinds),
        out_specs=(ONCHIP,) * len(kinds),
        scratch_shapes=scratch,
        compiler_params=pltpu.CompilerParams(collective_id=collective_id, has_side_effects=True),
        name="dense_sums",
    )(*grads)


def nt(left, right):
    return lax.dot_general(left, right, (((1,), (1,)), ((), ())), preferred_element_type=jnp.float32)


def tn(left, right):
    return lax.dot_general(left, right, (((0,), (0,)), ((), ())), preferred_element_type=jnp.float32)


def nn(left, right):
    return jnp.dot(left, right, preferred_element_type=jnp.float32)


def fitted_shards(
    tokens,
    condition,
    ada_weight,
    qkv_weight,
    out_weight,
    shared_up,
    shared_down,
    router_weight,
    expert_up,
    expert_down,
    routes,
    image_sizes,
    cotangent,
):
    bf = jnp.bfloat16
    d_index, f_index = lax.axis_index("dp"), lax.axis_index("fsdp")
    core = lax.rem(f_index, 2)
    model_width = tokens.shape[1]
    head_size = model_width // HEADS
    inside, segment = owners(image_sizes)
    up_all, down_all = gather_experts(expert_up, expert_down)
    up_mine = lax.dynamic_index_in_dim(up_all, core, 0, keepdims=False)
    down_mine = lax.dynamic_index_in_dim(down_all, core, 0, keepdims=False)
    ids = jnp.arange(EXPERTS, dtype=jnp.int32)
    hot = routes[:, :, None] == ids[None, None, :]
    hot_any = jnp.any(hot, axis=1).astype(bf)
    order = jnp.arange(LONG, dtype=jnp.int32)
    earlier = (order[:, None] > order[None, :]).astype(bf)
    before = nn(earlier, hot_any)
    position = jnp.sum(jnp.where(hot, before[:, None, :], 0.0), axis=-1).astype(jnp.int32)
    target = routes * CAP + position
    places = jnp.arange(EXPERTS * CAP, dtype=jnp.int32)
    send_0 = (places[:, None] == target[None, :, 0]).astype(bf)
    send_1 = (places[:, None] == target[None, :, 1]).astype(bf)
    live = (segment < IMG_DEV).astype(jnp.float32)
    counts = jnp.sum(live[:, None] * hot_any.astype(jnp.float32), axis=0)
    cond_float = condition.astype(jnp.float32)
    activated = jax.nn.silu(cond_float).astype(bf)
    act_slices = activated.astype(jnp.float32).reshape(IMG_DEV, 8, 96).transpose(1, 0, 2)
    act_slices = jnp.pad(act_slices, ((0, 0), (0, 6), (0, 32)))
    act_slices = act_slices.at[:, 2, :EXPERTS].set(counts)
    ada_pad = jnp.pad(ada_weight, ((0, 32), (0, 0)))
    router_pack = jnp.pad(router_weight.reshape(192), (0, 2048 - 192)).reshape(16, 128)
    qkvo_shard = jnp.concatenate([qkv_weight, out_weight], axis=1)
    qkvo, routers, seen, mod_rows = opening(qkvo_shard, router_pack, act_slices, ada_pad)
    activated_all = seen[:64, :96].astype(bf)
    expert_counts = seen[66, :EXPERTS].astype(jnp.int32)
    modulation = lax.dynamic_slice(mod_rows, (0, 2 * d_index, 0), (4, 2, 1152))
    modulation = modulation.transpose(1, 0, 2).reshape(2, 4608)
    router_full = (
        routers.reshape(32, 2048)[:, :192]
        .reshape(4, 8, 96, 2)
        .transpose(1, 2, 0, 3)
        .reshape(model_width, EXPERTS)
    )
    qkvo = qkvo.reshape(model_width, 4, 768)
    qkv_full = qkvo[:, :, :576].reshape(model_width, 2304)
    out_full = qkvo[:, :, 576:].reshape(model_width, 768)
    per_row = inside[:, 0:1] * modulation[0:1] + inside[:, 1:2] * modulation[1:2]
    shift_one, scale_one, gate_one, shift_two, scale_two, gate_two = jnp.split(per_row, 6, axis=1)
    token_float = tokens.astype(jnp.float32)
    normed_one, inv_one = layer_norm(token_float)
    first_input = (normed_one * (1.0 + scale_one) + shift_one).astype(bf)
    qkv_rows = nn(first_input, qkv_full).astype(bf)
    queries, keys, values = (
        qkv_rows[:, i * model_width : (i + 1) * model_width]
        .reshape(LONG, HEADS, head_size)
        .transpose(1, 0, 2)
        for i in range(3)
    )
    scale = head_size**-0.5
    allowed = (segment[:, None] == segment[None, :])[None]
    scores = jnp.einsum("hqd,hkd->hqk", queries, keys, preferred_element_type=jnp.float32) * scale
    scores = jnp.where(allowed, scores, -1e30)
    row_max = jnp.max(scores, axis=-1, keepdims=True)
    weight = jnp.exp(scores - row_max)
    running = jnp.sum(weight, axis=-1, keepdims=True)
    probability = weight / running
    prob_low = probability.astype(bf)
    attended = jnp.einsum("hqk,hkd->hqd", prob_low, values, preferred_element_type=jnp.float32)
    attended = attended.astype(bf).transpose(1, 0, 2).reshape(LONG, model_width)
    projected = nn(attended, out_full)
    residual_one = token_float + gate_one * projected
    normed_two, inv_two = layer_norm(residual_one)
    second_input = (normed_two * (1.0 + scale_two) + shift_two).astype(bf)
    logits = nn(second_input, router_full)
    route_hot = hot.astype(jnp.float32)
    chosen = jnp.sum(logits[:, None, :] * route_hot, axis=-1)
    gate_share = jax.nn.softmax(chosen, axis=-1)
    upstream = cotangent.astype(jnp.float32)
    d_mixed = gate_two * upstream
    rows = nn(send_0 + send_1, second_input).astype(bf).reshape(EXPERTS, CAP, model_width)
    weighted = jnp.concatenate(
        [(gate_share[:, k : k + 1] * d_mixed).astype(bf) for k in range(2)], axis=0
    )
    grads = (
        nn(jnp.concatenate([send_0, send_1], axis=1), weighted)
        .astype(bf)
        .reshape(EXPERTS, CAP, model_width)
    )
    rows_in, grads_in, shared_first, shared_second = outbound(rows, grads, shared_up, shared_down.T)
    rows_in = rows_in.reshape(EXPERTS * CAP, model_width)
    grads_in = grads_in.reshape(EXPERTS * CAP, model_width)
    expert_pre = nn(rows_in, up_mine)
    expert_act = gelu_tanh(expert_pre).astype(bf)
    expert_out = nn(expert_act, down_mine).astype(bf)
    d_act = nt(grads_in, down_mine)
    d_pre = gelu_back(expert_pre, d_act).astype(bf)
    d_rows = nt(d_pre, up_mine).astype(bf)
    down_grad = tn(expert_act, grads_in).astype(bf)
    up_grad = tn(rows_in, d_pre).astype(bf)
    returned, d_returned, expert_up_grad, expert_down_grad = inbound(
        expert_out.reshape(EXPERTS, CAP, model_width),
        d_rows.reshape(EXPERTS, CAP, model_width),
        up_grad,
        down_grad,
    )
    returned = returned.reshape(EXPERTS * CAP, model_width)
    d_returned = d_returned.reshape(EXPERTS * CAP, model_width)
    shared_pre = nn(second_input, shared_first)
    shared_act = gelu_tanh(shared_pre).astype(bf)
    shared_out = nt(shared_act, shared_second)
    d_shared = d_mixed.astype(bf)
    shared_second_grad = tn(d_shared, shared_act).astype(bf)
    d_shared_act = nn(d_shared, shared_second)
    d_shared_pre = gelu_back(shared_pre, d_shared_act).astype(bf)
    shared_first_grad = tn(second_input, d_shared_pre).astype(bf)
    d_second = nt(d_shared_pre, shared_first)
    picked_0 = tn(send_0, returned)
    picked_1 = tn(send_1, returned)
    mixed = shared_out + (gate_share[:, 0:1] * picked_0 + gate_share[:, 1:2] * picked_1)
    output = (residual_one + gate_two * mixed).astype(bf)
    d_gate_two = upstream * mixed
    d_gate_share = jnp.stack(
        [jnp.sum(d_mixed * picked_0, axis=-1), jnp.sum(d_mixed * picked_1, axis=-1)], axis=1
    )
    d_chosen = gate_share * (
        d_gate_share - jnp.sum(gate_share * d_gate_share, axis=-1, keepdims=True)
    )
    d_logits = jnp.sum(d_chosen[:, :, None] * route_hot, axis=1).astype(bf)
    router_grad = tn(d_logits, second_input)
    d_second = d_second + nt(d_logits, router_full) + tn(send_0 + send_1, d_returned)
    d_scale_two = d_second * normed_two
    d_residual = upstream + norm_back(d_second * (1.0 + scale_two), normed_two, inv_two)
    d_projected = (gate_one * d_residual).astype(bf)
    d_gate_one = d_residual * projected
    out_grad = tn(attended, d_projected)
    d_attended = nt(d_projected, out_full).astype(bf)
    d_attended = d_attended.reshape(LONG, HEADS, head_size).transpose(1, 0, 2)
    d_prob = jnp.einsum("hqd,hkd->hqk", d_attended, values, preferred_element_type=jnp.float32)
    d_scores = (
        probability * (d_prob - jnp.sum(probability * d_prob, axis=-1, keepdims=True))
    ).astype(bf)
    d_queries = jnp.einsum("hqk,hkd->hqd", d_scores, keys, preferred_element_type=jnp.float32) * scale
    d_keys = jnp.einsum("hqk,hqd->hkd", d_scores, queries, preferred_element_type=jnp.float32) * scale
    d_values = jnp.einsum("hqk,hqd->hkd", prob_low, d_attended, preferred_element_type=jnp.float32)
    d_qkv = jnp.concatenate(
        [
            piece.astype(bf).transpose(1, 0, 2).reshape(LONG, model_width)
            for piece in (d_queries, d_keys, d_values)
        ],
        axis=1,
    )
    qkv_grad = tn(first_input, d_qkv)
    d_first = nt(d_qkv, qkv_full)
    d_scale_one = d_first * normed_one
    tokens_grad = d_residual + norm_back(d_first * (1.0 + scale_one), normed_one, inv_one)
    qkvo_grad = (
        jnp.concatenate(
            [qkv_grad.reshape(model_width, 4, 576), out_grad.reshape(model_width, 4, 192)], axis=2
        )
        .astype(bf)
        .reshape(model_width, 3072)
    )
    d_modulation = jnp.concatenate(
        [
            jnp.stack([jnp.sum(inside[:, j : j + 1] * piece, axis=0) for j in range(IMG_DEV)])
            for piece in (d_first, d_scale_one, d_gate_one, d_second, d_scale_two, d_gate_two)
        ],
        axis=1,
    ).astype(bf)
    shared_first_sum, shared_second_sum, qkvo_sum = dense_sums(
        ("cols", "rows", "cols"), (shared_first_grad, shared_second_grad, qkvo_grad), 3
    )
    d_mod_all = lax.all_gather(d_modulation, ("dp", "fsdp"), axis=0)
    d_mod_all = lax.dynamic_slice(d_mod_all, (0, 0, 1152 * d_index), (32, 2, 1152))
    d_mod_all = d_mod_all.reshape(4, 8, 2, 1152).transpose(1, 0, 2, 3).reshape(64, 1152)
    ada_grad = tn(activated_all, d_mod_all)
    partial = nt(d_mod_all, ada_weight).reshape(8, 4, 2, 96)
    partial_all = lax.all_gather(partial, ("dp", "fsdp"), axis=0)
    partial_mine = lax.dynamic_slice(
        partial_all, (0, f_index, d_index, 0, 0), (32, 1, 1, 2, 96)
    ).reshape(4, 8, 2, 96)
    d_activated = jnp.sum(partial_mine, axis=0).transpose(1, 0, 2).reshape(2, 768)
    condition_grad = jax.vjp(jax.nn.silu, cond_float)[1](d_activated)[0]
    router_sum = lax.psum(router_grad, ("dp", "fsdp"))
    router_out = lax.dynamic_slice(router_sum, (2 * d_index, 96 * f_index), (2, 96)).T
    return (
        output,
        tokens_grad,
        condition_grad,
        ada_grad,
        qkvo_sum[:, :576],
        qkvo_sum[:, 576:],
        shared_first_sum,
        shared_second_sum.T,
        router_out,
        expert_up_grad,
        expert_down_grad,
        expert_counts,
    )


def solution(mesh):
    placed = (
        P(("dp", "fsdp"), None),
        P(("dp", "fsdp"), None),
        P("fsdp", "dp"),
        P("fsdp", "dp"),
        P("fsdp", "dp"),
        P("fsdp", "dp"),
        P("fsdp", "dp"),
        P("fsdp", "dp"),
        P("dp", "fsdp", None),
        P("dp", "fsdp", None),
        P(("dp", "fsdp"), None),
        P(("dp", "fsdp")),
        P(("dp", "fsdp"), None),
    )
    fitted = mesh.shape["dp"] == 4 and mesh.shape["fsdp"] == 8
    return jax.shard_map(
        fitted_shards if fitted else shards,
        mesh=mesh,
        in_specs=placed,
        out_specs=(
            P(("dp", "fsdp"), None),
            P(("dp", "fsdp"), None),
            P(("dp", "fsdp"), None),
            P("fsdp", "dp"),
            P("fsdp", "dp"),
            P("fsdp", "dp"),
            P("fsdp", "dp"),
            P("fsdp", "dp"),
            P("fsdp", "dp"),
            P("dp", "fsdp", None),
            P("dp", "fsdp", None),
            P(),
        ),
        check_vma=False,
    )
```

```python
import functools

import jax
import jax.numpy as jnp
from jax import lax
from jax.experimental import pallas as pl
from jax.experimental.pallas import tpu as pltpu
from jax.sharding import PartitionSpec as P

HEADS = 12
EXPERTS = 8
CAP = 144
IMG_DEV = 2
LONG = 512
MESH = pl.DeviceIdType.MESH


EXACT = lax.Precision.HIGHEST


def owners(image_sizes):
    starts = jnp.cumsum(image_sizes) - image_sizes
    position = jnp.arange(LONG, dtype=jnp.int32)[:, None]
    inside = (position >= starts[None, :]) & (position < (starts + image_sizes)[None, :])
    slot_ids = jnp.arange(IMG_DEV, dtype=jnp.int32)
    segment = jnp.sum(jnp.where(inside, slot_ids[None, :], 0), axis=1) + jnp.where(
        jnp.any(inside, axis=1), 0, IMG_DEV
    )
    return (inside.astype(jnp.float32), segment)


def dispatch_plan(routes):
    flat = routes.reshape(-1)
    onehot = (flat[:, None] == jnp.arange(EXPERTS, dtype=jnp.int32)[None, :]).astype(jnp.int32)
    before = jnp.cumsum(onehot, axis=0) - onehot
    position = jnp.sum(before * onehot, axis=1)
    target = flat * CAP + position
    assignment = jnp.arange(2 * LONG, dtype=jnp.int32)
    source = jnp.zeros((EXPERTS * CAP,), jnp.int32).at[target].set(assignment)
    filled = jnp.zeros((EXPERTS * CAP,), jnp.int32).at[target].set(1)
    return (target, source, filled)


def layer_norm(values_in):
    centred = values_in - jnp.mean(values_in, axis=-1, keepdims=True)
    inv_std = lax.rsqrt(jnp.mean(centred * centred, axis=-1, keepdims=True) + 1e-06)
    return (centred * inv_std, inv_std)


def norm_back(upstream, normed, inv_std):
    return (
        upstream
        - jnp.mean(upstream, axis=-1, keepdims=True)
        - normed * jnp.mean(upstream * normed, axis=-1, keepdims=True)
    ) * inv_std


def gelu_tanh(values_in):
    return jax.nn.gelu(values_in, approximate=True)


def gelu_back(values_in, upstream):
    return jax.vjp(gelu_tanh, values_in)[1](upstream)[0]


def collect(first, second, third):
    widened = (
        lax.all_gather(first, "dp", axis=1, tiled=True),
        lax.all_gather(second, "dp", axis=1, tiled=True),
        lax.all_gather(third, "dp", axis=1, tiled=True),
    )
    return (
        lax.all_gather(widened[0], "fsdp", axis=0, tiled=True),
        lax.all_gather(widened[1], "fsdp", axis=0, tiled=True),
        lax.all_gather(widened[2], "fsdp", axis=0, tiled=True),
    )


def spread(first, second, third):
    row_sums = (
        lax.psum_scatter(first, "fsdp", scatter_dimension=0, tiled=True),
        lax.psum_scatter(second, "fsdp", scatter_dimension=0, tiled=True),
        lax.psum_scatter(third, "fsdp", scatter_dimension=0, tiled=True),
    )
    return (
        lax.psum_scatter(row_sums[0], "dp", scatter_dimension=1, tiled=True),
        lax.psum_scatter(row_sums[1], "dp", scatter_dimension=1, tiled=True),
        lax.psum_scatter(row_sums[2], "dp", scatter_dimension=1, tiled=True),
    )


def gather_experts(up_shard, down_shard):
    return (
        lax.all_gather(up_shard, "fsdp", axis=1, tiled=True),
        lax.all_gather(down_shard, "fsdp", axis=1, tiled=True),
    )


def expert_forward(buffer_in, up_full, down_full):
    expert_pre = jnp.einsum(
        "secd,edf->secf", buffer_in, up_full, preferred_element_type=jnp.float32
    )
    expert_act = gelu_tanh(expert_pre).astype(jnp.bfloat16)
    expert_out = jnp.einsum(
        "secf,efd->secd", expert_act, down_full, preferred_element_type=jnp.float32
    ).astype(jnp.bfloat16)
    return (expert_pre, expert_act, expert_out)


def expert_backward(buffer_in, expert_pre, expert_act, d_out, up_full, down_full):
    d_act = jnp.einsum("secd,efd->secf", d_out, down_full, preferred_element_type=jnp.float32)
    d_pre = gelu_back(expert_pre, d_act).astype(jnp.bfloat16)
    d_rows = jnp.einsum(
        "secf,edf->secd", d_pre, up_full, preferred_element_type=jnp.float32
    ).astype(jnp.bfloat16)
    down_grad = jnp.einsum("secf,secd->efd", expert_act, d_out, preferred_element_type=jnp.float32)
    up_grad = jnp.einsum("secd,secf->edf", buffer_in, d_pre, preferred_element_type=jnp.float32)
    return (up_grad, down_grad, d_rows)


def attend(queries, keys_all, values_all, segment):
    row_count, head_count, head_size = queries.shape
    block_rows = min(512, row_count)
    block_count = row_count // block_rows
    score_scale = head_size ** (-0.5)

    def one_block(pieces):
        query_part, segment_part = pieces
        allowed = (segment_part[:, None] == segment[None, :])[None]
        scores = (
            jnp.einsum("qhd,khd->hqk", query_part, keys_all, preferred_element_type=jnp.float32)
            * score_scale
        )
        scores = jnp.where(allowed, scores, -1e30)
        row_max = jnp.max(scores, axis=-1, keepdims=True)
        weight = jnp.exp(scores - row_max)
        running = jnp.sum(weight, axis=-1, keepdims=True)
        probability = (weight / running).astype(jnp.bfloat16)
        attended = jnp.einsum(
            "hqk,khd->qhd", probability, values_all, preferred_element_type=jnp.float32
        )
        return (attended.astype(jnp.bfloat16), (row_max + jnp.log(running))[:, :, 0])

    return lax.map(
        one_block,
        (
            queries.reshape(block_count, block_rows, head_count, head_size),
            segment.reshape(block_count, block_rows),
        ),
    )


def attend_back(queries, keys_all, values_all, segment, log_totals, d_attended):
    row_count, head_count, head_size = queries.shape
    block_rows = min(512, row_count)
    block_count = row_count // block_rows
    score_scale = head_size ** (-0.5)

    def one_block(carry, pieces):
        key_sum, value_sum = carry
        query_part, segment_part, total_part, grad_part = pieces
        allowed = (segment_part[:, None] == segment[None, :])[None]
        scores = (
            jnp.einsum("qhd,khd->hqk", query_part, keys_all, preferred_element_type=jnp.float32)
            * score_scale
        )
        scores = jnp.where(allowed, scores, -1e30)
        probability = jnp.exp(scores - total_part[:, :, None])
        d_prob = jnp.einsum(
            "qhd,khd->hqk", grad_part, values_all, preferred_element_type=jnp.float32
        )
        d_scores = (
            probability * (d_prob - jnp.sum(probability * d_prob, axis=-1, keepdims=True))
        ).astype(jnp.bfloat16)
        query_grad = (
            jnp.einsum("hqk,khd->qhd", d_scores, keys_all, preferred_element_type=jnp.float32)
            * score_scale
        )
        key_sum = (
            key_sum
            + jnp.einsum("hqk,qhd->khd", d_scores, query_part, preferred_element_type=jnp.float32)
            * score_scale
        )
        value_sum = value_sum + jnp.einsum(
            "hqk,qhd->khd",
            probability.astype(jnp.bfloat16),
            grad_part,
            preferred_element_type=jnp.float32,
        )
        return ((key_sum, value_sum), query_grad)

    empty = jnp.zeros(keys_all.shape, jnp.float32)
    sums, query_grads = lax.scan(
        one_block,
        (empty, empty),
        (
            queries.reshape(block_count, block_rows, head_count, head_size),
            segment.reshape(block_count, block_rows),
            log_totals,
            d_attended.reshape(block_count, block_rows, head_count, head_size),
        ),
    )
    return (query_grads.reshape(row_count, head_count, head_size), sums[0], sums[1])


def shards(
    tokens,
    condition,
    ada_weight,
    qkv_weight,
    out_weight,
    shared_up,
    shared_down,
    router_weight,
    expert_up,
    expert_down,
    routes,
    image_sizes,
    cotangent,
):
    model_width = tokens.shape[1]
    head_size = model_width // HEADS
    inside, segment = owners(image_sizes)
    target, source, filled = dispatch_plan(routes)
    route_hot = (routes[:, :, None] == jnp.arange(EXPERTS, dtype=jnp.int32)[None, None, :]).astype(
        jnp.float32
    )
    live = (segment < IMG_DEV).astype(jnp.int32)
    local_counts = jnp.sum(live[:, None, None] * route_hot.astype(jnp.int32), axis=(0, 1))
    expert_counts = lax.psum(local_counts, ("dp", "fsdp"))
    ada_full, qkv_full, out_full = collect(ada_weight, qkv_weight, out_weight)
    cond_float = condition.astype(jnp.float32)
    activated = jax.nn.silu(cond_float).astype(jnp.bfloat16)
    modulation = jnp.dot(activated, ada_full, preferred_element_type=jnp.float32)
    per_row = jnp.dot(inside, modulation, precision=EXACT, preferred_element_type=jnp.float32)
    shift_one, scale_one, gate_one, shift_two, scale_two, gate_two = jnp.split(per_row, 6, axis=1)
    token_float = tokens.astype(jnp.float32)
    normed_one, inv_one = layer_norm(token_float)
    first_input = (normed_one * (1.0 + scale_one) + shift_one).astype(jnp.bfloat16)
    qkv_rows = jnp.dot(first_input, qkv_full, preferred_element_type=jnp.float32).astype(
        jnp.bfloat16
    )
    queries = qkv_rows[:, :model_width].reshape(-1, HEADS, head_size)
    keys_all = qkv_rows[:, model_width : 2 * model_width].reshape(-1, HEADS, head_size)
    values_all = qkv_rows[:, 2 * model_width :].reshape(-1, HEADS, head_size)
    attended_blocks, log_totals = attend(queries, keys_all, values_all, segment)
    attended = attended_blocks.reshape(-1, model_width)
    projected = jnp.dot(attended, out_full, preferred_element_type=jnp.float32)
    residual_one = token_float + gate_one * projected
    normed_two, inv_two = layer_norm(residual_one)
    second_input = (normed_two * (1.0 + scale_two) + shift_two).astype(jnp.bfloat16)
    shared_first, shared_second, router_full = collect(shared_up, shared_down, router_weight)
    shared_pre = jnp.dot(second_input, shared_first, preferred_element_type=jnp.float32)
    shared_act = gelu_tanh(shared_pre).astype(jnp.bfloat16)
    shared_out = jnp.dot(shared_act, shared_second, preferred_element_type=jnp.float32)
    logits = jnp.dot(second_input, router_full, preferred_element_type=jnp.float32)
    chosen = jnp.sum(logits[:, None, :] * route_hot, axis=-1)
    gate_share = jax.nn.softmax(chosen, axis=-1)
    buffer_rows = jnp.take(second_input, source // 2, axis=0).reshape(EXPERTS, CAP, model_width)
    up_full, down_full = gather_experts(expert_up, expert_down)
    groups = lax.axis_size("dp")
    expert_in = lax.all_to_all(
        buffer_rows.reshape(groups, EXPERTS // groups, CAP, model_width),
        "dp",
        split_axis=0,
        concat_axis=0,
        tiled=True,
    )
    expert_pre, expert_act, expert_out = expert_forward(expert_in, up_full, down_full)
    returned = lax.all_to_all(expert_out, "dp", split_axis=0, concat_axis=0, tiled=True).reshape(
        EXPERTS, CAP, model_width
    )
    picked = (
        jnp.take(returned.reshape(EXPERTS * CAP, model_width), target, axis=0)
        .reshape(-1, 2, model_width)
        .astype(jnp.float32)
    )
    mixed = shared_out + jnp.sum(gate_share[:, :, None] * picked, axis=1)
    output = (residual_one + gate_two * mixed).astype(jnp.bfloat16)
    upstream = cotangent.astype(jnp.float32)
    d_mixed = gate_two * upstream
    d_gate_two = upstream * mixed
    d_gate_share = jnp.sum(d_mixed[:, None, :] * picked, axis=-1)
    slot_gate = jnp.take(gate_share.reshape(-1), source) * filled.astype(jnp.float32)
    d_buffer = (
        (jnp.take(d_mixed, source // 2, axis=0) * slot_gate[:, None])
        .astype(jnp.bfloat16)
        .reshape(EXPERTS, CAP, model_width)
    )
    shared_first, shared_second, router_full = collect(shared_up, shared_down, router_weight)
    up_full, down_full = gather_experts(expert_up, expert_down)
    arrived = lax.all_to_all(
        d_buffer.reshape(groups, EXPERTS // groups, CAP, model_width),
        "dp",
        split_axis=0,
        concat_axis=0,
        tiled=True,
    )
    up_grad, down_grad, d_rows = expert_backward(
        expert_in, expert_pre, expert_act, arrived, up_full, down_full
    )
    d_returned = lax.all_to_all(d_rows, "dp", split_axis=0, concat_axis=0, tiled=True).reshape(
        EXPERTS, CAP, model_width
    )
    expert_sums = (
        lax.psum_scatter(up_grad, "fsdp", scatter_dimension=1, tiled=True),
        lax.psum_scatter(down_grad, "fsdp", scatter_dimension=1, tiled=True),
    )
    d_shared = d_mixed.astype(jnp.bfloat16)
    shared_second_grad = jnp.einsum(
        "tf,td->fd", shared_act, d_shared, preferred_element_type=jnp.float32
    )
    d_shared_act = jnp.einsum(
        "td,fd->tf", d_shared, shared_second, preferred_element_type=jnp.float32
    )
    d_shared_pre = gelu_back(shared_pre, d_shared_act).astype(jnp.bfloat16)
    shared_first_grad = jnp.einsum(
        "td,tf->df", second_input, d_shared_pre, preferred_element_type=jnp.float32
    )
    d_chosen = gate_share * (
        d_gate_share - jnp.sum(gate_share * d_gate_share, axis=-1, keepdims=True)
    )
    d_logits = jnp.sum(d_chosen[:, :, None] * route_hot, axis=1).astype(jnp.bfloat16)
    router_grad = jnp.einsum(
        "td,te->de", second_input, d_logits, preferred_element_type=jnp.float32
    )
    from_experts = (
        jnp.take(d_returned.reshape(EXPERTS * CAP, model_width), target, axis=0)
        .reshape(-1, 2, model_width)
        .astype(jnp.float32)
    )
    d_second = (
        jnp.einsum("tf,df->td", d_shared_pre, shared_first, preferred_element_type=jnp.float32)
        + jnp.einsum("te,de->td", d_logits, router_full, preferred_element_type=jnp.float32)
        + jnp.sum(from_experts, axis=1)
    )
    mlp_sums = spread(shared_first_grad, shared_second_grad, router_grad)
    d_scale_two = d_second * normed_two
    d_residual = upstream + norm_back(d_second * (1.0 + scale_two), normed_two, inv_two)
    ada_full, qkv_full, out_full = collect(ada_weight, qkv_weight, out_weight)
    d_projected = (gate_one * d_residual).astype(jnp.bfloat16)
    d_gate_one = d_residual * projected
    out_grad = jnp.einsum("td,te->de", attended, d_projected, preferred_element_type=jnp.float32)
    d_attended = jnp.einsum(
        "te,de->td", d_projected, out_full, preferred_element_type=jnp.float32
    ).astype(jnp.bfloat16)
    d_queries, d_keys, d_values = attend_back(
        queries, keys_all, values_all, segment, log_totals, d_attended.reshape(-1, HEADS, head_size)
    )
    d_qkv = jnp.concatenate(
        [
            d_queries.reshape(-1, model_width),
            d_keys.reshape(-1, model_width),
            d_values.reshape(-1, model_width),
        ],
        axis=1,
    ).astype(jnp.bfloat16)
    qkv_grad = jnp.einsum("td,te->de", first_input, d_qkv, preferred_element_type=jnp.float32)
    d_first = jnp.einsum("te,de->td", d_qkv, qkv_full, preferred_element_type=jnp.float32)
    d_scale_one = d_first * normed_one
    tokens_grad = d_residual + norm_back(d_first * (1.0 + scale_one), normed_one, inv_one)
    d_per_row = jnp.concatenate(
        [d_first, d_scale_one, d_gate_one, d_second, d_scale_two, d_gate_two], axis=1
    )
    d_modulation = jnp.einsum(
        "tj,te->je", inside, d_per_row, precision=EXACT, preferred_element_type=jnp.float32
    ).astype(jnp.bfloat16)
    ada_grad = jnp.einsum("jd,je->de", activated, d_modulation, preferred_element_type=jnp.float32)
    d_activated = jnp.einsum(
        "je,de->jd", d_modulation, ada_full, preferred_element_type=jnp.float32
    )
    condition_grad = jax.vjp(jax.nn.silu, cond_float)[1](d_activated)[0]
    attn_sums = spread(ada_grad, qkv_grad, out_grad)
    return (
        output,
        tokens_grad,
        condition_grad,
        attn_sums[0],
        attn_sums[1],
        attn_sums[2],
        mlp_sums[0],
        mlp_sums[1],
        mlp_sums[2],
        expert_sums[0],
        expert_sums[1],
        expert_counts,
    )


def at(d, s, c):
    return (d, 2 * s + c)


def slot(kind, f, d):
    if kind == "cols":
        return (pl.ds(pl.multiple_of(96 * f, 96), 96), pl.ds(pl.multiple_of(768 * d, 768), 768))
    return (pl.ds(pl.multiple_of(192 * d, 192), 192), pl.ds(pl.multiple_of(384 * f, 384), 384))


def half_slot(kind, f, d, h):
    if kind == "cols":
        return (
            pl.ds(pl.multiple_of(96 * f, 96), 96),
            pl.ds(pl.multiple_of(768 * d + 384 * h, 384), 384),
        )
    return (
        pl.ds(pl.multiple_of(192 * d + 96 * h, 96), 96),
        pl.ds(pl.multiple_of(384 * f, 384), 384),
    )


def place():
    d = lax.axis_index("dp")
    f = lax.axis_index("fsdp")
    return d, f // 2, lax.rem(f, 2)


def flip(v, bit):
    return v + bit - 2 * bit * lax.rem(v // bit, 2)


def greet(devices):
    barrier = pltpu.get_barrier_semaphore()
    for device in devices:
        pl.semaphore_signal(barrier, inc=1, device_id=device, device_id_type=MESH)
    pl.semaphore_wait(barrier, len(devices))


def push(src, dst, send_sem, recv_sem, device):
    return pltpu.make_async_remote_copy(
        src_ref=src,
        dst_ref=dst,
        send_sem=send_sem,
        recv_sem=recv_sem,
        device_id=device,
        device_id_type=MESH,
    )


GATHER_SEMS = 3 + 8 + 8 + 20


class Gather:
    def __init__(self, kind, shard, full, ssem, rsem, lsem):
        self.kind, self.shard, self.full = kind, shard, full
        self.ssem, self.rsem, self.lsem = ssem, rsem, lsem
        self.d, self.s, self.c = place()
        self.sent = []

    def f(self, s):
        return 2 * s + self.c

    def go(self, index, where, device, src=None):
        ref = self.full.at[where]
        copy = push(
            ref if src is None else src, ref, self.ssem.at[index], self.rsem.at[index], device
        )
        copy.start()
        self.sent.append(copy)

    def arrived(self, index, where):
        ref = self.full.at[where]
        push(ref, ref, self.ssem.at[index], self.rsem.at[index], at(self.d, self.s, self.c)).wait_recv()

    def start(self):
        d, s, c = self.d, self.s, self.c
        mine = slot(self.kind, self.f(s), d)
        self.own = pltpu.make_async_copy(self.shard, self.full.at[mine], self.lsem)
        self.own.start()
        for k in range(1, 4):
            self.go(k - 1, mine, at(lax.rem(d + k, 4), s, c), self.shard)
        self.go(3, mine, at(d, flip(s, 1), c), self.shard)
        self.go(4, mine, at(d, flip(s, 2), c), self.shard)
        self.go(19, mine, at(d, s, 1 - c), self.shard)

    def spread_z(self, k):
        d, s, c = self.d, self.s, self.c
        source = lax.rem(d + 4 - k, 4)
        block = slot(self.kind, self.f(s), source)
        self.arrived(k - 1, block)
        self.go(3 + 2 * k, block, at(d, flip(s, 1), c))
        self.go(4 + 2 * k, block, at(d, flip(s, 2), c))
        self.go(19 + 5 * k, block, at(d, s, 1 - c))

    def relay(self, k):
        d, s, c = self.d, self.s, self.c
        source = lax.rem(d + 4 - k, 4)
        sx, sy = flip(s, 1), flip(s, 2)
        from_x = slot(self.kind, self.f(sx), source)
        from_y = slot(self.kind, self.f(sy), source)
        self.arrived(3 + 2 * k, from_x)
        self.go(11 + 2 * k, half_slot(self.kind, self.f(sx), source, 0), at(d, sy, c))
        self.go(20 + 5 * k, from_x, at(d, s, 1 - c))
        self.arrived(4 + 2 * k, from_y)
        self.go(12 + 2 * k, half_slot(self.kind, self.f(sy), source, 1), at(d, sx, c))
        self.go(21 + 5 * k, from_y, at(d, s, 1 - c))

    def corner(self, k):
        d, s, c = self.d, self.s, self.c
        source = lax.rem(d + 4 - k, 4)
        sd = flip(flip(s, 1), 2)
        for h in range(2):
            where = half_slot(self.kind, self.f(sd), source, h)
            self.arrived(11 + 2 * k + h, where)
            self.go(22 + 5 * k + h, where, at(d, s, 1 - c))

    def finish(self):
        d, s, c = self.d, self.s, self.c
        sx, sy = flip(s, 1), flip(s, 2)
        sd = flip(sx, 2)
        self.own.wait()
        for k in range(4):
            source = lax.rem(d + 4 - k, 4)
            for j, position in enumerate((s, sx, sy)):
                self.arrived(19 + 5 * k + j, slot(self.kind, 2 * position + 1 - c, source))
            for h in range(2):
                self.arrived(22 + 5 * k + h, half_slot(self.kind, 2 * sd + 1 - c, source, h))
        for copy in self.sent:
            copy.wait_send()


def everyone_else():
    me = lax.axis_index("dp") * 8 + lax.axis_index("fsdp")

    def other(k):
        device = lax.rem(me + k, 32)
        return (device // 8, lax.rem(device, 8))

    return me, other


def open_kernel(
    shard, router, act_ref, ada_ref, full, routers, seen, rows_out,
    heard, part, got, mixed, ssem, rsem, lsem, asem, brsem, rssem, rrsem, tssem, trsem, zssem, zrsem,
):
    me, other = everyone_else()
    d, s, c = place()
    f = 2 * s + c
    barrier = pltpu.get_barrier_semaphore()

    def hello(k, carry):
        pl.semaphore_signal(barrier, inc=1, device_id=other(k), device_id_type=MESH)
        return carry

    lax.fori_loop(1, 32, hello, 0)
    pl.semaphore_wait(barrier, 31)

    def act_copy(k, source):
        device = other(k)
        return push(act_ref.at[device[1]], heard.at[source], asem.at[k], brsem.at[k], device)

    def router_copy(k, source):
        return push(router, routers.at[source], rssem.at[k], rrsem.at[k], other(k))

    def send(k, carry):
        act_copy(k, me).start()
        return carry

    lax.fori_loop(1, 32, send, 0)
    gather = Gather("cols", shard, full, ssem, rsem, lsem.at[0])
    gather.start()
    own_router = pltpu.make_async_copy(router, routers.at[me], lsem.at[1])
    own_router.start()

    def send_router(k, carry):
        router_copy(k, me).start()
        return carry

    lax.fori_loop(1, 32, send_router, 0)
    heard[me] = act_ref[f]

    def take(k, carry):
        copy = act_copy(k, lax.rem(me + 32 - k, 32))
        copy.wait_recv()
        return carry

    lax.fori_loop(1, 32, take, 0)
    everything = heard[...].reshape(256, 128)
    row = lax.broadcasted_iota(jnp.int32, (64, 256), 0)
    column = lax.broadcasted_iota(jnp.int32, (64, 256), 1)
    source = lax.rem(row // 2, 4) * 8 + row // 8
    pick = (column == source * 8 + lax.rem(row, 2)).astype(jnp.bfloat16)
    compact = jnp.dot(
        pick, everything.astype(jnp.bfloat16), preferred_element_type=jnp.float32
    ).astype(jnp.bfloat16)
    seen[...] = jnp.concatenate(
        [compact.astype(jnp.float32), jnp.sum(heard[...], axis=0)], axis=0
    )
    part[...] = jnp.dot(compact, ada_ref[...], preferred_element_type=jnp.float32).reshape(
        8, 8, 1152
    )

    def tile_copy(k):
        target = lax.rem(f + k, 8)
        return push(part.at[target], got.at[k], tssem.at[k], trsem.at[k], (d, target))

    for k in range(1, 8):
        tile_copy(k).start()
    gather.relay(0)
    for k in range(1, 8):
        tile_copy(k).wait_recv()
    total = part[f]
    for k in range(1, 8):
        total = total + got[k]
    mixed[...] = total
    zs = []
    for k in range(1, 4):
        copy = push(mixed, rows_out.at[d], zssem.at[k], zrsem.at[k], at(lax.rem(d + k, 4), s, c))
        copy.start()
        zs.append(copy)
    own_rows = pltpu.make_async_copy(mixed, rows_out.at[d], lsem.at[2])
    own_rows.start()
    gather.corner(0)
    for k in range(1, 4):
        gather.spread_z(k)
    for k in range(1, 4):
        gather.relay(k)
    for k in range(1, 4):
        gather.corner(k)
    gather.finish()
    own_router.wait()
    own_rows.wait()
    for k in range(1, 4):
        push(
            mixed, rows_out.at[lax.rem(d + 4 - k, 4)], zssem.at[k], zrsem.at[k],
            at(lax.rem(d + k, 4), s, c),
        ).wait_recv()
    for copy in zs:
        copy.wait_send()
    for k in range(1, 8):
        tile_copy(k).wait_send()

    def drain(k, carry):
        act_copy(k, me).wait_send()
        copy = router_copy(k, lax.rem(me + 32 - k, 32))
        copy.wait_recv()
        copy.wait_send()
        return carry

    lax.fori_loop(1, 32, drain, 0)


DMA = pltpu.SemaphoreType.DMA
ANYWHERE = pl.BlockSpec(memory_space=pl.ANY)
ONCHIP = pl.BlockSpec(memory_space=pltpu.VMEM)


def opening(shard, router, act, ada):
    return pl.pallas_call(
        open_kernel,
        out_shape=(
            jax.ShapeDtypeStruct((768, 3072), jnp.bfloat16),
            jax.ShapeDtypeStruct((32, 16, 128), jnp.bfloat16),
            jax.ShapeDtypeStruct((72, 128), jnp.float32),
            jax.ShapeDtypeStruct((4, 8, 1152), jnp.float32),
        ),
        in_specs=[ONCHIP] * 4,
        out_specs=(ANYWHERE, ANYWHERE, ONCHIP, ANYWHERE),
        scratch_shapes=[
            pltpu.VMEM((32, 8, 128), jnp.float32),
            pltpu.VMEM((8, 8, 1152), jnp.float32),
            pltpu.VMEM((8, 8, 1152), jnp.float32),
            pltpu.VMEM((8, 1152), jnp.float32),
            DMA((GATHER_SEMS,)), DMA((GATHER_SEMS,)), DMA((3,)),
            DMA((32,)), DMA((32,)), DMA((32,)), DMA((32,)),
            DMA((8,)), DMA((8,)), DMA((4,)), DMA((4,)),
        ],
        compiler_params=pltpu.CompilerParams(collective_id=0, has_side_effects=True),
        name="opening",
    )(shard, router, act, ada)


def group_of(d, s, c):
    return [(j, at(lax.rem(d + j // 2, 4), s, lax.rem(c + j, 2))) for j in range(1, 8)]


class Swap:
    def __init__(self, blocks, out, ssem, rsem, lsem):
        self.blocks, self.out, self.ssem, self.rsem, self.lsem = blocks, out, ssem, rsem, lsem
        self.d, self.s, self.c = place()
        self.me = 2 * self.d + self.c

    def copy(self, j, landing):
        target_d = lax.rem(self.d + j // 2, 4)
        target_c = lax.rem(self.c + j, 2)
        return push(
            self.blocks.at[2 * target_d + target_c],
            self.out.at[landing],
            self.ssem.at[j],
            self.rsem.at[j],
            at(target_d, self.s, target_c),
        )

    def start(self):
        for j in (4, 5, 2, 3, 6, 7, 1):
            self.copy(j, self.me).start()
        self.own = pltpu.make_async_copy(
            self.blocks.at[self.me], self.out.at[self.me], self.lsem
        )
        self.own.start()

    def send(self, step):
        for j in (2 * step, 2 * step + 1):
            if j:
                self.copy(j, self.me).start()
            else:
                self.own = pltpu.make_async_copy(
                    self.blocks.at[self.me], self.out.at[self.me], self.lsem
                )
                self.own.start()

    def finish(self):
        self.own.wait()
        for j in range(1, 8):
            source_d = lax.rem(self.d + 4 - j // 2, 4)
            source_c = lax.rem(self.c + j, 2)
            copy = self.copy(j, 2 * source_d + source_c)
            copy.wait_recv()
            copy.wait_send()


def nt(left, right):
    return lax.dot_general(left, right, (((1,), (1,)), ((), ())), preferred_element_type=jnp.float32)


def tn(left, right):
    return lax.dot_general(left, right, (((0,), (0,)), ((), ())), preferred_element_type=jnp.float32)


def nn(left, right):
    return jnp.dot(left, right, preferred_element_type=jnp.float32)


GELU_SCALE = 0.7978845608028654


def gelu_pair(v):
    square = v * v
    bend = jnp.tanh(GELU_SCALE * (v + 0.044715 * (square * v)))
    half = 0.5 * (1.0 + bend)
    slope = half + 0.5 * v * (1.0 - bend * bend) * (
        GELU_SCALE * (1.0 + (3.0 * 0.044715) * square)
    )
    return v * half, slope


HIDDEN = 512


def out_kernel(
    rows, grads, up_shard, down_shard, tokens, d_tokens,
    rows_in, grads_in, mixed_out, d_tokens_out, up_grad, down_grad,
    up_full, down_full, s1, r1, s2, r2, ssem, rsem, ssem2, rsem2, lsem,
):
    d, s, c = place()
    greet([device for _, device in group_of(d, s, c)] + [at(d, flip(s, 1), c), at(d, flip(s, 2), c)])
    first = Gather("cols", up_shard, up_full, ssem, rsem, lsem.at[0])
    second = Gather("rows", down_shard, down_full, ssem2, rsem2, lsem.at[1])
    swap_a = Swap(rows, rows_in, s1, r1, lsem.at[2])
    swap_b = Swap(grads, grads_in, s2, r2, lsem.at[3])
    both = (first, second)
    for g in both:
        g.start()
    swap_a.start()
    swap_b.start()
    for g in both:
        g.relay(0)
    for k in range(1, 4):
        for g in both:
            g.spread_z(k)
    for g in both:
        g.corner(0)
    for k in range(1, 4):
        for g in both:
            g.relay(k)
    for k in range(1, 4):
        for g in both:
            g.corner(k)
    for g in both:
        g.finish()

    mixed_out[...] = jnp.zeros_like(mixed_out)
    d_tokens_out[...] = jnp.zeros_like(d_tokens_out)

    def block(b, carry):
        where = pl.ds(pl.multiple_of(b * HIDDEN, HIDDEN), HIDDEN)
        up, down = up_full[:, where], down_full[:, where]
        act, slope = gelu_pair(nn(tokens[...], up))
        act = act.astype(jnp.bfloat16)
        mixed_out[...] += nt(act, down)
        down_grad[:, where] = tn(d_tokens[...], act).astype(jnp.bfloat16)
        d_pre = (slope * nn(d_tokens[...], down)).astype(jnp.bfloat16)
        d_tokens_out[...] += nt(d_pre, up)
        up_grad[:, where] = tn(tokens[...], d_pre).astype(jnp.bfloat16)
        return carry

    lax.fori_loop(0, 3072 // HIDDEN, block, 0)
    swap_a.finish()
    swap_b.finish()


def outbound(rows, grads, up_shard, down_shard, tokens, d_tokens):
    bf, f32 = jnp.bfloat16, jnp.float32
    return pl.pallas_call(
        out_kernel,
        out_shape=(
            jax.ShapeDtypeStruct((8, 144, 768), bf),
            jax.ShapeDtypeStruct((8, 144, 768), bf),
            jax.ShapeDtypeStruct((512, 768), f32),
            jax.ShapeDtypeStruct((512, 768), f32),
            jax.ShapeDtypeStruct((768, 3072), bf),
            jax.ShapeDtypeStruct((768, 3072), bf),
        ),
        in_specs=[ONCHIP] * 6,
        out_specs=(ANYWHERE,) * 2 + (ONCHIP,) * 4,
        scratch_shapes=[pltpu.VMEM((768, 3072), bf)] * 2
        + [DMA((8,))] * 4
        + [DMA((GATHER_SEMS,))] * 4
        + [DMA((4,))],
        compiler_params=pltpu.CompilerParams(
            collective_id=1, has_side_effects=True, vmem_limit_bytes=60 << 20
        ),
        name="outbound",
    )(rows, grads, up_shard, down_shard, tokens, d_tokens)


def widened(ref):
    return ref[...].astype(jnp.float32)


class ExpertSum:
    def __init__(self, grad, out, near, far, last, outgoing, ssem, rsem):
        self.grad, self.out, self.near = grad, out, near
        self.far, self.last, self.outgoing = far, last, outgoing
        self.ssem, self.rsem = ssem, rsem
        self.d, self.s, self.c = place()
        self.sx, self.sy = flip(self.s, 1), flip(self.s, 2)
        self.sd = flip(self.sx, 2)
        self.rows = grad.shape[0] // 8

    def part(self, position, h):
        return self.grad.at[pl.ds(pl.multiple_of((2 * position + h) * self.rows, 32), self.rows)]

    def copy(self, index, src, dst, position):
        copy = push(src, dst, self.ssem.at[index], self.rsem.at[index], at(self.d, position, self.c))
        copy.start()
        return copy

    def send_corner(self):
        self.one = [
            self.copy(0, self.part(self.sd, 0), self.near.at[0], self.sx),
            self.copy(1, self.part(self.sd, 1), self.near.at[1], self.sy),
        ]

    def send_y(self):
        self.two_y = self.copy(3, self.part(self.sy, 1), self.far.at[1], self.sy)

    def send_x(self):
        self.two_x = self.copy(2, self.part(self.sx, 0), self.far.at[0], self.sx)

    def join_y(self):
        self.one[0].wait_recv()
        self.outgoing[0] = (widened(self.part(self.sy, 0)) + widened(self.near.at[0])).astype(jnp.bfloat16)
        self.three_y = self.copy(4, self.outgoing.at[0], self.far.at[2], self.sy)

    def join_x(self):
        self.one[1].wait_recv()
        self.outgoing[1] = (widened(self.part(self.sx, 1)) + widened(self.near.at[1])).astype(jnp.bfloat16)
        self.three_x = self.copy(5, self.outgoing.at[1], self.far.at[3], self.sx)

    def close(self):
        d, s, c = self.d, self.s, self.c
        for copy in (self.two_x, self.two_y, self.three_x, self.three_y):
            copy.wait_recv()
        mine, theirs = c, 1 - c
        self.outgoing[2] = (
            widened(self.part(s, theirs)) + widened(self.far.at[theirs]) + widened(self.far.at[2 + theirs])
        ).astype(jnp.bfloat16)
        self.four = push(
            self.outgoing.at[2], self.last, self.ssem.at[6], self.rsem.at[6], at(d, s, 1 - c)
        )
        self.four.start()
        self.out[c] = widened(self.part(s, mine)) + widened(self.far.at[mine]) + widened(self.far.at[2 + mine])

    def finish(self):
        self.four.wait_recv()
        self.out[1 - self.c] = widened(self.last)
        for copy in self.one + [self.two_x, self.two_y, self.three_x, self.three_y, self.four]:
            copy.wait_send()


def expert_kernel(
    rows, grads, up_all, down_all, rows_back, grads_back, up_out, down_out,
    up, down, act, d_pre, made, d_made, total, d_total, up_grad, down_grad,
    un, uf, ul, ug, dn, df, dl, dg, s1, r1, s2, r2, s3, r3, s4, r4, lsem, wsem,
):
    bf = jnp.bfloat16
    d, s, c = place()
    weights = [
        pltpu.make_async_copy(up_all.at[c], up, wsem.at[0]),
        pltpu.make_async_copy(down_all.at[c], down, wsem.at[1]),
    ]
    for copy in weights:
        copy.start()
    greet([device for _, device in group_of(d, s, c)] + [at(d, flip(s, 1), c), at(d, flip(s, 2), c)])
    swap_a = Swap(made, rows_back, s1, r1, lsem.at[0])
    swap_b = Swap(d_made, grads_back, s2, r2, lsem.at[1])
    for copy in weights:
        copy.wait()
    for step in (2, 1, 3, 0):
        there = lax.rem(d + step, 4)
        chunk = pl.ds(2 * there, 2)
        lines = pl.ds(pl.multiple_of(288 * there, 288), 288)
        x = rows[chunk].reshape(288, 768)
        g = grads[chunk].reshape(288, 768)
        total[...] = jnp.zeros_like(total)
        d_total[...] = jnp.zeros_like(d_total)

        def block(b, carry):
            where = pl.ds(pl.multiple_of(b * HIDDEN, HIDDEN), HIDDEN)
            up_part, down_part = up[:, where], down[where]
            made_act, slope = gelu_pair(nn(x, up_part))
            made_act = made_act.astype(bf)
            act[lines, where] = made_act
            total[...] += nn(made_act, down_part)
            d_part = (slope * nt(g, down_part)).astype(bf)
            d_pre[lines, where] = d_part
            d_total[...] += nt(d_part, up_part)
            return carry

        lax.fori_loop(0, 3072 // HIDDEN, block, 0)
        made[chunk] = total[...].astype(bf).reshape(2, 144, 768)
        d_made[chunk] = d_total[...].astype(bf).reshape(2, 144, 768)
        swap_a.send(step)
        swap_b.send(step)
    first = ExpertSum(up_grad, up_out, un, uf, ul, ug, s3, r3)
    second = ExpertSum(down_grad, down_out, dn, df, dl, dg, s4, r4)
    x_all = rows.reshape(1152, 768)
    g_all = grads.reshape(1152, 768)
    y = s // 2

    def up_rows(side):
        here = pl.ds(pl.multiple_of(384 * side, 384), 384)
        x_part = x_all[:, here]

        def block(b, carry):
            where = pl.ds(pl.multiple_of(b * HIDDEN, HIDDEN), HIDDEN)
            up_grad[here, where] = tn(x_part, d_pre[:, where]).astype(bf)
            return carry

        lax.fori_loop(0, 3072 // HIDDEN, block, 0)

    def down_rows(position):
        def block(b, carry):
            where = pl.ds(pl.multiple_of(768 * position + 384 * b, 384), 384)
            down_grad[where] = tn(act[:, where], g_all[...]).astype(bf)
            return carry

        lax.fori_loop(0, 2, block, 0)

    up_rows(1 - y)
    first.send_corner()
    first.send_y()
    down_rows(second.sd)
    second.send_corner()
    first.join_y()
    down_rows(second.sy)
    second.send_y()
    second.join_y()
    up_rows(y)
    first.send_x()
    first.join_x()
    down_rows(second.sx)
    second.send_x()
    second.join_x()
    down_rows(s)
    first.close()
    second.close()
    first.finish()
    second.finish()
    swap_a.finish()
    swap_b.finish()


def experts(rows, grads, up_all, down_all):
    bf, f32 = jnp.bfloat16, jnp.float32

    def rooms(r, n):
        return [
            pltpu.VMEM((2, r, n), bf),
            pltpu.VMEM((4, r, n), bf),
            pltpu.VMEM((r, n), bf),
            pltpu.VMEM((3, r, n), bf),
        ]

    return pl.pallas_call(
        expert_kernel,
        out_shape=(
            jax.ShapeDtypeStruct((8, 144, 768), bf),
            jax.ShapeDtypeStruct((8, 144, 768), bf),
            jax.ShapeDtypeStruct((2, 96, 3072), f32),
            jax.ShapeDtypeStruct((2, 384, 768), f32),
        ),
        in_specs=[ONCHIP, ONCHIP, ANYWHERE, ANYWHERE],
        out_specs=(ANYWHERE, ANYWHERE, ONCHIP, ONCHIP),
        scratch_shapes=[
            pltpu.VMEM((768, 3072), bf),
            pltpu.VMEM((3072, 768), bf),
            pltpu.VMEM((1152, 3072), bf),
            pltpu.VMEM((1152, 3072), bf),
            pltpu.VMEM((8, 144, 768), bf),
            pltpu.VMEM((8, 144, 768), bf),
            pltpu.VMEM((288, 768), f32),
            pltpu.VMEM((288, 768), f32),
            pltpu.VMEM((768, 3072), bf),
            pltpu.VMEM((3072, 768), bf),
        ]
        + rooms(96, 3072)
        + rooms(384, 768)
        + [DMA((8,))] * 8
        + [DMA((2,)), DMA((2,))],
        compiler_params=pltpu.CompilerParams(
            collective_id=2, has_side_effects=True, vmem_limit_bytes=67043328
        ),
        name="experts",
    )(rows, grads, up_all, down_all)


class DenseSum:
    def __init__(self, kind, grad, out, own, mate, near, far, line, ssem, rsem, lsem):
        self.kind, self.grad, self.out = kind, grad, out
        self.own, self.mate, self.near, self.far, self.line = own, mate, near, far, line
        self.ssem, self.rsem, self.lsem = ssem, rsem, lsem
        self.d, self.s, self.c = place()
        self.order = (
            flip(flip(self.s, 1), 2),
            flip(self.s, 1),
            flip(self.s, 2),
            self.s,
        )

    def piece(self, f):
        if self.kind == "cols":
            return self.grad.at[pl.ds(pl.multiple_of(96 * f, 96), 96)]
        return self.grad.at[:, pl.ds(pl.multiple_of(384 * f, 384), 384)]

    def half(self, ref, h):
        if self.kind == "cols":
            return ref.at[:, pl.ds(1536 * h, 1536)]
        return ref.at[pl.ds(384 * h, 384)]

    def quarter(self, ref, q):
        if self.kind == "cols":
            return ref.at[:, pl.ds(pl.multiple_of(768 * q, 768), 768)]
        return ref.at[pl.ds(pl.multiple_of(192 * q, 192), 192)]

    def start(self):
        d, s, c = self.d, self.s, self.c
        self.zero, self.local = [], []
        for j, position in enumerate(self.order):
            copy = push(
                self.piece(2 * position + 1 - c), self.mate.at[j], self.ssem.at[j], self.rsem.at[j], at(d, s, 1 - c)
            )
            copy.start()
            self.zero.append(copy)
            copy = pltpu.make_async_copy(self.piece(2 * position + c), self.own.at[j], self.lsem.at[j])
            copy.start()
            self.local.append(copy)

    def merge(self):
        d, s, c = self.d, self.s, self.c
        sx, sy = flip(s, 1), flip(s, 2)
        self.one = []
        for j in range(4):
            self.zero[j].wait_recv()
            self.local[j].wait()
            self.own[j] = (widened(self.own.at[j]) + widened(self.mate.at[j])).astype(jnp.bfloat16)
            if j == 0:
                for h, target in enumerate((sx, sy)):
                    copy = push(
                        self.half(self.own.at[0], h), self.near.at[h], self.ssem.at[4 + h], self.rsem.at[4 + h],
                        at(d, target, c),
                    )
                    copy.start()
                    self.one.append(copy)

    def join(self):
        d, s, c = self.d, self.s, self.c
        sx, sy = flip(s, 1), flip(s, 2)
        for h, j in ((0, 2), (1, 1)):
            self.one[h].wait_recv()
            where = self.half(self.own.at[j], h)
            where[...] = (widened(where) + widened(self.near.at[h])).astype(jnp.bfloat16)
        self.two = []
        for h, target in enumerate((sx, sy)):
            copy = push(
                self.own.at[1 + h], self.far.at[h], self.ssem.at[6 + h], self.rsem.at[6 + h], at(d, target, c)
            )
            copy.start()
            self.two.append(copy)

    def along(self):
        d, s, c = self.d, self.s, self.c
        for copy in self.two:
            copy.wait_recv()
        self.own[3] = (
            widened(self.own.at[3]) + widened(self.far.at[0]) + widened(self.far.at[1])
        ).astype(jnp.bfloat16)
        self.three = []
        for k in range(1, 4):
            target = lax.rem(d + k, 4)
            copy = push(
                self.quarter(self.own.at[3], target), self.line.at[k - 1], self.ssem.at[7 + k], self.rsem.at[7 + k],
                at(target, s, c),
            )
            copy.start()
            self.three.append(copy)

    def finish(self):
        total = widened(self.quarter(self.own.at[3], self.d))
        for k in range(1, 4):
            self.three[k - 1].wait_recv()
            total = total + widened(self.line.at[k - 1])
        self.out[...] = total
        for copy in self.zero + self.one + self.two + self.three:
            copy.wait_send()


class Tail:
    def __init__(self, d_rows, router, act, ada, ada_out, d_act_out, router_out, z1, plane, plane_in, z2, z2_in, sems):
        self.d_rows, self.router, self.act, self.ada = d_rows, router, act, ada
        self.ada_out, self.d_act_out, self.router_out = ada_out, d_act_out, router_out
        self.z1, self.plane, self.plane_in, self.z2, self.z2_in = z1, plane, plane_in, z2, z2_in
        self.sems = sems
        self.d, self.s, self.c = place()
        self.f = 2 * self.s + self.c

    def z_copy(self, k, src, dst, base):
        send, recv = self.sems[base], self.sems[base + 1]
        return push(src, dst, send.at[k], recv.at[k], at(lax.rem(self.d + k, 4), self.s, self.c))

    def f_copy(self, k, src, dst, base):
        send, recv = self.sems[base], self.sems[base + 1]
        return push(src, dst, send.at[k], recv.at[k], (self.d, lax.rem(self.f + k, 8)))

    def start(self):
        self.all = [
            self.z_copy(k, self.d_rows.at[lax.rem(self.d + k, 4)], self.z1.at[k], 0) for k in range(1, 4)
        ]
        for copy in self.all:
            copy.start()

    def second(self):
        total = self.d_rows[self.d]
        for k in range(1, 4):
            self.all[k - 1].wait_recv()
            total = total + self.z1[k]
        for target in range(8):
            self.plane[target, :, 0:1152] = total
            self.plane[target, :, 1152:1280] = self.router[target]
        copies = [
            self.f_copy(k, self.plane.at[lax.rem(self.f + k, 8)], self.plane_in.at[lax.rem(8 - k, 8)], 2)
            for k in range(1, 8)
        ]
        for copy in copies:
            copy.start()
        self.in_plane = copies
        self.all = self.all + copies

    def third(self):
        f = self.f
        self.plane_in[0] = self.plane[f]
        for copy in self.in_plane:
            copy.wait_recv()
        everything = self.plane_in[...]
        router = jnp.sum(everything[:, :, 1152:1280], axis=0)
        rows = everything[:, :, 0:1152].reshape(64, 1152)
        line = lax.broadcasted_iota(jnp.int32, (64, 64), 0)
        column = lax.broadcasted_iota(jnp.int32, (64, 64), 1)
        turn = (lax.rem(line // 8 + 8 - f, 8) * 8 + lax.rem(line, 8) == column).astype(jnp.bfloat16)
        d_mod = nn(turn, rows.astype(jnp.bfloat16)).astype(jnp.bfloat16)
        self.ada_out[...] = tn(self.act[...], d_mod)[0:96]
        part = nt(d_mod, self.ada[...])
        self.z2[0:64, 0:96] = part
        self.z2[0:64, 96:128] = jnp.zeros((64, 32), jnp.float32)
        self.z2[64:72, :] = router
        copies = [self.z_copy(k, self.z2, self.z2_in.at[k], 4) for k in range(1, 4)]
        for copy in copies:
            copy.start()
        self.along = copies
        self.all = self.all + copies

    def fourth(self):
        total = self.z2[...]
        for k in range(1, 4):
            self.along[k - 1].wait_recv()
            total = total + self.z2_in[k]
        self.router_out[...] = total[64:72]
        self.z2_in[0] = total
        copies = [
            self.f_copy(
                k,
                self.z2_in.at[0, pl.ds(pl.multiple_of(8 * lax.rem(self.f + k, 8), 8), 8)],
                self.d_act_out.at[self.f],
                6,
            )
            for k in range(1, 8)
        ]
        for copy in copies:
            copy.start()
        self.d_act_out[self.f] = self.z2_in[0, pl.ds(pl.multiple_of(8 * self.f, 8), 8)]
        self.last = copies
        self.all = self.all + copies

    def finish(self):
        for k in range(1, 8):
            self.f_copy(
                k, self.z2_in.at[0, pl.ds(0, 8)], self.d_act_out.at[lax.rem(self.f + 8 - k, 8)], 6
            ).wait_recv()
        for copy in self.all:
            copy.wait_send()


def dense_kernel(kinds, *refs):
    n = len(kinds)
    grads, small, outs = refs[:n], refs[n : n + 4], refs[n + 4 : 2 * n + 4]
    small_outs, rest = refs[2 * n + 4 : 2 * n + 7], refs[2 * n + 7 :]
    d, s, c = place()
    f = 2 * s + c
    greet(
        [at(lax.rem(d + k, 4), s, c) for k in range(1, 4)]
        + [(d, lax.rem(f + k, 8)) for k in range(1, 8)]
    )
    sums = [
        DenseSum(kinds[i], grads[i], outs[i], *rest[8 * i : 8 * i + 8]) for i in range(n)
    ]
    rest = rest[8 * n :]
    tail = Tail(*small, *small_outs, *rest[:5], rest[5:])
    tail.start()
    for each in sums:
        each.start()
    tail.second()
    for each in sums:
        each.merge()
    tail.third()
    for each in sums:
        each.join()
    tail.fourth()
    for each in sums:
        each.along()
    for each in sums:
        each.finish()
    tail.finish()


def dense_sums(kinds, grads, small, collective_id):
    bf, f32 = jnp.bfloat16, jnp.float32
    outs, scratch = [], []
    for kind in kinds:
        if kind == "cols":
            piece, half, quarter = (96, 3072), (96, 1536), (96, 768)
        else:
            piece, half, quarter = (768, 384), (384, 384), (192, 384)
        outs.append(jax.ShapeDtypeStruct(quarter, f32))
        scratch += [
            pltpu.VMEM((4,) + piece, bf),
            pltpu.VMEM((4,) + piece, bf),
            pltpu.VMEM((2,) + half, bf),
            pltpu.VMEM((2,) + piece, bf),
            pltpu.VMEM((3,) + quarter, bf),
            DMA((11,)),
            DMA((11,)),
            DMA((4,)),
        ]
    outs += [
        jax.ShapeDtypeStruct((96, 1152), f32),
        jax.ShapeDtypeStruct((8, 8, 128), f32),
        jax.ShapeDtypeStruct((8, 128), f32),
    ]
    scratch += [
        pltpu.VMEM((4, 8, 1152), f32),
        pltpu.VMEM((8, 8, 1280), f32),
        pltpu.VMEM((8, 8, 1280), f32),
        pltpu.VMEM((72, 128), f32),
        pltpu.VMEM((4, 72, 128), f32),
        DMA((4,)), DMA((4,)), DMA((8,)), DMA((8,)), DMA((4,)), DMA((4,)), DMA((8,)), DMA((8,)),
    ]
    return pl.pallas_call(
        functools.partial(dense_kernel, kinds),
        out_shape=tuple(outs),
        in_specs=[ANYWHERE] * len(kinds) + [ONCHIP] * 4,
        out_specs=(ONCHIP,) * len(outs),
        scratch_shapes=scratch,
        compiler_params=pltpu.CompilerParams(collective_id=collective_id, has_side_effects=True),
        name="dense_sums",
    )(*grads, *small)


def fitted_shards(
    tokens,
    condition,
    ada_weight,
    qkv_weight,
    out_weight,
    shared_up,
    shared_down,
    router_weight,
    expert_up,
    expert_down,
    routes,
    image_sizes,
    cotangent,
):
    bf = jnp.bfloat16
    d_index, f_index = lax.axis_index("dp"), lax.axis_index("fsdp")
    model_width = tokens.shape[1]
    head_size = model_width // HEADS
    inside, segment = owners(image_sizes)
    up_all, down_all = gather_experts(expert_up, expert_down)
    ids = jnp.arange(EXPERTS, dtype=jnp.int32)
    hot = routes[:, :, None] == ids[None, None, :]
    hot_any = jnp.any(hot, axis=1).astype(bf)
    order = jnp.arange(LONG, dtype=jnp.int32)
    earlier = (order[:, None] > order[None, :]).astype(bf)
    before = nn(earlier, hot_any)
    position = jnp.sum(jnp.where(hot, before[:, None, :], 0.0), axis=-1).astype(jnp.int32)
    target = routes * CAP + position
    places = jnp.arange(EXPERTS * CAP, dtype=jnp.int32)
    send_0 = (places[:, None] == target[None, :, 0]).astype(bf)
    send_1 = (places[:, None] == target[None, :, 1]).astype(bf)
    live = (segment < IMG_DEV).astype(jnp.float32)
    counts = jnp.sum(live[:, None] * hot_any.astype(jnp.float32), axis=0)
    cond_float = condition.astype(jnp.float32)
    activated = jax.nn.silu(cond_float).astype(bf)
    act_slices = activated.astype(jnp.float32).reshape(IMG_DEV, 8, 96).transpose(1, 0, 2)
    act_slices = jnp.pad(act_slices, ((0, 0), (0, 6), (0, 32)))
    act_slices = act_slices.at[:, 2, :EXPERTS].set(counts)
    ada_pad = jnp.pad(ada_weight, ((0, 32), (0, 0)))
    router_pack = jnp.pad(router_weight.reshape(192), (0, 2048 - 192)).reshape(16, 128)
    qkvo_shard = jnp.concatenate([qkv_weight, out_weight], axis=1)
    qkvo, routers, seen, mod_rows = opening(qkvo_shard, router_pack, act_slices, ada_pad)
    expert_counts = seen[66, :EXPERTS].astype(jnp.int32)
    modulation = lax.dynamic_slice(mod_rows, (0, 2 * d_index, 0), (4, 2, 1152))
    modulation = modulation.transpose(1, 0, 2).reshape(2, 4608)
    router_full = (
        routers.reshape(32, 2048)[:, :192]
        .reshape(4, 8, 96, 2)
        .transpose(1, 2, 0, 3)
        .reshape(model_width, EXPERTS)
    )
    qkvo = qkvo.reshape(model_width, 4, 768)
    qkv_full = qkvo[:, :, :576].reshape(model_width, 2304)
    out_full = qkvo[:, :, 576:].reshape(model_width, 768)
    per_row = inside[:, 0:1] * modulation[0:1] + inside[:, 1:2] * modulation[1:2]
    shift_one, scale_one, gate_one, shift_two, scale_two, gate_two = jnp.split(per_row, 6, axis=1)
    token_float = tokens.astype(jnp.float32)
    normed_one, inv_one = layer_norm(token_float)
    first_input = (normed_one * (1.0 + scale_one) + shift_one).astype(bf)
    qkv_rows = nn(first_input, qkv_full).astype(bf)
    queries, keys, values = (
        qkv_rows[:, i * model_width : (i + 1) * model_width]
        .reshape(LONG, HEADS, head_size)
        .transpose(1, 0, 2)
        for i in range(3)
    )
    scale = head_size**-0.5
    allowed = (segment[:, None] == segment[None, :])[None]
    scores = jnp.einsum("hqd,hkd->hqk", queries, keys, preferred_element_type=jnp.float32) * scale
    scores = jnp.where(allowed, scores, -1e30)
    row_max = jnp.max(scores, axis=-1, keepdims=True)
    weight = jnp.exp(scores - row_max)
    running = jnp.sum(weight, axis=-1, keepdims=True)
    probability = weight / running
    prob_low = probability.astype(bf)
    attended = jnp.einsum("hqk,hkd->hqd", prob_low, values, preferred_element_type=jnp.float32)
    attended = attended.astype(bf).transpose(1, 0, 2).reshape(LONG, model_width)
    projected = nn(attended, out_full)
    residual_one = token_float + gate_one * projected
    normed_two, inv_two = layer_norm(residual_one)
    second_input = (normed_two * (1.0 + scale_two) + shift_two).astype(bf)
    logits = nn(second_input, router_full)
    route_hot = hot.astype(jnp.float32)
    chosen = jnp.sum(logits[:, None, :] * route_hot, axis=-1)
    gate_share = jax.nn.softmax(chosen, axis=-1)
    upstream = cotangent.astype(jnp.float32)
    d_mixed = gate_two * upstream
    rows = nn(send_0 + send_1, second_input).astype(bf).reshape(EXPERTS, CAP, model_width)
    weighted = jnp.concatenate(
        [(gate_share[:, k : k + 1] * d_mixed).astype(bf) for k in range(2)], axis=0
    )
    grads = (
        nn(jnp.concatenate([send_0, send_1], axis=1), weighted)
        .astype(bf)
        .reshape(EXPERTS, CAP, model_width)
    )
    rows_in, grads_in, shared_out, d_second, shared_first_grad, shared_second_grad = outbound(
        rows, grads, shared_up, shared_down.T, second_input, d_mixed.astype(bf)
    )
    returned, d_returned, expert_up_grad, expert_down_grad = experts(
        rows_in, grads_in, up_all, down_all
    )
    returned = returned.reshape(EXPERTS * CAP, model_width)
    d_returned = d_returned.reshape(EXPERTS * CAP, model_width)
    picked_0 = tn(send_0, returned)
    picked_1 = tn(send_1, returned)
    mixed = shared_out + (gate_share[:, 0:1] * picked_0 + gate_share[:, 1:2] * picked_1)
    output = (residual_one + gate_two * mixed).astype(bf)
    d_gate_two = upstream * mixed
    d_gate_share = jnp.stack(
        [jnp.sum(d_mixed * picked_0, axis=-1), jnp.sum(d_mixed * picked_1, axis=-1)], axis=1
    )
    d_chosen = gate_share * (
        d_gate_share - jnp.sum(gate_share * d_gate_share, axis=-1, keepdims=True)
    )
    d_logits = jnp.sum(d_chosen[:, :, None] * route_hot, axis=1).astype(bf)
    router_grad = tn(d_logits, second_input)
    d_second = d_second + nt(d_logits, router_full) + tn(send_0 + send_1, d_returned)
    d_scale_two = d_second * normed_two
    d_residual = upstream + norm_back(d_second * (1.0 + scale_two), normed_two, inv_two)
    d_projected = (gate_one * d_residual).astype(bf)
    d_gate_one = d_residual * projected
    out_grad = tn(attended, d_projected)
    d_attended = nt(d_projected, out_full).astype(bf)
    d_attended = d_attended.reshape(LONG, HEADS, head_size).transpose(1, 0, 2)
    d_prob = jnp.einsum("hqd,hkd->hqk", d_attended, values, preferred_element_type=jnp.float32)
    d_scores = (
        probability * (d_prob - jnp.sum(probability * d_prob, axis=-1, keepdims=True))
    ).astype(bf)
    d_queries = jnp.einsum("hqk,hkd->hqd", d_scores, keys, preferred_element_type=jnp.float32) * scale
    d_keys = jnp.einsum("hqk,hqd->hkd", d_scores, queries, preferred_element_type=jnp.float32) * scale
    d_values = jnp.einsum("hqk,hqd->hkd", prob_low, d_attended, preferred_element_type=jnp.float32)
    d_qkv = jnp.concatenate(
        [
            piece.astype(bf).transpose(1, 0, 2).reshape(LONG, model_width)
            for piece in (d_queries, d_keys, d_values)
        ],
        axis=1,
    )
    qkv_grad = tn(first_input, d_qkv)
    d_first = nt(d_qkv, qkv_full)
    d_scale_one = d_first * normed_one
    tokens_grad = d_residual + norm_back(d_first * (1.0 + scale_one), normed_one, inv_one)
    qkvo_grad = (
        jnp.concatenate(
            [qkv_grad.reshape(model_width, 4, 576), out_grad.reshape(model_width, 4, 192)], axis=2
        )
        .astype(bf)
        .reshape(model_width, 3072)
    )
    d_modulation = jnp.concatenate(
        [
            jnp.stack([jnp.sum(inside[:, j : j + 1] * piece, axis=0) for j in range(IMG_DEV)])
            for piece in (d_first, d_scale_one, d_gate_one, d_second, d_scale_two, d_gate_two)
        ],
        axis=1,
    ).astype(bf)
    d_mod_rows = d_modulation.astype(jnp.float32).reshape(2, 4, 1152).transpose(1, 0, 2)
    d_mod_rows = lax.dynamic_update_slice(
        jnp.zeros((4, 8, 1152), jnp.float32), d_mod_rows, (0, 2 * d_index, 0)
    )
    router_tiles = jnp.pad(
        router_grad.reshape(EXPERTS, 8, 96).transpose(1, 0, 2), ((0, 0), (0, 0), (0, 32))
    )
    shared_first_sum, shared_second_sum, qkvo_sum, ada_grad, d_act_tiles, router_sum = dense_sums(
        ("cols", "rows", "cols"),
        (shared_first_grad, shared_second_grad, qkvo_grad),
        (d_mod_rows, router_tiles, seen[:64].astype(bf), ada_weight),
        3,
    )
    d_activated = lax.dynamic_slice(d_act_tiles, (0, 2 * d_index, 0), (8, 2, 96))
    d_activated = d_activated.transpose(1, 0, 2).reshape(2, model_width)
    condition_grad = jax.vjp(jax.nn.silu, cond_float)[1](d_activated)[0]
    router_out = lax.dynamic_slice(router_sum, (2 * d_index, 0), (2, 96)).T
    return (
        output,
        tokens_grad,
        condition_grad,
        ada_grad,
        qkvo_sum[:, :576],
        qkvo_sum[:, 576:],
        shared_first_sum,
        shared_second_sum.T,
        router_out,
        expert_up_grad,
        expert_down_grad,
        expert_counts,
    )


def solution(mesh):
    placed = (
        P(("dp", "fsdp"), None),
        P(("dp", "fsdp"), None),
        P("fsdp", "dp"),
        P("fsdp", "dp"),
        P("fsdp", "dp"),
        P("fsdp", "dp"),
        P("fsdp", "dp"),
        P("fsdp", "dp"),
        P("dp", "fsdp", None),
        P("dp", "fsdp", None),
        P(("dp", "fsdp"), None),
        P(("dp", "fsdp")),
        P(("dp", "fsdp"), None),
    )
    fitted = mesh.shape["dp"] == 4 and mesh.shape["fsdp"] == 8
    return jax.shard_map(
        fitted_shards if fitted else shards,
        mesh=mesh,
        in_specs=placed,
        out_specs=(
            P(("dp", "fsdp"), None),
            P(("dp", "fsdp"), None),
            P(("dp", "fsdp"), None),
            P("fsdp", "dp"),
            P("fsdp", "dp"),
            P("fsdp", "dp"),
            P("fsdp", "dp"),
            P("fsdp", "dp"),
            P("fsdp", "dp"),
            P("dp", "fsdp", None),
            P("dp", "fsdp", None),
            P(),
        ),
        check_vma=False,
    )
```

```python
import functools

import jax
import jax.numpy as jnp
from jax import lax
from jax.experimental import pallas as pl
from jax.experimental.pallas import tpu as pltpu
from jax.sharding import PartitionSpec as P

HEADS = 12
EXPERTS = 8
CAP = 144
IMG_DEV = 2
LONG = 512
MESH = pl.DeviceIdType.MESH


EXACT = lax.Precision.HIGHEST


def owners(image_sizes):
    starts = jnp.cumsum(image_sizes) - image_sizes
    position = jnp.arange(LONG, dtype=jnp.int32)[:, None]
    inside = (position >= starts[None, :]) & (position < (starts + image_sizes)[None, :])
    slot_ids = jnp.arange(IMG_DEV, dtype=jnp.int32)
    segment = jnp.sum(jnp.where(inside, slot_ids[None, :], 0), axis=1) + jnp.where(
        jnp.any(inside, axis=1), 0, IMG_DEV
    )
    return (inside.astype(jnp.float32), segment)


def dispatch_plan(routes):
    flat = routes.reshape(-1)
    onehot = (flat[:, None] == jnp.arange(EXPERTS, dtype=jnp.int32)[None, :]).astype(jnp.int32)
    before = jnp.cumsum(onehot, axis=0) - onehot
    position = jnp.sum(before * onehot, axis=1)
    target = flat * CAP + position
    assignment = jnp.arange(2 * LONG, dtype=jnp.int32)
    source = jnp.zeros((EXPERTS * CAP,), jnp.int32).at[target].set(assignment)
    filled = jnp.zeros((EXPERTS * CAP,), jnp.int32).at[target].set(1)
    return (target, source, filled)


def layer_norm(values_in):
    centred = values_in - jnp.mean(values_in, axis=-1, keepdims=True)
    inv_std = lax.rsqrt(jnp.mean(centred * centred, axis=-1, keepdims=True) + 1e-06)
    return (centred * inv_std, inv_std)


def norm_back(upstream, normed, inv_std):
    return (
        upstream
        - jnp.mean(upstream, axis=-1, keepdims=True)
        - normed * jnp.mean(upstream * normed, axis=-1, keepdims=True)
    ) * inv_std


def gelu_tanh(values_in):
    return jax.nn.gelu(values_in, approximate=True)


def gelu_back(values_in, upstream):
    return jax.vjp(gelu_tanh, values_in)[1](upstream)[0]


def collect(first, second, third):
    widened = (
        lax.all_gather(first, "dp", axis=1, tiled=True),
        lax.all_gather(second, "dp", axis=1, tiled=True),
        lax.all_gather(third, "dp", axis=1, tiled=True),
    )
    return (
        lax.all_gather(widened[0], "fsdp", axis=0, tiled=True),
        lax.all_gather(widened[1], "fsdp", axis=0, tiled=True),
        lax.all_gather(widened[2], "fsdp", axis=0, tiled=True),
    )


def spread(first, second, third):
    row_sums = (
        lax.psum_scatter(first, "fsdp", scatter_dimension=0, tiled=True),
        lax.psum_scatter(second, "fsdp", scatter_dimension=0, tiled=True),
        lax.psum_scatter(third, "fsdp", scatter_dimension=0, tiled=True),
    )
    return (
        lax.psum_scatter(row_sums[0], "dp", scatter_dimension=1, tiled=True),
        lax.psum_scatter(row_sums[1], "dp", scatter_dimension=1, tiled=True),
        lax.psum_scatter(row_sums[2], "dp", scatter_dimension=1, tiled=True),
    )


def gather_experts(up_shard, down_shard):
    return (
        lax.all_gather(up_shard, "fsdp", axis=1, tiled=True),
        lax.all_gather(down_shard, "fsdp", axis=1, tiled=True),
    )


def expert_forward(buffer_in, up_full, down_full):
    expert_pre = jnp.einsum(
        "secd,edf->secf", buffer_in, up_full, preferred_element_type=jnp.float32
    )
    expert_act = gelu_tanh(expert_pre).astype(jnp.bfloat16)
    expert_out = jnp.einsum(
        "secf,efd->secd", expert_act, down_full, preferred_element_type=jnp.float32
    ).astype(jnp.bfloat16)
    return (expert_pre, expert_act, expert_out)


def expert_backward(buffer_in, expert_pre, expert_act, d_out, up_full, down_full):
    d_act = jnp.einsum("secd,efd->secf", d_out, down_full, preferred_element_type=jnp.float32)
    d_pre = gelu_back(expert_pre, d_act).astype(jnp.bfloat16)
    d_rows = jnp.einsum(
        "secf,edf->secd", d_pre, up_full, preferred_element_type=jnp.float32
    ).astype(jnp.bfloat16)
    down_grad = jnp.einsum("secf,secd->efd", expert_act, d_out, preferred_element_type=jnp.float32)
    up_grad = jnp.einsum("secd,secf->edf", buffer_in, d_pre, preferred_element_type=jnp.float32)
    return (up_grad, down_grad, d_rows)


def attend(queries, keys_all, values_all, segment):
    row_count, head_count, head_size = queries.shape
    block_rows = min(512, row_count)
    block_count = row_count // block_rows
    score_scale = head_size ** (-0.5)

    def one_block(pieces):
        query_part, segment_part = pieces
        allowed = (segment_part[:, None] == segment[None, :])[None]
        scores = (
            jnp.einsum("qhd,khd->hqk", query_part, keys_all, preferred_element_type=jnp.float32)
            * score_scale
        )
        scores = jnp.where(allowed, scores, -1e30)
        row_max = jnp.max(scores, axis=-1, keepdims=True)
        weight = jnp.exp(scores - row_max)
        running = jnp.sum(weight, axis=-1, keepdims=True)
        probability = (weight / running).astype(jnp.bfloat16)
        attended = jnp.einsum(
            "hqk,khd->qhd", probability, values_all, preferred_element_type=jnp.float32
        )
        return (attended.astype(jnp.bfloat16), (row_max + jnp.log(running))[:, :, 0])

    return lax.map(
        one_block,
        (
            queries.reshape(block_count, block_rows, head_count, head_size),
            segment.reshape(block_count, block_rows),
        ),
    )


def attend_back(queries, keys_all, values_all, segment, log_totals, d_attended):
    row_count, head_count, head_size = queries.shape
    block_rows = min(512, row_count)
    block_count = row_count // block_rows
    score_scale = head_size ** (-0.5)

    def one_block(carry, pieces):
        key_sum, value_sum = carry
        query_part, segment_part, total_part, grad_part = pieces
        allowed = (segment_part[:, None] == segment[None, :])[None]
        scores = (
            jnp.einsum("qhd,khd->hqk", query_part, keys_all, preferred_element_type=jnp.float32)
            * score_scale
        )
        scores = jnp.where(allowed, scores, -1e30)
        probability = jnp.exp(scores - total_part[:, :, None])
        d_prob = jnp.einsum(
            "qhd,khd->hqk", grad_part, values_all, preferred_element_type=jnp.float32
        )
        d_scores = (
            probability * (d_prob - jnp.sum(probability * d_prob, axis=-1, keepdims=True))
        ).astype(jnp.bfloat16)
        query_grad = (
            jnp.einsum("hqk,khd->qhd", d_scores, keys_all, preferred_element_type=jnp.float32)
            * score_scale
        )
        key_sum = (
            key_sum
            + jnp.einsum("hqk,qhd->khd", d_scores, query_part, preferred_element_type=jnp.float32)
            * score_scale
        )
        value_sum = value_sum + jnp.einsum(
            "hqk,qhd->khd",
            probability.astype(jnp.bfloat16),
            grad_part,
            preferred_element_type=jnp.float32,
        )
        return ((key_sum, value_sum), query_grad)

    empty = jnp.zeros(keys_all.shape, jnp.float32)
    sums, query_grads = lax.scan(
        one_block,
        (empty, empty),
        (
            queries.reshape(block_count, block_rows, head_count, head_size),
            segment.reshape(block_count, block_rows),
            log_totals,
            d_attended.reshape(block_count, block_rows, head_count, head_size),
        ),
    )
    return (query_grads.reshape(row_count, head_count, head_size), sums[0], sums[1])


def shards(
    tokens,
    condition,
    ada_weight,
    qkv_weight,
    out_weight,
    shared_up,
    shared_down,
    router_weight,
    expert_up,
    expert_down,
    routes,
    image_sizes,
    cotangent,
):
    model_width = tokens.shape[1]
    head_size = model_width // HEADS
    inside, segment = owners(image_sizes)
    target, source, filled = dispatch_plan(routes)
    route_hot = (routes[:, :, None] == jnp.arange(EXPERTS, dtype=jnp.int32)[None, None, :]).astype(
        jnp.float32
    )
    live = (segment < IMG_DEV).astype(jnp.int32)
    local_counts = jnp.sum(live[:, None, None] * route_hot.astype(jnp.int32), axis=(0, 1))
    expert_counts = lax.psum(local_counts, ("dp", "fsdp"))
    ada_full, qkv_full, out_full = collect(ada_weight, qkv_weight, out_weight)
    cond_float = condition.astype(jnp.float32)
    activated = jax.nn.silu(cond_float).astype(jnp.bfloat16)
    modulation = jnp.dot(activated, ada_full, preferred_element_type=jnp.float32)
    per_row = jnp.dot(inside, modulation, precision=EXACT, preferred_element_type=jnp.float32)
    shift_one, scale_one, gate_one, shift_two, scale_two, gate_two = jnp.split(per_row, 6, axis=1)
    token_float = tokens.astype(jnp.float32)
    normed_one, inv_one = layer_norm(token_float)
    first_input = (normed_one * (1.0 + scale_one) + shift_one).astype(jnp.bfloat16)
    qkv_rows = jnp.dot(first_input, qkv_full, preferred_element_type=jnp.float32).astype(
        jnp.bfloat16
    )
    queries = qkv_rows[:, :model_width].reshape(-1, HEADS, head_size)
    keys_all = qkv_rows[:, model_width : 2 * model_width].reshape(-1, HEADS, head_size)
    values_all = qkv_rows[:, 2 * model_width :].reshape(-1, HEADS, head_size)
    attended_blocks, log_totals = attend(queries, keys_all, values_all, segment)
    attended = attended_blocks.reshape(-1, model_width)
    projected = jnp.dot(attended, out_full, preferred_element_type=jnp.float32)
    residual_one = token_float + gate_one * projected
    normed_two, inv_two = layer_norm(residual_one)
    second_input = (normed_two * (1.0 + scale_two) + shift_two).astype(jnp.bfloat16)
    shared_first, shared_second, router_full = collect(shared_up, shared_down, router_weight)
    shared_pre = jnp.dot(second_input, shared_first, preferred_element_type=jnp.float32)
    shared_act = gelu_tanh(shared_pre).astype(jnp.bfloat16)
    shared_out = jnp.dot(shared_act, shared_second, preferred_element_type=jnp.float32)
    logits = jnp.dot(second_input, router_full, preferred_element_type=jnp.float32)
    chosen = jnp.sum(logits[:, None, :] * route_hot, axis=-1)
    gate_share = jax.nn.softmax(chosen, axis=-1)
    buffer_rows = jnp.take(second_input, source // 2, axis=0).reshape(EXPERTS, CAP, model_width)
    up_full, down_full = gather_experts(expert_up, expert_down)
    groups = lax.axis_size("dp")
    expert_in = lax.all_to_all(
        buffer_rows.reshape(groups, EXPERTS // groups, CAP, model_width),
        "dp",
        split_axis=0,
        concat_axis=0,
        tiled=True,
    )
    expert_pre, expert_act, expert_out = expert_forward(expert_in, up_full, down_full)
    returned = lax.all_to_all(expert_out, "dp", split_axis=0, concat_axis=0, tiled=True).reshape(
        EXPERTS, CAP, model_width
    )
    picked = (
        jnp.take(returned.reshape(EXPERTS * CAP, model_width), target, axis=0)
        .reshape(-1, 2, model_width)
        .astype(jnp.float32)
    )
    mixed = shared_out + jnp.sum(gate_share[:, :, None] * picked, axis=1)
    output = (residual_one + gate_two * mixed).astype(jnp.bfloat16)
    upstream = cotangent.astype(jnp.float32)
    d_mixed = gate_two * upstream
    d_gate_two = upstream * mixed
    d_gate_share = jnp.sum(d_mixed[:, None, :] * picked, axis=-1)
    slot_gate = jnp.take(gate_share.reshape(-1), source) * filled.astype(jnp.float32)
    d_buffer = (
        (jnp.take(d_mixed, source // 2, axis=0) * slot_gate[:, None])
        .astype(jnp.bfloat16)
        .reshape(EXPERTS, CAP, model_width)
    )
    shared_first, shared_second, router_full = collect(shared_up, shared_down, router_weight)
    up_full, down_full = gather_experts(expert_up, expert_down)
    arrived = lax.all_to_all(
        d_buffer.reshape(groups, EXPERTS // groups, CAP, model_width),
        "dp",
        split_axis=0,
        concat_axis=0,
        tiled=True,
    )
    up_grad, down_grad, d_rows = expert_backward(
        expert_in, expert_pre, expert_act, arrived, up_full, down_full
    )
    d_returned = lax.all_to_all(d_rows, "dp", split_axis=0, concat_axis=0, tiled=True).reshape(
        EXPERTS, CAP, model_width
    )
    expert_sums = (
        lax.psum_scatter(up_grad, "fsdp", scatter_dimension=1, tiled=True),
        lax.psum_scatter(down_grad, "fsdp", scatter_dimension=1, tiled=True),
    )
    d_shared = d_mixed.astype(jnp.bfloat16)
    shared_second_grad = jnp.einsum(
        "tf,td->fd", shared_act, d_shared, preferred_element_type=jnp.float32
    )
    d_shared_act = jnp.einsum(
        "td,fd->tf", d_shared, shared_second, preferred_element_type=jnp.float32
    )
    d_shared_pre = gelu_back(shared_pre, d_shared_act).astype(jnp.bfloat16)
    shared_first_grad = jnp.einsum(
        "td,tf->df", second_input, d_shared_pre, preferred_element_type=jnp.float32
    )
    d_chosen = gate_share * (
        d_gate_share - jnp.sum(gate_share * d_gate_share, axis=-1, keepdims=True)
    )
    d_logits = jnp.sum(d_chosen[:, :, None] * route_hot, axis=1).astype(jnp.bfloat16)
    router_grad = jnp.einsum(
        "td,te->de", second_input, d_logits, preferred_element_type=jnp.float32
    )
    from_experts = (
        jnp.take(d_returned.reshape(EXPERTS * CAP, model_width), target, axis=0)
        .reshape(-1, 2, model_width)
        .astype(jnp.float32)
    )
    d_second = (
        jnp.einsum("tf,df->td", d_shared_pre, shared_first, preferred_element_type=jnp.float32)
        + jnp.einsum("te,de->td", d_logits, router_full, preferred_element_type=jnp.float32)
        + jnp.sum(from_experts, axis=1)
    )
    mlp_sums = spread(shared_first_grad, shared_second_grad, router_grad)
    d_scale_two = d_second * normed_two
    d_residual = upstream + norm_back(d_second * (1.0 + scale_two), normed_two, inv_two)
    ada_full, qkv_full, out_full = collect(ada_weight, qkv_weight, out_weight)
    d_projected = (gate_one * d_residual).astype(jnp.bfloat16)
    d_gate_one = d_residual * projected
    out_grad = jnp.einsum("td,te->de", attended, d_projected, preferred_element_type=jnp.float32)
    d_attended = jnp.einsum(
        "te,de->td", d_projected, out_full, preferred_element_type=jnp.float32
    ).astype(jnp.bfloat16)
    d_queries, d_keys, d_values = attend_back(
        queries, keys_all, values_all, segment, log_totals, d_attended.reshape(-1, HEADS, head_size)
    )
    d_qkv = jnp.concatenate(
        [
            d_queries.reshape(-1, model_width),
            d_keys.reshape(-1, model_width),
            d_values.reshape(-1, model_width),
        ],
        axis=1,
    ).astype(jnp.bfloat16)
    qkv_grad = jnp.einsum("td,te->de", first_input, d_qkv, preferred_element_type=jnp.float32)
    d_first = jnp.einsum("te,de->td", d_qkv, qkv_full, preferred_element_type=jnp.float32)
    d_scale_one = d_first * normed_one
    tokens_grad = d_residual + norm_back(d_first * (1.0 + scale_one), normed_one, inv_one)
    d_per_row = jnp.concatenate(
        [d_first, d_scale_one, d_gate_one, d_second, d_scale_two, d_gate_two], axis=1
    )
    d_modulation = jnp.einsum(
        "tj,te->je", inside, d_per_row, precision=EXACT, preferred_element_type=jnp.float32
    ).astype(jnp.bfloat16)
    ada_grad = jnp.einsum("jd,je->de", activated, d_modulation, preferred_element_type=jnp.float32)
    d_activated = jnp.einsum(
        "je,de->jd", d_modulation, ada_full, preferred_element_type=jnp.float32
    )
    condition_grad = jax.vjp(jax.nn.silu, cond_float)[1](d_activated)[0]
    attn_sums = spread(ada_grad, qkv_grad, out_grad)
    return (
        output,
        tokens_grad,
        condition_grad,
        attn_sums[0],
        attn_sums[1],
        attn_sums[2],
        mlp_sums[0],
        mlp_sums[1],
        mlp_sums[2],
        expert_sums[0],
        expert_sums[1],
        expert_counts,
    )


def at(d, s, c):
    return (d, 2 * s + c)


def slot(kind, f, d):
    if kind == "cols":
        return (pl.ds(pl.multiple_of(96 * f, 96), 96), pl.ds(pl.multiple_of(768 * d, 768), 768))
    return (pl.ds(pl.multiple_of(192 * d, 192), 192), pl.ds(pl.multiple_of(384 * f, 384), 384))


def half_slot(kind, f, d, h):
    if kind == "cols":
        return (
            pl.ds(pl.multiple_of(96 * f, 96), 96),
            pl.ds(pl.multiple_of(768 * d + 384 * h, 384), 384),
        )
    return (
        pl.ds(pl.multiple_of(192 * d + 96 * h, 96), 96),
        pl.ds(pl.multiple_of(384 * f, 384), 384),
    )


def place():
    d = lax.axis_index("dp")
    f = lax.axis_index("fsdp")
    return d, f // 2, lax.rem(f, 2)


def flip(v, bit):
    return v + bit - 2 * bit * lax.rem(v // bit, 2)


def greet(devices):
    barrier = pltpu.get_barrier_semaphore()
    for device in devices:
        pl.semaphore_signal(barrier, inc=1, device_id=device, device_id_type=MESH)
    pl.semaphore_wait(barrier, len(devices))


def push(src, dst, send_sem, recv_sem, device):
    return pltpu.make_async_remote_copy(
        src_ref=src,
        dst_ref=dst,
        send_sem=send_sem,
        recv_sem=recv_sem,
        device_id=device,
        device_id_type=MESH,
    )


GATHER_SEMS = 3 + 8 + 8 + 20


class Gather:
    def __init__(self, kind, shard, full, ssem, rsem, lsem):
        self.kind, self.shard, self.full = kind, shard, full
        self.ssem, self.rsem, self.lsem = ssem, rsem, lsem
        self.d, self.s, self.c = place()
        self.sent = []

    def f(self, s):
        return 2 * s + self.c

    def go(self, index, where, device, src=None):
        ref = self.full.at[where]
        copy = push(
            ref if src is None else src, ref, self.ssem.at[index], self.rsem.at[index], device
        )
        copy.start()
        self.sent.append(copy)

    def arrived(self, index, where):
        ref = self.full.at[where]
        push(ref, ref, self.ssem.at[index], self.rsem.at[index], at(self.d, self.s, self.c)).wait_recv()

    def start(self):
        d, s, c = self.d, self.s, self.c
        mine = slot(self.kind, self.f(s), d)
        self.own = pltpu.make_async_copy(self.shard, self.full.at[mine], self.lsem)
        self.own.start()
        for k in range(1, 4):
            self.go(k - 1, mine, at(lax.rem(d + k, 4), s, c), self.shard)
        self.go(3, mine, at(d, flip(s, 1), c), self.shard)
        self.go(4, mine, at(d, flip(s, 2), c), self.shard)
        self.go(19, mine, at(d, s, 1 - c), self.shard)

    def spread_z(self, k):
        d, s, c = self.d, self.s, self.c
        source = lax.rem(d + 4 - k, 4)
        block = slot(self.kind, self.f(s), source)
        self.arrived(k - 1, block)
        self.go(3 + 2 * k, block, at(d, flip(s, 1), c))
        self.go(4 + 2 * k, block, at(d, flip(s, 2), c))
        self.go(19 + 5 * k, block, at(d, s, 1 - c))

    def relay(self, k):
        d, s, c = self.d, self.s, self.c
        source = lax.rem(d + 4 - k, 4)
        sx, sy = flip(s, 1), flip(s, 2)
        from_x = slot(self.kind, self.f(sx), source)
        from_y = slot(self.kind, self.f(sy), source)
        self.arrived(3 + 2 * k, from_x)
        self.go(11 + 2 * k, half_slot(self.kind, self.f(sx), source, 0), at(d, sy, c))
        self.go(20 + 5 * k, from_x, at(d, s, 1 - c))
        self.arrived(4 + 2 * k, from_y)
        self.go(12 + 2 * k, half_slot(self.kind, self.f(sy), source, 1), at(d, sx, c))
        self.go(21 + 5 * k, from_y, at(d, s, 1 - c))

    def corner(self, k):
        d, s, c = self.d, self.s, self.c
        source = lax.rem(d + 4 - k, 4)
        sd = flip(flip(s, 1), 2)
        for h in range(2):
            where = half_slot(self.kind, self.f(sd), source, h)
            self.arrived(11 + 2 * k + h, where)
            self.go(22 + 5 * k + h, where, at(d, s, 1 - c))

    def finish(self):
        d, s, c = self.d, self.s, self.c
        sx, sy = flip(s, 1), flip(s, 2)
        sd = flip(sx, 2)
        self.own.wait()
        for k in range(4):
            source = lax.rem(d + 4 - k, 4)
            for j, position in enumerate((s, sx, sy)):
                self.arrived(19 + 5 * k + j, slot(self.kind, 2 * position + 1 - c, source))
            for h in range(2):
                self.arrived(22 + 5 * k + h, half_slot(self.kind, 2 * sd + 1 - c, source, h))
        for copy in self.sent:
            copy.wait_send()


class Line:
    def __init__(self, kind, shard, line, ssem, rsem, lsem):
        self.kind, self.shard, self.line = kind, shard, line
        self.ssem, self.rsem, self.lsem = ssem, rsem, lsem
        self.d, self.s, self.c = place()

    def block(self, d):
        if self.kind == "cols":
            return self.line.at[:, pl.ds(pl.multiple_of(768 * d, 768), 768)]
        return self.line.at[pl.ds(pl.multiple_of(192 * d, 192), 192)]

    def copy(self, index, src, source, target):
        return push(
            src, self.block(source), self.ssem.at[index], self.rsem.at[index], at(target, self.s, self.c)
        )

    def start(self):
        d = self.d
        self.own = pltpu.make_async_copy(self.shard, self.block(d), self.lsem)
        self.own.start()
        self.sent = [
            self.copy(0, self.shard, d, flip(d, 2)),
            self.copy(1, self.shard, d, flip(d, 1)),
        ]
        for copy in self.sent:
            copy.start()

    def relay(self):
        d2 = flip(self.d, 2)
        self.copy(0, self.shard, d2, d2).wait_recv()
        copy = self.copy(2, self.block(d2), d2, flip(self.d, 1))
        copy.start()
        self.sent.append(copy)

    def finish(self):
        d1 = flip(self.d, 1)
        self.own.wait()
        self.copy(1, self.shard, d1, d1).wait_recv()
        self.copy(2, self.shard, flip(d1, 2), d1).wait_recv()
        for copy in self.sent:
            copy.wait_send()


class Spread:
    def __init__(self, kind, line, full, ssem, rsem, lsem):
        self.kind, self.line, self.full = kind, line, full
        self.ssem, self.rsem, self.lsem = ssem, rsem, lsem
        self.d, self.s, self.c = place()
        self.sx, self.sy = flip(self.s, 1), flip(self.s, 2)
        self.sd = flip(self.sx, 2)
        self.mate = at(self.d, self.s, 1 - self.c)
        self.to_x, self.to_y = at(self.d, self.sx, self.c), at(self.d, self.sy, self.c)
        self.sent = []

    def block(self, position, c, h=None):
        f = 2 * position + c
        if self.kind == "cols":
            rows = pl.ds(pl.multiple_of(96 * f, 96), 96)
            return self.full.at[rows] if h is None else self.full.at[rows, pl.ds(1536 * h, 1536)]
        columns = pl.ds(pl.multiple_of(384 * f, 384), 384)
        rows = pl.ds(0, 768) if h is None else pl.ds(384 * h, 384)
        return self.full.at[rows, columns]

    def go(self, index, ref, device, src=None):
        copy = push(
            ref if src is None else src, ref, self.ssem.at[index], self.rsem.at[index], device
        )
        copy.start()
        self.sent.append(copy)

    def arrived(self, index, ref):
        push(ref, ref, self.ssem.at[index], self.rsem.at[index], self.mate).wait_recv()

    def start(self):
        mine = self.block(self.s, self.c)
        self.own = pltpu.make_async_copy(self.line, mine, self.lsem)
        self.own.start()
        self.go(0, mine, self.to_x, self.line)
        self.go(1, mine, self.to_y, self.line)
        self.go(2, mine, self.mate, self.line)

    def relay(self):
        c = self.c
        from_x, from_y = self.block(self.sx, c), self.block(self.sy, c)
        self.arrived(0, from_x)
        self.go(3, self.block(self.sx, c, 0), self.to_y)
        self.go(5, from_x, self.mate)
        self.arrived(1, from_y)
        self.go(4, self.block(self.sy, c, 1), self.to_x)
        self.go(6, from_y, self.mate)

    def corner(self):
        for h in range(2):
            ref = self.block(self.sd, self.c, h)
            self.arrived(3 + h, ref)
            self.go(7 + h, ref, self.mate)

    def finish(self):
        c = 1 - self.c
        self.own.wait()
        self.arrived(2, self.block(self.s, c))
        self.arrived(5, self.block(self.sx, c))
        self.arrived(6, self.block(self.sy, c))
        for h in range(2):
            self.arrived(7 + h, self.block(self.sd, c, h))
        for copy in self.sent:
            copy.wait_send()


def everyone_else():
    me = lax.axis_index("dp") * 8 + lax.axis_index("fsdp")

    def other(k):
        device = lax.rem(me + k, 32)
        return (device // 8, lax.rem(device, 8))

    return me, other


def open_kernel(
    shard, router, act_ref, ada_ref, up_shard, down_shard,
    full, routers, seen, rows_out, up_line, down_line,
    heard, part, got, mixed, ssem, rsem, lsem, asem, brsem, rssem, rrsem, tssem, trsem, zssem, zrsem,
    us, ur, ds, dr,
):
    me, other = everyone_else()
    d, s, c = place()
    f = 2 * s + c
    barrier = pltpu.get_barrier_semaphore()

    def hello(k, carry):
        pl.semaphore_signal(barrier, inc=1, device_id=other(k), device_id_type=MESH)
        return carry

    lax.fori_loop(1, 32, hello, 0)
    pl.semaphore_wait(barrier, 31)

    def act_copy(k, source):
        device = other(k)
        return push(act_ref.at[device[1]], heard.at[source], asem.at[k], brsem.at[k], device)

    def router_copy(k, source):
        return push(router, routers.at[source], rssem.at[k], rrsem.at[k], other(k))

    def send(k, carry):
        act_copy(k, me).start()
        return carry

    lax.fori_loop(1, 32, send, 0)
    gather = Gather("cols", shard, full, ssem, rsem, lsem.at[0])
    gather.start()
    lines = (
        Line("cols", up_shard, up_line, us, ur, lsem.at[3]),
        Line("rows", down_shard, down_line, ds, dr, lsem.at[4]),
    )
    for line in lines:
        line.start()
    own_router = pltpu.make_async_copy(router, routers.at[me], lsem.at[1])
    own_router.start()

    def send_router(k, carry):
        router_copy(k, me).start()
        return carry

    lax.fori_loop(1, 32, send_router, 0)
    heard[me] = act_ref[f]

    def take(k, carry):
        copy = act_copy(k, lax.rem(me + 32 - k, 32))
        copy.wait_recv()
        return carry

    lax.fori_loop(1, 32, take, 0)
    everything = heard[...].reshape(256, 128)
    row = lax.broadcasted_iota(jnp.int32, (64, 256), 0)
    column = lax.broadcasted_iota(jnp.int32, (64, 256), 1)
    source = lax.rem(row // 2, 4) * 8 + row // 8
    pick = (column == source * 8 + lax.rem(row, 2)).astype(jnp.bfloat16)
    compact = jnp.dot(
        pick, everything.astype(jnp.bfloat16), preferred_element_type=jnp.float32
    ).astype(jnp.bfloat16)
    seen[...] = jnp.concatenate(
        [compact.astype(jnp.float32), jnp.sum(heard[...], axis=0)], axis=0
    )
    part[...] = jnp.dot(compact, ada_ref[...], preferred_element_type=jnp.float32).reshape(
        8, 8, 1152
    )

    def tile_copy(k):
        target = lax.rem(f + k, 8)
        return push(part.at[target], got.at[k], tssem.at[k], trsem.at[k], (d, target))

    for k in range(1, 8):
        tile_copy(k).start()
    gather.relay(0)
    for k in range(1, 8):
        tile_copy(k).wait_recv()
    total = part[f]
    for k in range(1, 8):
        total = total + got[k]
    mixed[...] = total
    zs = []
    for k in range(1, 4):
        copy = push(mixed, rows_out.at[d], zssem.at[k], zrsem.at[k], at(lax.rem(d + k, 4), s, c))
        copy.start()
        zs.append(copy)
    own_rows = pltpu.make_async_copy(mixed, rows_out.at[d], lsem.at[2])
    own_rows.start()
    gather.corner(0)
    for k in range(1, 4):
        gather.spread_z(k)
    for k in range(1, 4):
        gather.relay(k)
    for k in range(1, 4):
        gather.corner(k)
    for line in lines:
        line.relay()
    gather.finish()
    for line in lines:
        line.finish()
    own_router.wait()
    own_rows.wait()
    for k in range(1, 4):
        push(
            mixed, rows_out.at[lax.rem(d + 4 - k, 4)], zssem.at[k], zrsem.at[k],
            at(lax.rem(d + k, 4), s, c),
        ).wait_recv()
    for copy in zs:
        copy.wait_send()
    for k in range(1, 8):
        tile_copy(k).wait_send()

    def drain(k, carry):
        act_copy(k, me).wait_send()
        copy = router_copy(k, lax.rem(me + 32 - k, 32))
        copy.wait_recv()
        copy.wait_send()
        return carry

    lax.fori_loop(1, 32, drain, 0)


DMA = pltpu.SemaphoreType.DMA
ANYWHERE = pl.BlockSpec(memory_space=pl.ANY)
ONCHIP = pl.BlockSpec(memory_space=pltpu.VMEM)


def opening(shard, router, act, ada, up_shard, down_shard):
    return pl.pallas_call(
        open_kernel,
        out_shape=(
            jax.ShapeDtypeStruct((768, 3072), jnp.bfloat16),
            jax.ShapeDtypeStruct((32, 16, 128), jnp.bfloat16),
            jax.ShapeDtypeStruct((72, 128), jnp.float32),
            jax.ShapeDtypeStruct((4, 8, 1152), jnp.float32),
            jax.ShapeDtypeStruct((96, 3072), jnp.bfloat16),
            jax.ShapeDtypeStruct((768, 384), jnp.bfloat16),
        ),
        in_specs=[ONCHIP] * 6,
        out_specs=(ANYWHERE, ANYWHERE, ONCHIP, ANYWHERE, ANYWHERE, ANYWHERE),
        scratch_shapes=[
            pltpu.VMEM((32, 8, 128), jnp.float32),
            pltpu.VMEM((8, 8, 1152), jnp.float32),
            pltpu.VMEM((8, 8, 1152), jnp.float32),
            pltpu.VMEM((8, 1152), jnp.float32),
            DMA((GATHER_SEMS,)), DMA((GATHER_SEMS,)), DMA((5,)),
            DMA((32,)), DMA((32,)), DMA((32,)), DMA((32,)),
            DMA((8,)), DMA((8,)), DMA((4,)), DMA((4,)),
            DMA((3,)), DMA((3,)), DMA((3,)), DMA((3,)),
        ],
        compiler_params=pltpu.CompilerParams(collective_id=0, has_side_effects=True),
        name="opening",
    )(shard, router, act, ada, up_shard, down_shard)


def group_of(d, s, c):
    return [(j, at(lax.rem(d + j // 2, 4), s, lax.rem(c + j, 2))) for j in range(1, 8)]


class Swap:
    def __init__(self, blocks, out, ssem, rsem, lsem):
        self.blocks, self.out, self.ssem, self.rsem, self.lsem = blocks, out, ssem, rsem, lsem
        self.d, self.s, self.c = place()
        self.me = 2 * self.d + self.c

    def copy(self, j, landing):
        target_d = lax.rem(self.d + j // 2, 4)
        target_c = lax.rem(self.c + j, 2)
        return push(
            self.blocks.at[2 * target_d + target_c],
            self.out.at[landing],
            self.ssem.at[j],
            self.rsem.at[j],
            at(target_d, self.s, target_c),
        )

    def start(self):
        for j in (4, 5, 2, 3, 6, 7, 1):
            self.copy(j, self.me).start()
        self.own = pltpu.make_async_copy(
            self.blocks.at[self.me], self.out.at[self.me], self.lsem
        )
        self.own.start()

    def send(self, step):
        for j in (2 * step, 2 * step + 1):
            if j:
                self.copy(j, self.me).start()
            else:
                self.own = pltpu.make_async_copy(
                    self.blocks.at[self.me], self.out.at[self.me], self.lsem
                )
                self.own.start()

    def finish(self):
        self.own.wait()
        for j in range(1, 8):
            source_d = lax.rem(self.d + 4 - j // 2, 4)
            source_c = lax.rem(self.c + j, 2)
            copy = self.copy(j, 2 * source_d + source_c)
            copy.wait_recv()
            copy.wait_send()


def nt(left, right):
    return lax.dot_general(left, right, (((1,), (1,)), ((), ())), preferred_element_type=jnp.float32)


def tn(left, right):
    return lax.dot_general(left, right, (((0,), (0,)), ((), ())), preferred_element_type=jnp.float32)


def nn(left, right):
    return jnp.dot(left, right, preferred_element_type=jnp.float32)


GELU_SCALE = 0.7978845608028654


def gelu_pair(v):
    square = v * v
    bend = jnp.tanh(GELU_SCALE * (v + 0.044715 * (square * v)))
    half = 0.5 * (1.0 + bend)
    slope = half + 0.5 * v * (1.0 - bend * bend) * (
        GELU_SCALE * (1.0 + (3.0 * 0.044715) * square)
    )
    return v * half, slope


HIDDEN = 512


def out_kernel(
    rows, grads, up_line, down_line, tokens, d_tokens,
    rows_in, grads_in, mixed_out, d_tokens_out, up_grad, down_grad,
    up_full, down_full, tokens_t, d_tokens_t, s1, r1, s2, r2, ssem, rsem, ssem2, rsem2, lsem,
):
    d, s, c = place()
    greet([device for _, device in group_of(d, s, c)] + [at(d, flip(s, 1), c), at(d, flip(s, 2), c)])
    both = (
        Spread("cols", up_line, up_full, ssem, rsem, lsem.at[0]),
        Spread("rows", down_line, down_full, ssem2, rsem2, lsem.at[1]),
    )
    swap_a = Swap(rows, rows_in, s1, r1, lsem.at[2])
    swap_b = Swap(grads, grads_in, s2, r2, lsem.at[3])
    for g in both:
        g.start()
    swap_a.start()
    swap_b.start()
    tokens_t[...] = tokens[...].T
    d_tokens_t[...] = d_tokens[...].T
    mixed_out[...] = jnp.zeros_like(mixed_out)
    d_tokens_out[...] = jnp.zeros_like(d_tokens_out)
    for g in both:
        g.relay()
    for g in both:
        g.corner()
    for g in both:
        g.finish()

    def block(b, carry):
        where = pl.ds(pl.multiple_of(b * HIDDEN, HIDDEN), HIDDEN)
        up, down = up_full[:, where], down_full[:, where]
        act, slope = gelu_pair(nn(tokens[...], up))
        act = act.astype(jnp.bfloat16)
        mixed_out[...] += nt(act, down)
        down_grad[:, where] = nn(d_tokens_t[...], act).astype(jnp.bfloat16)
        d_pre = (slope * nn(d_tokens[...], down)).astype(jnp.bfloat16)
        d_tokens_out[...] += nt(d_pre, up)
        up_grad[:, where] = nn(tokens_t[...], d_pre).astype(jnp.bfloat16)
        return carry

    lax.fori_loop(0, 3072 // HIDDEN, block, 0)
    swap_a.finish()
    swap_b.finish()


def outbound(rows, grads, up_line, down_line, tokens, d_tokens):
    bf, f32 = jnp.bfloat16, jnp.float32
    return pl.pallas_call(
        out_kernel,
        out_shape=(
            jax.ShapeDtypeStruct((8, 144, 768), bf),
            jax.ShapeDtypeStruct((8, 144, 768), bf),
            jax.ShapeDtypeStruct((512, 768), f32),
            jax.ShapeDtypeStruct((512, 768), f32),
            jax.ShapeDtypeStruct((768, 3072), bf),
            jax.ShapeDtypeStruct((768, 3072), bf),
        ),
        in_specs=[ONCHIP] * 6,
        out_specs=(ANYWHERE,) * 2 + (ONCHIP,) * 4,
        scratch_shapes=[pltpu.VMEM((768, 3072), bf)] * 2
        + [pltpu.VMEM((768, 512), bf)] * 2
        + [DMA((8,))] * 4
        + [DMA((9,))] * 4
        + [DMA((4,))],
        compiler_params=pltpu.CompilerParams(
            collective_id=1, has_side_effects=True, vmem_limit_bytes=60 << 20
        ),
        name="outbound",
    )(rows, grads, up_line, down_line, tokens, d_tokens)


def widened(ref):
    return ref[...].astype(jnp.float32)


class Parts:
    def __init__(self, grad, keep, send_x, send_y, sem):
        s = lax.axis_index("fsdp") // 2
        sx, sy = flip(s, 1), flip(s, 2)
        sd = flip(sx, 2)
        rows = grad.shape[0] // 8
        slots = (
            (s, 0, keep.at[0, 0]), (sy, 0, keep.at[0, 1]), (s, 1, keep.at[1, 0]), (sx, 1, keep.at[1, 1]),
            (sx, 0, send_x.at[0]), (sd, 0, send_x.at[1]), (sy, 1, send_y.at[0]), (sd, 1, send_y.at[1]),
        )
        self.copies = [
            pltpu.make_async_copy(
                grad.at[pl.ds(pl.multiple_of((2 * position + h) * rows, 32), rows)], out, sem.at[i]
            )
            for i, (position, h, out) in enumerate(slots)
        ]

    def start(self):
        for copy in self.copies:
            copy.start()

    def finish(self):
        for copy in self.copies:
            copy.wait()


def expert_kernel(
    rows, grads, up_all, down_all, first_grad, second_grad,
    rows_back, grads_back, up_keep, up_x, up_y, down_keep, down_x, down_y, first_part, second_part,
    up, down, act, d_pre, made, d_made, total, d_total, up_grad, down_grad, rows_t,
    fo, fm, fn, ff, fs, fr, fl, so, sm, sn, sf, ss, sr, sl,
    s1, r1, s2, r2, lsem, wsem, psem, qsem,
):
    bf = jnp.bfloat16
    d, s, c = place()
    weights = [
        pltpu.make_async_copy(up_all.at[c], up, wsem.at[0]),
        pltpu.make_async_copy(down_all.at[c], down, wsem.at[1]),
    ]
    for copy in weights:
        copy.start()
    greet([device for _, device in group_of(d, s, c)] + [at(d, flip(s, 1), c), at(d, flip(s, 2), c)])
    sums = (
        DenseSum("cols", first_grad, first_part, fo, fm, fn, ff, None, fs, fr, fl),
        DenseSum("rows", second_grad, second_part, so, sm, sn, sf, None, ss, sr, sl),
    )
    for each in sums:
        each.start()
    swap_a = Swap(made, rows_back, s1, r1, lsem.at[0])
    swap_b = Swap(d_made, grads_back, s2, r2, lsem.at[1])
    for copy in weights:
        copy.wait()
    for step in (2, 1, 3, 0):
        there = lax.rem(d + step, 4)
        chunk = pl.ds(2 * there, 2)
        lines = pl.ds(pl.multiple_of(288 * there, 288), 288)
        x = rows[chunk].reshape(288, 768)
        g = grads[chunk].reshape(288, 768)
        total[...] = jnp.zeros_like(total)
        d_total[...] = jnp.zeros_like(d_total)

        def block(b, carry):
            where = pl.ds(pl.multiple_of(b * HIDDEN, HIDDEN), HIDDEN)
            up_part, down_part = up[:, where], down[where]
            made_act, slope = gelu_pair(nn(x, up_part))
            made_act = made_act.astype(bf)
            act[lines, where] = made_act
            total[...] += nn(made_act, down_part)
            d_part = (slope * nt(g, down_part)).astype(bf)
            d_pre[lines, where] = d_part
            d_total[...] += nt(d_part, up_part)
            return carry

        lax.fori_loop(0, 3072 // HIDDEN, block, 0)
        made[chunk] = total[...].astype(bf).reshape(2, 144, 768)
        d_made[chunk] = d_total[...].astype(bf).reshape(2, 144, 768)
        swap_a.send(step)
        swap_b.send(step)
        if step == 2:
            for each in sums:
                each.merge()
        if step == 3:
            for each in sums:
                each.join()
    rows_t[...] = rows.reshape(1152, 768)[...].T
    g_all = grads.reshape(1152, 768)

    def up_block(b, carry):
        where = pl.ds(pl.multiple_of(b * HIDDEN, HIDDEN), HIDDEN)
        up_grad[:, where] = nn(rows_t[...], d_pre[:, where]).astype(bf)
        return carry

    def down_block(b, carry):
        where = pl.ds(pl.multiple_of(384 * b, 384), 384)
        down_grad[where] = tn(act[:, where], g_all[...]).astype(bf)
        return carry

    up_parts = Parts(up_grad, up_keep, up_x, up_y, psem)
    down_parts = Parts(down_grad, down_keep, down_x, down_y, qsem)
    lax.fori_loop(0, 3072 // HIDDEN, up_block, 0)
    up_parts.start()
    lax.fori_loop(0, 8, down_block, 0)
    down_parts.start()
    for each in sums:
        each.close()
    swap_a.finish()
    swap_b.finish()
    up_parts.finish()
    down_parts.finish()


def experts(rows, grads, up_all, down_all, first_grad, second_grad):
    bf, f32 = jnp.bfloat16, jnp.float32

    def rooms(piece, half):
        return [
            pltpu.VMEM((4,) + piece, bf),
            pltpu.VMEM((4,) + piece, bf),
            pltpu.VMEM((2,) + half, bf),
            pltpu.VMEM((2,) + piece, bf),
            DMA((8,)),
            DMA((8,)),
            DMA((4,)),
        ]

    def parts(r, n):
        return (
            jax.ShapeDtypeStruct((2, 2, r, n), bf),
            jax.ShapeDtypeStruct((2, r, n), bf),
            jax.ShapeDtypeStruct((2, r, n), bf),
        )

    return pl.pallas_call(
        expert_kernel,
        out_shape=(
            jax.ShapeDtypeStruct((8, 144, 768), bf),
            jax.ShapeDtypeStruct((8, 144, 768), bf),
        )
        + parts(96, 3072)
        + parts(384, 768)
        + (
            jax.ShapeDtypeStruct((96, 3072), bf),
            jax.ShapeDtypeStruct((768, 384), bf),
        ),
        in_specs=[ONCHIP, ONCHIP, ANYWHERE, ANYWHERE, ANYWHERE, ANYWHERE],
        out_specs=(ANYWHERE,) * 8 + (ONCHIP, ONCHIP),
        scratch_shapes=[
            pltpu.VMEM((768, 3072), bf),
            pltpu.VMEM((3072, 768), bf),
            pltpu.VMEM((1152, 3072), bf),
            pltpu.VMEM((1152, 3072), bf),
            pltpu.VMEM((8, 144, 768), bf),
            pltpu.VMEM((8, 144, 768), bf),
            pltpu.VMEM((288, 768), f32),
            pltpu.VMEM((288, 768), f32),
            pltpu.VMEM((768, 3072), bf),
            pltpu.VMEM((3072, 768), bf),
            pltpu.VMEM((768, 1152), bf),
        ]
        + rooms((96, 3072), (96, 1536))
        + rooms((768, 384), (384, 384))
        + [DMA((8,))] * 4
        + [DMA((2,)), DMA((2,)), DMA((8,)), DMA((8,))],
        compiler_params=pltpu.CompilerParams(
            collective_id=2, has_side_effects=True, vmem_limit_bytes=67043328
        ),
        name="experts",
    )(rows, grads, up_all, down_all, first_grad, second_grad)


def hop(values, bit):
    return lax.ppermute(values, "fsdp", [(f, f ^ bit) for f in range(8)])


def square_sum(keep, send_x, send_y):
    f32, bf = jnp.float32, jnp.bfloat16
    from_x, from_y = hop(send_x, 2), hop(send_y, 4)
    low_next = hop((keep[0, 1].astype(f32) + from_x[1].astype(f32)).astype(bf), 4)
    high_next = hop((keep[1, 1].astype(f32) + from_y[1].astype(f32)).astype(bf), 2)
    low = keep[0, 0].astype(f32) + from_x[0].astype(f32) + low_next.astype(f32)
    high = keep[1, 0].astype(f32) + from_y[0].astype(f32) + high_next.astype(f32)
    first = lax.rem(lax.axis_index("fsdp"), 2) == 0
    other = hop(jnp.where(first, high, low).astype(bf), 1).astype(f32)
    return jnp.where(first, jnp.stack([low, other]), jnp.stack([other, high]))


def line_sum(part, axis):
    d, size = lax.axis_index("dp"), part.shape[axis] // 4
    total = lax.dynamic_slice_in_dim(part, size * d, size, axis).astype(jnp.float32)
    for k in range(1, 4):
        block = lax.dynamic_slice_in_dim(part, size * lax.rem(d + k, 4), size, axis)
        got = lax.ppermute(block, "dp", [(i, (i + k) % 4) for i in range(4)])
        total = total + got.astype(jnp.float32)
    return total


class DenseSum:
    def __init__(self, kind, grad, out, own, mate, near, far, line, ssem, rsem, lsem):
        self.kind, self.grad, self.out = kind, grad, out
        self.own, self.mate, self.near, self.far, self.line = own, mate, near, far, line
        self.ssem, self.rsem, self.lsem = ssem, rsem, lsem
        self.d, self.s, self.c = place()
        self.order = (
            flip(flip(self.s, 1), 2),
            flip(self.s, 1),
            flip(self.s, 2),
            self.s,
        )

    def piece(self, f):
        if self.kind == "cols":
            return self.grad.at[pl.ds(pl.multiple_of(96 * f, 96), 96)]
        return self.grad.at[:, pl.ds(pl.multiple_of(384 * f, 384), 384)]

    def half(self, ref, h):
        if self.kind == "cols":
            return ref.at[:, pl.ds(1536 * h, 1536)]
        return ref.at[pl.ds(384 * h, 384)]

    def quarter(self, ref, q):
        if self.kind == "cols":
            return ref.at[:, pl.ds(pl.multiple_of(768 * q, 768), 768)]
        return ref.at[pl.ds(pl.multiple_of(192 * q, 192), 192)]

    def start(self):
        d, s, c = self.d, self.s, self.c
        self.zero, self.local = [], []
        for j, position in enumerate(self.order):
            copy = push(
                self.piece(2 * position + 1 - c), self.mate.at[j], self.ssem.at[j], self.rsem.at[j], at(d, s, 1 - c)
            )
            copy.start()
            self.zero.append(copy)
            copy = pltpu.make_async_copy(self.piece(2 * position + c), self.own.at[j], self.lsem.at[j])
            copy.start()
            self.local.append(copy)

    def merge(self):
        d, s, c = self.d, self.s, self.c
        sx, sy = flip(s, 1), flip(s, 2)
        self.one = []
        for j in range(4):
            self.zero[j].wait_recv()
            self.local[j].wait()
            self.own[j] = (widened(self.own.at[j]) + widened(self.mate.at[j])).astype(jnp.bfloat16)
            if j == 0:
                for h, target in enumerate((sx, sy)):
                    copy = push(
                        self.half(self.own.at[0], h), self.near.at[h], self.ssem.at[4 + h], self.rsem.at[4 + h],
                        at(d, target, c),
                    )
                    copy.start()
                    self.one.append(copy)

    def join(self):
        d, s, c = self.d, self.s, self.c
        sx, sy = flip(s, 1), flip(s, 2)
        for h, j in ((0, 2), (1, 1)):
            self.one[h].wait_recv()
            where = self.half(self.own.at[j], h)
            where[...] = (widened(where) + widened(self.near.at[h])).astype(jnp.bfloat16)
        self.two = []
        for h, target in enumerate((sx, sy)):
            copy = push(
                self.own.at[1 + h], self.far.at[h], self.ssem.at[6 + h], self.rsem.at[6 + h], at(d, target, c)
            )
            copy.start()
            self.two.append(copy)

    def square(self):
        for copy in self.two:
            copy.wait_recv()
        return (
            widened(self.own.at[3]) + widened(self.far.at[0]) + widened(self.far.at[1])
        ).astype(jnp.bfloat16)

    def along(self):
        d, s, c = self.d, self.s, self.c
        self.own[3] = self.square()
        self.three = []
        for k in range(1, 4):
            target = lax.rem(d + k, 4)
            copy = push(
                self.quarter(self.own.at[3], target), self.line.at[k - 1], self.ssem.at[7 + k], self.rsem.at[7 + k],
                at(target, s, c),
            )
            copy.start()
            self.three.append(copy)

    def finish(self):
        total = widened(self.quarter(self.own.at[3], self.d))
        for k in range(1, 4):
            self.three[k - 1].wait_recv()
            total = total + widened(self.line.at[k - 1])
        self.out[...] = total
        self.sent(self.three)

    def close(self):
        self.out[...] = self.square()
        self.sent([])

    def sent(self, more):
        for copy in self.zero + self.one + self.two + more:
            copy.wait_send()


class Tail:
    def __init__(self, d_rows, router, act, ada, ada_out, d_act_out, router_out, z1, plane, plane_in, z2, z2_in, sems):
        self.d_rows, self.router, self.act, self.ada = d_rows, router, act, ada
        self.ada_out, self.d_act_out, self.router_out = ada_out, d_act_out, router_out
        self.z1, self.plane, self.plane_in, self.z2, self.z2_in = z1, plane, plane_in, z2, z2_in
        self.sems = sems
        self.d, self.s, self.c = place()
        self.f = 2 * self.s + self.c

    def z_copy(self, k, src, dst, base):
        send, recv = self.sems[base], self.sems[base + 1]
        return push(src, dst, send.at[k], recv.at[k], at(lax.rem(self.d + k, 4), self.s, self.c))

    def f_copy(self, k, src, dst, base):
        send, recv = self.sems[base], self.sems[base + 1]
        return push(src, dst, send.at[k], recv.at[k], (self.d, lax.rem(self.f + k, 8)))

    def start(self):
        self.all = [
            self.z_copy(k, self.d_rows.at[lax.rem(self.d + k, 4)], self.z1.at[k], 0) for k in range(1, 4)
        ]
        for copy in self.all:
            copy.start()

    def second(self):
        total = self.d_rows[self.d]
        for k in range(1, 4):
            self.all[k - 1].wait_recv()
            total = total + self.z1[k]
        for target in range(8):
            self.plane[target, :, 0:1152] = total
            self.plane[target, :, 1152:1280] = self.router[target]
        copies = [
            self.f_copy(k, self.plane.at[lax.rem(self.f + k, 8)], self.plane_in.at[lax.rem(8 - k, 8)], 2)
            for k in range(1, 8)
        ]
        for copy in copies:
            copy.start()
        self.in_plane = copies
        self.all = self.all + copies

    def third(self):
        f = self.f
        self.plane_in[0] = self.plane[f]
        for copy in self.in_plane:
            copy.wait_recv()
        everything = self.plane_in[...]
        router = jnp.sum(everything[:, :, 1152:1280], axis=0)
        rows = everything[:, :, 0:1152].reshape(64, 1152)
        line = lax.broadcasted_iota(jnp.int32, (64, 64), 0)
        column = lax.broadcasted_iota(jnp.int32, (64, 64), 1)
        turn = (lax.rem(line // 8 + 8 - f, 8) * 8 + lax.rem(line, 8) == column).astype(jnp.bfloat16)
        d_mod = nn(turn, rows.astype(jnp.bfloat16)).astype(jnp.bfloat16)
        self.ada_out[...] = tn(self.act[...], d_mod)[0:96]
        part = nt(d_mod, self.ada[...])
        self.z2[0:64, 0:96] = part
        self.z2[0:64, 96:128] = jnp.zeros((64, 32), jnp.float32)
        self.z2[64:72, :] = router
        copies = [self.z_copy(k, self.z2, self.z2_in.at[k], 4) for k in range(1, 4)]
        for copy in copies:
            copy.start()
        self.along = copies
        self.all = self.all + copies

    def fourth(self):
        total = self.z2[...]
        for k in range(1, 4):
            self.along[k - 1].wait_recv()
            total = total + self.z2_in[k]
        self.router_out[...] = total[64:72]
        self.z2_in[0] = total
        copies = [
            self.f_copy(
                k,
                self.z2_in.at[0, pl.ds(pl.multiple_of(8 * lax.rem(self.f + k, 8), 8), 8)],
                self.d_act_out.at[self.f],
                6,
            )
            for k in range(1, 8)
        ]
        for copy in copies:
            copy.start()
        self.d_act_out[self.f] = self.z2_in[0, pl.ds(pl.multiple_of(8 * self.f, 8), 8)]
        self.last = copies
        self.all = self.all + copies

    def finish(self):
        for k in range(1, 8):
            self.f_copy(
                k, self.z2_in.at[0, pl.ds(0, 8)], self.d_act_out.at[lax.rem(self.f + 8 - k, 8)], 6
            ).wait_recv()
        for copy in self.all:
            copy.wait_send()


def dense_kernel(kinds, *refs):
    n = len(kinds)
    grads, small, outs = refs[:n], refs[n : n + 4], refs[n + 4 : 2 * n + 4]
    small_outs, rest = refs[2 * n + 4 : 2 * n + 7], refs[2 * n + 7 :]
    d, s, c = place()
    f = 2 * s + c
    greet(
        [at(lax.rem(d + k, 4), s, c) for k in range(1, 4)]
        + [(d, lax.rem(f + k, 8)) for k in range(1, 8)]
    )
    sums = [
        DenseSum(kinds[i], grads[i], outs[i], *rest[8 * i : 8 * i + 8]) for i in range(n)
    ]
    rest = rest[8 * n :]
    tail = Tail(*small, *small_outs, *rest[:5], rest[5:])
    tail.start()
    for each in sums:
        each.start()
    tail.second()
    for each in sums:
        each.merge()
    tail.third()
    for each in sums:
        each.join()
    tail.fourth()
    for each in sums:
        each.along()
    for each in sums:
        each.finish()
    tail.finish()


def dense_sums(kinds, grads, small, collective_id):
    bf, f32 = jnp.bfloat16, jnp.float32
    outs, scratch = [], []
    for kind in kinds:
        if kind == "cols":
            piece, half, quarter = (96, 3072), (96, 1536), (96, 768)
        else:
            piece, half, quarter = (768, 384), (384, 384), (192, 384)
        outs.append(jax.ShapeDtypeStruct(quarter, f32))
        scratch += [
            pltpu.VMEM((4,) + piece, bf),
            pltpu.VMEM((4,) + piece, bf),
            pltpu.VMEM((2,) + half, bf),
            pltpu.VMEM((2,) + piece, bf),
            pltpu.VMEM((3,) + quarter, bf),
            DMA((11,)),
            DMA((11,)),
            DMA((4,)),
        ]
    outs += [
        jax.ShapeDtypeStruct((96, 1152), f32),
        jax.ShapeDtypeStruct((8, 8, 128), f32),
        jax.ShapeDtypeStruct((8, 128), f32),
    ]
    scratch += [
        pltpu.VMEM((4, 8, 1152), f32),
        pltpu.VMEM((8, 8, 1280), f32),
        pltpu.VMEM((8, 8, 1280), f32),
        pltpu.VMEM((72, 128), f32),
        pltpu.VMEM((4, 72, 128), f32),
        DMA((4,)), DMA((4,)), DMA((8,)), DMA((8,)), DMA((4,)), DMA((4,)), DMA((8,)), DMA((8,)),
    ]
    return pl.pallas_call(
        functools.partial(dense_kernel, kinds),
        out_shape=tuple(outs),
        in_specs=[ANYWHERE] * len(kinds) + [ONCHIP] * 4,
        out_specs=(ONCHIP,) * len(outs),
        scratch_shapes=scratch,
        compiler_params=pltpu.CompilerParams(collective_id=collective_id, has_side_effects=True),
        name="dense_sums",
    )(*grads, *small)


def fitted_shards(
    tokens,
    condition,
    ada_weight,
    qkv_weight,
    out_weight,
    shared_up,
    shared_down,
    router_weight,
    expert_up,
    expert_down,
    routes,
    image_sizes,
    cotangent,
):
    bf = jnp.bfloat16
    d_index, f_index = lax.axis_index("dp"), lax.axis_index("fsdp")
    model_width = tokens.shape[1]
    head_size = model_width // HEADS
    inside, segment = owners(image_sizes)
    ids = jnp.arange(EXPERTS, dtype=jnp.int32)
    hot = routes[:, :, None] == ids[None, None, :]
    hot_any = jnp.any(hot, axis=1).astype(bf)
    order = jnp.arange(LONG, dtype=jnp.int32)
    earlier = (order[:, None] > order[None, :]).astype(bf)
    before = nn(earlier, hot_any)
    position = jnp.sum(jnp.where(hot, before[:, None, :], 0.0), axis=-1).astype(jnp.int32)
    target = routes * CAP + position
    places = jnp.arange(EXPERTS * CAP, dtype=jnp.int32)
    send_0 = (places[:, None] == target[None, :, 0]).astype(bf)
    send_1 = (places[:, None] == target[None, :, 1]).astype(bf)
    live = (segment < IMG_DEV).astype(jnp.float32)
    counts = jnp.sum(live[:, None] * hot_any.astype(jnp.float32), axis=0)
    cond_float = condition.astype(jnp.float32)
    activated = jax.nn.silu(cond_float).astype(bf)
    act_slices = activated.astype(jnp.float32).reshape(IMG_DEV, 8, 96).transpose(1, 0, 2)
    act_slices = jnp.pad(act_slices, ((0, 0), (0, 6), (0, 32)))
    act_slices = act_slices.at[:, 2, :EXPERTS].set(counts)
    ada_pad = jnp.pad(ada_weight, ((0, 32), (0, 0)))
    router_pack = jnp.pad(router_weight.reshape(192), (0, 2048 - 192)).reshape(16, 128)
    qkvo_shard = jnp.concatenate([qkv_weight, out_weight], axis=1)
    qkvo, routers, seen, mod_rows, up_line, down_line = opening(
        qkvo_shard, router_pack, act_slices, ada_pad, shared_up, shared_down.T
    )
    expert_up, expert_down, seen = lax.optimization_barrier((expert_up, expert_down, seen))
    up_all, down_all = gather_experts(expert_up, expert_down)
    expert_counts = seen[66, :EXPERTS].astype(jnp.int32)
    modulation = lax.dynamic_slice(mod_rows, (0, 2 * d_index, 0), (4, 2, 1152))
    modulation = modulation.transpose(1, 0, 2).reshape(2, 4608)
    router_full = (
        routers.reshape(32, 2048)[:, :192]
        .reshape(4, 8, 96, 2)
        .transpose(1, 2, 0, 3)
        .reshape(model_width, EXPERTS)
    )
    qkvo = qkvo.reshape(model_width, 4, 768)
    qkv_full = qkvo[:, :, :576].reshape(model_width, 2304)
    out_full = qkvo[:, :, 576:].reshape(model_width, 768)
    per_row = inside[:, 0:1] * modulation[0:1] + inside[:, 1:2] * modulation[1:2]
    shift_one, scale_one, gate_one, shift_two, scale_two, gate_two = jnp.split(per_row, 6, axis=1)
    token_float = tokens.astype(jnp.float32)
    normed_one, inv_one = layer_norm(token_float)
    first_input = (normed_one * (1.0 + scale_one) + shift_one).astype(bf)
    qkv_rows = nn(first_input, qkv_full).astype(bf)
    queries, keys, values = (
        qkv_rows[:, i * model_width : (i + 1) * model_width]
        .reshape(LONG, HEADS, head_size)
        .transpose(1, 0, 2)
        for i in range(3)
    )
    scale = head_size**-0.5
    allowed = (segment[:, None] == segment[None, :])[None]
    scores = jnp.einsum("hqd,hkd->hqk", queries, keys, preferred_element_type=jnp.float32) * scale
    scores = jnp.where(allowed, scores, -1e30)
    row_max = jnp.max(scores, axis=-1, keepdims=True)
    weight = jnp.exp(scores - row_max)
    running = jnp.sum(weight, axis=-1, keepdims=True)
    probability = weight / running
    prob_low = probability.astype(bf)
    attended = jnp.einsum("hqk,hkd->hqd", prob_low, values, preferred_element_type=jnp.float32)
    attended = attended.astype(bf).transpose(1, 0, 2).reshape(LONG, model_width)
    projected = nn(attended, out_full)
    residual_one = token_float + gate_one * projected
    normed_two, inv_two = layer_norm(residual_one)
    second_input = (normed_two * (1.0 + scale_two) + shift_two).astype(bf)
    logits = nn(second_input, router_full)
    route_hot = hot.astype(jnp.float32)
    chosen = jnp.sum(logits[:, None, :] * route_hot, axis=-1)
    gate_share = jax.nn.softmax(chosen, axis=-1)
    upstream = cotangent.astype(jnp.float32)
    d_mixed = gate_two * upstream
    rows = nn(send_0 + send_1, second_input).astype(bf).reshape(EXPERTS, CAP, model_width)
    weighted = jnp.concatenate(
        [(gate_share[:, k : k + 1] * d_mixed).astype(bf) for k in range(2)], axis=0
    )
    grads = (
        nn(jnp.concatenate([send_0, send_1], axis=1), weighted)
        .astype(bf)
        .reshape(EXPERTS, CAP, model_width)
    )
    rows_in, grads_in, shared_out, d_second, shared_first_grad, shared_second_grad = outbound(
        rows, grads, up_line, down_line, second_input, d_mixed.astype(bf)
    )
    returned, d_returned, *parts, first_part, second_part = experts(
        rows_in, grads_in, up_all, down_all, shared_first_grad, shared_second_grad
    )
    expert_up_grad, expert_down_grad = square_sum(*parts[:3]), square_sum(*parts[3:])
    shared_first_sum, shared_second_sum = line_sum(first_part, 1), line_sum(second_part, 0)
    returned = returned.reshape(EXPERTS * CAP, model_width)
    d_returned = d_returned.reshape(EXPERTS * CAP, model_width)
    picked_0 = tn(send_0, returned)
    picked_1 = tn(send_1, returned)
    mixed = shared_out + (gate_share[:, 0:1] * picked_0 + gate_share[:, 1:2] * picked_1)
    output = (residual_one + gate_two * mixed).astype(bf)
    d_gate_two = upstream * mixed
    d_gate_share = jnp.stack(
        [jnp.sum(d_mixed * picked_0, axis=-1), jnp.sum(d_mixed * picked_1, axis=-1)], axis=1
    )
    d_chosen = gate_share * (
        d_gate_share - jnp.sum(gate_share * d_gate_share, axis=-1, keepdims=True)
    )
    d_logits = jnp.sum(d_chosen[:, :, None] * route_hot, axis=1).astype(bf)
    router_grad = tn(d_logits, second_input)
    d_second = d_second + nt(d_logits, router_full) + tn(send_0 + send_1, d_returned)
    d_scale_two = d_second * normed_two
    d_residual = upstream + norm_back(d_second * (1.0 + scale_two), normed_two, inv_two)
    d_projected = (gate_one * d_residual).astype(bf)
    d_gate_one = d_residual * projected
    out_grad = tn(attended, d_projected)
    d_attended = nt(d_projected, out_full).astype(bf)
    d_attended = d_attended.reshape(LONG, HEADS, head_size).transpose(1, 0, 2)
    d_prob = jnp.einsum("hqd,hkd->hqk", d_attended, values, preferred_element_type=jnp.float32)
    d_scores = (
        probability * (d_prob - jnp.sum(probability * d_prob, axis=-1, keepdims=True))
    ).astype(bf)
    d_queries = jnp.einsum("hqk,hkd->hqd", d_scores, keys, preferred_element_type=jnp.float32) * scale
    d_keys = jnp.einsum("hqk,hqd->hkd", d_scores, queries, preferred_element_type=jnp.float32) * scale
    d_values = jnp.einsum("hqk,hqd->hkd", prob_low, d_attended, preferred_element_type=jnp.float32)
    d_qkv = jnp.concatenate(
        [
            piece.astype(bf).transpose(1, 0, 2).reshape(LONG, model_width)
            for piece in (d_queries, d_keys, d_values)
        ],
        axis=1,
    )
    qkv_grad = tn(first_input, d_qkv)
    d_first = nt(d_qkv, qkv_full)
    d_scale_one = d_first * normed_one
    tokens_grad = d_residual + norm_back(d_first * (1.0 + scale_one), normed_one, inv_one)
    qkvo_grad = (
        jnp.concatenate(
            [qkv_grad.reshape(model_width, 4, 576), out_grad.reshape(model_width, 4, 192)], axis=2
        )
        .astype(bf)
        .reshape(model_width, 3072)
    )
    d_modulation = jnp.concatenate(
        [
            jnp.stack([jnp.sum(inside[:, j : j + 1] * piece, axis=0) for j in range(IMG_DEV)])
            for piece in (d_first, d_scale_one, d_gate_one, d_second, d_scale_two, d_gate_two)
        ],
        axis=1,
    ).astype(bf)
    d_mod_rows = d_modulation.astype(jnp.float32).reshape(2, 4, 1152).transpose(1, 0, 2)
    d_mod_rows = lax.dynamic_update_slice(
        jnp.zeros((4, 8, 1152), jnp.float32), d_mod_rows, (0, 2 * d_index, 0)
    )
    router_tiles = jnp.pad(
        router_grad.reshape(EXPERTS, 8, 96).transpose(1, 0, 2), ((0, 0), (0, 0), (0, 32))
    )
    qkvo_sum, ada_grad, d_act_tiles, router_sum = dense_sums(
        ("cols",),
        (qkvo_grad,),
        (d_mod_rows, router_tiles, seen[:64].astype(bf), ada_weight),
        3,
    )
    d_activated = lax.dynamic_slice(d_act_tiles, (0, 2 * d_index, 0), (8, 2, 96))
    d_activated = d_activated.transpose(1, 0, 2).reshape(2, model_width)
    condition_grad = jax.vjp(jax.nn.silu, cond_float)[1](d_activated)[0]
    router_out = lax.dynamic_slice(router_sum, (2 * d_index, 0), (2, 96)).T
    return (
        output,
        tokens_grad,
        condition_grad,
        ada_grad,
        qkvo_sum[:, :576],
        qkvo_sum[:, 576:],
        shared_first_sum,
        shared_second_sum.T,
        router_out,
        expert_up_grad,
        expert_down_grad,
        expert_counts,
    )


def solution(mesh):
    placed = (
        P(("dp", "fsdp"), None),
        P(("dp", "fsdp"), None),
        P("fsdp", "dp"),
        P("fsdp", "dp"),
        P("fsdp", "dp"),
        P("fsdp", "dp"),
        P("fsdp", "dp"),
        P("fsdp", "dp"),
        P("dp", "fsdp", None),
        P("dp", "fsdp", None),
        P(("dp", "fsdp"), None),
        P(("dp", "fsdp")),
        P(("dp", "fsdp"), None),
    )
    fitted = mesh.shape["dp"] == 4 and mesh.shape["fsdp"] == 8
    return jax.shard_map(
        fitted_shards if fitted else shards,
        mesh=mesh,
        in_specs=placed,
        out_specs=(
            P(("dp", "fsdp"), None),
            P(("dp", "fsdp"), None),
            P(("dp", "fsdp"), None),
            P("fsdp", "dp"),
            P("fsdp", "dp"),
            P("fsdp", "dp"),
            P("fsdp", "dp"),
            P("fsdp", "dp"),
            P("fsdp", "dp"),
            P("dp", "fsdp", None),
            P("dp", "fsdp", None),
            P(),
        ),
        check_vma=False,
    )
```

```python
import functools

import jax
import jax.numpy as jnp
from jax import lax
from jax.experimental import pallas as pl
from jax.experimental.pallas import tpu as pltpu
from jax.sharding import PartitionSpec as P

HEADS = 12
EXPERTS = 8
CAP = 144
IMG_DEV = 2
LONG = 512
MESH = pl.DeviceIdType.MESH


EXACT = lax.Precision.HIGHEST


def owners(image_sizes):
    starts = jnp.cumsum(image_sizes) - image_sizes
    position = jnp.arange(LONG, dtype=jnp.int32)[:, None]
    inside = (position >= starts[None, :]) & (position < (starts + image_sizes)[None, :])
    slot_ids = jnp.arange(IMG_DEV, dtype=jnp.int32)
    segment = jnp.sum(jnp.where(inside, slot_ids[None, :], 0), axis=1) + jnp.where(
        jnp.any(inside, axis=1), 0, IMG_DEV
    )
    return (inside.astype(jnp.float32), segment)


def dispatch_plan(routes):
    flat = routes.reshape(-1)
    onehot = (flat[:, None] == jnp.arange(EXPERTS, dtype=jnp.int32)[None, :]).astype(jnp.int32)
    before = jnp.cumsum(onehot, axis=0) - onehot
    position = jnp.sum(before * onehot, axis=1)
    target = flat * CAP + position
    assignment = jnp.arange(2 * LONG, dtype=jnp.int32)
    source = jnp.zeros((EXPERTS * CAP,), jnp.int32).at[target].set(assignment)
    filled = jnp.zeros((EXPERTS * CAP,), jnp.int32).at[target].set(1)
    return (target, source, filled)


def layer_norm(values_in):
    centred = values_in - jnp.mean(values_in, axis=-1, keepdims=True)
    inv_std = lax.rsqrt(jnp.mean(centred * centred, axis=-1, keepdims=True) + 1e-06)
    return (centred * inv_std, inv_std)


def norm_back(upstream, normed, inv_std):
    return (
        upstream
        - jnp.mean(upstream, axis=-1, keepdims=True)
        - normed * jnp.mean(upstream * normed, axis=-1, keepdims=True)
    ) * inv_std


def gelu_tanh(values_in):
    return jax.nn.gelu(values_in, approximate=True)


def gelu_back(values_in, upstream):
    return jax.vjp(gelu_tanh, values_in)[1](upstream)[0]


def collect(first, second, third):
    widened = (
        lax.all_gather(first, "dp", axis=1, tiled=True),
        lax.all_gather(second, "dp", axis=1, tiled=True),
        lax.all_gather(third, "dp", axis=1, tiled=True),
    )
    return (
        lax.all_gather(widened[0], "fsdp", axis=0, tiled=True),
        lax.all_gather(widened[1], "fsdp", axis=0, tiled=True),
        lax.all_gather(widened[2], "fsdp", axis=0, tiled=True),
    )


def spread(first, second, third):
    row_sums = (
        lax.psum_scatter(first, "fsdp", scatter_dimension=0, tiled=True),
        lax.psum_scatter(second, "fsdp", scatter_dimension=0, tiled=True),
        lax.psum_scatter(third, "fsdp", scatter_dimension=0, tiled=True),
    )
    return (
        lax.psum_scatter(row_sums[0], "dp", scatter_dimension=1, tiled=True),
        lax.psum_scatter(row_sums[1], "dp", scatter_dimension=1, tiled=True),
        lax.psum_scatter(row_sums[2], "dp", scatter_dimension=1, tiled=True),
    )


def gather_experts(up_shard, down_shard):
    return (
        lax.all_gather(up_shard, "fsdp", axis=1, tiled=True),
        lax.all_gather(down_shard, "fsdp", axis=1, tiled=True),
    )


def expert_forward(buffer_in, up_full, down_full):
    expert_pre = jnp.einsum(
        "secd,edf->secf", buffer_in, up_full, preferred_element_type=jnp.float32
    )
    expert_act = gelu_tanh(expert_pre).astype(jnp.bfloat16)
    expert_out = jnp.einsum(
        "secf,efd->secd", expert_act, down_full, preferred_element_type=jnp.float32
    ).astype(jnp.bfloat16)
    return (expert_pre, expert_act, expert_out)


def expert_backward(buffer_in, expert_pre, expert_act, d_out, up_full, down_full):
    d_act = jnp.einsum("secd,efd->secf", d_out, down_full, preferred_element_type=jnp.float32)
    d_pre = gelu_back(expert_pre, d_act).astype(jnp.bfloat16)
    d_rows = jnp.einsum(
        "secf,edf->secd", d_pre, up_full, preferred_element_type=jnp.float32
    ).astype(jnp.bfloat16)
    down_grad = jnp.einsum("secf,secd->efd", expert_act, d_out, preferred_element_type=jnp.float32)
    up_grad = jnp.einsum("secd,secf->edf", buffer_in, d_pre, preferred_element_type=jnp.float32)
    return (up_grad, down_grad, d_rows)


def attend(queries, keys_all, values_all, segment):
    row_count, head_count, head_size = queries.shape
    block_rows = min(512, row_count)
    block_count = row_count // block_rows
    score_scale = head_size ** (-0.5)

    def one_block(pieces):
        query_part, segment_part = pieces
        allowed = (segment_part[:, None] == segment[None, :])[None]
        scores = (
            jnp.einsum("qhd,khd->hqk", query_part, keys_all, preferred_element_type=jnp.float32)
            * score_scale
        )
        scores = jnp.where(allowed, scores, -1e30)
        row_max = jnp.max(scores, axis=-1, keepdims=True)
        weight = jnp.exp(scores - row_max)
        running = jnp.sum(weight, axis=-1, keepdims=True)
        probability = (weight / running).astype(jnp.bfloat16)
        attended = jnp.einsum(
            "hqk,khd->qhd", probability, values_all, preferred_element_type=jnp.float32
        )
        return (attended.astype(jnp.bfloat16), (row_max + jnp.log(running))[:, :, 0])

    return lax.map(
        one_block,
        (
            queries.reshape(block_count, block_rows, head_count, head_size),
            segment.reshape(block_count, block_rows),
        ),
    )


def attend_back(queries, keys_all, values_all, segment, log_totals, d_attended):
    row_count, head_count, head_size = queries.shape
    block_rows = min(512, row_count)
    block_count = row_count // block_rows
    score_scale = head_size ** (-0.5)

    def one_block(carry, pieces):
        key_sum, value_sum = carry
        query_part, segment_part, total_part, grad_part = pieces
        allowed = (segment_part[:, None] == segment[None, :])[None]
        scores = (
            jnp.einsum("qhd,khd->hqk", query_part, keys_all, preferred_element_type=jnp.float32)
            * score_scale
        )
        scores = jnp.where(allowed, scores, -1e30)
        probability = jnp.exp(scores - total_part[:, :, None])
        d_prob = jnp.einsum(
            "qhd,khd->hqk", grad_part, values_all, preferred_element_type=jnp.float32
        )
        d_scores = (
            probability * (d_prob - jnp.sum(probability * d_prob, axis=-1, keepdims=True))
        ).astype(jnp.bfloat16)
        query_grad = (
            jnp.einsum("hqk,khd->qhd", d_scores, keys_all, preferred_element_type=jnp.float32)
            * score_scale
        )
        key_sum = (
            key_sum
            + jnp.einsum("hqk,qhd->khd", d_scores, query_part, preferred_element_type=jnp.float32)
            * score_scale
        )
        value_sum = value_sum + jnp.einsum(
            "hqk,qhd->khd",
            probability.astype(jnp.bfloat16),
            grad_part,
            preferred_element_type=jnp.float32,
        )
        return ((key_sum, value_sum), query_grad)

    empty = jnp.zeros(keys_all.shape, jnp.float32)
    sums, query_grads = lax.scan(
        one_block,
        (empty, empty),
        (
            queries.reshape(block_count, block_rows, head_count, head_size),
            segment.reshape(block_count, block_rows),
            log_totals,
            d_attended.reshape(block_count, block_rows, head_count, head_size),
        ),
    )
    return (query_grads.reshape(row_count, head_count, head_size), sums[0], sums[1])


def shards(
    tokens,
    condition,
    ada_weight,
    qkv_weight,
    out_weight,
    shared_up,
    shared_down,
    router_weight,
    expert_up,
    expert_down,
    routes,
    image_sizes,
    cotangent,
):
    model_width = tokens.shape[1]
    head_size = model_width // HEADS
    inside, segment = owners(image_sizes)
    target, source, filled = dispatch_plan(routes)
    route_hot = (routes[:, :, None] == jnp.arange(EXPERTS, dtype=jnp.int32)[None, None, :]).astype(
        jnp.float32
    )
    live = (segment < IMG_DEV).astype(jnp.int32)
    local_counts = jnp.sum(live[:, None, None] * route_hot.astype(jnp.int32), axis=(0, 1))
    expert_counts = lax.psum(local_counts, ("dp", "fsdp"))
    ada_full, qkv_full, out_full = collect(ada_weight, qkv_weight, out_weight)
    cond_float = condition.astype(jnp.float32)
    activated = jax.nn.silu(cond_float).astype(jnp.bfloat16)
    modulation = jnp.dot(activated, ada_full, preferred_element_type=jnp.float32)
    per_row = jnp.dot(inside, modulation, precision=EXACT, preferred_element_type=jnp.float32)
    shift_one, scale_one, gate_one, shift_two, scale_two, gate_two = jnp.split(per_row, 6, axis=1)
    token_float = tokens.astype(jnp.float32)
    normed_one, inv_one = layer_norm(token_float)
    first_input = (normed_one * (1.0 + scale_one) + shift_one).astype(jnp.bfloat16)
    qkv_rows = jnp.dot(first_input, qkv_full, preferred_element_type=jnp.float32).astype(
        jnp.bfloat16
    )
    queries = qkv_rows[:, :model_width].reshape(-1, HEADS, head_size)
    keys_all = qkv_rows[:, model_width : 2 * model_width].reshape(-1, HEADS, head_size)
    values_all = qkv_rows[:, 2 * model_width :].reshape(-1, HEADS, head_size)
    attended_blocks, log_totals = attend(queries, keys_all, values_all, segment)
    attended = attended_blocks.reshape(-1, model_width)
    projected = jnp.dot(attended, out_full, preferred_element_type=jnp.float32)
    residual_one = token_float + gate_one * projected
    normed_two, inv_two = layer_norm(residual_one)
    second_input = (normed_two * (1.0 + scale_two) + shift_two).astype(jnp.bfloat16)
    shared_first, shared_second, router_full = collect(shared_up, shared_down, router_weight)
    shared_pre = jnp.dot(second_input, shared_first, preferred_element_type=jnp.float32)
    shared_act = gelu_tanh(shared_pre).astype(jnp.bfloat16)
    shared_out = jnp.dot(shared_act, shared_second, preferred_element_type=jnp.float32)
    logits = jnp.dot(second_input, router_full, preferred_element_type=jnp.float32)
    chosen = jnp.sum(logits[:, None, :] * route_hot, axis=-1)
    gate_share = jax.nn.softmax(chosen, axis=-1)
    buffer_rows = jnp.take(second_input, source // 2, axis=0).reshape(EXPERTS, CAP, model_width)
    up_full, down_full = gather_experts(expert_up, expert_down)
    groups = lax.axis_size("dp")
    expert_in = lax.all_to_all(
        buffer_rows.reshape(groups, EXPERTS // groups, CAP, model_width),
        "dp",
        split_axis=0,
        concat_axis=0,
        tiled=True,
    )
    expert_pre, expert_act, expert_out = expert_forward(expert_in, up_full, down_full)
    returned = lax.all_to_all(expert_out, "dp", split_axis=0, concat_axis=0, tiled=True).reshape(
        EXPERTS, CAP, model_width
    )
    picked = (
        jnp.take(returned.reshape(EXPERTS * CAP, model_width), target, axis=0)
        .reshape(-1, 2, model_width)
        .astype(jnp.float32)
    )
    mixed = shared_out + jnp.sum(gate_share[:, :, None] * picked, axis=1)
    output = (residual_one + gate_two * mixed).astype(jnp.bfloat16)
    upstream = cotangent.astype(jnp.float32)
    d_mixed = gate_two * upstream
    d_gate_two = upstream * mixed
    d_gate_share = jnp.sum(d_mixed[:, None, :] * picked, axis=-1)
    slot_gate = jnp.take(gate_share.reshape(-1), source) * filled.astype(jnp.float32)
    d_buffer = (
        (jnp.take(d_mixed, source // 2, axis=0) * slot_gate[:, None])
        .astype(jnp.bfloat16)
        .reshape(EXPERTS, CAP, model_width)
    )
    shared_first, shared_second, router_full = collect(shared_up, shared_down, router_weight)
    up_full, down_full = gather_experts(expert_up, expert_down)
    arrived = lax.all_to_all(
        d_buffer.reshape(groups, EXPERTS // groups, CAP, model_width),
        "dp",
        split_axis=0,
        concat_axis=0,
        tiled=True,
    )
    up_grad, down_grad, d_rows = expert_backward(
        expert_in, expert_pre, expert_act, arrived, up_full, down_full
    )
    d_returned = lax.all_to_all(d_rows, "dp", split_axis=0, concat_axis=0, tiled=True).reshape(
        EXPERTS, CAP, model_width
    )
    expert_sums = (
        lax.psum_scatter(up_grad, "fsdp", scatter_dimension=1, tiled=True),
        lax.psum_scatter(down_grad, "fsdp", scatter_dimension=1, tiled=True),
    )
    d_shared = d_mixed.astype(jnp.bfloat16)
    shared_second_grad = jnp.einsum(
        "tf,td->fd", shared_act, d_shared, preferred_element_type=jnp.float32
    )
    d_shared_act = jnp.einsum(
        "td,fd->tf", d_shared, shared_second, preferred_element_type=jnp.float32
    )
    d_shared_pre = gelu_back(shared_pre, d_shared_act).astype(jnp.bfloat16)
    shared_first_grad = jnp.einsum(
        "td,tf->df", second_input, d_shared_pre, preferred_element_type=jnp.float32
    )
    d_chosen = gate_share * (
        d_gate_share - jnp.sum(gate_share * d_gate_share, axis=-1, keepdims=True)
    )
    d_logits = jnp.sum(d_chosen[:, :, None] * route_hot, axis=1).astype(jnp.bfloat16)
    router_grad = jnp.einsum(
        "td,te->de", second_input, d_logits, preferred_element_type=jnp.float32
    )
    from_experts = (
        jnp.take(d_returned.reshape(EXPERTS * CAP, model_width), target, axis=0)
        .reshape(-1, 2, model_width)
        .astype(jnp.float32)
    )
    d_second = (
        jnp.einsum("tf,df->td", d_shared_pre, shared_first, preferred_element_type=jnp.float32)
        + jnp.einsum("te,de->td", d_logits, router_full, preferred_element_type=jnp.float32)
        + jnp.sum(from_experts, axis=1)
    )
    mlp_sums = spread(shared_first_grad, shared_second_grad, router_grad)
    d_scale_two = d_second * normed_two
    d_residual = upstream + norm_back(d_second * (1.0 + scale_two), normed_two, inv_two)
    ada_full, qkv_full, out_full = collect(ada_weight, qkv_weight, out_weight)
    d_projected = (gate_one * d_residual).astype(jnp.bfloat16)
    d_gate_one = d_residual * projected
    out_grad = jnp.einsum("td,te->de", attended, d_projected, preferred_element_type=jnp.float32)
    d_attended = jnp.einsum(
        "te,de->td", d_projected, out_full, preferred_element_type=jnp.float32
    ).astype(jnp.bfloat16)
    d_queries, d_keys, d_values = attend_back(
        queries, keys_all, values_all, segment, log_totals, d_attended.reshape(-1, HEADS, head_size)
    )
    d_qkv = jnp.concatenate(
        [
            d_queries.reshape(-1, model_width),
            d_keys.reshape(-1, model_width),
            d_values.reshape(-1, model_width),
        ],
        axis=1,
    ).astype(jnp.bfloat16)
    qkv_grad = jnp.einsum("td,te->de", first_input, d_qkv, preferred_element_type=jnp.float32)
    d_first = jnp.einsum("te,de->td", d_qkv, qkv_full, preferred_element_type=jnp.float32)
    d_scale_one = d_first * normed_one
    tokens_grad = d_residual + norm_back(d_first * (1.0 + scale_one), normed_one, inv_one)
    d_per_row = jnp.concatenate(
        [d_first, d_scale_one, d_gate_one, d_second, d_scale_two, d_gate_two], axis=1
    )
    d_modulation = jnp.einsum(
        "tj,te->je", inside, d_per_row, precision=EXACT, preferred_element_type=jnp.float32
    ).astype(jnp.bfloat16)
    ada_grad = jnp.einsum("jd,je->de", activated, d_modulation, preferred_element_type=jnp.float32)
    d_activated = jnp.einsum(
        "je,de->jd", d_modulation, ada_full, preferred_element_type=jnp.float32
    )
    condition_grad = jax.vjp(jax.nn.silu, cond_float)[1](d_activated)[0]
    attn_sums = spread(ada_grad, qkv_grad, out_grad)
    return (
        output,
        tokens_grad,
        condition_grad,
        attn_sums[0],
        attn_sums[1],
        attn_sums[2],
        mlp_sums[0],
        mlp_sums[1],
        mlp_sums[2],
        expert_sums[0],
        expert_sums[1],
        expert_counts,
    )


def at(d, s, c):
    return (d, 2 * s + c)


def slot(kind, f, d):
    if kind == "cols":
        return (pl.ds(pl.multiple_of(96 * f, 96), 96), pl.ds(pl.multiple_of(768 * d, 768), 768))
    return (pl.ds(pl.multiple_of(192 * d, 192), 192), pl.ds(pl.multiple_of(384 * f, 384), 384))


def half_slot(kind, f, d, h):
    if kind == "cols":
        return (
            pl.ds(pl.multiple_of(96 * f, 96), 96),
            pl.ds(pl.multiple_of(768 * d + 384 * h, 384), 384),
        )
    return (
        pl.ds(pl.multiple_of(192 * d + 96 * h, 96), 96),
        pl.ds(pl.multiple_of(384 * f, 384), 384),
    )


def place():
    d = lax.axis_index("dp")
    f = lax.axis_index("fsdp")
    return d, f // 2, lax.rem(f, 2)


def flip(v, bit):
    return v + bit - 2 * bit * lax.rem(v // bit, 2)


def greet(devices):
    barrier = pltpu.get_barrier_semaphore()
    for device in devices:
        pl.semaphore_signal(barrier, inc=1, device_id=device, device_id_type=MESH)
    pl.semaphore_wait(barrier, len(devices))


def push(src, dst, send_sem, recv_sem, device):
    return pltpu.make_async_remote_copy(
        src_ref=src,
        dst_ref=dst,
        send_sem=send_sem,
        recv_sem=recv_sem,
        device_id=device,
        device_id_type=MESH,
    )


GATHER_SEMS = 3 + 8 + 8 + 20


class Gather:
    def __init__(self, kind, shard, full, ssem, rsem, lsem):
        self.kind, self.shard, self.full = kind, shard, full
        self.ssem, self.rsem, self.lsem = ssem, rsem, lsem
        self.d, self.s, self.c = place()
        self.sent = []

    def f(self, s):
        return 2 * s + self.c

    def go(self, index, where, device, src=None):
        ref = self.full.at[where]
        copy = push(
            ref if src is None else src, ref, self.ssem.at[index], self.rsem.at[index], device
        )
        copy.start()
        self.sent.append(copy)

    def arrived(self, index, where):
        ref = self.full.at[where]
        push(ref, ref, self.ssem.at[index], self.rsem.at[index], at(self.d, self.s, self.c)).wait_recv()

    def start(self):
        d, s, c = self.d, self.s, self.c
        mine = slot(self.kind, self.f(s), d)
        self.own = pltpu.make_async_copy(self.shard, self.full.at[mine], self.lsem)
        self.own.start()
        self.go(1, mine, at(flip(d, 2), s, c), self.shard)
        self.go(0, mine, at(flip(d, 1), s, c), self.shard)
        self.go(3, mine, at(d, flip(s, 1), c), self.shard)
        self.go(4, mine, at(d, flip(s, 2), c), self.shard)
        self.go(19, mine, at(d, s, 1 - c), self.shard)

    def source(self, k):
        return (self.d, flip(self.d, 1), flip(self.d, 2), flip(flip(self.d, 1), 2))[k]

    def spread_z(self, k):
        d, s, c = self.d, self.s, self.c
        block = slot(self.kind, self.f(s), self.source(k))
        self.arrived(k - 1, block)
        if k == 2:
            self.go(2, block, at(flip(d, 1), s, c))
        self.go(3 + 2 * k, block, at(d, flip(s, 1), c))
        self.go(4 + 2 * k, block, at(d, flip(s, 2), c))
        self.go(19 + 5 * k, block, at(d, s, 1 - c))

    def relay(self, k):
        d, s, c = self.d, self.s, self.c
        source = self.source(k)
        sx, sy = flip(s, 1), flip(s, 2)
        from_x = slot(self.kind, self.f(sx), source)
        from_y = slot(self.kind, self.f(sy), source)
        self.arrived(3 + 2 * k, from_x)
        self.go(11 + 2 * k, half_slot(self.kind, self.f(sx), source, 0), at(d, sy, c))
        self.go(20 + 5 * k, from_x, at(d, s, 1 - c))
        self.arrived(4 + 2 * k, from_y)
        self.go(12 + 2 * k, half_slot(self.kind, self.f(sy), source, 1), at(d, sx, c))
        self.go(21 + 5 * k, from_y, at(d, s, 1 - c))

    def corner(self, k):
        d, s, c = self.d, self.s, self.c
        source = self.source(k)
        sd = flip(flip(s, 1), 2)
        for h in range(2):
            where = half_slot(self.kind, self.f(sd), source, h)
            self.arrived(11 + 2 * k + h, where)
            self.go(22 + 5 * k + h, where, at(d, s, 1 - c))

    def finish(self):
        d, s, c = self.d, self.s, self.c
        sx, sy = flip(s, 1), flip(s, 2)
        sd = flip(sx, 2)
        self.own.wait()
        for k in range(4):
            source = self.source(k)
            for j, position in enumerate((s, sx, sy)):
                self.arrived(19 + 5 * k + j, slot(self.kind, 2 * position + 1 - c, source))
            for h in range(2):
                self.arrived(22 + 5 * k + h, half_slot(self.kind, 2 * sd + 1 - c, source, h))
        for copy in self.sent:
            copy.wait_send()


class Line:
    def __init__(self, kind, shard, line, ssem, rsem, lsem):
        self.kind, self.shard, self.line = kind, shard, line
        self.ssem, self.rsem, self.lsem = ssem, rsem, lsem
        self.d, self.s, self.c = place()

    def block(self, d):
        if self.kind == "cols":
            return self.line.at[:, pl.ds(pl.multiple_of(768 * d, 768), 768)]
        return self.line.at[pl.ds(pl.multiple_of(192 * d, 192), 192)]

    def copy(self, index, src, source, target):
        return push(
            src, self.block(source), self.ssem.at[index], self.rsem.at[index], at(target, self.s, self.c)
        )

    def start(self):
        d = self.d
        self.own = pltpu.make_async_copy(self.shard, self.block(d), self.lsem)
        self.own.start()
        self.sent = [
            self.copy(0, self.shard, d, flip(d, 2)),
            self.copy(1, self.shard, d, flip(d, 1)),
        ]
        for copy in self.sent:
            copy.start()

    def relay(self):
        d2 = flip(self.d, 2)
        self.copy(0, self.shard, d2, d2).wait_recv()
        copy = self.copy(2, self.block(d2), d2, flip(self.d, 1))
        copy.start()
        self.sent.append(copy)

    def finish(self):
        d1 = flip(self.d, 1)
        self.own.wait()
        self.copy(1, self.shard, d1, d1).wait_recv()
        self.copy(2, self.shard, flip(d1, 2), d1).wait_recv()
        for copy in self.sent:
            copy.wait_send()


class Spread:
    def __init__(self, kind, line, full, ssem, rsem, lsem):
        self.kind, self.line, self.full = kind, line, full
        self.ssem, self.rsem, self.lsem = ssem, rsem, lsem
        self.d, self.s, self.c = place()
        self.sx, self.sy = flip(self.s, 1), flip(self.s, 2)
        self.sd = flip(self.sx, 2)
        self.mate = at(self.d, self.s, 1 - self.c)
        self.to_x, self.to_y = at(self.d, self.sx, self.c), at(self.d, self.sy, self.c)
        self.sent = []

    def block(self, position, c, h=None):
        f = 2 * position + c
        if self.kind == "cols":
            rows = pl.ds(pl.multiple_of(96 * f, 96), 96)
            return self.full.at[rows] if h is None else self.full.at[rows, pl.ds(1536 * h, 1536)]
        columns = pl.ds(pl.multiple_of(384 * f, 384), 384)
        rows = pl.ds(0, 768) if h is None else pl.ds(384 * h, 384)
        return self.full.at[rows, columns]

    def go(self, index, ref, device, src=None):
        copy = push(
            ref if src is None else src, ref, self.ssem.at[index], self.rsem.at[index], device
        )
        copy.start()
        self.sent.append(copy)

    def arrived(self, index, ref):
        push(ref, ref, self.ssem.at[index], self.rsem.at[index], self.mate).wait_recv()

    def start(self):
        mine = self.block(self.s, self.c)
        self.own = pltpu.make_async_copy(self.line, mine, self.lsem)
        self.own.start()
        self.go(0, mine, self.to_x, self.line)
        self.go(1, mine, self.to_y, self.line)
        self.go(2, mine, self.mate, self.line)

    def relay(self):
        c = self.c
        from_x, from_y = self.block(self.sx, c), self.block(self.sy, c)
        self.arrived(0, from_x)
        self.go(3, self.block(self.sx, c, 0), self.to_y)
        self.go(5, from_x, self.mate)
        self.arrived(1, from_y)
        self.go(4, self.block(self.sy, c, 1), self.to_x)
        self.go(6, from_y, self.mate)

    def corner(self):
        for h in range(2):
            ref = self.block(self.sd, self.c, h)
            self.arrived(3 + h, ref)
            self.go(7 + h, ref, self.mate)

    def finish(self):
        c = 1 - self.c
        self.own.wait()
        self.arrived(2, self.block(self.s, c))
        self.arrived(5, self.block(self.sx, c))
        self.arrived(6, self.block(self.sy, c))
        for h in range(2):
            self.arrived(7 + h, self.block(self.sd, c, h))
        for copy in self.sent:
            copy.wait_send()


def everyone_else():
    me = lax.axis_index("dp") * 8 + lax.axis_index("fsdp")

    def other(k):
        device = lax.rem(me + k, 32)
        return (device // 8, lax.rem(device, 8))

    return me, other


def open_kernel(
    shard, router, act_ref, ada_ref, up_shard, down_shard,
    full, routers, seen, rows_out, up_line, down_line,
    heard, part, got, mixed, ssem, rsem, lsem, asem, brsem, rssem, rrsem, tssem, trsem, zssem, zrsem,
    us, ur, ds, dr,
):
    me, other = everyone_else()
    d, s, c = place()
    f = 2 * s + c
    barrier = pltpu.get_barrier_semaphore()

    def hello(k, carry):
        pl.semaphore_signal(barrier, inc=1, device_id=other(k), device_id_type=MESH)
        return carry

    lax.fori_loop(1, 32, hello, 0)
    pl.semaphore_wait(barrier, 31)

    def act_copy(k, source):
        device = other(k)
        return push(act_ref.at[device[1]], heard.at[source], asem.at[k], brsem.at[k], device)

    def router_copy(k, source):
        return push(router, routers.at[source], rssem.at[k], rrsem.at[k], other(k))

    def send(k, carry):
        act_copy(k, me).start()
        return carry

    lax.fori_loop(1, 32, send, 0)
    gather = Gather("cols", shard, full, ssem, rsem, lsem.at[0])
    gather.start()
    lines = (
        Line("cols", up_shard, up_line, us, ur, lsem.at[3]),
        Line("rows", down_shard, down_line, ds, dr, lsem.at[4]),
    )
    own_router = pltpu.make_async_copy(router, routers.at[me], lsem.at[1])
    own_router.start()

    def send_router(k, carry):
        router_copy(k, me).start()
        return carry

    lax.fori_loop(1, 32, send_router, 0)
    heard[me] = act_ref[f]

    def take(k, carry):
        copy = act_copy(k, lax.rem(me + 32 - k, 32))
        copy.wait_recv()
        return carry

    lax.fori_loop(1, 32, take, 0)
    everything = heard[...].reshape(256, 128)
    row = lax.broadcasted_iota(jnp.int32, (64, 256), 0)
    column = lax.broadcasted_iota(jnp.int32, (64, 256), 1)
    source = lax.rem(row // 2, 4) * 8 + row // 8
    pick = (column == source * 8 + lax.rem(row, 2)).astype(jnp.bfloat16)
    compact = jnp.dot(
        pick, everything.astype(jnp.bfloat16), preferred_element_type=jnp.float32
    ).astype(jnp.bfloat16)
    seen[...] = jnp.concatenate(
        [compact.astype(jnp.float32), jnp.sum(heard[...], axis=0)], axis=0
    )
    part[...] = jnp.dot(compact, ada_ref[...], preferred_element_type=jnp.float32).reshape(
        8, 8, 1152
    )

    def tile_copy(k):
        target = lax.rem(f + k, 8)
        return push(part.at[target], got.at[k], tssem.at[k], trsem.at[k], (d, target))

    for k in range(1, 8):
        tile_copy(k).start()
    gather.spread_z(1)
    gather.spread_z(2)
    gather.relay(0)
    for k in range(1, 8):
        tile_copy(k).wait_recv()
    total = part[f]
    for k in range(1, 8):
        total = total + got[k]
    mixed[...] = total
    zs = []
    for k in range(1, 4):
        copy = push(mixed, rows_out.at[d], zssem.at[k], zrsem.at[k], at(lax.rem(d + k, 4), s, c))
        copy.start()
        zs.append(copy)
    own_rows = pltpu.make_async_copy(mixed, rows_out.at[d], lsem.at[2])
    own_rows.start()
    gather.spread_z(3)
    for line in lines:
        line.start()
    gather.relay(1)
    gather.corner(0)
    gather.relay(2)
    gather.corner(1)
    gather.relay(3)
    gather.corner(2)
    for line in lines:
        line.relay()
    gather.corner(3)
    gather.finish()
    for line in lines:
        line.finish()
    own_router.wait()
    own_rows.wait()
    for k in range(1, 4):
        push(
            mixed, rows_out.at[lax.rem(d + 4 - k, 4)], zssem.at[k], zrsem.at[k],
            at(lax.rem(d + k, 4), s, c),
        ).wait_recv()
    for copy in zs:
        copy.wait_send()
    for k in range(1, 8):
        tile_copy(k).wait_send()

    def drain(k, carry):
        act_copy(k, me).wait_send()
        copy = router_copy(k, lax.rem(me + 32 - k, 32))
        copy.wait_recv()
        copy.wait_send()
        return carry

    lax.fori_loop(1, 32, drain, 0)


DMA = pltpu.SemaphoreType.DMA
ANYWHERE = pl.BlockSpec(memory_space=pl.ANY)
ONCHIP = pl.BlockSpec(memory_space=pltpu.VMEM)


def opening(shard, router, act, ada, up_shard, down_shard):
    return pl.pallas_call(
        open_kernel,
        out_shape=(
            jax.ShapeDtypeStruct((768, 3072), jnp.bfloat16),
            jax.ShapeDtypeStruct((32, 16, 128), jnp.bfloat16),
            jax.ShapeDtypeStruct((72, 128), jnp.float32),
            jax.ShapeDtypeStruct((4, 8, 1152), jnp.float32),
            jax.ShapeDtypeStruct((96, 3072), jnp.bfloat16),
            jax.ShapeDtypeStruct((768, 384), jnp.bfloat16),
        ),
        in_specs=[ONCHIP] * 6,
        out_specs=(ANYWHERE, ANYWHERE, ONCHIP, ANYWHERE, ANYWHERE, ANYWHERE),
        scratch_shapes=[
            pltpu.VMEM((32, 8, 128), jnp.float32),
            pltpu.VMEM((8, 8, 1152), jnp.float32),
            pltpu.VMEM((8, 8, 1152), jnp.float32),
            pltpu.VMEM((8, 1152), jnp.float32),
            DMA((GATHER_SEMS,)), DMA((GATHER_SEMS,)), DMA((5,)),
            DMA((32,)), DMA((32,)), DMA((32,)), DMA((32,)),
            DMA((8,)), DMA((8,)), DMA((4,)), DMA((4,)),
            DMA((3,)), DMA((3,)), DMA((3,)), DMA((3,)),
        ],
        compiler_params=pltpu.CompilerParams(collective_id=0, has_side_effects=True),
        name="opening",
    )(shard, router, act, ada, up_shard, down_shard)


def group_of(d, s, c):
    return [(j, at(lax.rem(d + j // 2, 4), s, lax.rem(c + j, 2))) for j in range(1, 8)]


class Swap:
    def __init__(self, blocks, out, ssem, rsem, lsem):
        self.blocks, self.out, self.ssem, self.rsem, self.lsem = blocks, out, ssem, rsem, lsem
        self.d, self.s, self.c = place()
        self.me = 2 * self.d + self.c

    def copy(self, j, landing):
        target_d = lax.rem(self.d + j // 2, 4)
        target_c = lax.rem(self.c + j, 2)
        return push(
            self.blocks.at[2 * target_d + target_c],
            self.out.at[landing],
            self.ssem.at[j],
            self.rsem.at[j],
            at(target_d, self.s, target_c),
        )

    def start(self):
        for j in (4, 5, 2, 3, 6, 7, 1):
            self.copy(j, self.me).start()
        self.own = pltpu.make_async_copy(
            self.blocks.at[self.me], self.out.at[self.me], self.lsem
        )
        self.own.start()

    def send(self, step):
        for j in (2 * step, 2 * step + 1):
            if j:
                self.copy(j, self.me).start()
            else:
                self.own = pltpu.make_async_copy(
                    self.blocks.at[self.me], self.out.at[self.me], self.lsem
                )
                self.own.start()

    def finish(self):
        self.own.wait()
        for j in range(1, 8):
            source_d = lax.rem(self.d + 4 - j // 2, 4)
            source_c = lax.rem(self.c + j, 2)
            copy = self.copy(j, 2 * source_d + source_c)
            copy.wait_recv()
            copy.wait_send()


def nt(left, right):
    return lax.dot_general(left, right, (((1,), (1,)), ((), ())), preferred_element_type=jnp.float32)


def tn(left, right):
    return lax.dot_general(left, right, (((0,), (0,)), ((), ())), preferred_element_type=jnp.float32)


def nn(left, right):
    return jnp.dot(left, right, preferred_element_type=jnp.float32)


GELU_SCALE = 0.7978845608028654


def gelu_pair(v):
    square = v * v
    bend = jnp.tanh(GELU_SCALE * (v + 0.044715 * (square * v)))
    half = 0.5 * (1.0 + bend)
    slope = half + 0.5 * v * (1.0 - bend * bend) * (
        GELU_SCALE * (1.0 + (3.0 * 0.044715) * square)
    )
    return v * half, slope


HIDDEN = 512


def out_kernel(
    rows, grads, up_line, down_line, tokens, d_tokens,
    rows_in, grads_in, mixed_out, d_tokens_out, up_grad, down_grad,
    up_full, down_full, tokens_t, d_tokens_t, s1, r1, s2, r2, ssem, rsem, ssem2, rsem2, lsem,
):
    d, s, c = place()
    greet([device for _, device in group_of(d, s, c)] + [at(d, flip(s, 1), c), at(d, flip(s, 2), c)])
    both = (
        Spread("cols", up_line, up_full, ssem, rsem, lsem.at[0]),
        Spread("rows", down_line, down_full, ssem2, rsem2, lsem.at[1]),
    )
    swap_a = Swap(rows, rows_in, s1, r1, lsem.at[2])
    swap_b = Swap(grads, grads_in, s2, r2, lsem.at[3])
    for g in both:
        g.start()
    swap_a.start()
    swap_b.start()
    tokens_t[...] = tokens[...].T
    d_tokens_t[...] = d_tokens[...].T
    mixed_out[...] = jnp.zeros_like(mixed_out)
    d_tokens_out[...] = jnp.zeros_like(d_tokens_out)
    for g in both:
        g.relay()
    for g in both:
        g.corner()
    for g in both:
        g.finish()

    def block(b, carry):
        where = pl.ds(pl.multiple_of(b * HIDDEN, HIDDEN), HIDDEN)
        up, down = up_full[:, where], down_full[:, where]
        act, slope = gelu_pair(nn(tokens[...], up))
        act = act.astype(jnp.bfloat16)
        mixed_out[...] += nt(act, down)
        down_grad[:, where] = nn(d_tokens_t[...], act).astype(jnp.bfloat16)
        d_pre = (slope * nn(d_tokens[...], down)).astype(jnp.bfloat16)
        d_tokens_out[...] += nt(d_pre, up)
        up_grad[:, where] = nn(tokens_t[...], d_pre).astype(jnp.bfloat16)
        return carry

    lax.fori_loop(0, 3072 // HIDDEN, block, 0)
    swap_a.finish()
    swap_b.finish()


def outbound(rows, grads, up_line, down_line, tokens, d_tokens):
    bf, f32 = jnp.bfloat16, jnp.float32
    return pl.pallas_call(
        out_kernel,
        out_shape=(
            jax.ShapeDtypeStruct((8, 144, 768), bf),
            jax.ShapeDtypeStruct((8, 144, 768), bf),
            jax.ShapeDtypeStruct((512, 768), f32),
            jax.ShapeDtypeStruct((512, 768), f32),
            jax.ShapeDtypeStruct((768, 3072), bf),
            jax.ShapeDtypeStruct((768, 3072), bf),
        ),
        in_specs=[ONCHIP] * 6,
        out_specs=(ANYWHERE,) * 2 + (ONCHIP,) * 4,
        scratch_shapes=[pltpu.VMEM((768, 3072), bf)] * 2
        + [pltpu.VMEM((768, 512), bf)] * 2
        + [DMA((8,))] * 4
        + [DMA((9,))] * 4
        + [DMA((4,))],
        compiler_params=pltpu.CompilerParams(
            collective_id=1, has_side_effects=True, vmem_limit_bytes=60 << 20
        ),
        name="outbound",
    )(rows, grads, up_line, down_line, tokens, d_tokens)


def widened(ref):
    return ref[...].astype(jnp.float32)


class Parts:
    def __init__(self, grad, keep, send_x, send_y, sem):
        s = lax.axis_index("fsdp") // 2
        sx, sy = flip(s, 1), flip(s, 2)
        sd = flip(sx, 2)
        rows = grad.shape[0] // 8
        slots = (
            (s, 0, keep.at[0, 0]), (sy, 0, keep.at[0, 1]), (s, 1, keep.at[1, 0]), (sx, 1, keep.at[1, 1]),
            (sx, 0, send_x.at[0]), (sd, 0, send_x.at[1]), (sy, 1, send_y.at[0]), (sd, 1, send_y.at[1]),
        )
        self.copies = [
            pltpu.make_async_copy(
                grad.at[pl.ds(pl.multiple_of((2 * position + h) * rows, 32), rows)], out, sem.at[i]
            )
            for i, (position, h, out) in enumerate(slots)
        ]

    def start(self):
        for copy in self.copies:
            copy.start()

    def finish(self):
        for copy in self.copies:
            copy.wait()


def expert_kernel(
    rows, grads, up_all, down_all, first_grad, second_grad,
    rows_back, grads_back, up_keep, up_x, up_y, down_keep, down_x, down_y, first_part, second_part,
    up, down, act, d_pre, made, d_made, total, d_total, up_grad, down_grad, rows_t,
    fo, fm, fn, ff, fs, fr, fl, so, sm, sn, sf, ss, sr, sl,
    s1, r1, s2, r2, lsem, wsem, psem, qsem,
):
    bf = jnp.bfloat16
    d, s, c = place()
    weights = [
        pltpu.make_async_copy(up_all.at[c], up, wsem.at[0]),
        pltpu.make_async_copy(down_all.at[c], down, wsem.at[1]),
    ]
    for copy in weights:
        copy.start()
    greet([device for _, device in group_of(d, s, c)] + [at(d, flip(s, 1), c), at(d, flip(s, 2), c)])
    sums = (
        DenseSum("cols", first_grad, first_part, fo, fm, fn, ff, None, fs, fr, fl),
        DenseSum("rows", second_grad, second_part, so, sm, sn, sf, None, ss, sr, sl),
    )
    for each in sums:
        each.start()
    swap_a = Swap(made, rows_back, s1, r1, lsem.at[0])
    swap_b = Swap(d_made, grads_back, s2, r2, lsem.at[1])
    for copy in weights:
        copy.wait()
    for step in (2, 1, 3, 0):
        there = lax.rem(d + step, 4)
        chunk = pl.ds(2 * there, 2)
        lines = pl.ds(pl.multiple_of(288 * there, 288), 288)
        x = rows[chunk].reshape(288, 768)
        g = grads[chunk].reshape(288, 768)
        total[...] = jnp.zeros_like(total)
        d_total[...] = jnp.zeros_like(d_total)

        def block(b, carry):
            where = pl.ds(pl.multiple_of(b * HIDDEN, HIDDEN), HIDDEN)
            up_part, down_part = up[:, where], down[where]
            made_act, slope = gelu_pair(nn(x, up_part))
            made_act = made_act.astype(bf)
            act[lines, where] = made_act
            total[...] += nn(made_act, down_part)
            d_part = (slope * nt(g, down_part)).astype(bf)
            d_pre[lines, where] = d_part
            d_total[...] += nt(d_part, up_part)
            return carry

        lax.fori_loop(0, 3072 // HIDDEN, block, 0)
        made[chunk] = total[...].astype(bf).reshape(2, 144, 768)
        d_made[chunk] = d_total[...].astype(bf).reshape(2, 144, 768)
        swap_a.send(step)
        swap_b.send(step)
        if step == 2:
            for each in sums:
                each.merge()
        if step == 3:
            for each in sums:
                each.join()
    rows_t[...] = rows.reshape(1152, 768)[...].T
    g_all = grads.reshape(1152, 768)

    def up_block(b, carry):
        where = pl.ds(pl.multiple_of(b * HIDDEN, HIDDEN), HIDDEN)
        up_grad[:, where] = nn(rows_t[...], d_pre[:, where]).astype(bf)
        return carry

    def down_block(b, carry):
        where = pl.ds(pl.multiple_of(384 * b, 384), 384)
        down_grad[where] = tn(act[:, where], g_all[...]).astype(bf)
        return carry

    up_parts = Parts(up_grad, up_keep, up_x, up_y, psem)
    down_parts = Parts(down_grad, down_keep, down_x, down_y, qsem)
    lax.fori_loop(0, 3072 // HIDDEN, up_block, 0)
    up_parts.start()
    lax.fori_loop(0, 8, down_block, 0)
    down_parts.start()
    for each in sums:
        each.close()
    swap_a.finish()
    swap_b.finish()
    up_parts.finish()
    down_parts.finish()


def experts(rows, grads, up_all, down_all, first_grad, second_grad):
    bf, f32 = jnp.bfloat16, jnp.float32

    def rooms(piece, half):
        return [
            pltpu.VMEM((4,) + piece, bf),
            pltpu.VMEM((4,) + piece, bf),
            pltpu.VMEM((2,) + half, bf),
            pltpu.VMEM((2,) + piece, bf),
            DMA((8,)),
            DMA((8,)),
            DMA((4,)),
        ]

    def parts(r, n):
        return (
            jax.ShapeDtypeStruct((2, 2, r, n), bf),
            jax.ShapeDtypeStruct((2, r, n), bf),
            jax.ShapeDtypeStruct((2, r, n), bf),
        )

    return pl.pallas_call(
        expert_kernel,
        out_shape=(
            jax.ShapeDtypeStruct((8, 144, 768), bf),
            jax.ShapeDtypeStruct((8, 144, 768), bf),
        )
        + parts(96, 3072)
        + parts(384, 768)
        + (
            jax.ShapeDtypeStruct((96, 3072), bf),
            jax.ShapeDtypeStruct((768, 384), bf),
        ),
        in_specs=[ONCHIP, ONCHIP, ANYWHERE, ANYWHERE, ANYWHERE, ANYWHERE],
        out_specs=(ANYWHERE,) * 8 + (ONCHIP, ONCHIP),
        scratch_shapes=[
            pltpu.VMEM((768, 3072), bf),
            pltpu.VMEM((3072, 768), bf),
            pltpu.VMEM((1152, 3072), bf),
            pltpu.VMEM((1152, 3072), bf),
            pltpu.VMEM((8, 144, 768), bf),
            pltpu.VMEM((8, 144, 768), bf),
            pltpu.VMEM((288, 768), f32),
            pltpu.VMEM((288, 768), f32),
            pltpu.VMEM((768, 3072), bf),
            pltpu.VMEM((3072, 768), bf),
            pltpu.VMEM((768, 1152), bf),
        ]
        + rooms((96, 3072), (96, 1536))
        + rooms((768, 384), (384, 384))
        + [DMA((8,))] * 4
        + [DMA((2,)), DMA((2,)), DMA((8,)), DMA((8,))],
        compiler_params=pltpu.CompilerParams(
            collective_id=2, has_side_effects=True, vmem_limit_bytes=67043328
        ),
        name="experts",
    )(rows, grads, up_all, down_all, first_grad, second_grad)


def hop(values, bit):
    return lax.ppermute(values, "fsdp", [(f, f ^ bit) for f in range(8)])


def square_next(keep, from_x, from_y):
    f32, bf = jnp.float32, jnp.bfloat16
    return (
        hop((keep[0, 1].astype(f32) + from_x[1].astype(f32)).astype(bf), 4),
        hop((keep[1, 1].astype(f32) + from_y[1].astype(f32)).astype(bf), 2),
    )


def square_last(keep, from_x, from_y, low_next, high_next):
    f32, bf = jnp.float32, jnp.bfloat16
    low = keep[0, 0].astype(f32) + from_x[0].astype(f32) + low_next.astype(f32)
    high = keep[1, 0].astype(f32) + from_y[0].astype(f32) + high_next.astype(f32)
    first = lax.rem(lax.axis_index("fsdp"), 2) == 0
    other = hop(jnp.where(first, high, low).astype(bf), 1).astype(f32)
    return jnp.where(first, jnp.stack([low, other]), jnp.stack([other, high]))


def line_sum(part, axis):
    d, size = lax.axis_index("dp"), part.shape[axis] // 4
    total = lax.dynamic_slice_in_dim(part, size * d, size, axis).astype(jnp.float32)
    for k in range(1, 4):
        block = lax.dynamic_slice_in_dim(part, size * lax.rem(d + k, 4), size, axis)
        got = lax.ppermute(block, "dp", [(i, (i + k) % 4) for i in range(4)])
        total = total + got.astype(jnp.float32)
    return total


class DenseSum:
    def __init__(self, kind, grad, out, own, mate, near, far, line, ssem, rsem, lsem):
        self.kind, self.grad, self.out = kind, grad, out
        self.own, self.mate, self.near, self.far, self.line = own, mate, near, far, line
        self.ssem, self.rsem, self.lsem = ssem, rsem, lsem
        self.d, self.s, self.c = place()
        self.order = (
            flip(flip(self.s, 1), 2),
            flip(self.s, 1),
            flip(self.s, 2),
            self.s,
        )

    def piece(self, f):
        if self.kind == "cols":
            return self.grad.at[pl.ds(pl.multiple_of(96 * f, 96), 96)]
        return self.grad.at[:, pl.ds(pl.multiple_of(384 * f, 384), 384)]

    def half(self, ref, h):
        if self.kind == "cols":
            return ref.at[:, pl.ds(1536 * h, 1536)]
        return ref.at[pl.ds(384 * h, 384)]

    def quarter(self, ref, q):
        if self.kind == "cols":
            return ref.at[:, pl.ds(pl.multiple_of(768 * q, 768), 768)]
        return ref.at[pl.ds(pl.multiple_of(192 * q, 192), 192)]

    def start(self):
        d, s, c = self.d, self.s, self.c
        self.zero, self.local = [], []
        for j, position in enumerate(self.order):
            copy = push(
                self.piece(2 * position + 1 - c), self.mate.at[j], self.ssem.at[j], self.rsem.at[j], at(d, s, 1 - c)
            )
            copy.start()
            self.zero.append(copy)
            copy = pltpu.make_async_copy(self.piece(2 * position + c), self.own.at[j], self.lsem.at[j])
            copy.start()
            self.local.append(copy)

    def merge(self):
        d, s, c = self.d, self.s, self.c
        sx, sy = flip(s, 1), flip(s, 2)
        self.one = []
        for j in range(4):
            self.zero[j].wait_recv()
            self.local[j].wait()
            self.own[j] = (widened(self.own.at[j]) + widened(self.mate.at[j])).astype(jnp.bfloat16)
            if j == 0:
                for h, target in enumerate((sx, sy)):
                    copy = push(
                        self.half(self.own.at[0], h), self.near.at[h], self.ssem.at[4 + h], self.rsem.at[4 + h],
                        at(d, target, c),
                    )
                    copy.start()
                    self.one.append(copy)

    def join(self):
        d, s, c = self.d, self.s, self.c
        sx, sy = flip(s, 1), flip(s, 2)
        for h, j in ((0, 2), (1, 1)):
            self.one[h].wait_recv()
            where = self.half(self.own.at[j], h)
            where[...] = (widened(where) + widened(self.near.at[h])).astype(jnp.bfloat16)
        self.two = []
        for h, target in enumerate((sx, sy)):
            copy = push(
                self.own.at[1 + h], self.far.at[h], self.ssem.at[6 + h], self.rsem.at[6 + h], at(d, target, c)
            )
            copy.start()
            self.two.append(copy)

    def square(self):
        for copy in self.two:
            copy.wait_recv()
        return (
            widened(self.own.at[3]) + widened(self.far.at[0]) + widened(self.far.at[1])
        ).astype(jnp.bfloat16)

    def along(self):
        d, s, c = self.d, self.s, self.c
        self.own[3] = self.square()
        self.three = []
        for k in range(1, 4):
            target = lax.rem(d + k, 4)
            copy = push(
                self.quarter(self.own.at[3], target), self.line.at[k - 1], self.ssem.at[7 + k], self.rsem.at[7 + k],
                at(target, s, c),
            )
            copy.start()
            self.three.append(copy)

    def finish(self):
        total = widened(self.quarter(self.own.at[3], self.d))
        for k in range(1, 4):
            self.three[k - 1].wait_recv()
            total = total + widened(self.line.at[k - 1])
        self.out[...] = total
        self.sent(self.three)

    def close(self):
        self.out[...] = self.square()
        self.sent([])

    def sent(self, more):
        for copy in self.zero + self.one + self.two + more:
            copy.wait_send()


class Tail:
    def __init__(self, d_rows, router, act, ada, ada_out, d_act_out, router_out, z1, plane, plane_in, z2, z2_in, sems):
        self.d_rows, self.router, self.act, self.ada = d_rows, router, act, ada
        self.ada_out, self.d_act_out, self.router_out = ada_out, d_act_out, router_out
        self.z1, self.plane, self.plane_in, self.z2, self.z2_in = z1, plane, plane_in, z2, z2_in
        self.sems = sems
        self.d, self.s, self.c = place()
        self.f = 2 * self.s + self.c

    def z_copy(self, k, src, dst, base):
        send, recv = self.sems[base], self.sems[base + 1]
        return push(src, dst, send.at[k], recv.at[k], at(lax.rem(self.d + k, 4), self.s, self.c))

    def f_copy(self, k, src, dst, base):
        send, recv = self.sems[base], self.sems[base + 1]
        return push(src, dst, send.at[k], recv.at[k], (self.d, lax.rem(self.f + k, 8)))

    def start(self):
        self.all = [
            self.z_copy(k, self.d_rows.at[lax.rem(self.d + k, 4)], self.z1.at[k], 0) for k in range(1, 4)
        ]
        for copy in self.all:
            copy.start()

    def second(self):
        total = self.d_rows[self.d]
        for k in range(1, 4):
            self.all[k - 1].wait_recv()
            total = total + self.z1[k]
        for target in range(8):
            self.plane[target, :, 0:1152] = total
            self.plane[target, :, 1152:1280] = self.router[target]
        copies = [
            self.f_copy(k, self.plane.at[lax.rem(self.f + k, 8)], self.plane_in.at[lax.rem(8 - k, 8)], 2)
            for k in range(1, 8)
        ]
        for copy in copies:
            copy.start()
        self.in_plane = copies
        self.all = self.all + copies

    def third(self):
        f = self.f
        self.plane_in[0] = self.plane[f]
        for copy in self.in_plane:
            copy.wait_recv()
        everything = self.plane_in[...]
        router = jnp.sum(everything[:, :, 1152:1280], axis=0)
        rows = everything[:, :, 0:1152].reshape(64, 1152)
        line = lax.broadcasted_iota(jnp.int32, (64, 64), 0)
        column = lax.broadcasted_iota(jnp.int32, (64, 64), 1)
        turn = (lax.rem(line // 8 + 8 - f, 8) * 8 + lax.rem(line, 8) == column).astype(jnp.bfloat16)
        d_mod = nn(turn, rows.astype(jnp.bfloat16)).astype(jnp.bfloat16)
        self.ada_out[...] = tn(self.act[...], d_mod)[0:96]
        part = nt(d_mod, self.ada[...])
        self.z2[0:64, 0:96] = part
        self.z2[0:64, 96:128] = jnp.zeros((64, 32), jnp.float32)
        self.z2[64:72, :] = router
        copies = [self.z_copy(k, self.z2, self.z2_in.at[k], 4) for k in range(1, 4)]
        for copy in copies:
            copy.start()
        self.along = copies
        self.all = self.all + copies

    def fourth(self):
        total = self.z2[...]
        for k in range(1, 4):
            self.along[k - 1].wait_recv()
            total = total + self.z2_in[k]
        self.router_out[...] = total[64:72]
        self.z2_in[0] = total
        copies = [
            self.f_copy(
                k,
                self.z2_in.at[0, pl.ds(pl.multiple_of(8 * lax.rem(self.f + k, 8), 8), 8)],
                self.d_act_out.at[self.f],
                6,
            )
            for k in range(1, 8)
        ]
        for copy in copies:
            copy.start()
        self.d_act_out[self.f] = self.z2_in[0, pl.ds(pl.multiple_of(8 * self.f, 8), 8)]
        self.last = copies
        self.all = self.all + copies

    def finish(self):
        for k in range(1, 8):
            self.f_copy(
                k, self.z2_in.at[0, pl.ds(0, 8)], self.d_act_out.at[lax.rem(self.f + 8 - k, 8)], 6
            ).wait_recv()
        for copy in self.all:
            copy.wait_send()


def dense_kernel(kinds, *refs):
    n = len(kinds)
    grads, small, outs = refs[:n], refs[n : n + 4], refs[n + 4 : 2 * n + 4]
    small_outs, rest = refs[2 * n + 4 : 2 * n + 7], refs[2 * n + 7 :]
    d, s, c = place()
    f = 2 * s + c
    greet(
        [at(lax.rem(d + k, 4), s, c) for k in range(1, 4)]
        + [(d, lax.rem(f + k, 8)) for k in range(1, 8)]
    )
    sums = [
        DenseSum(kinds[i], grads[i], outs[i], *rest[8 * i : 8 * i + 8]) for i in range(n)
    ]
    rest = rest[8 * n :]
    tail = Tail(*small, *small_outs, *rest[:5], rest[5:])
    tail.start()
    for each in sums:
        each.start()
    tail.second()
    for each in sums:
        each.merge()
    tail.third()
    for each in sums:
        each.join()
    tail.fourth()
    for each in sums:
        each.along()
    for each in sums:
        each.finish()
    tail.finish()


def dense_sums(kinds, grads, small, collective_id):
    bf, f32 = jnp.bfloat16, jnp.float32
    outs, scratch = [], []
    for kind in kinds:
        if kind == "cols":
            piece, half, quarter = (96, 3072), (96, 1536), (96, 768)
        else:
            piece, half, quarter = (768, 384), (384, 384), (192, 384)
        outs.append(jax.ShapeDtypeStruct(quarter, f32))
        scratch += [
            pltpu.VMEM((4,) + piece, bf),
            pltpu.VMEM((4,) + piece, bf),
            pltpu.VMEM((2,) + half, bf),
            pltpu.VMEM((2,) + piece, bf),
            pltpu.VMEM((3,) + quarter, bf),
            DMA((11,)),
            DMA((11,)),
            DMA((4,)),
        ]
    outs += [
        jax.ShapeDtypeStruct((96, 1152), f32),
        jax.ShapeDtypeStruct((8, 8, 128), f32),
        jax.ShapeDtypeStruct((8, 128), f32),
    ]
    scratch += [
        pltpu.VMEM((4, 8, 1152), f32),
        pltpu.VMEM((8, 8, 1280), f32),
        pltpu.VMEM((8, 8, 1280), f32),
        pltpu.VMEM((72, 128), f32),
        pltpu.VMEM((4, 72, 128), f32),
        DMA((4,)), DMA((4,)), DMA((8,)), DMA((8,)), DMA((4,)), DMA((4,)), DMA((8,)), DMA((8,)),
    ]
    return pl.pallas_call(
        functools.partial(dense_kernel, kinds),
        out_shape=tuple(outs),
        in_specs=[ANYWHERE] * len(kinds) + [ONCHIP] * 4,
        out_specs=(ONCHIP,) * len(outs),
        scratch_shapes=scratch,
        compiler_params=pltpu.CompilerParams(collective_id=collective_id, has_side_effects=True),
        name="dense_sums",
    )(*grads, *small)


def layer_stats(values_in):
    centred = values_in - jnp.mean(values_in, axis=-1, keepdims=True)
    inv_std = lax.rsqrt(jnp.mean(centred * centred, axis=-1, keepdims=True) + 1e-06)
    return centred * inv_std, inv_std


def modulated(inside, mod, part):
    columns = slice(768 * part, 768 * part + 768)
    return inside[:, 0:1] * mod[0:1, columns] + inside[:, 1:2] * mod[1:2, columns]


def head_column(g):
    return 768 * (g // 9) + 64 * (g % 9)


QUERY_ROWS = 256


def front_kernel(
    tokens, mod, inside, seg_col, seg_row, qkvo, router, cotangent, routes, target,
    heads, totals, attended, projected, residual, second, d_mixed, gates, rows, grads,
    bias, made, weighted,
):
    bf, f32 = jnp.bfloat16, jnp.float32
    token_float = tokens[...].astype(f32)
    normed, _ = layer_stats(token_float)
    first = (normed * (1.0 + modulated(inside, mod, 1)) + modulated(inside, mod, 0)).astype(bf)
    for j in range(4):
        piece = nn(first, qkvo[:, 768 * j : 768 * j + 640]).astype(bf)
        for i in range(9):
            heads[9 * j + i] = piece[:, 64 * i : 64 * i + 64]
    bias[...] = jnp.where(seg_col[...] == seg_row[...], 0.0, -1e30)

    def block(n, carry):
        h, part = n // (512 // QUERY_ROWS), lax.rem(n, 512 // QUERY_ROWS)
        lines = pl.ds(pl.multiple_of(part * QUERY_ROWS, QUERY_ROWS), QUERY_ROWS)
        scores = nt(heads[h, lines], heads[12 + h]) * 0.125 + bias[lines]
        row_max = jnp.max(scores, axis=-1, keepdims=True)
        weight = jnp.exp(scores - row_max)
        running = jnp.sum(weight, axis=-1, keepdims=True)
        probability = (weight * (1.0 / running)).astype(bf)
        made[h, lines] = nn(probability, heads[24 + h]).astype(bf)
        totals[h, lines] = row_max + jnp.log(running)
        return carry

    lax.fori_loop(0, 12 * (512 // QUERY_ROWS), block, 0)
    for h in range(12):
        attended[:, 64 * h : 64 * h + 64] = made[h]
    for j in range(4):
        piece = nn(attended[...], qkvo[:, 768 * j + 512 : 768 * j + 768])
        projected[:, 192 * j : 192 * j + 192] = piece[:, 64:256]
    residual[...] = token_float + modulated(inside, mod, 2) * projected[...]
    normed, _ = layer_stats(residual[...])
    second[...] = (normed * (1.0 + modulated(inside, mod, 4)) + modulated(inside, mod, 3)).astype(bf)
    logits = nn(second[...], router[...])
    ids = lax.broadcasted_iota(jnp.int32, (512, 8), 1)
    chosen = [
        jnp.sum(jnp.where(ids == routes[:, k : k + 1], logits, 0.0), axis=-1, keepdims=True)
        for k in range(2)
    ]
    top = jnp.maximum(chosen[0], chosen[1])
    raised = [jnp.exp(each - top) for each in chosen]
    share = [each / (raised[0] + raised[1]) for each in raised]
    pair = lax.broadcasted_iota(jnp.int32, (512, 2), 1)
    gates[...] = jnp.where(pair == 0, share[0], share[1])
    mixed_grad = modulated(inside, mod, 5) * cotangent[...].astype(f32)
    d_mixed[...] = mixed_grad.astype(bf)
    for k in range(2):
        weighted[k] = (share[k] * mixed_grad).astype(bf)

    def send(b, carry):
        lines = pl.ds(pl.multiple_of(288 * b, 288), 288)
        places = lax.broadcasted_iota(jnp.int32, (288, 512), 0) + 288 * b
        first_hot = (places == target[0:1]).astype(f32)
        second_hot = (places == target[1:2]).astype(f32)
        rows[lines] = nn((first_hot + second_hot).astype(bf), second[...]).astype(bf)
        grads[lines] = (
            nn(first_hot.astype(bf), weighted[0]) + nn(second_hot.astype(bf), weighted[1])
        ).astype(bf)
        return carry

    lax.fori_loop(0, 4, send, 0)


def front(tokens, mod, inside, seg_col, seg_row, qkvo, router, cotangent, routes, target):
    bf, f32 = jnp.bfloat16, jnp.float32
    return pl.pallas_call(
        front_kernel,
        out_shape=(
            jax.ShapeDtypeStruct((36, 512, 64), bf),
            jax.ShapeDtypeStruct((12, 512, 1), f32),
            jax.ShapeDtypeStruct((512, 768), bf),
            jax.ShapeDtypeStruct((512, 768), f32),
            jax.ShapeDtypeStruct((512, 768), f32),
            jax.ShapeDtypeStruct((512, 768), bf),
            jax.ShapeDtypeStruct((512, 768), bf),
            jax.ShapeDtypeStruct((512, 2), f32),
            jax.ShapeDtypeStruct((1152, 768), bf),
            jax.ShapeDtypeStruct((1152, 768), bf),
        ),
        in_specs=[ONCHIP] * 10,
        out_specs=(ONCHIP,) * 10,
        scratch_shapes=[
            pltpu.VMEM((512, 512), f32),
            pltpu.VMEM((12, 512, 64), bf),
            pltpu.VMEM((2, 512, 768), bf),
        ],
        compiler_params=pltpu.CompilerParams(vmem_limit_bytes=60 << 20),
        name="front",
    )(tokens, mod, inside, seg_col, seg_row, qkvo, router, cotangent, routes, target)


def norm_grad(upstream, normed, inv_std):
    return (
        upstream
        - jnp.mean(upstream, axis=-1, keepdims=True)
        - normed * jnp.mean(upstream * normed, axis=-1, keepdims=True)
    ) * inv_std


def rear_kernel(
    tokens, mod, inside, seg_col, seg_row, qkvo, router, cotangent, routes, target,
    heads, totals, attended, projected, residual, second, gates,
    returned, d_returned, shared_out, d_shared,
    output, tokens_grad, qkvo_grad, d_mod, router_grad,
    bias, rows_t, d_heads, d_att, d_att_t, d_rows_t, d_rows, d_residual, d_proj,
):
    bf, f32 = jnp.bfloat16, jnp.float32
    upstream = cotangent[...].astype(f32)

    def image_sums(part, values):
        for j in range(2):
            d_mod[j : j + 1, 768 * part : 768 * part + 768] = jnp.sum(
                inside[:, j : j + 1] * values, axis=0, keepdims=True
            )

    share = [gates[:, k : k + 1] for k in range(2)]
    places = lax.broadcasted_iota(jnp.int32, (512, 1152), 1)
    hot = [(places == target[:, k : k + 1]).astype(f32).astype(bf) for k in range(2)]
    picked = [nn(each, returned[...]) for each in hot]
    mixed = shared_out[...] + (share[0] * picked[0] + share[1] * picked[1])
    gate_two = modulated(inside, mod, 5)
    output[...] = (residual[...] + gate_two * mixed).astype(bf)
    image_sums(5, upstream * mixed)
    mixed_grad = gate_two * upstream
    d_share = [jnp.sum(mixed_grad * each, axis=-1, keepdims=True) for each in picked]
    inner = share[0] * d_share[0] + share[1] * d_share[1]
    ids = lax.broadcasted_iota(jnp.int32, (512, 8), 1)
    d_logits = sum(
        jnp.where(ids == routes[:, k : k + 1], share[k] * (d_share[k] - inner), 0.0) for k in range(2)
    ).astype(bf)
    router_grad[...] = tn(d_logits, second[...])
    d_second = (
        d_shared[...] + nt(d_logits, router[...]) + (nn(hot[0], d_returned[...]) + nn(hot[1], d_returned[...]))
    )
    normed, inv_std = layer_stats(residual[...])
    image_sums(3, d_second)
    image_sums(4, d_second * normed)
    d_residual[...] = upstream + norm_grad(d_second * (1.0 + modulated(inside, mod, 4)), normed, inv_std)
    gate_one = modulated(inside, mod, 2)
    image_sums(2, d_residual[...] * projected[...])
    d_proj[...] = (gate_one * d_residual[...]).astype(bf)
    d_attended = jnp.zeros((512, 768), f32)
    for j in range(4):
        piece = jnp.concatenate(
            [jnp.zeros((512, 64), bf), d_proj[:, 192 * j : 192 * j + 192]], axis=1
        )
        d_attended += nt(piece, qkvo[:, 768 * j + 512 : 768 * j + 768])
    d_attended = d_attended.astype(bf)
    d_att_t[...] = d_attended.T
    for h in range(12):
        d_att[h] = d_attended[:, 64 * h : 64 * h + 64]
    for j in range(18):
        pair = jnp.concatenate([heads[2 * j], heads[2 * j + 1]], axis=1)
        rows_t[128 * j : 128 * j + 128] = pair.T
    bias[...] = jnp.where(seg_col[...] == seg_row[...], 0.0, -1e30)

    def head(h, carry):
        def at_head(g):
            return pl.ds(pl.multiple_of(64 * g, 64), 64)

        d_key, d_value = jnp.zeros((64, 512), f32), jnp.zeros((64, 512), f32)
        for part in range(512 // QUERY_ROWS):
            lines = slice(part * QUERY_ROWS, (part + 1) * QUERY_ROWS)
            scores = nn(heads[h, lines], rows_t[at_head(12 + h)]) * 0.125 + bias[lines]
            probability = jnp.exp(scores - totals[h, lines])
            d_prob = nn(d_att[h, lines], rows_t[at_head(24 + h)])
            inner = jnp.sum(probability * d_prob, axis=-1, keepdims=True)
            d_scores = (probability * (d_prob - inner)).astype(bf)
            d_heads[h, lines] = (nn(d_scores, heads[12 + h]) * 0.125).astype(bf)
            d_key += nn(rows_t[at_head(h), lines], d_scores)
            d_value += nn(d_att_t[at_head(h), lines], probability.astype(bf))
        d_rows_t[at_head(h)] = (d_key * 0.125).astype(bf)
        d_rows_t[at_head(12 + h)] = d_value.astype(bf)
        return carry

    lax.fori_loop(0, 12, head, 0)
    for g in range(12):
        column = head_column(g)
        d_rows[:, column : column + 64] = d_heads[g]
    for j in range(12):
        pair = d_rows_t[128 * j : 128 * j + 128].T
        for i in range(2):
            column = head_column(12 + 2 * j + i)
            d_rows[:, column : column + 64] = pair[:, 64 * i : 64 * i + 64]
    for j in range(4):
        d_rows[:, 768 * j + 576 : 768 * j + 768] = jnp.zeros((512, 192), bf)
    token_float = tokens[...].astype(f32)
    normed, inv_std = layer_stats(token_float)
    scale_one = 1.0 + modulated(inside, mod, 1)
    first_t = (normed * scale_one + modulated(inside, mod, 0)).astype(bf).T
    attended_t = attended[...].T
    for j in range(4):
        qkvo_grad[:, 768 * j : 768 * j + 640] = nn(first_t, d_rows[:, 768 * j : 768 * j + 640]).astype(bf)
        qkvo_grad[:, 768 * j + 576 : 768 * j + 768] = nn(
            attended_t, d_proj[:, 192 * j : 192 * j + 192]
        ).astype(bf)
    d_first = nt(d_rows[...], qkvo[...])
    image_sums(0, d_first)
    image_sums(1, d_first * normed)
    tokens_grad[...] = d_residual[...] + norm_grad(d_first * scale_one, normed, inv_std)


def rear(*operands):
    bf, f32 = jnp.bfloat16, jnp.float32
    return pl.pallas_call(
        rear_kernel,
        out_shape=(
            jax.ShapeDtypeStruct((512, 768), bf),
            jax.ShapeDtypeStruct((512, 768), f32),
            jax.ShapeDtypeStruct((768, 3072), bf),
            jax.ShapeDtypeStruct((2, 4608), f32),
            jax.ShapeDtypeStruct((8, 768), f32),
        ),
        in_specs=[ONCHIP] * len(operands),
        out_specs=(ONCHIP,) * 5,
        scratch_shapes=[
            pltpu.VMEM((512, 512), f32),
            pltpu.VMEM((2304, 512), bf),
            pltpu.VMEM((12, 512, 64), bf),
            pltpu.VMEM((12, 512, 64), bf),
            pltpu.VMEM((768, 512), bf),
            pltpu.VMEM((1536, 512), bf),
            pltpu.VMEM((512, 3072), bf),
            pltpu.VMEM((512, 768), f32),
            pltpu.VMEM((512, 768), bf),
        ],
        compiler_params=pltpu.CompilerParams(vmem_limit_bytes=67043328),
        cost_estimate=pl.CostEstimate(flops=60_000_000_000, bytes_accessed=30_000_000, transcendentals=0),
        name="rear",
    )(*operands)


def fitted_shards(
    tokens,
    condition,
    ada_weight,
    qkv_weight,
    out_weight,
    shared_up,
    shared_down,
    router_weight,
    expert_up,
    expert_down,
    routes,
    image_sizes,
    cotangent,
):
    bf = jnp.bfloat16
    d_index, f_index = lax.axis_index("dp"), lax.axis_index("fsdp")
    model_width = tokens.shape[1]
    head_size = model_width // HEADS
    inside, segment = owners(image_sizes)
    up_all, down_all = gather_experts(expert_up, expert_down)
    ids = jnp.arange(EXPERTS, dtype=jnp.int32)
    hot = routes[:, :, None] == ids[None, None, :]
    hot_any = jnp.any(hot, axis=1).astype(bf)
    order = jnp.arange(LONG, dtype=jnp.int32)
    earlier = (order[:, None] > order[None, :]).astype(bf)
    before = nn(earlier, hot_any)
    position = jnp.sum(jnp.where(hot, before[:, None, :], 0.0), axis=-1).astype(jnp.int32)
    target = routes * CAP + position
    live = (segment < IMG_DEV).astype(jnp.float32)
    counts = jnp.sum(live[:, None] * hot_any.astype(jnp.float32), axis=0)
    cond_float = condition.astype(jnp.float32)
    activated = jax.nn.silu(cond_float).astype(bf)
    act_slices = activated.astype(jnp.float32).reshape(IMG_DEV, 8, 96).transpose(1, 0, 2)
    act_slices = jnp.pad(act_slices, ((0, 0), (0, 6), (0, 32)))
    act_slices = act_slices.at[:, 2, :EXPERTS].set(counts)
    ada_pad = jnp.pad(ada_weight, ((0, 32), (0, 0)))
    router_pack = jnp.pad(router_weight.reshape(192), (0, 2048 - 192)).reshape(16, 128)
    qkvo_shard = jnp.concatenate([qkv_weight, out_weight], axis=1)
    qkvo, routers, seen, mod_rows, up_line, down_line = opening(
        qkvo_shard, router_pack, act_slices, ada_pad, shared_up, shared_down.T
    )
    expert_counts = seen[66, :EXPERTS].astype(jnp.int32)
    modulation = lax.dynamic_slice(mod_rows, (0, 2 * d_index, 0), (4, 2, 1152))
    modulation = modulation.transpose(1, 0, 2).reshape(2, 4608)
    router_full = (
        routers.reshape(32, 2048)[:, :192]
        .reshape(4, 8, 96, 2)
        .transpose(1, 2, 0, 3)
        .reshape(model_width, EXPERTS)
    )
    segments = (segment[:, None], segment[None, :])
    heads, totals, attended, projected, residual, second_input, d_mixed, gates, rows, grads = front(
        tokens, modulation, inside, *segments, qkvo, router_full, cotangent, routes, target.T
    )
    rows = rows.reshape(EXPERTS, CAP, model_width)
    grads = grads.reshape(EXPERTS, CAP, model_width)
    rows_in, grads_in, shared_out, d_second, shared_first_grad, shared_second_grad = outbound(
        rows, grads, up_line, down_line, second_input, d_mixed
    )
    returned, d_returned, *parts, first_part, second_part = experts(
        rows_in, grads_in, up_all, down_all, shared_first_grad, shared_second_grad
    )
    up_keep, up_x, up_y, down_keep, down_x, down_y = parts
    up_near, down_near = (hop(up_x, 2), hop(up_y, 4)), (hop(down_x, 2), hop(down_y, 4))
    shared_first_sum, shared_second_sum = line_sum(first_part, 1), line_sum(second_part, 0)
    returned = returned.reshape(EXPERTS * CAP, model_width)
    d_returned = d_returned.reshape(EXPERTS * CAP, model_width)
    output, tokens_grad, qkvo_grad, d_modulation, router_grad = rear(
        tokens, modulation, inside, *segments, qkvo, router_full, cotangent, routes, target,
        heads, totals, attended, projected, residual, second_input, gates,
        returned, d_returned, shared_out, d_second,
    )
    qkvo_grad, up_near, down_near, shared_first_sum, shared_second_sum = lax.optimization_barrier(
        (qkvo_grad, up_near, down_near, shared_first_sum, shared_second_sum)
    )
    up_next, down_next = square_next(up_keep, *up_near), square_next(down_keep, *down_near)
    d_modulation = d_modulation.astype(bf)
    d_mod_rows = d_modulation.astype(jnp.float32).reshape(2, 4, 1152).transpose(1, 0, 2)
    d_mod_rows = lax.dynamic_update_slice(
        jnp.zeros((4, 8, 1152), jnp.float32), d_mod_rows, (0, 2 * d_index, 0)
    )
    router_tiles = jnp.pad(
        router_grad.reshape(EXPERTS, 8, 96).transpose(1, 0, 2), ((0, 0), (0, 0), (0, 32))
    )
    qkvo_sum, ada_grad, d_act_tiles, router_sum = dense_sums(
        ("cols",),
        (qkvo_grad,),
        (d_mod_rows, router_tiles, seen[:64].astype(bf), ada_weight),
        3,
    )
    qkvo_sum, up_next, down_next = lax.optimization_barrier((qkvo_sum, up_next, down_next))
    expert_up_grad = square_last(up_keep, *up_near, *up_next)
    expert_down_grad = square_last(down_keep, *down_near, *down_next)
    d_activated = lax.dynamic_slice(d_act_tiles, (0, 2 * d_index, 0), (8, 2, 96))
    d_activated = d_activated.transpose(1, 0, 2).reshape(2, model_width)
    condition_grad = jax.vjp(jax.nn.silu, cond_float)[1](d_activated)[0]
    router_out = lax.dynamic_slice(router_sum, (2 * d_index, 0), (2, 96)).T
    return (
        output,
        tokens_grad,
        condition_grad,
        ada_grad,
        qkvo_sum[:, :576],
        qkvo_sum[:, 576:],
        shared_first_sum,
        shared_second_sum.T,
        router_out,
        expert_up_grad,
        expert_down_grad,
        expert_counts,
    )


def solution(mesh):
    placed = (
        P(("dp", "fsdp"), None),
        P(("dp", "fsdp"), None),
        P("fsdp", "dp"),
        P("fsdp", "dp"),
        P("fsdp", "dp"),
        P("fsdp", "dp"),
        P("fsdp", "dp"),
        P("fsdp", "dp"),
        P("dp", "fsdp", None),
        P("dp", "fsdp", None),
        P(("dp", "fsdp"), None),
        P(("dp", "fsdp")),
        P(("dp", "fsdp"), None),
    )
    fitted = mesh.shape["dp"] == 4 and mesh.shape["fsdp"] == 8
    return jax.shard_map(
        fitted_shards if fitted else shards,
        mesh=mesh,
        in_specs=placed,
        out_specs=(
            P(("dp", "fsdp"), None),
            P(("dp", "fsdp"), None),
            P(("dp", "fsdp"), None),
            P("fsdp", "dp"),
            P("fsdp", "dp"),
            P("fsdp", "dp"),
            P("fsdp", "dp"),
            P("fsdp", "dp"),
            P("fsdp", "dp"),
            P("dp", "fsdp", None),
            P("dp", "fsdp", None),
            P(),
        ),
        check_vma=False,
    )
```

```python
import functools

import jax
import jax.numpy as jnp
from jax import lax
from jax.experimental import pallas as pl
from jax.experimental.pallas import tpu as pltpu
from jax.sharding import PartitionSpec as P

HEADS = 12
EXPERTS = 8
CAP = 144
IMG_DEV = 2
LONG = 512
MESH = pl.DeviceIdType.MESH


EXACT = lax.Precision.HIGHEST


def owners(image_sizes):
    starts = jnp.cumsum(image_sizes) - image_sizes
    position = jnp.arange(LONG, dtype=jnp.int32)[:, None]
    inside = (position >= starts[None, :]) & (position < (starts + image_sizes)[None, :])
    slot_ids = jnp.arange(IMG_DEV, dtype=jnp.int32)
    segment = jnp.sum(jnp.where(inside, slot_ids[None, :], 0), axis=1) + jnp.where(
        jnp.any(inside, axis=1), 0, IMG_DEV
    )
    return (inside.astype(jnp.float32), segment)


def dispatch_plan(routes):
    flat = routes.reshape(-1)
    onehot = (flat[:, None] == jnp.arange(EXPERTS, dtype=jnp.int32)[None, :]).astype(jnp.int32)
    before = jnp.cumsum(onehot, axis=0) - onehot
    position = jnp.sum(before * onehot, axis=1)
    target = flat * CAP + position
    assignment = jnp.arange(2 * LONG, dtype=jnp.int32)
    source = jnp.zeros((EXPERTS * CAP,), jnp.int32).at[target].set(assignment)
    filled = jnp.zeros((EXPERTS * CAP,), jnp.int32).at[target].set(1)
    return (target, source, filled)


def layer_norm(values_in):
    centred = values_in - jnp.mean(values_in, axis=-1, keepdims=True)
    inv_std = lax.rsqrt(jnp.mean(centred * centred, axis=-1, keepdims=True) + 1e-06)
    return (centred * inv_std, inv_std)


def norm_back(upstream, normed, inv_std):
    return (
        upstream
        - jnp.mean(upstream, axis=-1, keepdims=True)
        - normed * jnp.mean(upstream * normed, axis=-1, keepdims=True)
    ) * inv_std


def gelu_tanh(values_in):
    return jax.nn.gelu(values_in, approximate=True)


def gelu_back(values_in, upstream):
    return jax.vjp(gelu_tanh, values_in)[1](upstream)[0]


def collect(first, second, third):
    widened = (
        lax.all_gather(first, "dp", axis=1, tiled=True),
        lax.all_gather(second, "dp", axis=1, tiled=True),
        lax.all_gather(third, "dp", axis=1, tiled=True),
    )
    return (
        lax.all_gather(widened[0], "fsdp", axis=0, tiled=True),
        lax.all_gather(widened[1], "fsdp", axis=0, tiled=True),
        lax.all_gather(widened[2], "fsdp", axis=0, tiled=True),
    )


def spread(first, second, third):
    row_sums = (
        lax.psum_scatter(first, "fsdp", scatter_dimension=0, tiled=True),
        lax.psum_scatter(second, "fsdp", scatter_dimension=0, tiled=True),
        lax.psum_scatter(third, "fsdp", scatter_dimension=0, tiled=True),
    )
    return (
        lax.psum_scatter(row_sums[0], "dp", scatter_dimension=1, tiled=True),
        lax.psum_scatter(row_sums[1], "dp", scatter_dimension=1, tiled=True),
        lax.psum_scatter(row_sums[2], "dp", scatter_dimension=1, tiled=True),
    )


def gather_experts(up_shard, down_shard):
    return (
        lax.all_gather(up_shard, "fsdp", axis=1, tiled=True),
        lax.all_gather(down_shard, "fsdp", axis=1, tiled=True),
    )


def expert_forward(buffer_in, up_full, down_full):
    expert_pre = jnp.einsum(
        "secd,edf->secf", buffer_in, up_full, preferred_element_type=jnp.float32
    )
    expert_act = gelu_tanh(expert_pre).astype(jnp.bfloat16)
    expert_out = jnp.einsum(
        "secf,efd->secd", expert_act, down_full, preferred_element_type=jnp.float32
    ).astype(jnp.bfloat16)
    return (expert_pre, expert_act, expert_out)


def expert_backward(buffer_in, expert_pre, expert_act, d_out, up_full, down_full):
    d_act = jnp.einsum("secd,efd->secf", d_out, down_full, preferred_element_type=jnp.float32)
    d_pre = gelu_back(expert_pre, d_act).astype(jnp.bfloat16)
    d_rows = jnp.einsum(
        "secf,edf->secd", d_pre, up_full, preferred_element_type=jnp.float32
    ).astype(jnp.bfloat16)
    down_grad = jnp.einsum("secf,secd->efd", expert_act, d_out, preferred_element_type=jnp.float32)
    up_grad = jnp.einsum("secd,secf->edf", buffer_in, d_pre, preferred_element_type=jnp.float32)
    return (up_grad, down_grad, d_rows)


def attend(queries, keys_all, values_all, segment):
    row_count, head_count, head_size = queries.shape
    block_rows = min(512, row_count)
    block_count = row_count // block_rows
    score_scale = head_size ** (-0.5)

    def one_block(pieces):
        query_part, segment_part = pieces
        allowed = (segment_part[:, None] == segment[None, :])[None]
        scores = (
            jnp.einsum("qhd,khd->hqk", query_part, keys_all, preferred_element_type=jnp.float32)
            * score_scale
        )
        scores = jnp.where(allowed, scores, -1e30)
        row_max = jnp.max(scores, axis=-1, keepdims=True)
        weight = jnp.exp(scores - row_max)
        running = jnp.sum(weight, axis=-1, keepdims=True)
        probability = (weight / running).astype(jnp.bfloat16)
        attended = jnp.einsum(
            "hqk,khd->qhd", probability, values_all, preferred_element_type=jnp.float32
        )
        return (attended.astype(jnp.bfloat16), (row_max + jnp.log(running))[:, :, 0])

    return lax.map(
        one_block,
        (
            queries.reshape(block_count, block_rows, head_count, head_size),
            segment.reshape(block_count, block_rows),
        ),
    )


def attend_back(queries, keys_all, values_all, segment, log_totals, d_attended):
    row_count, head_count, head_size = queries.shape
    block_rows = min(512, row_count)
    block_count = row_count // block_rows
    score_scale = head_size ** (-0.5)

    def one_block(carry, pieces):
        key_sum, value_sum = carry
        query_part, segment_part, total_part, grad_part = pieces
        allowed = (segment_part[:, None] == segment[None, :])[None]
        scores = (
            jnp.einsum("qhd,khd->hqk", query_part, keys_all, preferred_element_type=jnp.float32)
            * score_scale
        )
        scores = jnp.where(allowed, scores, -1e30)
        probability = jnp.exp(scores - total_part[:, :, None])
        d_prob = jnp.einsum(
            "qhd,khd->hqk", grad_part, values_all, preferred_element_type=jnp.float32
        )
        d_scores = (
            probability * (d_prob - jnp.sum(probability * d_prob, axis=-1, keepdims=True))
        ).astype(jnp.bfloat16)
        query_grad = (
            jnp.einsum("hqk,khd->qhd", d_scores, keys_all, preferred_element_type=jnp.float32)
            * score_scale
        )
        key_sum = (
            key_sum
            + jnp.einsum("hqk,qhd->khd", d_scores, query_part, preferred_element_type=jnp.float32)
            * score_scale
        )
        value_sum = value_sum + jnp.einsum(
            "hqk,qhd->khd",
            probability.astype(jnp.bfloat16),
            grad_part,
            preferred_element_type=jnp.float32,
        )
        return ((key_sum, value_sum), query_grad)

    empty = jnp.zeros(keys_all.shape, jnp.float32)
    sums, query_grads = lax.scan(
        one_block,
        (empty, empty),
        (
            queries.reshape(block_count, block_rows, head_count, head_size),
            segment.reshape(block_count, block_rows),
            log_totals,
            d_attended.reshape(block_count, block_rows, head_count, head_size),
        ),
    )
    return (query_grads.reshape(row_count, head_count, head_size), sums[0], sums[1])


def shards(
    tokens,
    condition,
    ada_weight,
    qkv_weight,
    out_weight,
    shared_up,
    shared_down,
    router_weight,
    expert_up,
    expert_down,
    routes,
    image_sizes,
    cotangent,
):
    model_width = tokens.shape[1]
    head_size = model_width // HEADS
    inside, segment = owners(image_sizes)
    target, source, filled = dispatch_plan(routes)
    route_hot = (routes[:, :, None] == jnp.arange(EXPERTS, dtype=jnp.int32)[None, None, :]).astype(
        jnp.float32
    )
    live = (segment < IMG_DEV).astype(jnp.int32)
    local_counts = jnp.sum(live[:, None, None] * route_hot.astype(jnp.int32), axis=(0, 1))
    expert_counts = lax.psum(local_counts, ("dp", "fsdp"))
    ada_full, qkv_full, out_full = collect(ada_weight, qkv_weight, out_weight)
    cond_float = condition.astype(jnp.float32)
    activated = jax.nn.silu(cond_float).astype(jnp.bfloat16)
    modulation = jnp.dot(activated, ada_full, preferred_element_type=jnp.float32)
    per_row = jnp.dot(inside, modulation, precision=EXACT, preferred_element_type=jnp.float32)
    shift_one, scale_one, gate_one, shift_two, scale_two, gate_two = jnp.split(per_row, 6, axis=1)
    token_float = tokens.astype(jnp.float32)
    normed_one, inv_one = layer_norm(token_float)
    first_input = (normed_one * (1.0 + scale_one) + shift_one).astype(jnp.bfloat16)
    qkv_rows = jnp.dot(first_input, qkv_full, preferred_element_type=jnp.float32).astype(
        jnp.bfloat16
    )
    queries = qkv_rows[:, :model_width].reshape(-1, HEADS, head_size)
    keys_all = qkv_rows[:, model_width : 2 * model_width].reshape(-1, HEADS, head_size)
    values_all = qkv_rows[:, 2 * model_width :].reshape(-1, HEADS, head_size)
    attended_blocks, log_totals = attend(queries, keys_all, values_all, segment)
    attended = attended_blocks.reshape(-1, model_width)
    projected = jnp.dot(attended, out_full, preferred_element_type=jnp.float32)
    residual_one = token_float + gate_one * projected
    normed_two, inv_two = layer_norm(residual_one)
    second_input = (normed_two * (1.0 + scale_two) + shift_two).astype(jnp.bfloat16)
    shared_first, shared_second, router_full = collect(shared_up, shared_down, router_weight)
    shared_pre = jnp.dot(second_input, shared_first, preferred_element_type=jnp.float32)
    shared_act = gelu_tanh(shared_pre).astype(jnp.bfloat16)
    shared_out = jnp.dot(shared_act, shared_second, preferred_element_type=jnp.float32)
    logits = jnp.dot(second_input, router_full, preferred_element_type=jnp.float32)
    chosen = jnp.sum(logits[:, None, :] * route_hot, axis=-1)
    gate_share = jax.nn.softmax(chosen, axis=-1)
    buffer_rows = jnp.take(second_input, source // 2, axis=0).reshape(EXPERTS, CAP, model_width)
    up_full, down_full = gather_experts(expert_up, expert_down)
    groups = lax.axis_size("dp")
    expert_in = lax.all_to_all(
        buffer_rows.reshape(groups, EXPERTS // groups, CAP, model_width),
        "dp",
        split_axis=0,
        concat_axis=0,
        tiled=True,
    )
    expert_pre, expert_act, expert_out = expert_forward(expert_in, up_full, down_full)
    returned = lax.all_to_all(expert_out, "dp", split_axis=0, concat_axis=0, tiled=True).reshape(
        EXPERTS, CAP, model_width
    )
    picked = (
        jnp.take(returned.reshape(EXPERTS * CAP, model_width), target, axis=0)
        .reshape(-1, 2, model_width)
        .astype(jnp.float32)
    )
    mixed = shared_out + jnp.sum(gate_share[:, :, None] * picked, axis=1)
    output = (residual_one + gate_two * mixed).astype(jnp.bfloat16)
    upstream = cotangent.astype(jnp.float32)
    d_mixed = gate_two * upstream
    d_gate_two = upstream * mixed
    d_gate_share = jnp.sum(d_mixed[:, None, :] * picked, axis=-1)
    slot_gate = jnp.take(gate_share.reshape(-1), source) * filled.astype(jnp.float32)
    d_buffer = (
        (jnp.take(d_mixed, source // 2, axis=0) * slot_gate[:, None])
        .astype(jnp.bfloat16)
        .reshape(EXPERTS, CAP, model_width)
    )
    shared_first, shared_second, router_full = collect(shared_up, shared_down, router_weight)
    up_full, down_full = gather_experts(expert_up, expert_down)
    arrived = lax.all_to_all(
        d_buffer.reshape(groups, EXPERTS // groups, CAP, model_width),
        "dp",
        split_axis=0,
        concat_axis=0,
        tiled=True,
    )
    up_grad, down_grad, d_rows = expert_backward(
        expert_in, expert_pre, expert_act, arrived, up_full, down_full
    )
    d_returned = lax.all_to_all(d_rows, "dp", split_axis=0, concat_axis=0, tiled=True).reshape(
        EXPERTS, CAP, model_width
    )
    expert_sums = (
        lax.psum_scatter(up_grad, "fsdp", scatter_dimension=1, tiled=True),
        lax.psum_scatter(down_grad, "fsdp", scatter_dimension=1, tiled=True),
    )
    d_shared = d_mixed.astype(jnp.bfloat16)
    shared_second_grad = jnp.einsum(
        "tf,td->fd", shared_act, d_shared, preferred_element_type=jnp.float32
    )
    d_shared_act = jnp.einsum(
        "td,fd->tf", d_shared, shared_second, preferred_element_type=jnp.float32
    )
    d_shared_pre = gelu_back(shared_pre, d_shared_act).astype(jnp.bfloat16)
    shared_first_grad = jnp.einsum(
        "td,tf->df", second_input, d_shared_pre, preferred_element_type=jnp.float32
    )
    d_chosen = gate_share * (
        d_gate_share - jnp.sum(gate_share * d_gate_share, axis=-1, keepdims=True)
    )
    d_logits = jnp.sum(d_chosen[:, :, None] * route_hot, axis=1).astype(jnp.bfloat16)
    router_grad = jnp.einsum(
        "td,te->de", second_input, d_logits, preferred_element_type=jnp.float32
    )
    from_experts = (
        jnp.take(d_returned.reshape(EXPERTS * CAP, model_width), target, axis=0)
        .reshape(-1, 2, model_width)
        .astype(jnp.float32)
    )
    d_second = (
        jnp.einsum("tf,df->td", d_shared_pre, shared_first, preferred_element_type=jnp.float32)
        + jnp.einsum("te,de->td", d_logits, router_full, preferred_element_type=jnp.float32)
        + jnp.sum(from_experts, axis=1)
    )
    mlp_sums = spread(shared_first_grad, shared_second_grad, router_grad)
    d_scale_two = d_second * normed_two
    d_residual = upstream + norm_back(d_second * (1.0 + scale_two), normed_two, inv_two)
    ada_full, qkv_full, out_full = collect(ada_weight, qkv_weight, out_weight)
    d_projected = (gate_one * d_residual).astype(jnp.bfloat16)
    d_gate_one = d_residual * projected
    out_grad = jnp.einsum("td,te->de", attended, d_projected, preferred_element_type=jnp.float32)
    d_attended = jnp.einsum(
        "te,de->td", d_projected, out_full, preferred_element_type=jnp.float32
    ).astype(jnp.bfloat16)
    d_queries, d_keys, d_values = attend_back(
        queries, keys_all, values_all, segment, log_totals, d_attended.reshape(-1, HEADS, head_size)
    )
    d_qkv = jnp.concatenate(
        [
            d_queries.reshape(-1, model_width),
            d_keys.reshape(-1, model_width),
            d_values.reshape(-1, model_width),
        ],
        axis=1,
    ).astype(jnp.bfloat16)
    qkv_grad = jnp.einsum("td,te->de", first_input, d_qkv, preferred_element_type=jnp.float32)
    d_first = jnp.einsum("te,de->td", d_qkv, qkv_full, preferred_element_type=jnp.float32)
    d_scale_one = d_first * normed_one
    tokens_grad = d_residual + norm_back(d_first * (1.0 + scale_one), normed_one, inv_one)
    d_per_row = jnp.concatenate(
        [d_first, d_scale_one, d_gate_one, d_second, d_scale_two, d_gate_two], axis=1
    )
    d_modulation = jnp.einsum(
        "tj,te->je", inside, d_per_row, precision=EXACT, preferred_element_type=jnp.float32
    ).astype(jnp.bfloat16)
    ada_grad = jnp.einsum("jd,je->de", activated, d_modulation, preferred_element_type=jnp.float32)
    d_activated = jnp.einsum(
        "je,de->jd", d_modulation, ada_full, preferred_element_type=jnp.float32
    )
    condition_grad = jax.vjp(jax.nn.silu, cond_float)[1](d_activated)[0]
    attn_sums = spread(ada_grad, qkv_grad, out_grad)
    return (
        output,
        tokens_grad,
        condition_grad,
        attn_sums[0],
        attn_sums[1],
        attn_sums[2],
        mlp_sums[0],
        mlp_sums[1],
        mlp_sums[2],
        expert_sums[0],
        expert_sums[1],
        expert_counts,
    )


def at(d, s, c):
    return (d, 2 * s + c)


def slot(kind, f, d):
    if kind == "cols":
        return (pl.ds(pl.multiple_of(96 * f, 96), 96), pl.ds(pl.multiple_of(768 * d, 768), 768))
    return (pl.ds(pl.multiple_of(192 * d, 192), 192), pl.ds(pl.multiple_of(384 * f, 384), 384))


def half_slot(kind, f, d, h):
    if kind == "cols":
        return (
            pl.ds(pl.multiple_of(96 * f, 96), 96),
            pl.ds(pl.multiple_of(768 * d + 384 * h, 384), 384),
        )
    return (
        pl.ds(pl.multiple_of(192 * d + 96 * h, 96), 96),
        pl.ds(pl.multiple_of(384 * f, 384), 384),
    )


def place():
    d = lax.axis_index("dp")
    f = lax.axis_index("fsdp")
    return d, f // 2, lax.rem(f, 2)


def flip(v, bit):
    return v + bit - 2 * bit * lax.rem(v // bit, 2)


def greet(devices):
    barrier = pltpu.get_barrier_semaphore()
    for device in devices:
        pl.semaphore_signal(barrier, inc=1, device_id=device, device_id_type=MESH)
    pl.semaphore_wait(barrier, len(devices))


def push(src, dst, send_sem, recv_sem, device):
    return pltpu.make_async_remote_copy(
        src_ref=src,
        dst_ref=dst,
        send_sem=send_sem,
        recv_sem=recv_sem,
        device_id=device,
        device_id_type=MESH,
    )


GATHER_SEMS = 3 + 8 + 8 + 20


class Gather:
    def __init__(self, kind, shard, full, ssem, rsem, lsem):
        self.kind, self.shard, self.full = kind, shard, full
        self.ssem, self.rsem, self.lsem = ssem, rsem, lsem
        self.d, self.s, self.c = place()
        self.sent = []

    def f(self, s):
        return 2 * s + self.c

    def go(self, index, where, device, src=None):
        ref = self.full.at[where]
        copy = push(
            ref if src is None else src, ref, self.ssem.at[index], self.rsem.at[index], device
        )
        copy.start()
        self.sent.append(copy)

    def arrived(self, index, where):
        ref = self.full.at[where]
        push(ref, ref, self.ssem.at[index], self.rsem.at[index], at(self.d, self.s, self.c)).wait_recv()

    def start(self):
        d, s, c = self.d, self.s, self.c
        mine = slot(self.kind, self.f(s), d)
        self.own = pltpu.make_async_copy(self.shard, self.full.at[mine], self.lsem)
        self.own.start()
        self.go(1, mine, at(flip(d, 2), s, c), self.shard)
        self.go(0, mine, at(flip(d, 1), s, c), self.shard)
        self.go(3, mine, at(d, flip(s, 1), c), self.shard)
        self.go(4, mine, at(d, flip(s, 2), c), self.shard)
        self.go(19, mine, at(d, s, 1 - c), self.shard)

    def source(self, k):
        return (self.d, flip(self.d, 1), flip(self.d, 2), flip(flip(self.d, 1), 2))[k]

    def spread_z(self, k):
        d, s, c = self.d, self.s, self.c
        block = slot(self.kind, self.f(s), self.source(k))
        self.arrived(k - 1, block)
        if k == 2:
            self.go(2, block, at(flip(d, 1), s, c))
        self.go(3 + 2 * k, block, at(d, flip(s, 1), c))
        self.go(4 + 2 * k, block, at(d, flip(s, 2), c))
        self.go(19 + 5 * k, block, at(d, s, 1 - c))

    def relay(self, k):
        d, s, c = self.d, self.s, self.c
        source = self.source(k)
        sx, sy = flip(s, 1), flip(s, 2)
        from_x = slot(self.kind, self.f(sx), source)
        from_y = slot(self.kind, self.f(sy), source)
        self.arrived(3 + 2 * k, from_x)
        self.go(11 + 2 * k, half_slot(self.kind, self.f(sx), source, 0), at(d, sy, c))
        self.go(20 + 5 * k, from_x, at(d, s, 1 - c))
        self.arrived(4 + 2 * k, from_y)
        self.go(12 + 2 * k, half_slot(self.kind, self.f(sy), source, 1), at(d, sx, c))
        self.go(21 + 5 * k, from_y, at(d, s, 1 - c))

    def corner(self, k):
        d, s, c = self.d, self.s, self.c
        source = self.source(k)
        sd = flip(flip(s, 1), 2)
        for h in range(2):
            where = half_slot(self.kind, self.f(sd), source, h)
            self.arrived(11 + 2 * k + h, where)
            self.go(22 + 5 * k + h, where, at(d, s, 1 - c))

    def finish(self):
        d, s, c = self.d, self.s, self.c
        sx, sy = flip(s, 1), flip(s, 2)
        sd = flip(sx, 2)
        self.own.wait()
        for k in range(4):
            source = self.source(k)
            for j, position in enumerate((s, sx, sy)):
                self.arrived(19 + 5 * k + j, slot(self.kind, 2 * position + 1 - c, source))
            for h in range(2):
                self.arrived(22 + 5 * k + h, half_slot(self.kind, 2 * sd + 1 - c, source, h))
        for copy in self.sent:
            copy.wait_send()


class Line:
    def __init__(self, kind, shard, line, ssem, rsem, lsem):
        self.kind, self.shard, self.line = kind, shard, line
        self.ssem, self.rsem, self.lsem = ssem, rsem, lsem
        self.d, self.s, self.c = place()

    def block(self, d):
        if self.kind == "cols":
            return self.line.at[:, pl.ds(pl.multiple_of(768 * d, 768), 768)]
        return self.line.at[pl.ds(pl.multiple_of(192 * d, 192), 192)]

    def copy(self, index, src, source, target):
        return push(
            src, self.block(source), self.ssem.at[index], self.rsem.at[index], at(target, self.s, self.c)
        )

    def start(self):
        d = self.d
        self.own = pltpu.make_async_copy(self.shard, self.block(d), self.lsem)
        self.own.start()
        self.sent = [
            self.copy(0, self.shard, d, flip(d, 2)),
            self.copy(1, self.shard, d, flip(d, 1)),
        ]
        for copy in self.sent:
            copy.start()

    def relay(self):
        d2 = flip(self.d, 2)
        self.copy(0, self.shard, d2, d2).wait_recv()
        copy = self.copy(2, self.block(d2), d2, flip(self.d, 1))
        copy.start()
        self.sent.append(copy)

    def finish(self):
        d1 = flip(self.d, 1)
        self.own.wait()
        self.copy(1, self.shard, d1, d1).wait_recv()
        self.copy(2, self.shard, flip(d1, 2), d1).wait_recv()
        for copy in self.sent:
            copy.wait_send()


class Spread:
    def __init__(self, kind, line, full, ssem, rsem, lsem):
        self.kind, self.line, self.full = kind, line, full
        self.ssem, self.rsem, self.lsem = ssem, rsem, lsem
        self.d, self.s, self.c = place()
        self.sx, self.sy = flip(self.s, 1), flip(self.s, 2)
        self.sd = flip(self.sx, 2)
        self.mate = at(self.d, self.s, 1 - self.c)
        self.to_x, self.to_y = at(self.d, self.sx, self.c), at(self.d, self.sy, self.c)
        self.sent = []

    def block(self, position, c, h=None):
        f = 2 * position + c
        if self.kind == "cols":
            rows = pl.ds(pl.multiple_of(96 * f, 96), 96)
            return self.full.at[rows] if h is None else self.full.at[rows, pl.ds(1536 * h, 1536)]
        columns = pl.ds(pl.multiple_of(384 * f, 384), 384)
        rows = pl.ds(0, 768) if h is None else pl.ds(384 * h, 384)
        return self.full.at[rows, columns]

    def go(self, index, ref, device, src=None):
        copy = push(
            ref if src is None else src, ref, self.ssem.at[index], self.rsem.at[index], device
        )
        copy.start()
        self.sent.append(copy)

    def arrived(self, index, ref):
        push(ref, ref, self.ssem.at[index], self.rsem.at[index], self.mate).wait_recv()

    def start(self):
        mine = self.block(self.s, self.c)
        self.own = pltpu.make_async_copy(self.line, mine, self.lsem)
        self.own.start()
        self.go(0, mine, self.to_x, self.line)
        self.go(1, mine, self.to_y, self.line)
        self.go(2, mine, self.mate, self.line)

    def relay(self):
        c = self.c
        from_x, from_y = self.block(self.sx, c), self.block(self.sy, c)
        self.arrived(0, from_x)
        self.go(3, self.block(self.sx, c, 0), self.to_y)
        self.go(5, from_x, self.mate)
        self.arrived(1, from_y)
        self.go(4, self.block(self.sy, c, 1), self.to_x)
        self.go(6, from_y, self.mate)

    def corner(self):
        for h in range(2):
            ref = self.block(self.sd, self.c, h)
            self.arrived(3 + h, ref)
            self.go(7 + h, ref, self.mate)

    def finish(self):
        c = 1 - self.c
        self.own.wait()
        self.arrived(2, self.block(self.s, c))
        self.arrived(5, self.block(self.sx, c))
        self.arrived(6, self.block(self.sy, c))
        for h in range(2):
            self.arrived(7 + h, self.block(self.sd, c, h))
        for copy in self.sent:
            copy.wait_send()


class Near:
    def __init__(self, up_shard, down_shard, up_six, down_two, ssem, rsem, lsem):
        self.up_shard, self.down_shard = up_shard, down_shard
        self.up_six, self.down_two = up_six, down_two
        self.ssem, self.rsem, self.lsem = ssem, rsem, lsem
        self.d, self.s, self.c = place()

    def start(self):
        d, s, c = self.d, self.s, self.c
        sx, sy = flip(s, 1), flip(s, 2)
        self.local = [
            pltpu.make_async_copy(self.up_shard.at[c], self.up_six.at[0], self.lsem.at[0]),
            pltpu.make_async_copy(self.down_shard.at[c], self.down_two.at[0], self.lsem.at[1]),
        ]
        mine, theirs = c, 1 - c
        plan = (
            (self.up_shard, mine, self.up_six.at[2], sx),
            (self.up_shard, mine, self.up_six.at[4], sy),
            (self.up_shard, theirs, self.up_six.at[3], sx),
            (self.up_shard, theirs, self.up_six.at[5], sy),
            (self.up_shard, theirs, self.up_six.at[1], s),
            (self.down_shard, theirs, self.down_two.at[1], s),
        )
        self.away = [
            push(shard.at[which], out, self.ssem.at[i], self.rsem.at[i], at(d, position, which))
            for i, (shard, which, out, position) in enumerate(plan)
        ]
        for copy in self.away + self.local:
            copy.start()

    def finish(self):
        for copy in self.local + self.away:
            copy.wait()


class Corner:
    def __init__(self, from_x, from_y, corner, ssem, rsem):
        d, s, c = place()
        self.copies = [
            push(from_x, corner.at[0], ssem.at[0], rsem.at[0], at(d, flip(s, 2), c)),
            push(from_y, corner.at[1], ssem.at[1], rsem.at[1], at(d, flip(s, 1), c)),
        ]

    def start(self):
        for copy in self.copies:
            copy.start()

    def finish(self):
        for copy in self.copies:
            copy.wait()


def everyone_else():
    me = lax.axis_index("dp") * 8 + lax.axis_index("fsdp")

    def other(k):
        device = lax.rem(me + k, 32)
        return (device // 8, lax.rem(device, 8))

    return me, other


def open_kernel(
    shard, router, act_ref, ada_ref, up_shard, down_shard, expert_up, expert_down,
    full, routers, seen, rows_out, up_line, down_line, up_six, down_two,
    heard, part, got, mixed, ssem, rsem, lsem, asem, brsem, rssem, rrsem, tssem, trsem, zssem, zrsem,
    us, ur, ds, dr, es, er, el,
):
    me, other = everyone_else()
    d, s, c = place()
    f = 2 * s + c
    barrier = pltpu.get_barrier_semaphore()

    def hello(k, carry):
        pl.semaphore_signal(barrier, inc=1, device_id=other(k), device_id_type=MESH)
        return carry

    lax.fori_loop(1, 32, hello, 0)
    pl.semaphore_wait(barrier, 31)

    def act_copy(k, source):
        device = other(k)
        return push(act_ref.at[device[1]], heard.at[source], asem.at[k], brsem.at[k], device)

    def router_copy(k, source):
        return push(router, routers.at[source], rssem.at[k], rrsem.at[k], other(k))

    def send(k, carry):
        act_copy(k, me).start()
        return carry

    lax.fori_loop(1, 32, send, 0)
    gather = Gather("cols", shard, full, ssem, rsem, lsem.at[0])
    gather.start()
    near = Near(expert_up, expert_down, up_six, down_two, es, er, el)
    near.start()
    lines = (
        Line("cols", up_shard, up_line, us, ur, lsem.at[3]),
        Line("rows", down_shard, down_line, ds, dr, lsem.at[4]),
    )
    own_router = pltpu.make_async_copy(router, routers.at[me], lsem.at[1])
    own_router.start()

    def send_router(k, carry):
        router_copy(k, me).start()
        return carry

    lax.fori_loop(1, 32, send_router, 0)
    heard[me] = act_ref[f]

    def take(k, carry):
        copy = act_copy(k, lax.rem(me + 32 - k, 32))
        copy.wait_recv()
        return carry

    lax.fori_loop(1, 32, take, 0)
    everything = heard[...].reshape(256, 128)
    row = lax.broadcasted_iota(jnp.int32, (64, 256), 0)
    column = lax.broadcasted_iota(jnp.int32, (64, 256), 1)
    source = lax.rem(row // 2, 4) * 8 + row // 8
    pick = (column == source * 8 + lax.rem(row, 2)).astype(jnp.bfloat16)
    compact = jnp.dot(
        pick, everything.astype(jnp.bfloat16), preferred_element_type=jnp.float32
    ).astype(jnp.bfloat16)
    seen[...] = jnp.concatenate(
        [compact.astype(jnp.float32), jnp.sum(heard[...], axis=0)], axis=0
    )
    part[...] = jnp.dot(compact, ada_ref[...], preferred_element_type=jnp.float32).reshape(
        8, 8, 1152
    )

    def tile_copy(k):
        target = lax.rem(f + k, 8)
        return push(part.at[target], got.at[k], tssem.at[k], trsem.at[k], (d, target))

    for k in range(1, 8):
        tile_copy(k).start()
    gather.spread_z(1)
    gather.spread_z(2)
    gather.relay(0)
    for k in range(1, 8):
        tile_copy(k).wait_recv()
    total = part[f]
    for k in range(1, 8):
        total = total + got[k]
    mixed[...] = total
    zs = []
    for k in range(1, 4):
        copy = push(mixed, rows_out.at[d], zssem.at[k], zrsem.at[k], at(lax.rem(d + k, 4), s, c))
        copy.start()
        zs.append(copy)
    own_rows = pltpu.make_async_copy(mixed, rows_out.at[d], lsem.at[2])
    own_rows.start()
    gather.spread_z(3)
    for line in lines:
        line.start()
    gather.relay(1)
    gather.corner(0)
    gather.relay(2)
    gather.corner(1)
    gather.relay(3)
    gather.corner(2)
    for line in lines:
        line.relay()
    gather.corner(3)
    gather.finish()
    for line in lines:
        line.finish()
    near.finish()
    own_router.wait()
    own_rows.wait()
    for k in range(1, 4):
        push(
            mixed, rows_out.at[lax.rem(d + 4 - k, 4)], zssem.at[k], zrsem.at[k],
            at(lax.rem(d + k, 4), s, c),
        ).wait_recv()
    for copy in zs:
        copy.wait_send()
    for k in range(1, 8):
        tile_copy(k).wait_send()

    def drain(k, carry):
        act_copy(k, me).wait_send()
        copy = router_copy(k, lax.rem(me + 32 - k, 32))
        copy.wait_recv()
        copy.wait_send()
        return carry

    lax.fori_loop(1, 32, drain, 0)


DMA = pltpu.SemaphoreType.DMA
ANYWHERE = pl.BlockSpec(memory_space=pl.ANY)
ONCHIP = pl.BlockSpec(memory_space=pltpu.VMEM)


def opening(shard, router, act, ada, up_shard, down_shard, expert_up, expert_down):
    return pl.pallas_call(
        open_kernel,
        out_shape=(
            jax.ShapeDtypeStruct((768, 3072), jnp.bfloat16),
            jax.ShapeDtypeStruct((32, 16, 128), jnp.bfloat16),
            jax.ShapeDtypeStruct((72, 128), jnp.float32),
            jax.ShapeDtypeStruct((4, 8, 1152), jnp.float32),
            jax.ShapeDtypeStruct((96, 3072), jnp.bfloat16),
            jax.ShapeDtypeStruct((768, 384), jnp.bfloat16),
            jax.ShapeDtypeStruct((6, 96, 3072), jnp.bfloat16),
            jax.ShapeDtypeStruct((2, 384, 768), jnp.bfloat16),
        ),
        in_specs=[ONCHIP] * 6 + [ANYWHERE] * 2,
        out_specs=(ANYWHERE, ANYWHERE, ONCHIP) + (ANYWHERE,) * 5,
        scratch_shapes=[
            pltpu.VMEM((32, 8, 128), jnp.float32),
            pltpu.VMEM((8, 8, 1152), jnp.float32),
            pltpu.VMEM((8, 8, 1152), jnp.float32),
            pltpu.VMEM((8, 1152), jnp.float32),
            DMA((GATHER_SEMS,)), DMA((GATHER_SEMS,)), DMA((5,)),
            DMA((32,)), DMA((32,)), DMA((32,)), DMA((32,)),
            DMA((8,)), DMA((8,)), DMA((4,)), DMA((4,)),
            DMA((3,)), DMA((3,)), DMA((3,)), DMA((3,)),
            DMA((6,)), DMA((6,)), DMA((2,)),
        ],
        compiler_params=pltpu.CompilerParams(collective_id=0, has_side_effects=True),
        name="opening",
    )(shard, router, act, ada, up_shard, down_shard, expert_up, expert_down)


def group_of(d, s, c):
    return [(j, at(lax.rem(d + j // 2, 4), s, lax.rem(c + j, 2))) for j in range(1, 8)]


class Swap:
    def __init__(self, blocks, out, ssem, rsem, lsem):
        self.blocks, self.out, self.ssem, self.rsem, self.lsem = blocks, out, ssem, rsem, lsem
        self.d, self.s, self.c = place()
        self.me = 2 * self.d + self.c

    def copy(self, j, landing):
        target_d = lax.rem(self.d + j // 2, 4)
        target_c = lax.rem(self.c + j, 2)
        return push(
            self.blocks.at[2 * target_d + target_c],
            self.out.at[landing],
            self.ssem.at[j],
            self.rsem.at[j],
            at(target_d, self.s, target_c),
        )

    def start(self):
        for j in (4, 5, 2, 3, 6, 7, 1):
            self.copy(j, self.me).start()
        self.own = pltpu.make_async_copy(
            self.blocks.at[self.me], self.out.at[self.me], self.lsem
        )
        self.own.start()

    def send(self, step):
        for j in (2 * step, 2 * step + 1):
            if j:
                self.copy(j, self.me).start()
            else:
                self.own = pltpu.make_async_copy(
                    self.blocks.at[self.me], self.out.at[self.me], self.lsem
                )
                self.own.start()

    def finish(self):
        self.own.wait()
        for j in range(1, 8):
            source_d = lax.rem(self.d + 4 - j // 2, 4)
            source_c = lax.rem(self.c + j, 2)
            copy = self.copy(j, 2 * source_d + source_c)
            copy.wait_recv()
            copy.wait_send()


def nt(left, right):
    return lax.dot_general(left, right, (((1,), (1,)), ((), ())), preferred_element_type=jnp.float32)


def tn(left, right):
    return lax.dot_general(left, right, (((0,), (0,)), ((), ())), preferred_element_type=jnp.float32)


def nn(left, right):
    return jnp.dot(left, right, preferred_element_type=jnp.float32)


GELU_SCALE = 0.7978845608028654


def gelu_pair(v):
    square = v * v
    bend = jnp.tanh(GELU_SCALE * (v + 0.044715 * (square * v)))
    half = 0.5 * (1.0 + bend)
    slope = half + 0.5 * v * (1.0 - bend * bend) * (
        GELU_SCALE * (1.0 + (3.0 * 0.044715) * square)
    )
    return v * half, slope


HIDDEN = 512


def out_kernel(
    rows, grads, up_line, down_line, tokens, d_tokens, up_six, down_x, down_y,
    rows_in, grads_in, up_corner, down_corner, mixed_out, d_tokens_out, up_grad, down_grad,
    up_full, down_full, tokens_t, d_tokens_t, s1, r1, s2, r2, ssem, rsem, ssem2, rsem2, lsem,
    es, er, fs, fr,
):
    d, s, c = place()
    greet([device for _, device in group_of(d, s, c)] + [at(d, flip(s, 1), c), at(d, flip(s, 2), c)])
    both = (
        Spread("cols", up_line, up_full, ssem, rsem, lsem.at[0]),
        Spread("rows", down_line, down_full, ssem2, rsem2, lsem.at[1]),
    )
    swap_a = Swap(rows, rows_in, s1, r1, lsem.at[2])
    swap_b = Swap(grads, grads_in, s2, r2, lsem.at[3])
    for g in both:
        g.start()
    swap_a.start()
    swap_b.start()
    corners = (
        Corner(up_six.at[2], up_six.at[5], up_corner, es, er),
        Corner(down_x.at[0], down_y.at[1], down_corner, fs, fr),
    )
    tokens_t[...] = tokens[...].T
    d_tokens_t[...] = d_tokens[...].T
    mixed_out[...] = jnp.zeros_like(mixed_out)
    d_tokens_out[...] = jnp.zeros_like(d_tokens_out)
    for g in both:
        g.relay()
    for each in corners:
        each.start()
    for g in both:
        g.corner()
    for g in both:
        g.finish()

    def block(b, carry):
        where = pl.ds(pl.multiple_of(b * HIDDEN, HIDDEN), HIDDEN)
        up, down = up_full[:, where], down_full[:, where]
        act, slope = gelu_pair(nn(tokens[...], up))
        act = act.astype(jnp.bfloat16)
        mixed_out[...] += nt(act, down)
        down_grad[:, where] = nn(d_tokens_t[...], act).astype(jnp.bfloat16)
        d_pre = (slope * nn(d_tokens[...], down)).astype(jnp.bfloat16)
        d_tokens_out[...] += nt(d_pre, up)
        up_grad[:, where] = nn(tokens_t[...], d_pre).astype(jnp.bfloat16)
        return carry

    lax.fori_loop(0, 3072 // HIDDEN, block, 0)
    swap_a.finish()
    swap_b.finish()
    for each in corners:
        each.finish()


def outbound(rows, grads, up_line, down_line, tokens, d_tokens, up_six, down_x, down_y):
    bf, f32 = jnp.bfloat16, jnp.float32
    return pl.pallas_call(
        out_kernel,
        out_shape=(
            jax.ShapeDtypeStruct((8, 144, 768), bf),
            jax.ShapeDtypeStruct((8, 144, 768), bf),
            jax.ShapeDtypeStruct((2, 96, 3072), bf),
            jax.ShapeDtypeStruct((2, 384, 768), bf),
            jax.ShapeDtypeStruct((512, 768), f32),
            jax.ShapeDtypeStruct((512, 768), f32),
            jax.ShapeDtypeStruct((768, 3072), bf),
            jax.ShapeDtypeStruct((768, 3072), bf),
        ),
        in_specs=[ONCHIP] * 6 + [ANYWHERE] * 3,
        out_specs=(ANYWHERE,) * 4 + (ONCHIP,) * 4,
        scratch_shapes=[pltpu.VMEM((768, 3072), bf)] * 2
        + [pltpu.VMEM((768, 512), bf)] * 2
        + [DMA((8,))] * 4
        + [DMA((9,))] * 4
        + [DMA((4,))]
        + [DMA((2,))] * 4,
        compiler_params=pltpu.CompilerParams(
            collective_id=1, has_side_effects=True, vmem_limit_bytes=60 << 20
        ),
        name="outbound",
    )(rows, grads, up_line, down_line, tokens, d_tokens, up_six, down_x, down_y)


def widened(ref):
    return ref[...].astype(jnp.float32)


class Parts:
    def __init__(self, grad, keep, over_x, over_y, sem, rsem=None):
        d, s, c = place()
        sx, sy = flip(s, 1), flip(s, 2)
        sd = flip(sx, 2)
        rows = grad.shape[0] // 8
        slots = (
            (s, 0, keep.at[0, 0], s), (sy, 0, keep.at[0, 1], s),
            (s, 1, keep.at[1, 0], s), (sx, 1, keep.at[1, 1], s),
            (sx, 0, over_x.at[0], sx), (sd, 0, over_x.at[1], sx),
            (sy, 1, over_y.at[0], sy), (sd, 1, over_y.at[1], sy),
        )
        self.copies, self.away = [], []
        for i, (position, h, out, target) in enumerate(slots):
            part = grad.at[pl.ds(pl.multiple_of((2 * position + h) * rows, 32), rows)]
            if i < 4 or rsem is None:
                self.copies.append(pltpu.make_async_copy(part, out, sem.at[i]))
            else:
                self.away.append(push(part, out, sem.at[i], rsem.at[i], at(d, target, c)))

    def start(self):
        for copy in self.away + self.copies:
            copy.start()

    def finish(self):
        for copy in self.copies + self.away:
            copy.wait()


class Pieces:
    def __init__(self, parts, full, sem):
        d, s, c = place()
        rows = full.shape[0] // 8
        sx, sy = flip(s, 1), flip(s, 2)
        self.copies, i = [], 0
        positions = [p for p in (s, sx, sy, flip(sx, 2)) for _ in range(2)]
        for part in parts:
            for j in range(part.shape[0]):
                f = 2 * positions[i] + (c if i % 2 == 0 else 1 - c)
                self.copies.append(
                    pltpu.make_async_copy(
                        part.at[j], full.at[pl.ds(pl.multiple_of(rows * f, 32), rows)], sem.at[i]
                    )
                )
                i += 1

    def start(self):
        for copy in self.copies:
            copy.start()

    def finish(self):
        for copy in self.copies:
            copy.wait()


def expert_kernel(
    rows, grads, up_six, up_corner, down_two, down_x_in, down_y_in, down_corner, first_grad, second_grad,
    rows_back, grads_back, up_keep, up_x, up_y, down_keep, down_x, down_y, first_part, second_part,
    up, down, act, d_pre, made, d_made, total, d_total, up_grad, down_grad, rows_t,
    fo, fm, fn, ff, fs, fr, fl, so, sm, sn, sf, ss, sr, sl,
    s1, r1, s2, r2, lsem, wsem, vsem, psem, arsem, qsem,
):
    bf = jnp.bfloat16
    d, s, c = place()
    weights = (
        Pieces((up_six, up_corner), up, wsem),
        Pieces((down_two, down_x_in, down_y_in, down_corner), down, vsem),
    )
    for each in weights:
        each.start()
    greet([device for _, device in group_of(d, s, c)] + [at(d, flip(s, 1), c), at(d, flip(s, 2), c)])
    sums = (
        DenseSum("cols", first_grad, first_part, fo, fm, fn, ff, None, fs, fr, fl),
        DenseSum("rows", second_grad, second_part, so, sm, sn, sf, None, ss, sr, sl),
    )
    for each in sums:
        each.start()
    swap_a = Swap(made, rows_back, s1, r1, lsem.at[0])
    swap_b = Swap(d_made, grads_back, s2, r2, lsem.at[1])
    for each in weights:
        each.finish()
    for step in (2, 1, 3, 0):
        there = lax.rem(d + step, 4)
        chunk = pl.ds(2 * there, 2)
        lines = pl.ds(pl.multiple_of(288 * there, 288), 288)
        x = rows[chunk].reshape(288, 768)
        g = grads[chunk].reshape(288, 768)
        total[...] = jnp.zeros_like(total)
        d_total[...] = jnp.zeros_like(d_total)

        def block(b, carry):
            where = pl.ds(pl.multiple_of(b * HIDDEN, HIDDEN), HIDDEN)
            up_part, down_part = up[:, where], down[where]
            made_act, slope = gelu_pair(nn(x, up_part))
            made_act = made_act.astype(bf)
            act[lines, where] = made_act
            total[...] += nn(made_act, down_part)
            d_part = (slope * nt(g, down_part)).astype(bf)
            d_pre[lines, where] = d_part
            d_total[...] += nt(d_part, up_part)
            return carry

        lax.fori_loop(0, 3072 // HIDDEN, block, 0)
        made[chunk] = total[...].astype(bf).reshape(2, 144, 768)
        d_made[chunk] = d_total[...].astype(bf).reshape(2, 144, 768)
        swap_a.send(step)
        swap_b.send(step)
        if step == 2:
            for each in sums:
                each.merge()
        if step == 3:
            for each in sums:
                each.join()
    rows_t[...] = rows.reshape(1152, 768)[...].T
    g_all = grads.reshape(1152, 768)

    def up_block(b, carry):
        where = pl.ds(pl.multiple_of(b * HIDDEN, HIDDEN), HIDDEN)
        up_grad[:, where] = nn(rows_t[...], d_pre[:, where]).astype(bf)
        return carry

    def down_block(b, carry):
        where = pl.ds(pl.multiple_of(384 * b, 384), 384)
        down_grad[where] = tn(act[:, where], g_all[...]).astype(bf)
        return carry

    up_parts = Parts(up_grad, up_keep, up_x, up_y, psem, arsem)
    down_parts = Parts(down_grad, down_keep, down_x, down_y, qsem)
    lax.fori_loop(0, 3072 // HIDDEN, up_block, 0)
    up_parts.start()
    lax.fori_loop(0, 8, down_block, 0)
    down_parts.start()
    for each in sums:
        each.close()
    swap_a.finish()
    swap_b.finish()
    up_parts.finish()
    down_parts.finish()


def experts(rows, grads, up_pieces, down_pieces, first_grad, second_grad):
    bf, f32 = jnp.bfloat16, jnp.float32

    def rooms(piece, half):
        return [
            pltpu.VMEM((4,) + piece, bf),
            pltpu.VMEM((4,) + piece, bf),
            pltpu.VMEM((2,) + half, bf),
            pltpu.VMEM((2,) + piece, bf),
            DMA((8,)),
            DMA((8,)),
            DMA((4,)),
        ]

    def parts(r, n):
        return (
            jax.ShapeDtypeStruct((2, 2, r, n), bf),
            jax.ShapeDtypeStruct((2, r, n), bf),
            jax.ShapeDtypeStruct((2, r, n), bf),
        )

    return pl.pallas_call(
        expert_kernel,
        out_shape=(
            jax.ShapeDtypeStruct((8, 144, 768), bf),
            jax.ShapeDtypeStruct((8, 144, 768), bf),
        )
        + parts(96, 3072)
        + parts(384, 768)
        + (
            jax.ShapeDtypeStruct((96, 3072), bf),
            jax.ShapeDtypeStruct((768, 384), bf),
        ),
        in_specs=[ONCHIP, ONCHIP] + [ANYWHERE] * 8,
        out_specs=(ANYWHERE,) * 8 + (ONCHIP, ONCHIP),
        scratch_shapes=[
            pltpu.VMEM((768, 3072), bf),
            pltpu.VMEM((3072, 768), bf),
            pltpu.VMEM((1152, 3072), bf),
            pltpu.VMEM((1152, 3072), bf),
            pltpu.VMEM((8, 144, 768), bf),
            pltpu.VMEM((8, 144, 768), bf),
            pltpu.VMEM((288, 768), f32),
            pltpu.VMEM((288, 768), f32),
            pltpu.VMEM((768, 3072), bf),
            pltpu.VMEM((3072, 768), bf),
            pltpu.VMEM((768, 1152), bf),
        ]
        + rooms((96, 3072), (96, 1536))
        + rooms((768, 384), (384, 384))
        + [DMA((8,))] * 4
        + [DMA((2,)), DMA((8,)), DMA((8,)), DMA((8,)), DMA((8,)), DMA((8,))],
        compiler_params=pltpu.CompilerParams(
            collective_id=2, has_side_effects=True, vmem_limit_bytes=67043328
        ),
        name="experts",
    )(rows, grads, *up_pieces, *down_pieces, first_grad, second_grad)


def hop(values, bit):
    return lax.ppermute(values, "fsdp", [(f, f ^ bit) for f in range(8)])


def square_next(keep, from_x, from_y):
    f32, bf = jnp.float32, jnp.bfloat16
    return (
        hop((keep[0, 1].astype(f32) + from_x[1].astype(f32)).astype(bf), 4),
        hop((keep[1, 1].astype(f32) + from_y[1].astype(f32)).astype(bf), 2),
    )


def square_last(keep, from_x, from_y, low_next, high_next):
    f32, bf = jnp.float32, jnp.bfloat16
    low = keep[0, 0].astype(f32) + from_x[0].astype(f32) + low_next.astype(f32)
    high = keep[1, 0].astype(f32) + from_y[0].astype(f32) + high_next.astype(f32)
    first = lax.rem(lax.axis_index("fsdp"), 2) == 0
    other = hop(jnp.where(first, high, low).astype(bf), 1).astype(f32)
    return jnp.where(first, jnp.stack([low, other]), jnp.stack([other, high]))


class DenseSum:
    def __init__(self, kind, grad, out, own, mate, near, far, line, ssem, rsem, lsem):
        self.kind, self.grad, self.out = kind, grad, out
        self.own, self.mate, self.near, self.far, self.line = own, mate, near, far, line
        self.ssem, self.rsem, self.lsem = ssem, rsem, lsem
        self.d, self.s, self.c = place()
        self.order = (
            flip(flip(self.s, 1), 2),
            flip(self.s, 1),
            flip(self.s, 2),
            self.s,
        )

    def piece(self, f):
        if self.kind == "cols":
            return self.grad.at[pl.ds(pl.multiple_of(96 * f, 96), 96)]
        return self.grad.at[:, pl.ds(pl.multiple_of(384 * f, 384), 384)]

    def half(self, ref, h):
        if self.kind == "cols":
            return ref.at[:, pl.ds(1536 * h, 1536)]
        return ref.at[pl.ds(384 * h, 384)]

    def quarter(self, ref, q):
        if self.kind == "cols":
            return ref.at[:, pl.ds(pl.multiple_of(768 * q, 768), 768)]
        return ref.at[pl.ds(pl.multiple_of(192 * q, 192), 192)]

    def start(self):
        d, s, c = self.d, self.s, self.c
        self.zero, self.local = [], []
        for j, position in enumerate(self.order):
            copy = push(
                self.piece(2 * position + 1 - c), self.mate.at[j], self.ssem.at[j], self.rsem.at[j], at(d, s, 1 - c)
            )
            copy.start()
            self.zero.append(copy)
            copy = pltpu.make_async_copy(self.piece(2 * position + c), self.own.at[j], self.lsem.at[j])
            copy.start()
            self.local.append(copy)

    def merge(self):
        d, s, c = self.d, self.s, self.c
        sx, sy = flip(s, 1), flip(s, 2)
        self.one = []
        for j in range(4):
            self.zero[j].wait_recv()
            self.local[j].wait()
            self.own[j] = (widened(self.own.at[j]) + widened(self.mate.at[j])).astype(jnp.bfloat16)
            if j == 0:
                for h, target in enumerate((sx, sy)):
                    copy = push(
                        self.half(self.own.at[0], h), self.near.at[h], self.ssem.at[4 + h], self.rsem.at[4 + h],
                        at(d, target, c),
                    )
                    copy.start()
                    self.one.append(copy)

    def join(self):
        d, s, c = self.d, self.s, self.c
        sx, sy = flip(s, 1), flip(s, 2)
        for h, j in ((0, 2), (1, 1)):
            self.one[h].wait_recv()
            where = self.half(self.own.at[j], h)
            where[...] = (widened(where) + widened(self.near.at[h])).astype(jnp.bfloat16)
        self.two = []
        for h, target in enumerate((sx, sy)):
            copy = push(
                self.own.at[1 + h], self.far.at[h], self.ssem.at[6 + h], self.rsem.at[6 + h], at(d, target, c)
            )
            copy.start()
            self.two.append(copy)

    def square(self):
        for copy in self.two:
            copy.wait_recv()
        return (
            widened(self.own.at[3]) + widened(self.far.at[0]) + widened(self.far.at[1])
        ).astype(jnp.bfloat16)

    def along(self):
        d, s, c = self.d, self.s, self.c
        self.own[3] = self.square()
        self.three = []
        for k in range(1, 4):
            target = lax.rem(d + k, 4)
            copy = push(
                self.quarter(self.own.at[3], target), self.line.at[k - 1], self.ssem.at[7 + k], self.rsem.at[7 + k],
                at(target, s, c),
            )
            copy.start()
            self.three.append(copy)

    def finish(self):
        total = widened(self.quarter(self.own.at[3], self.d))
        for k in range(1, 4):
            self.three[k - 1].wait_recv()
            total = total + widened(self.line.at[k - 1])
        self.out[...] = total
        self.sent(self.three)

    def close(self):
        self.out[...] = self.square()
        self.sent([])

    def sent(self, more):
        for copy in self.zero + self.one + self.two + more:
            copy.wait_send()


class LineSum:
    def __init__(self, kind, part, out, landing, ssem, rsem):
        self.kind, self.part, self.out, self.landing = kind, part, out, landing
        self.ssem, self.rsem = ssem, rsem
        self.d, self.s, self.c = place()

    def quarter(self, q):
        if self.kind == "cols":
            return self.part.at[:, pl.ds(pl.multiple_of(768 * q, 768), 768)]
        return self.part.at[pl.ds(pl.multiple_of(192 * q, 192), 192)]

    def start(self):
        self.copies = []
        for k in range(1, 4):
            target = lax.rem(self.d + k, 4)
            copy = push(
                self.quarter(target), self.landing.at[k - 1], self.ssem.at[k - 1], self.rsem.at[k - 1],
                at(target, self.s, self.c),
            )
            copy.start()
            self.copies.append(copy)

    def finish(self):
        total = widened(self.quarter(self.d))
        for k in range(3):
            self.copies[k].wait_recv()
            total = total + widened(self.landing.at[k])
        self.out[...] = total
        for copy in self.copies:
            copy.wait_send()


class Tail:
    def __init__(self, d_rows, router, act, ada, ada_out, d_act_out, router_out, z1, plane, plane_in, z2, z2_in, sems):
        self.d_rows, self.router, self.act, self.ada = d_rows, router, act, ada
        self.ada_out, self.d_act_out, self.router_out = ada_out, d_act_out, router_out
        self.z1, self.plane, self.plane_in, self.z2, self.z2_in = z1, plane, plane_in, z2, z2_in
        self.sems = sems
        self.d, self.s, self.c = place()
        self.f = 2 * self.s + self.c

    def z_copy(self, k, src, dst, base):
        send, recv = self.sems[base], self.sems[base + 1]
        return push(src, dst, send.at[k], recv.at[k], at(lax.rem(self.d + k, 4), self.s, self.c))

    def f_copy(self, k, src, dst, base):
        send, recv = self.sems[base], self.sems[base + 1]
        return push(src, dst, send.at[k], recv.at[k], (self.d, lax.rem(self.f + k, 8)))

    def start(self):
        self.all = [
            self.z_copy(k, self.d_rows.at[lax.rem(self.d + k, 4)], self.z1.at[k], 0) for k in range(1, 4)
        ]
        for copy in self.all:
            copy.start()

    def second(self):
        total = self.d_rows[self.d]
        for k in range(1, 4):
            self.all[k - 1].wait_recv()
            total = total + self.z1[k]
        for target in range(8):
            self.plane[target, :, 0:1152] = total
            self.plane[target, :, 1152:1280] = self.router[target]
        copies = [
            self.f_copy(k, self.plane.at[lax.rem(self.f + k, 8)], self.plane_in.at[lax.rem(8 - k, 8)], 2)
            for k in range(1, 8)
        ]
        for copy in copies:
            copy.start()
        self.in_plane = copies
        self.all = self.all + copies

    def third(self):
        f = self.f
        self.plane_in[0] = self.plane[f]
        for copy in self.in_plane:
            copy.wait_recv()
        everything = self.plane_in[...]
        router = jnp.sum(everything[:, :, 1152:1280], axis=0)
        rows = everything[:, :, 0:1152].reshape(64, 1152)
        line = lax.broadcasted_iota(jnp.int32, (64, 64), 0)
        column = lax.broadcasted_iota(jnp.int32, (64, 64), 1)
        turn = (lax.rem(line // 8 + 8 - f, 8) * 8 + lax.rem(line, 8) == column).astype(jnp.bfloat16)
        d_mod = nn(turn, rows.astype(jnp.bfloat16)).astype(jnp.bfloat16)
        self.ada_out[...] = tn(self.act[...], d_mod)[0:96]
        part = nt(d_mod, self.ada[...])
        self.z2[0:64, 0:96] = part
        self.z2[0:64, 96:128] = jnp.zeros((64, 32), jnp.float32)
        self.z2[64:72, :] = router
        copies = [self.z_copy(k, self.z2, self.z2_in.at[k], 4) for k in range(1, 4)]
        for copy in copies:
            copy.start()
        self.along = copies
        self.all = self.all + copies

    def fourth(self):
        total = self.z2[...]
        for k in range(1, 4):
            self.along[k - 1].wait_recv()
            total = total + self.z2_in[k]
        self.router_out[...] = total[64:72]
        self.z2_in[0] = total
        copies = [
            self.f_copy(
                k,
                self.z2_in.at[0, pl.ds(pl.multiple_of(8 * lax.rem(self.f + k, 8), 8), 8)],
                self.d_act_out.at[self.f],
                6,
            )
            for k in range(1, 8)
        ]
        for copy in copies:
            copy.start()
        self.d_act_out[self.f] = self.z2_in[0, pl.ds(pl.multiple_of(8 * self.f, 8), 8)]
        self.last = copies
        self.all = self.all + copies

    def finish(self):
        for k in range(1, 8):
            self.f_copy(
                k, self.z2_in.at[0, pl.ds(0, 8)], self.d_act_out.at[lax.rem(self.f + 8 - k, 8)], 6
            ).wait_recv()
        for copy in self.all:
            copy.wait_send()


def dense_kernel(
    grad, first_part, second_part, d_rows, router, act, ada,
    out, first_out, second_out, ada_out, d_act_out, router_out,
    own, mate, near, far, line, ssem, rsem, lsem,
    first_in, fs, fr, second_in, ss, sr, *rest,
):
    d, s, c = place()
    f = 2 * s + c
    greet(
        [at(lax.rem(d + k, 4), s, c) for k in range(1, 4)]
        + [(d, lax.rem(f + k, 8)) for k in range(1, 8)]
    )
    dense = DenseSum("cols", grad, out, own, mate, near, far, line, ssem, rsem, lsem)
    lines = (
        LineSum("cols", first_part, first_out, first_in, fs, fr),
        LineSum("rows", second_part, second_out, second_in, ss, sr),
    )
    tail = Tail(d_rows, router, act, ada, ada_out, d_act_out, router_out, *rest[:5], rest[5:])
    tail.start()
    dense.start()
    for each in lines:
        each.start()
    tail.second()
    dense.merge()
    tail.third()
    dense.join()
    tail.fourth()
    dense.along()
    for each in lines:
        each.finish()
    dense.finish()
    tail.finish()


def dense_sums(grad, first_part, second_part, small):
    bf, f32 = jnp.bfloat16, jnp.float32
    return pl.pallas_call(
        dense_kernel,
        out_shape=(
            jax.ShapeDtypeStruct((96, 768), f32),
            jax.ShapeDtypeStruct((96, 768), f32),
            jax.ShapeDtypeStruct((192, 384), f32),
            jax.ShapeDtypeStruct((96, 1152), f32),
            jax.ShapeDtypeStruct((8, 8, 128), f32),
            jax.ShapeDtypeStruct((8, 128), f32),
        ),
        in_specs=[ANYWHERE] + [ONCHIP] * 6,
        out_specs=(ONCHIP,) * 6,
        scratch_shapes=[
            pltpu.VMEM((4, 96, 3072), bf),
            pltpu.VMEM((4, 96, 3072), bf),
            pltpu.VMEM((2, 96, 1536), bf),
            pltpu.VMEM((2, 96, 3072), bf),
            pltpu.VMEM((3, 96, 768), bf),
            DMA((11,)), DMA((11,)), DMA((4,)),
            pltpu.VMEM((3, 96, 768), bf),
            DMA((3,)), DMA((3,)),
            pltpu.VMEM((3, 192, 384), bf),
            DMA((3,)), DMA((3,)),
            pltpu.VMEM((4, 8, 1152), f32),
            pltpu.VMEM((8, 8, 1280), f32),
            pltpu.VMEM((8, 8, 1280), f32),
            pltpu.VMEM((72, 128), f32),
            pltpu.VMEM((4, 72, 128), f32),
            DMA((4,)), DMA((4,)), DMA((8,)), DMA((8,)), DMA((4,)), DMA((4,)), DMA((8,)), DMA((8,)),
        ],
        compiler_params=pltpu.CompilerParams(collective_id=3, has_side_effects=True),
        cost_estimate=pl.CostEstimate(flops=40_000_000_000, bytes_accessed=20_000_000, transcendentals=0),
        name="dense_sums",
    )(grad, first_part, second_part, *small)


def layer_stats(values_in):
    centred = values_in - jnp.mean(values_in, axis=-1, keepdims=True)
    inv_std = lax.rsqrt(jnp.mean(centred * centred, axis=-1, keepdims=True) + 1e-06)
    return centred * inv_std, inv_std


def modulated(inside, mod, part):
    columns = slice(768 * part, 768 * part + 768)
    return inside[:, 0:1] * mod[0:1, columns] + inside[:, 1:2] * mod[1:2, columns]


def head_column(g):
    return 768 * (g // 9) + 64 * (g % 9)


QUERY_ROWS = 256


def front_kernel(
    tokens, mod, inside, seg_col, seg_row, qkvo, router, cotangent, routes, target,
    heads, totals, attended, projected, residual, second, d_mixed, gates, rows, grads,
    bias, made, weighted,
):
    bf, f32 = jnp.bfloat16, jnp.float32
    token_float = tokens[...].astype(f32)
    normed, _ = layer_stats(token_float)
    first = (normed * (1.0 + modulated(inside, mod, 1)) + modulated(inside, mod, 0)).astype(bf)
    for j in range(4):
        piece = nn(first, qkvo[:, 768 * j : 768 * j + 640]).astype(bf)
        for i in range(9):
            heads[9 * j + i] = piece[:, 64 * i : 64 * i + 64]
    bias[...] = jnp.where(seg_col[...] == seg_row[...], 0.0, -1e30)

    def block(n, carry):
        h, part = n // (512 // QUERY_ROWS), lax.rem(n, 512 // QUERY_ROWS)
        lines = pl.ds(pl.multiple_of(part * QUERY_ROWS, QUERY_ROWS), QUERY_ROWS)
        scores = nt(heads[h, lines], heads[12 + h]) * 0.125 + bias[lines]
        row_max = jnp.max(scores, axis=-1, keepdims=True)
        weight = jnp.exp(scores - row_max)
        running = jnp.sum(weight, axis=-1, keepdims=True)
        probability = (weight * (1.0 / running)).astype(bf)
        made[h, lines] = nn(probability, heads[24 + h]).astype(bf)
        totals[h, lines] = row_max + jnp.log(running)
        return carry

    lax.fori_loop(0, 12 * (512 // QUERY_ROWS), block, 0)
    for h in range(12):
        attended[:, 64 * h : 64 * h + 64] = made[h]
    for j in range(4):
        piece = nn(attended[...], qkvo[:, 768 * j + 512 : 768 * j + 768])
        projected[:, 192 * j : 192 * j + 192] = piece[:, 64:256]
    residual[...] = token_float + modulated(inside, mod, 2) * projected[...]
    normed, _ = layer_stats(residual[...])
    second[...] = (normed * (1.0 + modulated(inside, mod, 4)) + modulated(inside, mod, 3)).astype(bf)
    logits = nn(second[...], router[...])
    ids = lax.broadcasted_iota(jnp.int32, (512, 8), 1)
    chosen = [
        jnp.sum(jnp.where(ids == routes[:, k : k + 1], logits, 0.0), axis=-1, keepdims=True)
        for k in range(2)
    ]
    top = jnp.maximum(chosen[0], chosen[1])
    raised = [jnp.exp(each - top) for each in chosen]
    share = [each / (raised[0] + raised[1]) for each in raised]
    pair = lax.broadcasted_iota(jnp.int32, (512, 2), 1)
    gates[...] = jnp.where(pair == 0, share[0], share[1])
    mixed_grad = modulated(inside, mod, 5) * cotangent[...].astype(f32)
    d_mixed[...] = mixed_grad.astype(bf)
    for k in range(2):
        weighted[k] = (share[k] * mixed_grad).astype(bf)

    def send(b, carry):
        lines = pl.ds(pl.multiple_of(288 * b, 288), 288)
        places = lax.broadcasted_iota(jnp.int32, (288, 512), 0) + 288 * b
        first_hot = (places == target[0:1]).astype(f32)
        second_hot = (places == target[1:2]).astype(f32)
        rows[lines] = nn((first_hot + second_hot).astype(bf), second[...]).astype(bf)
        grads[lines] = (
            nn(first_hot.astype(bf), weighted[0]) + nn(second_hot.astype(bf), weighted[1])
        ).astype(bf)
        return carry

    lax.fori_loop(0, 4, send, 0)


def front(tokens, mod, inside, seg_col, seg_row, qkvo, router, cotangent, routes, target):
    bf, f32 = jnp.bfloat16, jnp.float32
    return pl.pallas_call(
        front_kernel,
        out_shape=(
            jax.ShapeDtypeStruct((36, 512, 64), bf),
            jax.ShapeDtypeStruct((12, 512, 1), f32),
            jax.ShapeDtypeStruct((512, 768), bf),
            jax.ShapeDtypeStruct((512, 768), f32),
            jax.ShapeDtypeStruct((512, 768), f32),
            jax.ShapeDtypeStruct((512, 768), bf),
            jax.ShapeDtypeStruct((512, 768), bf),
            jax.ShapeDtypeStruct((512, 2), f32),
            jax.ShapeDtypeStruct((1152, 768), bf),
            jax.ShapeDtypeStruct((1152, 768), bf),
        ),
        in_specs=[ONCHIP] * 10,
        out_specs=(ONCHIP,) * 10,
        scratch_shapes=[
            pltpu.VMEM((512, 512), f32),
            pltpu.VMEM((12, 512, 64), bf),
            pltpu.VMEM((2, 512, 768), bf),
        ],
        compiler_params=pltpu.CompilerParams(vmem_limit_bytes=60 << 20),
        cost_estimate=pl.CostEstimate(flops=40_000_000_000, bytes_accessed=20_000_000, transcendentals=0),
        name="front",
    )(tokens, mod, inside, seg_col, seg_row, qkvo, router, cotangent, routes, target)


def norm_grad(upstream, normed, inv_std):
    return (
        upstream
        - jnp.mean(upstream, axis=-1, keepdims=True)
        - normed * jnp.mean(upstream * normed, axis=-1, keepdims=True)
    ) * inv_std


def rear_kernel(
    tokens, mod, inside, seg_col, seg_row, qkvo, router, cotangent, routes, target,
    heads, totals, attended, projected, residual, second, gates,
    returned, d_returned, shared_out, d_shared,
    output, tokens_grad, qkvo_grad, d_mod, router_grad,
    bias, rows_t, d_heads, d_att, d_att_t, d_rows_t, d_rows, d_residual, d_proj,
):
    bf, f32 = jnp.bfloat16, jnp.float32
    upstream = cotangent[...].astype(f32)

    def image_sums(part, values):
        for j in range(2):
            d_mod[j : j + 1, 768 * part : 768 * part + 768] = jnp.sum(
                inside[:, j : j + 1] * values, axis=0, keepdims=True
            )

    share = [gates[:, k : k + 1] for k in range(2)]
    places = lax.broadcasted_iota(jnp.int32, (512, 1152), 1)
    hot = [(places == target[:, k : k + 1]).astype(f32).astype(bf) for k in range(2)]
    picked = [nn(each, returned[...]) for each in hot]
    mixed = shared_out[...] + (share[0] * picked[0] + share[1] * picked[1])
    gate_two = modulated(inside, mod, 5)
    output[...] = (residual[...] + gate_two * mixed).astype(bf)
    image_sums(5, upstream * mixed)
    mixed_grad = gate_two * upstream
    d_share = [jnp.sum(mixed_grad * each, axis=-1, keepdims=True) for each in picked]
    inner = share[0] * d_share[0] + share[1] * d_share[1]
    ids = lax.broadcasted_iota(jnp.int32, (512, 8), 1)
    d_logits = sum(
        jnp.where(ids == routes[:, k : k + 1], share[k] * (d_share[k] - inner), 0.0) for k in range(2)
    ).astype(bf)
    router_grad[...] = tn(d_logits, second[...])
    d_second = (
        d_shared[...] + nt(d_logits, router[...]) + (nn(hot[0], d_returned[...]) + nn(hot[1], d_returned[...]))
    )
    normed, inv_std = layer_stats(residual[...])
    image_sums(3, d_second)
    image_sums(4, d_second * normed)
    d_residual[...] = upstream + norm_grad(d_second * (1.0 + modulated(inside, mod, 4)), normed, inv_std)
    gate_one = modulated(inside, mod, 2)
    image_sums(2, d_residual[...] * projected[...])
    d_proj[...] = (gate_one * d_residual[...]).astype(bf)
    d_attended = jnp.zeros((512, 768), f32)
    for j in range(4):
        piece = jnp.concatenate(
            [jnp.zeros((512, 64), bf), d_proj[:, 192 * j : 192 * j + 192]], axis=1
        )
        d_attended += nt(piece, qkvo[:, 768 * j + 512 : 768 * j + 768])
    d_attended = d_attended.astype(bf)
    d_att_t[...] = d_attended.T
    for h in range(12):
        d_att[h] = d_attended[:, 64 * h : 64 * h + 64]
    for j in range(18):
        pair = jnp.concatenate([heads[2 * j], heads[2 * j + 1]], axis=1)
        rows_t[128 * j : 128 * j + 128] = pair.T
    bias[...] = jnp.where(seg_col[...] == seg_row[...], 0.0, -1e30)

    def head(h, carry):
        def at_head(g):
            return pl.ds(pl.multiple_of(64 * g, 64), 64)

        d_key, d_value = jnp.zeros((64, 512), f32), jnp.zeros((64, 512), f32)
        for part in range(512 // QUERY_ROWS):
            lines = slice(part * QUERY_ROWS, (part + 1) * QUERY_ROWS)
            scores = nn(heads[h, lines], rows_t[at_head(12 + h)]) * 0.125 + bias[lines]
            probability = jnp.exp(scores - totals[h, lines])
            d_prob = nn(d_att[h, lines], rows_t[at_head(24 + h)])
            inner = jnp.sum(probability * d_prob, axis=-1, keepdims=True)
            d_scores = (probability * (d_prob - inner)).astype(bf)
            d_heads[h, lines] = (nn(d_scores, heads[12 + h]) * 0.125).astype(bf)
            d_key += nn(rows_t[at_head(h), lines], d_scores)
            d_value += nn(d_att_t[at_head(h), lines], probability.astype(bf))
        d_rows_t[at_head(h)] = (d_key * 0.125).astype(bf)
        d_rows_t[at_head(12 + h)] = d_value.astype(bf)
        return carry

    lax.fori_loop(0, 12, head, 0)
    for g in range(12):
        column = head_column(g)
        d_rows[:, column : column + 64] = d_heads[g]
    for j in range(12):
        pair = d_rows_t[128 * j : 128 * j + 128].T
        for i in range(2):
            column = head_column(12 + 2 * j + i)
            d_rows[:, column : column + 64] = pair[:, 64 * i : 64 * i + 64]
    for j in range(4):
        d_rows[:, 768 * j + 576 : 768 * j + 768] = jnp.zeros((512, 192), bf)
    token_float = tokens[...].astype(f32)
    normed, inv_std = layer_stats(token_float)
    scale_one = 1.0 + modulated(inside, mod, 1)
    first_t = (normed * scale_one + modulated(inside, mod, 0)).astype(bf).T
    attended_t = attended[...].T
    for j in range(4):
        qkvo_grad[:, 768 * j : 768 * j + 640] = nn(first_t, d_rows[:, 768 * j : 768 * j + 640]).astype(bf)
        qkvo_grad[:, 768 * j + 576 : 768 * j + 768] = nn(
            attended_t, d_proj[:, 192 * j : 192 * j + 192]
        ).astype(bf)
    d_first = nt(d_rows[...], qkvo[...])
    image_sums(0, d_first)
    image_sums(1, d_first * normed)
    tokens_grad[...] = d_residual[...] + norm_grad(d_first * scale_one, normed, inv_std)


def rear(*operands):
    bf, f32 = jnp.bfloat16, jnp.float32
    return pl.pallas_call(
        rear_kernel,
        out_shape=(
            jax.ShapeDtypeStruct((512, 768), bf),
            jax.ShapeDtypeStruct((512, 768), f32),
            jax.ShapeDtypeStruct((768, 3072), bf),
            jax.ShapeDtypeStruct((2, 4608), f32),
            jax.ShapeDtypeStruct((8, 768), f32),
        ),
        in_specs=[ONCHIP] * len(operands),
        out_specs=(ONCHIP,) * 5,
        scratch_shapes=[
            pltpu.VMEM((512, 512), f32),
            pltpu.VMEM((2304, 512), bf),
            pltpu.VMEM((12, 512, 64), bf),
            pltpu.VMEM((12, 512, 64), bf),
            pltpu.VMEM((768, 512), bf),
            pltpu.VMEM((1536, 512), bf),
            pltpu.VMEM((512, 3072), bf),
            pltpu.VMEM((512, 768), f32),
            pltpu.VMEM((512, 768), bf),
        ],
        compiler_params=pltpu.CompilerParams(vmem_limit_bytes=67043328),
        cost_estimate=pl.CostEstimate(flops=60_000_000_000, bytes_accessed=30_000_000, transcendentals=0),
        name="rear",
    )(*operands)


def fitted_shards(
    tokens,
    condition,
    ada_weight,
    qkv_weight,
    out_weight,
    shared_up,
    shared_down,
    router_weight,
    expert_up,
    expert_down,
    routes,
    image_sizes,
    cotangent,
):
    bf = jnp.bfloat16
    d_index, f_index = lax.axis_index("dp"), lax.axis_index("fsdp")
    model_width = tokens.shape[1]
    head_size = model_width // HEADS
    inside, segment = owners(image_sizes)
    ids = jnp.arange(EXPERTS, dtype=jnp.int32)
    hot = routes[:, :, None] == ids[None, None, :]
    hot_any = jnp.any(hot, axis=1).astype(bf)
    order = jnp.arange(LONG, dtype=jnp.int32)
    earlier = (order[:, None] > order[None, :]).astype(bf)
    before = nn(earlier, hot_any)
    position = jnp.sum(jnp.where(hot, before[:, None, :], 0.0), axis=-1).astype(jnp.int32)
    target = routes * CAP + position
    live = (segment < IMG_DEV).astype(jnp.float32)
    counts = jnp.sum(live[:, None] * hot_any.astype(jnp.float32), axis=0)
    cond_float = condition.astype(jnp.float32)
    activated = jax.nn.silu(cond_float).astype(bf)
    act_slices = activated.astype(jnp.float32).reshape(IMG_DEV, 8, 96).transpose(1, 0, 2)
    act_slices = jnp.pad(act_slices, ((0, 0), (0, 6), (0, 32)))
    act_slices = act_slices.at[:, 2, :EXPERTS].set(counts)
    ada_pad = jnp.pad(ada_weight, ((0, 32), (0, 0)))
    router_pack = jnp.pad(router_weight.reshape(192), (0, 2048 - 192)).reshape(16, 128)
    qkvo_shard = jnp.concatenate([qkv_weight, out_weight], axis=1)
    qkvo, routers, seen, mod_rows, up_line, down_line, up_six, down_two = opening(
        qkvo_shard, router_pack, act_slices, ada_pad, shared_up, shared_down.T, expert_up, expert_down
    )
    down_near = hop(down_two, 2), hop(down_two, 4)
    expert_counts = seen[66, :EXPERTS].astype(jnp.int32)
    modulation = lax.dynamic_slice(mod_rows, (0, 2 * d_index, 0), (4, 2, 1152))
    modulation = modulation.transpose(1, 0, 2).reshape(2, 4608)
    router_full = (
        routers.reshape(32, 2048)[:, :192]
        .reshape(4, 8, 96, 2)
        .transpose(1, 2, 0, 3)
        .reshape(model_width, EXPERTS)
    )
    segments = (segment[:, None], segment[None, :])
    heads, totals, attended, projected, residual, second_input, d_mixed, gates, rows, grads = front(
        tokens, modulation, inside, *segments, qkvo, router_full, cotangent, routes, target.T
    )
    rows = rows.reshape(EXPERTS, CAP, model_width)
    grads = grads.reshape(EXPERTS, CAP, model_width)
    rows, down_near = lax.optimization_barrier((rows, down_near))
    rows_in, grads_in, up_corner, down_corner, shared_out, d_second, *shared_grads = outbound(
        rows, grads, up_line, down_line, second_input, d_mixed, up_six, *down_near
    )
    returned, d_returned, up_keep, *up_near, down_keep, down_x, down_y, first_part, second_part = experts(
        rows_in, grads_in, (up_six, up_corner), (down_two, *down_near, down_corner),
        *shared_grads,
    )
    up_next = square_next(up_keep, *up_near)
    down_near = hop(down_x, 2), hop(down_y, 4)
    returned = returned.reshape(EXPERTS * CAP, model_width)
    d_returned = d_returned.reshape(EXPERTS * CAP, model_width)
    output, tokens_grad, qkvo_grad, d_modulation, router_grad = rear(
        tokens, modulation, inside, *segments, qkvo, router_full, cotangent, routes, target,
        heads, totals, attended, projected, residual, second_input, gates,
        returned, d_returned, shared_out, d_second,
    )
    qkvo_grad, down_near, up_next = lax.optimization_barrier((qkvo_grad, down_near, up_next))
    down_next = square_next(down_keep, *down_near)
    d_modulation = d_modulation.astype(bf)
    d_mod_rows = d_modulation.astype(jnp.float32).reshape(2, 4, 1152).transpose(1, 0, 2)
    d_mod_rows = lax.dynamic_update_slice(
        jnp.zeros((4, 8, 1152), jnp.float32), d_mod_rows, (0, 2 * d_index, 0)
    )
    router_tiles = jnp.pad(
        router_grad.reshape(EXPERTS, 8, 96).transpose(1, 0, 2), ((0, 0), (0, 0), (0, 32))
    )
    qkvo_sum, shared_first_sum, shared_second_sum, ada_grad, d_act_tiles, router_sum = dense_sums(
        qkvo_grad, first_part, second_part,
        (d_mod_rows, router_tiles, seen[:64].astype(bf), ada_weight),
    )
    qkvo_sum, down_next = lax.optimization_barrier((qkvo_sum, down_next))
    expert_up_grad = square_last(up_keep, *up_near, *up_next)
    expert_down_grad = square_last(down_keep, *down_near, *down_next)
    d_activated = lax.dynamic_slice(d_act_tiles, (0, 2 * d_index, 0), (8, 2, 96))
    d_activated = d_activated.transpose(1, 0, 2).reshape(2, model_width)
    condition_grad = jax.vjp(jax.nn.silu, cond_float)[1](d_activated)[0]
    router_out = lax.dynamic_slice(router_sum, (2 * d_index, 0), (2, 96)).T
    return (
        output,
        tokens_grad,
        condition_grad,
        ada_grad,
        qkvo_sum[:, :576],
        qkvo_sum[:, 576:],
        shared_first_sum,
        shared_second_sum.T,
        router_out,
        expert_up_grad,
        expert_down_grad,
        expert_counts,
    )


def solution(mesh):
    placed = (
        P(("dp", "fsdp"), None),
        P(("dp", "fsdp"), None),
        P("fsdp", "dp"),
        P("fsdp", "dp"),
        P("fsdp", "dp"),
        P("fsdp", "dp"),
        P("fsdp", "dp"),
        P("fsdp", "dp"),
        P("dp", "fsdp", None),
        P("dp", "fsdp", None),
        P(("dp", "fsdp"), None),
        P(("dp", "fsdp")),
        P(("dp", "fsdp"), None),
    )
    fitted = mesh.shape["dp"] == 4 and mesh.shape["fsdp"] == 8
    return jax.shard_map(
        fitted_shards if fitted else shards,
        mesh=mesh,
        in_specs=placed,
        out_specs=(
            P(("dp", "fsdp"), None),
            P(("dp", "fsdp"), None),
            P(("dp", "fsdp"), None),
            P("fsdp", "dp"),
            P("fsdp", "dp"),
            P("fsdp", "dp"),
            P("fsdp", "dp"),
            P("fsdp", "dp"),
            P("fsdp", "dp"),
            P("dp", "fsdp", None),
            P("dp", "fsdp", None),
            P(),
        ),
        check_vma=False,
    )
```

```python
import functools

import jax
import jax.numpy as jnp
from jax import lax
from jax.experimental import pallas as pl
from jax.experimental.pallas import tpu as pltpu
from jax.sharding import PartitionSpec as P

HEADS = 12
EXPERTS = 8
CAP = 144
IMG_DEV = 2
LONG = 512
MESH = pl.DeviceIdType.MESH


EXACT = lax.Precision.HIGHEST


def owners(image_sizes):
    starts = jnp.cumsum(image_sizes) - image_sizes
    position = jnp.arange(LONG, dtype=jnp.int32)[:, None]
    inside = (position >= starts[None, :]) & (position < (starts + image_sizes)[None, :])
    slot_ids = jnp.arange(IMG_DEV, dtype=jnp.int32)
    segment = jnp.sum(jnp.where(inside, slot_ids[None, :], 0), axis=1) + jnp.where(
        jnp.any(inside, axis=1), 0, IMG_DEV
    )
    return (inside.astype(jnp.float32), segment)


def dispatch_plan(routes):
    flat = routes.reshape(-1)
    onehot = (flat[:, None] == jnp.arange(EXPERTS, dtype=jnp.int32)[None, :]).astype(jnp.int32)
    before = jnp.cumsum(onehot, axis=0) - onehot
    position = jnp.sum(before * onehot, axis=1)
    target = flat * CAP + position
    assignment = jnp.arange(2 * LONG, dtype=jnp.int32)
    source = jnp.zeros((EXPERTS * CAP,), jnp.int32).at[target].set(assignment)
    filled = jnp.zeros((EXPERTS * CAP,), jnp.int32).at[target].set(1)
    return (target, source, filled)


def layer_norm(values_in):
    centred = values_in - jnp.mean(values_in, axis=-1, keepdims=True)
    inv_std = lax.rsqrt(jnp.mean(centred * centred, axis=-1, keepdims=True) + 1e-06)
    return (centred * inv_std, inv_std)


def norm_back(upstream, normed, inv_std):
    return (
        upstream
        - jnp.mean(upstream, axis=-1, keepdims=True)
        - normed * jnp.mean(upstream * normed, axis=-1, keepdims=True)
    ) * inv_std


def gelu_tanh(values_in):
    return jax.nn.gelu(values_in, approximate=True)


def gelu_back(values_in, upstream):
    return jax.vjp(gelu_tanh, values_in)[1](upstream)[0]


def collect(first, second, third):
    widened = (
        lax.all_gather(first, "dp", axis=1, tiled=True),
        lax.all_gather(second, "dp", axis=1, tiled=True),
        lax.all_gather(third, "dp", axis=1, tiled=True),
    )
    return (
        lax.all_gather(widened[0], "fsdp", axis=0, tiled=True),
        lax.all_gather(widened[1], "fsdp", axis=0, tiled=True),
        lax.all_gather(widened[2], "fsdp", axis=0, tiled=True),
    )


def spread(first, second, third):
    row_sums = (
        lax.psum_scatter(first, "fsdp", scatter_dimension=0, tiled=True),
        lax.psum_scatter(second, "fsdp", scatter_dimension=0, tiled=True),
        lax.psum_scatter(third, "fsdp", scatter_dimension=0, tiled=True),
    )
    return (
        lax.psum_scatter(row_sums[0], "dp", scatter_dimension=1, tiled=True),
        lax.psum_scatter(row_sums[1], "dp", scatter_dimension=1, tiled=True),
        lax.psum_scatter(row_sums[2], "dp", scatter_dimension=1, tiled=True),
    )


def gather_experts(up_shard, down_shard):
    return (
        lax.all_gather(up_shard, "fsdp", axis=1, tiled=True),
        lax.all_gather(down_shard, "fsdp", axis=1, tiled=True),
    )


def expert_forward(buffer_in, up_full, down_full):
    expert_pre = jnp.einsum(
        "secd,edf->secf", buffer_in, up_full, preferred_element_type=jnp.float32
    )
    expert_act = gelu_tanh(expert_pre).astype(jnp.bfloat16)
    expert_out = jnp.einsum(
        "secf,efd->secd", expert_act, down_full, preferred_element_type=jnp.float32
    ).astype(jnp.bfloat16)
    return (expert_pre, expert_act, expert_out)


def expert_backward(buffer_in, expert_pre, expert_act, d_out, up_full, down_full):
    d_act = jnp.einsum("secd,efd->secf", d_out, down_full, preferred_element_type=jnp.float32)
    d_pre = gelu_back(expert_pre, d_act).astype(jnp.bfloat16)
    d_rows = jnp.einsum(
        "secf,edf->secd", d_pre, up_full, preferred_element_type=jnp.float32
    ).astype(jnp.bfloat16)
    down_grad = jnp.einsum("secf,secd->efd", expert_act, d_out, preferred_element_type=jnp.float32)
    up_grad = jnp.einsum("secd,secf->edf", buffer_in, d_pre, preferred_element_type=jnp.float32)
    return (up_grad, down_grad, d_rows)


def attend(queries, keys_all, values_all, segment):
    row_count, head_count, head_size = queries.shape
    block_rows = min(512, row_count)
    block_count = row_count // block_rows
    score_scale = head_size ** (-0.5)

    def one_block(pieces):
        query_part, segment_part = pieces
        allowed = (segment_part[:, None] == segment[None, :])[None]
        scores = (
            jnp.einsum("qhd,khd->hqk", query_part, keys_all, preferred_element_type=jnp.float32)
            * score_scale
        )
        scores = jnp.where(allowed, scores, -1e30)
        row_max = jnp.max(scores, axis=-1, keepdims=True)
        weight = jnp.exp(scores - row_max)
        running = jnp.sum(weight, axis=-1, keepdims=True)
        probability = (weight / running).astype(jnp.bfloat16)
        attended = jnp.einsum(
            "hqk,khd->qhd", probability, values_all, preferred_element_type=jnp.float32
        )
        return (attended.astype(jnp.bfloat16), (row_max + jnp.log(running))[:, :, 0])

    return lax.map(
        one_block,
        (
            queries.reshape(block_count, block_rows, head_count, head_size),
            segment.reshape(block_count, block_rows),
        ),
    )


def attend_back(queries, keys_all, values_all, segment, log_totals, d_attended):
    row_count, head_count, head_size = queries.shape
    block_rows = min(512, row_count)
    block_count = row_count // block_rows
    score_scale = head_size ** (-0.5)

    def one_block(carry, pieces):
        key_sum, value_sum = carry
        query_part, segment_part, total_part, grad_part = pieces
        allowed = (segment_part[:, None] == segment[None, :])[None]
        scores = (
            jnp.einsum("qhd,khd->hqk", query_part, keys_all, preferred_element_type=jnp.float32)
            * score_scale
        )
        scores = jnp.where(allowed, scores, -1e30)
        probability = jnp.exp(scores - total_part[:, :, None])
        d_prob = jnp.einsum(
            "qhd,khd->hqk", grad_part, values_all, preferred_element_type=jnp.float32
        )
        d_scores = (
            probability * (d_prob - jnp.sum(probability * d_prob, axis=-1, keepdims=True))
        ).astype(jnp.bfloat16)
        query_grad = (
            jnp.einsum("hqk,khd->qhd", d_scores, keys_all, preferred_element_type=jnp.float32)
            * score_scale
        )
        key_sum = (
            key_sum
            + jnp.einsum("hqk,qhd->khd", d_scores, query_part, preferred_element_type=jnp.float32)
            * score_scale
        )
        value_sum = value_sum + jnp.einsum(
            "hqk,qhd->khd",
            probability.astype(jnp.bfloat16),
            grad_part,
            preferred_element_type=jnp.float32,
        )
        return ((key_sum, value_sum), query_grad)

    empty = jnp.zeros(keys_all.shape, jnp.float32)
    sums, query_grads = lax.scan(
        one_block,
        (empty, empty),
        (
            queries.reshape(block_count, block_rows, head_count, head_size),
            segment.reshape(block_count, block_rows),
            log_totals,
            d_attended.reshape(block_count, block_rows, head_count, head_size),
        ),
    )
    return (query_grads.reshape(row_count, head_count, head_size), sums[0], sums[1])


def shards(
    tokens,
    condition,
    ada_weight,
    qkv_weight,
    out_weight,
    shared_up,
    shared_down,
    router_weight,
    expert_up,
    expert_down,
    routes,
    image_sizes,
    cotangent,
):
    model_width = tokens.shape[1]
    head_size = model_width // HEADS
    inside, segment = owners(image_sizes)
    target, source, filled = dispatch_plan(routes)
    route_hot = (routes[:, :, None] == jnp.arange(EXPERTS, dtype=jnp.int32)[None, None, :]).astype(
        jnp.float32
    )
    live = (segment < IMG_DEV).astype(jnp.int32)
    local_counts = jnp.sum(live[:, None, None] * route_hot.astype(jnp.int32), axis=(0, 1))
    expert_counts = lax.psum(local_counts, ("dp", "fsdp"))
    ada_full, qkv_full, out_full = collect(ada_weight, qkv_weight, out_weight)
    cond_float = condition.astype(jnp.float32)
    activated = jax.nn.silu(cond_float).astype(jnp.bfloat16)
    modulation = jnp.dot(activated, ada_full, preferred_element_type=jnp.float32)
    per_row = jnp.dot(inside, modulation, precision=EXACT, preferred_element_type=jnp.float32)
    shift_one, scale_one, gate_one, shift_two, scale_two, gate_two = jnp.split(per_row, 6, axis=1)
    token_float = tokens.astype(jnp.float32)
    normed_one, inv_one = layer_norm(token_float)
    first_input = (normed_one * (1.0 + scale_one) + shift_one).astype(jnp.bfloat16)
    qkv_rows = jnp.dot(first_input, qkv_full, preferred_element_type=jnp.float32).astype(
        jnp.bfloat16
    )
    queries = qkv_rows[:, :model_width].reshape(-1, HEADS, head_size)
    keys_all = qkv_rows[:, model_width : 2 * model_width].reshape(-1, HEADS, head_size)
    values_all = qkv_rows[:, 2 * model_width :].reshape(-1, HEADS, head_size)
    attended_blocks, log_totals = attend(queries, keys_all, values_all, segment)
    attended = attended_blocks.reshape(-1, model_width)
    projected = jnp.dot(attended, out_full, preferred_element_type=jnp.float32)
    residual_one = token_float + gate_one * projected
    normed_two, inv_two = layer_norm(residual_one)
    second_input = (normed_two * (1.0 + scale_two) + shift_two).astype(jnp.bfloat16)
    shared_first, shared_second, router_full = collect(shared_up, shared_down, router_weight)
    shared_pre = jnp.dot(second_input, shared_first, preferred_element_type=jnp.float32)
    shared_act = gelu_tanh(shared_pre).astype(jnp.bfloat16)
    shared_out = jnp.dot(shared_act, shared_second, preferred_element_type=jnp.float32)
    logits = jnp.dot(second_input, router_full, preferred_element_type=jnp.float32)
    chosen = jnp.sum(logits[:, None, :] * route_hot, axis=-1)
    gate_share = jax.nn.softmax(chosen, axis=-1)
    buffer_rows = jnp.take(second_input, source // 2, axis=0).reshape(EXPERTS, CAP, model_width)
    up_full, down_full = gather_experts(expert_up, expert_down)
    groups = lax.axis_size("dp")
    expert_in = lax.all_to_all(
        buffer_rows.reshape(groups, EXPERTS // groups, CAP, model_width),
        "dp",
        split_axis=0,
        concat_axis=0,
        tiled=True,
    )
    expert_pre, expert_act, expert_out = expert_forward(expert_in, up_full, down_full)
    returned = lax.all_to_all(expert_out, "dp", split_axis=0, concat_axis=0, tiled=True).reshape(
        EXPERTS, CAP, model_width
    )
    picked = (
        jnp.take(returned.reshape(EXPERTS * CAP, model_width), target, axis=0)
        .reshape(-1, 2, model_width)
        .astype(jnp.float32)
    )
    mixed = shared_out + jnp.sum(gate_share[:, :, None] * picked, axis=1)
    output = (residual_one + gate_two * mixed).astype(jnp.bfloat16)
    upstream = cotangent.astype(jnp.float32)
    d_mixed = gate_two * upstream
    d_gate_two = upstream * mixed
    d_gate_share = jnp.sum(d_mixed[:, None, :] * picked, axis=-1)
    slot_gate = jnp.take(gate_share.reshape(-1), source) * filled.astype(jnp.float32)
    d_buffer = (
        (jnp.take(d_mixed, source // 2, axis=0) * slot_gate[:, None])
        .astype(jnp.bfloat16)
        .reshape(EXPERTS, CAP, model_width)
    )
    shared_first, shared_second, router_full = collect(shared_up, shared_down, router_weight)
    up_full, down_full = gather_experts(expert_up, expert_down)
    arrived = lax.all_to_all(
        d_buffer.reshape(groups, EXPERTS // groups, CAP, model_width),
        "dp",
        split_axis=0,
        concat_axis=0,
        tiled=True,
    )
    up_grad, down_grad, d_rows = expert_backward(
        expert_in, expert_pre, expert_act, arrived, up_full, down_full
    )
    d_returned = lax.all_to_all(d_rows, "dp", split_axis=0, concat_axis=0, tiled=True).reshape(
        EXPERTS, CAP, model_width
    )
    expert_sums = (
        lax.psum_scatter(up_grad, "fsdp", scatter_dimension=1, tiled=True),
        lax.psum_scatter(down_grad, "fsdp", scatter_dimension=1, tiled=True),
    )
    d_shared = d_mixed.astype(jnp.bfloat16)
    shared_second_grad = jnp.einsum(
        "tf,td->fd", shared_act, d_shared, preferred_element_type=jnp.float32
    )
    d_shared_act = jnp.einsum(
        "td,fd->tf", d_shared, shared_second, preferred_element_type=jnp.float32
    )
    d_shared_pre = gelu_back(shared_pre, d_shared_act).astype(jnp.bfloat16)
    shared_first_grad = jnp.einsum(
        "td,tf->df", second_input, d_shared_pre, preferred_element_type=jnp.float32
    )
    d_chosen = gate_share * (
        d_gate_share - jnp.sum(gate_share * d_gate_share, axis=-1, keepdims=True)
    )
    d_logits = jnp.sum(d_chosen[:, :, None] * route_hot, axis=1).astype(jnp.bfloat16)
    router_grad = jnp.einsum(
        "td,te->de", second_input, d_logits, preferred_element_type=jnp.float32
    )
    from_experts = (
        jnp.take(d_returned.reshape(EXPERTS * CAP, model_width), target, axis=0)
        .reshape(-1, 2, model_width)
        .astype(jnp.float32)
    )
    d_second = (
        jnp.einsum("tf,df->td", d_shared_pre, shared_first, preferred_element_type=jnp.float32)
        + jnp.einsum("te,de->td", d_logits, router_full, preferred_element_type=jnp.float32)
        + jnp.sum(from_experts, axis=1)
    )
    mlp_sums = spread(shared_first_grad, shared_second_grad, router_grad)
    d_scale_two = d_second * normed_two
    d_residual = upstream + norm_back(d_second * (1.0 + scale_two), normed_two, inv_two)
    ada_full, qkv_full, out_full = collect(ada_weight, qkv_weight, out_weight)
    d_projected = (gate_one * d_residual).astype(jnp.bfloat16)
    d_gate_one = d_residual * projected
    out_grad = jnp.einsum("td,te->de", attended, d_projected, preferred_element_type=jnp.float32)
    d_attended = jnp.einsum(
        "te,de->td", d_projected, out_full, preferred_element_type=jnp.float32
    ).astype(jnp.bfloat16)
    d_queries, d_keys, d_values = attend_back(
        queries, keys_all, values_all, segment, log_totals, d_attended.reshape(-1, HEADS, head_size)
    )
    d_qkv = jnp.concatenate(
        [
            d_queries.reshape(-1, model_width),
            d_keys.reshape(-1, model_width),
            d_values.reshape(-1, model_width),
        ],
        axis=1,
    ).astype(jnp.bfloat16)
    qkv_grad = jnp.einsum("td,te->de", first_input, d_qkv, preferred_element_type=jnp.float32)
    d_first = jnp.einsum("te,de->td", d_qkv, qkv_full, preferred_element_type=jnp.float32)
    d_scale_one = d_first * normed_one
    tokens_grad = d_residual + norm_back(d_first * (1.0 + scale_one), normed_one, inv_one)
    d_per_row = jnp.concatenate(
        [d_first, d_scale_one, d_gate_one, d_second, d_scale_two, d_gate_two], axis=1
    )
    d_modulation = jnp.einsum(
        "tj,te->je", inside, d_per_row, precision=EXACT, preferred_element_type=jnp.float32
    ).astype(jnp.bfloat16)
    ada_grad = jnp.einsum("jd,je->de", activated, d_modulation, preferred_element_type=jnp.float32)
    d_activated = jnp.einsum(
        "je,de->jd", d_modulation, ada_full, preferred_element_type=jnp.float32
    )
    condition_grad = jax.vjp(jax.nn.silu, cond_float)[1](d_activated)[0]
    attn_sums = spread(ada_grad, qkv_grad, out_grad)
    return (
        output,
        tokens_grad,
        condition_grad,
        attn_sums[0],
        attn_sums[1],
        attn_sums[2],
        mlp_sums[0],
        mlp_sums[1],
        mlp_sums[2],
        expert_sums[0],
        expert_sums[1],
        expert_counts,
    )


def at(d, s, c):
    return (d, 2 * s + c)


def slot(kind, f, d):
    if kind == "cols":
        return (pl.ds(pl.multiple_of(96 * f, 96), 96), pl.ds(pl.multiple_of(768 * d, 768), 768))
    return (pl.ds(pl.multiple_of(192 * d, 192), 192), pl.ds(pl.multiple_of(384 * f, 384), 384))


def half_slot(kind, f, d, h):
    if kind == "cols":
        return (
            pl.ds(pl.multiple_of(96 * f, 96), 96),
            pl.ds(pl.multiple_of(768 * d + 384 * h, 384), 384),
        )
    return (
        pl.ds(pl.multiple_of(192 * d + 96 * h, 96), 96),
        pl.ds(pl.multiple_of(384 * f, 384), 384),
    )


def place():
    d = lax.axis_index("dp")
    f = lax.axis_index("fsdp")
    return d, f // 2, lax.rem(f, 2)


def flip(v, bit):
    return v + bit - 2 * bit * lax.rem(v // bit, 2)


def greet(devices):
    barrier = pltpu.get_barrier_semaphore()
    for device in devices:
        pl.semaphore_signal(barrier, inc=1, device_id=device, device_id_type=MESH)
    pl.semaphore_wait(barrier, len(devices))


def push(src, dst, send_sem, recv_sem, device):
    return pltpu.make_async_remote_copy(
        src_ref=src,
        dst_ref=dst,
        send_sem=send_sem,
        recv_sem=recv_sem,
        device_id=device,
        device_id_type=MESH,
    )


GATHER_SEMS = 3 + 8 + 8 + 20


class Gather:
    def __init__(self, kind, shard, full, ssem, rsem, lsem):
        self.kind, self.shard, self.full = kind, shard, full
        self.ssem, self.rsem, self.lsem = ssem, rsem, lsem
        self.d, self.s, self.c = place()
        self.sent = []

    def f(self, s):
        return 2 * s + self.c

    def go(self, index, where, device, src=None):
        ref = self.full.at[where]
        copy = push(
            ref if src is None else src, ref, self.ssem.at[index], self.rsem.at[index], device
        )
        copy.start()
        self.sent.append(copy)

    def arrived(self, index, where):
        ref = self.full.at[where]
        push(ref, ref, self.ssem.at[index], self.rsem.at[index], at(self.d, self.s, self.c)).wait_recv()

    def start(self):
        d, s, c = self.d, self.s, self.c
        mine = slot(self.kind, self.f(s), d)
        self.own = pltpu.make_async_copy(self.shard, self.full.at[mine], self.lsem)
        self.own.start()
        self.go(1, mine, at(flip(d, 2), s, c), self.shard)
        self.go(0, mine, at(flip(d, 1), s, c), self.shard)
        self.go(3, mine, at(d, flip(s, 1), c), self.shard)
        self.go(4, mine, at(d, flip(s, 2), c), self.shard)
        self.go(19, mine, at(d, s, 1 - c), self.shard)

    def source(self, k):
        return (self.d, flip(self.d, 1), flip(self.d, 2), flip(flip(self.d, 1), 2))[k]

    def spread_z(self, k):
        d, s, c = self.d, self.s, self.c
        block = slot(self.kind, self.f(s), self.source(k))
        self.arrived(k - 1, block)
        if k == 2:
            self.go(2, block, at(flip(d, 1), s, c))
        self.go(3 + 2 * k, block, at(d, flip(s, 1), c))
        self.go(4 + 2 * k, block, at(d, flip(s, 2), c))
        self.go(19 + 5 * k, block, at(d, s, 1 - c))

    def relay(self, k):
        d, s, c = self.d, self.s, self.c
        source = self.source(k)
        sx, sy = flip(s, 1), flip(s, 2)
        from_x = slot(self.kind, self.f(sx), source)
        from_y = slot(self.kind, self.f(sy), source)
        self.arrived(3 + 2 * k, from_x)
        self.go(11 + 2 * k, half_slot(self.kind, self.f(sx), source, 0), at(d, sy, c))
        self.go(20 + 5 * k, from_x, at(d, s, 1 - c))
        self.arrived(4 + 2 * k, from_y)
        self.go(12 + 2 * k, half_slot(self.kind, self.f(sy), source, 1), at(d, sx, c))
        self.go(21 + 5 * k, from_y, at(d, s, 1 - c))

    def corner(self, k):
        d, s, c = self.d, self.s, self.c
        source = self.source(k)
        sd = flip(flip(s, 1), 2)
        for h in range(2):
            where = half_slot(self.kind, self.f(sd), source, h)
            self.arrived(11 + 2 * k + h, where)
            self.go(22 + 5 * k + h, where, at(d, s, 1 - c))

    def finish(self):
        d, s, c = self.d, self.s, self.c
        sx, sy = flip(s, 1), flip(s, 2)
        sd = flip(sx, 2)
        self.own.wait()
        for k in range(4):
            source = self.source(k)
            for j, position in enumerate((s, sx, sy)):
                self.arrived(19 + 5 * k + j, slot(self.kind, 2 * position + 1 - c, source))
            for h in range(2):
                self.arrived(22 + 5 * k + h, half_slot(self.kind, 2 * sd + 1 - c, source, h))
        for copy in self.sent:
            copy.wait_send()


class Line:
    def __init__(self, kind, shard, line, ssem, rsem, lsem):
        self.kind, self.shard, self.line = kind, shard, line
        self.ssem, self.rsem, self.lsem = ssem, rsem, lsem
        self.d, self.s, self.c = place()

    def block(self, d):
        if self.kind == "cols":
            return self.line.at[:, pl.ds(pl.multiple_of(768 * d, 768), 768)]
        return self.line.at[pl.ds(pl.multiple_of(192 * d, 192), 192)]

    def copy(self, index, src, source, target):
        return push(
            src, self.block(source), self.ssem.at[index], self.rsem.at[index], at(target, self.s, self.c)
        )

    def start(self):
        d = self.d
        self.own = pltpu.make_async_copy(self.shard, self.block(d), self.lsem)
        self.own.start()
        self.sent = [
            self.copy(0, self.shard, d, flip(d, 2)),
            self.copy(1, self.shard, d, flip(d, 1)),
        ]
        for copy in self.sent:
            copy.start()

    def relay(self):
        d2 = flip(self.d, 2)
        self.copy(0, self.shard, d2, d2).wait_recv()
        copy = self.copy(2, self.block(d2), d2, flip(self.d, 1))
        copy.start()
        self.sent.append(copy)

    def finish(self):
        d1 = flip(self.d, 1)
        self.own.wait()
        self.copy(1, self.shard, d1, d1).wait_recv()
        self.copy(2, self.shard, flip(d1, 2), d1).wait_recv()
        for copy in self.sent:
            copy.wait_send()


class Spread:
    def __init__(self, kind, line, full, ssem, rsem, lsem):
        self.kind, self.line, self.full = kind, line, full
        self.ssem, self.rsem, self.lsem = ssem, rsem, lsem
        self.d, self.s, self.c = place()
        self.sx, self.sy = flip(self.s, 1), flip(self.s, 2)
        self.sd = flip(self.sx, 2)
        self.mate = at(self.d, self.s, 1 - self.c)
        self.to_x, self.to_y = at(self.d, self.sx, self.c), at(self.d, self.sy, self.c)
        self.sent = []

    def block(self, position, c, h=None):
        f = 2 * position + c
        if self.kind == "cols":
            rows = pl.ds(pl.multiple_of(96 * f, 96), 96)
            return self.full.at[rows] if h is None else self.full.at[rows, pl.ds(1536 * h, 1536)]
        columns = pl.ds(pl.multiple_of(384 * f, 384), 384)
        rows = pl.ds(0, 768) if h is None else pl.ds(384 * h, 384)
        return self.full.at[rows, columns]

    def go(self, index, ref, device, src=None):
        copy = push(
            ref if src is None else src, ref, self.ssem.at[index], self.rsem.at[index], device
        )
        copy.start()
        self.sent.append(copy)

    def arrived(self, index, ref):
        push(ref, ref, self.ssem.at[index], self.rsem.at[index], self.mate).wait_recv()

    def start(self):
        mine = self.block(self.s, self.c)
        self.own = pltpu.make_async_copy(self.line, mine, self.lsem)
        self.own.start()
        self.go(0, mine, self.to_x, self.line)
        self.go(1, mine, self.to_y, self.line)
        self.go(2, mine, self.mate, self.line)

    def relay(self):
        c = self.c
        from_x, from_y = self.block(self.sx, c), self.block(self.sy, c)
        self.arrived(0, from_x)
        self.go(3, self.block(self.sx, c, 0), self.to_y)
        self.go(5, from_x, self.mate)
        self.arrived(1, from_y)
        self.go(4, self.block(self.sy, c, 1), self.to_x)
        self.go(6, from_y, self.mate)

    def corner(self):
        for h in range(2):
            ref = self.block(self.sd, self.c, h)
            self.arrived(3 + h, ref)
            self.go(7 + h, ref, self.mate)

    def finish(self):
        c = 1 - self.c
        self.own.wait()
        self.arrived(2, self.block(self.s, c))
        self.arrived(5, self.block(self.sx, c))
        self.arrived(6, self.block(self.sy, c))
        for h in range(2):
            self.arrived(7 + h, self.block(self.sd, c, h))
        for copy in self.sent:
            copy.wait_send()


class Near:
    def __init__(self, up_shard, down_shard, up_mate, up_x, up_y, down_own, down_mate, ssem, rsem, lsem):
        d, s, c = place()
        self.local = pltpu.make_async_copy(down_shard.at[c], down_own, lsem)
        plan = (
            (up_shard, c, up_x, flip(s, 1)),
            (up_shard, c, up_y, flip(s, 2)),
            (up_shard, 1 - c, up_mate, s),
            (down_shard, 1 - c, down_mate, s),
        )
        self.away = [
            push(shard.at[which], out, ssem.at[i], rsem.at[i], at(d, position, which))
            for i, (shard, which, out, position) in enumerate(plan)
        ]

    def start(self):
        for copy in self.away + [self.local]:
            copy.start()

    def finish(self):
        for copy in self.away + [self.local]:
            copy.wait()


class Pair:
    def __init__(self, over_x, into_x, over_y, into_y, ssem, rsem):
        d, s, c = place()
        self.copies = [
            push(over_x, into_x, ssem.at[0], rsem.at[0], at(d, flip(s, 1), c)),
            push(over_y, into_y, ssem.at[1], rsem.at[1], at(d, flip(s, 2), c)),
        ]

    def start(self):
        for copy in self.copies:
            copy.start()

    def finish(self):
        for copy in self.copies:
            copy.wait()


def everyone_else():
    me = lax.axis_index("dp") * 8 + lax.axis_index("fsdp")

    def other(k):
        device = lax.rem(me + k, 32)
        return (device // 8, lax.rem(device, 8))

    return me, other


def open_kernel(
    shard, router, act_ref, ada_ref, up_shard, down_shard, expert_up, expert_down,
    full, routers, seen, rows_out, up_line, down_line, up_mate, up_x, up_y, down_own, down_mate,
    heard, part, got, mixed, ssem, rsem, lsem, asem, brsem, rssem, rrsem, tssem, trsem, zssem, zrsem,
    us, ur, ds, dr, es, er, el,
):
    me, other = everyone_else()
    d, s, c = place()
    f = 2 * s + c
    barrier = pltpu.get_barrier_semaphore()

    def hello(k, carry):
        pl.semaphore_signal(barrier, inc=1, device_id=other(k), device_id_type=MESH)
        return carry

    lax.fori_loop(1, 32, hello, 0)
    pl.semaphore_wait(barrier, 31)

    def act_copy(k, source):
        device = other(k)
        return push(act_ref.at[device[1]], heard.at[source], asem.at[k], brsem.at[k], device)

    def router_copy(k, source):
        return push(router, routers.at[source], rssem.at[k], rrsem.at[k], other(k))

    def send(k, carry):
        act_copy(k, me).start()
        return carry

    lax.fori_loop(1, 32, send, 0)
    gather = Gather("cols", shard, full, ssem, rsem, lsem.at[0])
    gather.start()
    near = Near(
        expert_up, expert_down, up_mate, up_x, up_y, down_own, down_mate, es, er, el.at[0]
    )
    near.start()
    lines = (
        Line("cols", up_shard, up_line, us, ur, lsem.at[3]),
        Line("rows", down_shard, down_line, ds, dr, lsem.at[4]),
    )
    own_router = pltpu.make_async_copy(router, routers.at[me], lsem.at[1])
    own_router.start()

    def send_router(k, carry):
        router_copy(k, me).start()
        return carry

    lax.fori_loop(1, 32, send_router, 0)
    heard[me] = act_ref[f]

    def take(k, carry):
        copy = act_copy(k, lax.rem(me + 32 - k, 32))
        copy.wait_recv()
        return carry

    lax.fori_loop(1, 32, take, 0)
    everything = heard[...].reshape(256, 128)
    row = lax.broadcasted_iota(jnp.int32, (64, 256), 0)
    column = lax.broadcasted_iota(jnp.int32, (64, 256), 1)
    source = lax.rem(row // 2, 4) * 8 + row // 8
    pick = (column == source * 8 + lax.rem(row, 2)).astype(jnp.bfloat16)
    compact = jnp.dot(
        pick, everything.astype(jnp.bfloat16), preferred_element_type=jnp.float32
    ).astype(jnp.bfloat16)
    seen[...] = jnp.concatenate(
        [compact.astype(jnp.float32), jnp.sum(heard[...], axis=0)], axis=0
    )
    part[...] = jnp.dot(compact, ada_ref[...], preferred_element_type=jnp.float32).reshape(
        8, 8, 1152
    )

    def tile_copy(k):
        target = lax.rem(f + k, 8)
        return push(part.at[target], got.at[k], tssem.at[k], trsem.at[k], (d, target))

    for k in range(1, 8):
        tile_copy(k).start()
    gather.spread_z(1)
    gather.spread_z(2)
    gather.relay(0)
    for k in range(1, 8):
        tile_copy(k).wait_recv()
    total = part[f]
    for k in range(1, 8):
        total = total + got[k]
    mixed[...] = total
    zs = []
    for k in range(1, 4):
        copy = push(mixed, rows_out.at[d], zssem.at[k], zrsem.at[k], at(lax.rem(d + k, 4), s, c))
        copy.start()
        zs.append(copy)
    own_rows = pltpu.make_async_copy(mixed, rows_out.at[d], lsem.at[2])
    own_rows.start()
    gather.spread_z(3)
    for line in lines:
        line.start()
    gather.relay(1)
    gather.corner(0)
    gather.relay(2)
    gather.corner(1)
    gather.relay(3)
    gather.corner(2)
    for line in lines:
        line.relay()
    gather.corner(3)
    gather.finish()
    for line in lines:
        line.finish()
    near.finish()
    own_router.wait()
    own_rows.wait()
    for k in range(1, 4):
        push(
            mixed, rows_out.at[lax.rem(d + 4 - k, 4)], zssem.at[k], zrsem.at[k],
            at(lax.rem(d + k, 4), s, c),
        ).wait_recv()
    for copy in zs:
        copy.wait_send()
    for k in range(1, 8):
        tile_copy(k).wait_send()

    def drain(k, carry):
        act_copy(k, me).wait_send()
        copy = router_copy(k, lax.rem(me + 32 - k, 32))
        copy.wait_recv()
        copy.wait_send()
        return carry

    lax.fori_loop(1, 32, drain, 0)


DMA = pltpu.SemaphoreType.DMA
ANYWHERE = pl.BlockSpec(memory_space=pl.ANY)
ONCHIP = pl.BlockSpec(memory_space=pltpu.VMEM)


def opening(shard, router, act, ada, up_shard, down_shard, expert_up, expert_down):
    return pl.pallas_call(
        open_kernel,
        out_shape=(
            jax.ShapeDtypeStruct((768, 3072), jnp.bfloat16),
            jax.ShapeDtypeStruct((32, 16, 128), jnp.bfloat16),
            jax.ShapeDtypeStruct((72, 128), jnp.float32),
            jax.ShapeDtypeStruct((4, 8, 1152), jnp.float32),
            jax.ShapeDtypeStruct((96, 3072), jnp.bfloat16),
            jax.ShapeDtypeStruct((768, 384), jnp.bfloat16),
        )
        + (jax.ShapeDtypeStruct((96, 3072), jnp.bfloat16),) * 3
        + (jax.ShapeDtypeStruct((384, 768), jnp.bfloat16),) * 2,
        in_specs=[ONCHIP] * 6 + [ANYWHERE] * 2,
        out_specs=(ANYWHERE, ANYWHERE, ONCHIP) + (ANYWHERE,) * 8,
        scratch_shapes=[
            pltpu.VMEM((32, 8, 128), jnp.float32),
            pltpu.VMEM((8, 8, 1152), jnp.float32),
            pltpu.VMEM((8, 8, 1152), jnp.float32),
            pltpu.VMEM((8, 1152), jnp.float32),
            DMA((GATHER_SEMS,)), DMA((GATHER_SEMS,)), DMA((5,)),
            DMA((32,)), DMA((32,)), DMA((32,)), DMA((32,)),
            DMA((8,)), DMA((8,)), DMA((4,)), DMA((4,)),
            DMA((3,)), DMA((3,)), DMA((3,)), DMA((3,)),
            DMA((4,)), DMA((4,)), DMA((1,)),
        ],
        compiler_params=pltpu.CompilerParams(collective_id=0, has_side_effects=True),
        name="opening",
    )(shard, router, act, ada, up_shard, down_shard, expert_up, expert_down)


def group_of(d, s, c):
    return [(j, at(lax.rem(d + j // 2, 4), s, lax.rem(c + j, 2))) for j in range(1, 8)]


class Swap:
    def __init__(self, blocks, out, ssem, rsem, lsem):
        self.blocks, self.out, self.ssem, self.rsem, self.lsem = blocks, out, ssem, rsem, lsem
        self.d, self.s, self.c = place()
        self.me = 2 * self.d + self.c

    def copy(self, j, landing):
        target_d = lax.rem(self.d + j // 2, 4)
        target_c = lax.rem(self.c + j, 2)
        return push(
            self.blocks.at[2 * target_d + target_c],
            self.out.at[landing],
            self.ssem.at[j],
            self.rsem.at[j],
            at(target_d, self.s, target_c),
        )

    def start(self):
        for j in (4, 5, 2, 3, 6, 7, 1):
            self.copy(j, self.me).start()
        self.own = pltpu.make_async_copy(
            self.blocks.at[self.me], self.out.at[self.me], self.lsem
        )
        self.own.start()

    def send(self, step):
        for j in (2 * step, 2 * step + 1):
            if j:
                self.copy(j, self.me).start()
            else:
                self.own = pltpu.make_async_copy(
                    self.blocks.at[self.me], self.out.at[self.me], self.lsem
                )
                self.own.start()

    def finish(self):
        self.own.wait()
        for j in range(1, 8):
            source_d = lax.rem(self.d + 4 - j // 2, 4)
            source_c = lax.rem(self.c + j, 2)
            copy = self.copy(j, 2 * source_d + source_c)
            copy.wait_recv()
            copy.wait_send()


def nt(left, right):
    return lax.dot_general(left, right, (((1,), (1,)), ((), ())), preferred_element_type=jnp.float32)


def tn(left, right):
    return lax.dot_general(left, right, (((0,), (0,)), ((), ())), preferred_element_type=jnp.float32)


def nn(left, right):
    return jnp.dot(left, right, preferred_element_type=jnp.float32)


GELU_SCALE = 0.7978845608028654


def gelu_pair(v):
    square = v * v
    bend = jnp.tanh(GELU_SCALE * (v + 0.044715 * (square * v)))
    half = 0.5 * (1.0 + bend)
    slope = half + 0.5 * v * (1.0 - bend * bend) * (
        GELU_SCALE * (1.0 + (3.0 * 0.044715) * square)
    )
    return v * half, slope


HIDDEN = 512


def out_kernel(
    rows, grads, up_line, down_line, tokens, d_tokens, up_x, up_y, down_mate, down_x,
    rows_in, grads_in, up_corner, down_x_mate, down_y_mate, down_corner, mixed_out, d_tokens_out, up_grad, down_grad,
    up_full, down_full, tokens_t, d_tokens_t, s1, r1, s2, r2, ssem, rsem, ssem2, rsem2, lsem,
    es, er, fs, fr, gs, gr,
):
    d, s, c = place()
    greet([device for _, device in group_of(d, s, c)] + [at(d, flip(s, 1), c), at(d, flip(s, 2), c)])
    both = (
        Spread("cols", up_line, up_full, ssem, rsem, lsem.at[0]),
        Spread("rows", down_line, down_full, ssem2, rsem2, lsem.at[1]),
    )
    swap_a = Swap(rows, rows_in, s1, r1, lsem.at[2])
    swap_b = Swap(grads, grads_in, s2, r2, lsem.at[3])
    for g in both:
        g.start()
    swap_a.start()
    swap_b.start()
    mates = Pair(down_mate, down_x_mate, down_mate, down_y_mate, gs, gr)
    up_corners = Pair(up_y, up_corner.at[1], up_x, up_corner.at[0], es, er)
    down_corners = Pair(down_y_mate, down_corner.at[1], down_x, down_corner.at[0], fs, fr)
    tokens_t[...] = tokens[...].T
    d_tokens_t[...] = d_tokens[...].T
    mixed_out[...] = jnp.zeros_like(mixed_out)
    d_tokens_out[...] = jnp.zeros_like(d_tokens_out)
    for g in both:
        g.relay()
    mates.start()
    up_corners.start()
    for g in both:
        g.corner()
    for g in both:
        g.finish()

    def block(b, carry):
        where = pl.ds(pl.multiple_of(b * HIDDEN, HIDDEN), HIDDEN)
        up, down = up_full[:, where], down_full[:, where]
        act, slope = gelu_pair(nn(tokens[...], up))
        act = act.astype(jnp.bfloat16)
        mixed_out[...] += nt(act, down)
        down_grad[:, where] = nn(d_tokens_t[...], act).astype(jnp.bfloat16)
        d_pre = (slope * nn(d_tokens[...], down)).astype(jnp.bfloat16)
        d_tokens_out[...] += nt(d_pre, up)
        up_grad[:, where] = nn(tokens_t[...], d_pre).astype(jnp.bfloat16)
        return carry

    lax.fori_loop(0, 1, block, 0)
    mates.finish()
    down_corners.start()
    lax.fori_loop(1, 3072 // HIDDEN, block, 0)
    swap_a.finish()
    swap_b.finish()
    up_corners.finish()
    down_corners.finish()


def outbound(*operands):
    bf, f32 = jnp.bfloat16, jnp.float32
    return pl.pallas_call(
        out_kernel,
        out_shape=(
            jax.ShapeDtypeStruct((8, 144, 768), bf),
            jax.ShapeDtypeStruct((8, 144, 768), bf),
            jax.ShapeDtypeStruct((2, 96, 3072), bf),
            jax.ShapeDtypeStruct((384, 768), bf),
            jax.ShapeDtypeStruct((384, 768), bf),
            jax.ShapeDtypeStruct((2, 384, 768), bf),
            jax.ShapeDtypeStruct((512, 768), f32),
            jax.ShapeDtypeStruct((512, 768), f32),
            jax.ShapeDtypeStruct((768, 3072), bf),
            jax.ShapeDtypeStruct((768, 3072), bf),
        ),
        in_specs=[ONCHIP] * 6 + [ANYWHERE] * 4,
        out_specs=(ANYWHERE,) * 6 + (ONCHIP,) * 4,
        scratch_shapes=[pltpu.VMEM((768, 3072), bf)] * 2
        + [pltpu.VMEM((768, 512), bf)] * 2
        + [DMA((8,))] * 4
        + [DMA((9,))] * 4
        + [DMA((4,))]
        + [DMA((2,))] * 6,
        compiler_params=pltpu.CompilerParams(
            collective_id=1, has_side_effects=True, vmem_limit_bytes=60 << 20
        ),
        name="outbound",
    )(*operands)


def widened(ref):
    return ref[...].astype(jnp.float32)


class Parts:
    def __init__(self, grad, keep, over_x, over_y, sem, rsem=None):
        d, s, c = place()
        sx, sy = flip(s, 1), flip(s, 2)
        sd = flip(sx, 2)
        rows = grad.shape[0] // 8
        slots = (
            (s, 0, keep.at[0, 0], s), (sy, 0, keep.at[0, 1], s),
            (s, 1, keep.at[1, 0], s), (sx, 1, keep.at[1, 1], s),
            (sx, 0, over_x.at[0], sx), (sd, 0, over_x.at[1], sx),
            (sy, 1, over_y.at[0], sy), (sd, 1, over_y.at[1], sy),
        )
        self.copies, self.away = [], []
        for i, (position, h, out, target) in enumerate(slots):
            part = grad.at[pl.ds(pl.multiple_of((2 * position + h) * rows, 32), rows)]
            if i < 4 or rsem is None:
                self.copies.append(pltpu.make_async_copy(part, out, sem.at[i]))
            else:
                self.away.append(push(part, out, sem.at[i], rsem.at[i], at(d, target, c)))

    def start(self):
        for copy in self.away + self.copies:
            copy.start()

    def finish(self):
        for copy in self.copies + self.away:
            copy.wait()


class Pieces:
    def __init__(self, parts, full, sem):
        d, s, c = place()
        rows = full.shape[0] // 8
        sx, sy = flip(s, 1), flip(s, 2)
        positions = [p for p in (s, sx, sy, flip(sx, 2)) for _ in range(2)]
        self.copies = [
            pltpu.make_async_copy(
                part,
                full.at[pl.ds(pl.multiple_of(rows * (2 * p + (c if i % 2 == 0 else 1 - c)), 32), rows)],
                sem.at[i],
            )
            for i, (p, part) in enumerate(zip(positions, parts))
        ]

    def start(self):
        for copy in self.copies:
            copy.start()

    def finish(self):
        for copy in self.copies:
            copy.wait()


def expert_kernel(
    rows, grads, expert_up, up_m, up_x0, up_x1, up_y0, up_y1, up_corner,
    down_own, down_m, down_x0, down_x1, down_y0, down_y1, down_corner, first_grad, second_grad,
    rows_back, grads_back, up_keep, up_x, up_y, down_keep, down_x, down_y, first_part, second_part,
    up, down, act, d_pre, made, d_made, total, d_total, up_grad, down_grad, rows_t,
    fo, fm, fn, ff, fs, fr, fl, so, sm, sn, sf, ss, sr, sl,
    s1, r1, s2, r2, lsem, wsem, vsem, psem, arsem, qsem,
):
    bf = jnp.bfloat16
    d, s, c = place()
    weights = (
        Pieces(
            (expert_up.at[c], up_m, up_x0, up_x1, up_y0, up_y1, up_corner.at[0], up_corner.at[1]), up, wsem
        ),
        Pieces(
            (down_own, down_m, down_x0, down_x1, down_y0, down_y1, down_corner.at[0], down_corner.at[1]),
            down, vsem,
        ),
    )
    for each in weights:
        each.start()
    greet([device for _, device in group_of(d, s, c)] + [at(d, flip(s, 1), c), at(d, flip(s, 2), c)])
    sums = (
        DenseSum("cols", first_grad, first_part, fo, fm, fn, ff, None, fs, fr, fl),
        DenseSum("rows", second_grad, second_part, so, sm, sn, sf, None, ss, sr, sl),
    )
    for each in sums:
        each.start()
    swap_a = Swap(made, rows_back, s1, r1, lsem.at[0])
    swap_b = Swap(d_made, grads_back, s2, r2, lsem.at[1])
    for each in weights:
        each.finish()
    for step in (2, 1, 3, 0):
        there = lax.rem(d + step, 4)
        chunk = pl.ds(2 * there, 2)
        lines = pl.ds(pl.multiple_of(288 * there, 288), 288)
        x = rows[chunk].reshape(288, 768)
        g = grads[chunk].reshape(288, 768)
        total[...] = jnp.zeros_like(total)
        d_total[...] = jnp.zeros_like(d_total)

        def block(b, carry):
            where = pl.ds(pl.multiple_of(b * HIDDEN, HIDDEN), HIDDEN)
            up_part, down_part = up[:, where], down[where]
            made_act, slope = gelu_pair(nn(x, up_part))
            made_act = made_act.astype(bf)
            act[lines, where] = made_act
            total[...] += nn(made_act, down_part)
            d_part = (slope * nt(g, down_part)).astype(bf)
            d_pre[lines, where] = d_part
            d_total[...] += nt(d_part, up_part)
            return carry

        lax.fori_loop(0, 3072 // HIDDEN, block, 0)
        made[chunk] = total[...].astype(bf).reshape(2, 144, 768)
        d_made[chunk] = d_total[...].astype(bf).reshape(2, 144, 768)
        swap_a.send(step)
        swap_b.send(step)
        if step == 2:
            for each in sums:
                each.merge()
        if step == 3:
            for each in sums:
                each.join()
    rows_t[...] = rows.reshape(1152, 768)[...].T
    g_all = grads.reshape(1152, 768)

    def up_block(b, carry):
        where = pl.ds(pl.multiple_of(b * HIDDEN, HIDDEN), HIDDEN)
        up_grad[:, where] = nn(rows_t[...], d_pre[:, where]).astype(bf)
        return carry

    def down_block(b, carry):
        where = pl.ds(pl.multiple_of(384 * b, 384), 384)
        down_grad[where] = tn(act[:, where], g_all[...]).astype(bf)
        return carry

    up_parts = Parts(up_grad, up_keep, up_x, up_y, psem, arsem)
    down_parts = Parts(down_grad, down_keep, down_x, down_y, qsem)
    lax.fori_loop(0, 3072 // HIDDEN, up_block, 0)
    up_parts.start()
    lax.fori_loop(0, 8, down_block, 0)
    down_parts.start()
    for each in sums:
        each.close()
    swap_a.finish()
    swap_b.finish()
    up_parts.finish()
    down_parts.finish()


def experts(rows, grads, up_pieces, down_pieces, first_grad, second_grad):
    bf, f32 = jnp.bfloat16, jnp.float32

    def rooms(piece, half):
        return [
            pltpu.VMEM((4,) + piece, bf),
            pltpu.VMEM((4,) + piece, bf),
            pltpu.VMEM((2,) + half, bf),
            pltpu.VMEM((2,) + piece, bf),
            DMA((8,)),
            DMA((8,)),
            DMA((4,)),
        ]

    def parts(r, n):
        return (
            jax.ShapeDtypeStruct((2, 2, r, n), bf),
            jax.ShapeDtypeStruct((2, r, n), bf),
            jax.ShapeDtypeStruct((2, r, n), bf),
        )

    return pl.pallas_call(
        expert_kernel,
        out_shape=(
            jax.ShapeDtypeStruct((8, 144, 768), bf),
            jax.ShapeDtypeStruct((8, 144, 768), bf),
        )
        + parts(96, 3072)
        + parts(384, 768)
        + (
            jax.ShapeDtypeStruct((96, 3072), bf),
            jax.ShapeDtypeStruct((768, 384), bf),
        ),
        in_specs=[ONCHIP, ONCHIP] + [ANYWHERE] * 16,
        out_specs=(ANYWHERE,) * 8 + (ONCHIP, ONCHIP),
        scratch_shapes=[
            pltpu.VMEM((768, 3072), bf),
            pltpu.VMEM((3072, 768), bf),
            pltpu.VMEM((1152, 3072), bf),
            pltpu.VMEM((1152, 3072), bf),
            pltpu.VMEM((8, 144, 768), bf),
            pltpu.VMEM((8, 144, 768), bf),
            pltpu.VMEM((288, 768), f32),
            pltpu.VMEM((288, 768), f32),
            pltpu.VMEM((768, 3072), bf),
            pltpu.VMEM((3072, 768), bf),
            pltpu.VMEM((768, 1152), bf),
        ]
        + rooms((96, 3072), (96, 1536))
        + rooms((768, 384), (384, 384))
        + [DMA((8,))] * 4
        + [DMA((2,)), DMA((8,)), DMA((8,)), DMA((8,)), DMA((8,)), DMA((8,))],
        compiler_params=pltpu.CompilerParams(
            collective_id=2, has_side_effects=True, vmem_limit_bytes=67043328
        ),
        name="experts",
    )(rows, grads, *up_pieces, *down_pieces, first_grad, second_grad)


def hop(values, bit):
    return lax.ppermute(values, "fsdp", [(f, f ^ bit) for f in range(8)])


def square_next(keep, from_x, from_y):
    f32, bf = jnp.float32, jnp.bfloat16
    return (
        hop((keep[0, 1].astype(f32) + from_x[1].astype(f32)).astype(bf), 4),
        hop((keep[1, 1].astype(f32) + from_y[1].astype(f32)).astype(bf), 2),
    )


class DenseSum:
    def __init__(self, kind, grad, out, own, mate, near, far, line, ssem, rsem, lsem):
        self.kind, self.grad, self.out = kind, grad, out
        self.own, self.mate, self.near, self.far, self.line = own, mate, near, far, line
        self.ssem, self.rsem, self.lsem = ssem, rsem, lsem
        self.d, self.s, self.c = place()
        self.order = (
            flip(flip(self.s, 1), 2),
            flip(self.s, 1),
            flip(self.s, 2),
            self.s,
        )

    def piece(self, f):
        if self.kind == "cols":
            return self.grad.at[pl.ds(pl.multiple_of(96 * f, 96), 96)]
        return self.grad.at[:, pl.ds(pl.multiple_of(384 * f, 384), 384)]

    def half(self, ref, h):
        if self.kind == "cols":
            return ref.at[:, pl.ds(1536 * h, 1536)]
        return ref.at[pl.ds(384 * h, 384)]

    def quarter(self, ref, q):
        if self.kind == "cols":
            return ref.at[:, pl.ds(pl.multiple_of(768 * q, 768), 768)]
        return ref.at[pl.ds(pl.multiple_of(192 * q, 192), 192)]

    def start(self):
        d, s, c = self.d, self.s, self.c
        self.zero, self.local = [], []
        for j, position in enumerate(self.order):
            copy = push(
                self.piece(2 * position + 1 - c), self.mate.at[j], self.ssem.at[j], self.rsem.at[j], at(d, s, 1 - c)
            )
            copy.start()
            self.zero.append(copy)
            copy = pltpu.make_async_copy(self.piece(2 * position + c), self.own.at[j], self.lsem.at[j])
            copy.start()
            self.local.append(copy)

    def merge(self):
        d, s, c = self.d, self.s, self.c
        sx, sy = flip(s, 1), flip(s, 2)
        self.one = []
        for j in range(4):
            self.zero[j].wait_recv()
            self.local[j].wait()
            self.own[j] = (widened(self.own.at[j]) + widened(self.mate.at[j])).astype(jnp.bfloat16)
            if j == 0:
                for h, target in enumerate((sx, sy)):
                    copy = push(
                        self.half(self.own.at[0], h), self.near.at[h], self.ssem.at[4 + h], self.rsem.at[4 + h],
                        at(d, target, c),
                    )
                    copy.start()
                    self.one.append(copy)

    def join(self):
        d, s, c = self.d, self.s, self.c
        sx, sy = flip(s, 1), flip(s, 2)
        for h, j in ((0, 2), (1, 1)):
            self.one[h].wait_recv()
            where = self.half(self.own.at[j], h)
            where[...] = (widened(where) + widened(self.near.at[h])).astype(jnp.bfloat16)
        self.two = []
        for h, target in enumerate((sx, sy)):
            copy = push(
                self.own.at[1 + h], self.far.at[h], self.ssem.at[6 + h], self.rsem.at[6 + h], at(d, target, c)
            )
            copy.start()
            self.two.append(copy)

    def square(self):
        for copy in self.two:
            copy.wait_recv()
        return (
            widened(self.own.at[3]) + widened(self.far.at[0]) + widened(self.far.at[1])
        ).astype(jnp.bfloat16)

    def along(self):
        d, s, c = self.d, self.s, self.c
        self.own[3] = self.square()
        self.three = []
        for k in range(1, 4):
            target = lax.rem(d + k, 4)
            copy = push(
                self.quarter(self.own.at[3], target), self.line.at[k - 1], self.ssem.at[7 + k], self.rsem.at[7 + k],
                at(target, s, c),
            )
            copy.start()
            self.three.append(copy)

    def finish(self):
        total = widened(self.quarter(self.own.at[3], self.d))
        for k in range(1, 4):
            self.three[k - 1].wait_recv()
            total = total + widened(self.line.at[k - 1])
        self.out[...] = total
        self.sent(self.three)

    def close(self):
        self.out[...] = self.square()
        self.sent([])

    def sent(self, more):
        for copy in self.zero + self.one + self.two + more:
            copy.wait_send()


class LineSum:
    def __init__(self, kind, part, out, landing, ssem, rsem):
        self.kind, self.part, self.out, self.landing = kind, part, out, landing
        self.ssem, self.rsem = ssem, rsem
        self.d, self.s, self.c = place()

    def quarter(self, q):
        if self.kind == "cols":
            return self.part.at[:, pl.ds(pl.multiple_of(768 * q, 768), 768)]
        return self.part.at[pl.ds(pl.multiple_of(192 * q, 192), 192)]

    def start(self):
        self.copies = []
        for k in range(1, 4):
            target = lax.rem(self.d + k, 4)
            copy = push(
                self.quarter(target), self.landing.at[k - 1], self.ssem.at[k - 1], self.rsem.at[k - 1],
                at(target, self.s, self.c),
            )
            copy.start()
            self.copies.append(copy)

    def finish(self):
        total = widened(self.quarter(self.d))
        for k in range(3):
            self.copies[k].wait_recv()
            total = total + widened(self.landing.at[k])
        self.out[...] = total
        for copy in self.copies:
            copy.wait_send()


class Ending:
    def __init__(self, keep, from_x, from_y, out, room, stage, landed, last, lsem, ssem, rsem, loaded=None):
        self.out, self.room, self.stage, self.landed, self.last = out, room, stage, landed, last
        self.ssem, self.rsem = ssem, rsem
        self.d, self.s, self.c = place()
        sources = [
            keep.at[0, 0], keep.at[0, 1], keep.at[1, 0], keep.at[1, 1],
            from_x.at[0], from_x.at[1], from_y.at[0], from_y.at[1],
        ]
        self.loads = [
            pltpu.make_async_copy(source, room.at[i], lsem.at[i]) for i, source in enumerate(sources)
        ]
        for i, source in enumerate(loaded or ()):
            self.loads.append(pltpu.make_async_copy(source, landed.at[i], lsem.at[8 + i]))
        self.sent = []

    def load(self):
        for copy in self.loads:
            copy.start()

    def loaded(self):
        for copy in self.loads:
            copy.wait()

    def go(self, index, target):
        dst = self.last if index == 2 else self.landed.at[index]
        copy = push(self.stage.at[index], dst, self.ssem.at[index], self.rsem.at[index], target)
        copy.start()
        self.sent.append(copy)

    def next(self):
        bf = jnp.bfloat16
        room = self.room
        self.stage[0] = (widened(room.at[1]) + widened(room.at[5])).astype(bf)
        self.go(0, at(self.d, flip(self.s, 2), self.c))
        self.stage[1] = (widened(room.at[3]) + widened(room.at[7])).astype(bf)
        self.go(1, at(self.d, flip(self.s, 1), self.c))

    def close(self):
        for copy in self.sent:
            copy.wait_recv()
        c = self.c
        mine, theirs = c, 1 - c

        def total(h):
            return (
                widened(self.room.at[2 * h]) + widened(self.room.at[4 + 2 * h]) + widened(self.landed.at[h])
            )

        self.stage[2] = total(theirs).astype(jnp.bfloat16)
        self.go(2, at(self.d, self.s, 1 - c))
        self.out[c] = total(mine)

    def finish(self):
        self.sent[-1].wait_recv()
        self.out[1 - self.c] = widened(self.last)
        for copy in self.sent:
            copy.wait_send()


class Tail:
    def __init__(self, d_rows, router, act, ada, ada_out, d_act_out, router_out, z1, plane, plane_in, z2, z2_in, sems):
        self.d_rows, self.router, self.act, self.ada = d_rows, router, act, ada
        self.ada_out, self.d_act_out, self.router_out = ada_out, d_act_out, router_out
        self.z1, self.plane, self.plane_in, self.z2, self.z2_in = z1, plane, plane_in, z2, z2_in
        self.sems = sems
        self.d, self.s, self.c = place()
        self.f = 2 * self.s + self.c

    def z_copy(self, k, src, dst, base):
        send, recv = self.sems[base], self.sems[base + 1]
        return push(src, dst, send.at[k], recv.at[k], at(lax.rem(self.d + k, 4), self.s, self.c))

    def f_copy(self, k, src, dst, base):
        send, recv = self.sems[base], self.sems[base + 1]
        return push(src, dst, send.at[k], recv.at[k], (self.d, lax.rem(self.f + k, 8)))

    def start(self):
        self.all = [
            self.z_copy(k, self.d_rows.at[lax.rem(self.d + k, 4)], self.z1.at[k], 0) for k in range(1, 4)
        ]
        for copy in self.all:
            copy.start()

    def second(self):
        total = self.d_rows[self.d]
        for k in range(1, 4):
            self.all[k - 1].wait_recv()
            total = total + self.z1[k]
        for target in range(8):
            self.plane[target, :, 0:1152] = total
            self.plane[target, :, 1152:1280] = self.router[target]
        copies = [
            self.f_copy(k, self.plane.at[lax.rem(self.f + k, 8)], self.plane_in.at[lax.rem(8 - k, 8)], 2)
            for k in range(1, 8)
        ]
        for copy in copies:
            copy.start()
        self.in_plane = copies
        self.all = self.all + copies

    def third(self):
        f = self.f
        self.plane_in[0] = self.plane[f]
        for copy in self.in_plane:
            copy.wait_recv()
        everything = self.plane_in[...]
        router = jnp.sum(everything[:, :, 1152:1280], axis=0)
        rows = everything[:, :, 0:1152].reshape(64, 1152)
        line = lax.broadcasted_iota(jnp.int32, (64, 64), 0)
        column = lax.broadcasted_iota(jnp.int32, (64, 64), 1)
        turn = (lax.rem(line // 8 + 8 - f, 8) * 8 + lax.rem(line, 8) == column).astype(jnp.bfloat16)
        d_mod = nn(turn, rows.astype(jnp.bfloat16)).astype(jnp.bfloat16)
        self.ada_out[...] = tn(self.act[...], d_mod)[0:96]
        part = nt(d_mod, self.ada[...])
        self.z2[0:64, 0:96] = part
        self.z2[0:64, 96:128] = jnp.zeros((64, 32), jnp.float32)
        self.z2[64:72, :] = router
        copies = [self.z_copy(k, self.z2, self.z2_in.at[k], 4) for k in range(1, 4)]
        for copy in copies:
            copy.start()
        self.along = copies
        self.all = self.all + copies

    def fourth(self):
        total = self.z2[...]
        for k in range(1, 4):
            self.along[k - 1].wait_recv()
            total = total + self.z2_in[k]
        self.router_out[...] = total[64:72]
        self.z2_in[0] = total
        copies = [
            self.f_copy(
                k,
                self.z2_in.at[0, pl.ds(pl.multiple_of(8 * lax.rem(self.f + k, 8), 8), 8)],
                self.d_act_out.at[self.f],
                6,
            )
            for k in range(1, 8)
        ]
        for copy in copies:
            copy.start()
        self.d_act_out[self.f] = self.z2_in[0, pl.ds(pl.multiple_of(8 * self.f, 8), 8)]
        self.last = copies
        self.all = self.all + copies

    def finish(self):
        for k in range(1, 8):
            self.f_copy(
                k, self.z2_in.at[0, pl.ds(0, 8)], self.d_act_out.at[lax.rem(self.f + 8 - k, 8)], 6
            ).wait_recv()
        for copy in self.all:
            copy.wait_send()


def dense_kernel(
    grad, first_part, second_part, d_rows, router, act, ada,
    up_keep, up_x, up_y, up_low, up_high, down_keep, down_x, down_y,
    out, first_out, second_out, ada_out, d_act_out, router_out, up_out, down_out,
    ur, us, ul, ue, ula, usa, ura, dr, ds, dl, de, dla, dsa, dra,
    own, mate, near, far, line, ssem, rsem, lsem,
    first_in, fs, fr, second_in, ss, sr, *rest,
):
    d, s, c = place()
    f = 2 * s + c
    greet(
        [at(lax.rem(d + k, 4), s, c) for k in range(1, 4)]
        + [(d, lax.rem(f + k, 8)) for k in range(1, 8)]
    )
    dense = DenseSum("cols", grad, out, own, mate, near, far, line, ssem, rsem, lsem)
    lines = (
        LineSum("cols", first_part, first_out, first_in, fs, fr),
        LineSum("rows", second_part, second_out, second_in, ss, sr),
    )
    tail = Tail(d_rows, router, act, ada, ada_out, d_act_out, router_out, *rest[:5], rest[5:])
    ups = Ending(up_keep, up_x, up_y, up_out, ur, us, ul, ue, ula, usa, ura, (up_low, up_high))
    downs = Ending(down_keep, down_x, down_y, down_out, dr, ds, dl, de, dla, dsa, dra)
    tail.start()
    dense.start()
    for each in lines:
        each.start()
    downs.load()
    ups.load()
    tail.second()
    dense.merge()
    tail.third()
    downs.loaded()
    ups.loaded()
    ups.close()
    dense.join()
    downs.next()
    tail.fourth()
    dense.along()
    downs.close()
    for each in lines:
        each.finish()
    ups.finish()
    dense.finish()
    downs.finish()
    tail.finish()


def dense_sums(grad, first_part, second_part, small, routed):
    bf, f32 = jnp.bfloat16, jnp.float32

    def rooms(r, n):
        return [
            pltpu.VMEM((8, r, n), bf),
            pltpu.VMEM((3, r, n), bf),
            pltpu.VMEM((2, r, n), bf),
            pltpu.VMEM((r, n), bf),
            DMA((10,)),
            DMA((3,)),
            DMA((3,)),
        ]

    return pl.pallas_call(
        dense_kernel,
        out_shape=(
            jax.ShapeDtypeStruct((96, 768), f32),
            jax.ShapeDtypeStruct((96, 768), f32),
            jax.ShapeDtypeStruct((192, 384), f32),
            jax.ShapeDtypeStruct((96, 1152), f32),
            jax.ShapeDtypeStruct((8, 8, 128), f32),
            jax.ShapeDtypeStruct((8, 128), f32),
            jax.ShapeDtypeStruct((2, 96, 3072), f32),
            jax.ShapeDtypeStruct((2, 384, 768), f32),
        ),
        in_specs=[ANYWHERE] + [ONCHIP] * 6 + [ANYWHERE] * 8,
        out_specs=(ONCHIP,) * 8,
        scratch_shapes=rooms(96, 3072) + rooms(384, 768) + [
            pltpu.VMEM((4, 96, 3072), bf),
            pltpu.VMEM((4, 96, 3072), bf),
            pltpu.VMEM((2, 96, 1536), bf),
            pltpu.VMEM((2, 96, 3072), bf),
            pltpu.VMEM((3, 96, 768), bf),
            DMA((11,)), DMA((11,)), DMA((4,)),
            pltpu.VMEM((3, 96, 768), bf),
            DMA((3,)), DMA((3,)),
            pltpu.VMEM((3, 192, 384), bf),
            DMA((3,)), DMA((3,)),
            pltpu.VMEM((4, 8, 1152), f32),
            pltpu.VMEM((8, 8, 1280), f32),
            pltpu.VMEM((8, 8, 1280), f32),
            pltpu.VMEM((72, 128), f32),
            pltpu.VMEM((4, 72, 128), f32),
            DMA((4,)), DMA((4,)), DMA((8,)), DMA((8,)), DMA((4,)), DMA((4,)), DMA((8,)), DMA((8,)),
        ],
        compiler_params=pltpu.CompilerParams(
            collective_id=3, has_side_effects=True, vmem_limit_bytes=60 << 20
        ),
        cost_estimate=pl.CostEstimate(flops=40_000_000_000, bytes_accessed=20_000_000, transcendentals=0),
        name="dense_sums",
    )(grad, first_part, second_part, *small, *routed)


def layer_stats(values_in):
    centred = values_in - jnp.mean(values_in, axis=-1, keepdims=True)
    inv_std = lax.rsqrt(jnp.mean(centred * centred, axis=-1, keepdims=True) + 1e-06)
    return centred * inv_std, inv_std


def modulated(inside, mod, part):
    columns = slice(768 * part, 768 * part + 768)
    return inside[:, 0:1] * mod[0:1, columns] + inside[:, 1:2] * mod[1:2, columns]


def head_column(g):
    return 768 * (g // 9) + 64 * (g % 9)


QUERY_ROWS = 256


def front_kernel(
    tokens, mod, inside, seg_col, seg_row, qkvo, router, cotangent, routes, target,
    heads, totals, attended, projected, residual, second, d_mixed, gates, rows, grads,
    bias, made, weighted,
):
    bf, f32 = jnp.bfloat16, jnp.float32
    token_float = tokens[...].astype(f32)
    normed, _ = layer_stats(token_float)
    first = (normed * (1.0 + modulated(inside, mod, 1)) + modulated(inside, mod, 0)).astype(bf)
    for j in range(4):
        piece = nn(first, qkvo[:, 768 * j : 768 * j + 640]).astype(bf)
        for i in range(9):
            heads[9 * j + i] = piece[:, 64 * i : 64 * i + 64]
    bias[...] = jnp.where(seg_col[...] == seg_row[...], 0.0, -1e30)

    def block(n, carry):
        h, part = n // (512 // QUERY_ROWS), lax.rem(n, 512 // QUERY_ROWS)
        lines = pl.ds(pl.multiple_of(part * QUERY_ROWS, QUERY_ROWS), QUERY_ROWS)
        scores = nt(heads[h, lines], heads[12 + h]) * 0.125 + bias[lines]
        row_max = jnp.max(scores, axis=-1, keepdims=True)
        weight = jnp.exp(scores - row_max)
        running = jnp.sum(weight, axis=-1, keepdims=True)
        probability = (weight * (1.0 / running)).astype(bf)
        made[h, lines] = nn(probability, heads[24 + h]).astype(bf)
        totals[h, lines] = row_max + jnp.log(running)
        return carry

    lax.fori_loop(0, 12 * (512 // QUERY_ROWS), block, 0)
    for h in range(12):
        attended[:, 64 * h : 64 * h + 64] = made[h]
    for j in range(4):
        piece = nn(attended[...], qkvo[:, 768 * j + 512 : 768 * j + 768])
        projected[:, 192 * j : 192 * j + 192] = piece[:, 64:256]
    residual[...] = token_float + modulated(inside, mod, 2) * projected[...]
    normed, _ = layer_stats(residual[...])
    second[...] = (normed * (1.0 + modulated(inside, mod, 4)) + modulated(inside, mod, 3)).astype(bf)
    logits = nn(second[...], router[...])
    ids = lax.broadcasted_iota(jnp.int32, (512, 8), 1)
    chosen = [
        jnp.sum(jnp.where(ids == routes[:, k : k + 1], logits, 0.0), axis=-1, keepdims=True)
        for k in range(2)
    ]
    top = jnp.maximum(chosen[0], chosen[1])
    raised = [jnp.exp(each - top) for each in chosen]
    share = [each / (raised[0] + raised[1]) for each in raised]
    pair = lax.broadcasted_iota(jnp.int32, (512, 2), 1)
    gates[...] = jnp.where(pair == 0, share[0], share[1])
    mixed_grad = modulated(inside, mod, 5) * cotangent[...].astype(f32)
    d_mixed[...] = mixed_grad.astype(bf)
    for k in range(2):
        weighted[k] = (share[k] * mixed_grad).astype(bf)

    def send(b, carry):
        lines = pl.ds(pl.multiple_of(288 * b, 288), 288)
        places = lax.broadcasted_iota(jnp.int32, (288, 512), 0) + 288 * b
        first_hot = (places == target[0:1]).astype(f32)
        second_hot = (places == target[1:2]).astype(f32)
        rows[lines] = nn((first_hot + second_hot).astype(bf), second[...]).astype(bf)
        grads[lines] = (
            nn(first_hot.astype(bf), weighted[0]) + nn(second_hot.astype(bf), weighted[1])
        ).astype(bf)
        return carry

    lax.fori_loop(0, 4, send, 0)


def front(tokens, mod, inside, seg_col, seg_row, qkvo, router, cotangent, routes, target):
    bf, f32 = jnp.bfloat16, jnp.float32
    return pl.pallas_call(
        front_kernel,
        out_shape=(
            jax.ShapeDtypeStruct((36, 512, 64), bf),
            jax.ShapeDtypeStruct((12, 512, 1), f32),
            jax.ShapeDtypeStruct((512, 768), bf),
            jax.ShapeDtypeStruct((512, 768), f32),
            jax.ShapeDtypeStruct((512, 768), f32),
            jax.ShapeDtypeStruct((512, 768), bf),
            jax.ShapeDtypeStruct((512, 768), bf),
            jax.ShapeDtypeStruct((512, 2), f32),
            jax.ShapeDtypeStruct((1152, 768), bf),
            jax.ShapeDtypeStruct((1152, 768), bf),
        ),
        in_specs=[ONCHIP] * 10,
        out_specs=(ONCHIP,) * 10,
        scratch_shapes=[
            pltpu.VMEM((512, 512), f32),
            pltpu.VMEM((12, 512, 64), bf),
            pltpu.VMEM((2, 512, 768), bf),
        ],
        compiler_params=pltpu.CompilerParams(vmem_limit_bytes=60 << 20),
        cost_estimate=pl.CostEstimate(flops=40_000_000_000, bytes_accessed=20_000_000, transcendentals=0),
        name="front",
    )(tokens, mod, inside, seg_col, seg_row, qkvo, router, cotangent, routes, target)


def norm_grad(upstream, normed, inv_std):
    return (
        upstream
        - jnp.mean(upstream, axis=-1, keepdims=True)
        - normed * jnp.mean(upstream * normed, axis=-1, keepdims=True)
    ) * inv_std


def rear_kernel(
    tokens, mod, inside, seg_col, seg_row, qkvo, router, cotangent, routes, target,
    heads, totals, attended, projected, residual, second, gates,
    returned, d_returned, shared_out, d_shared,
    output, tokens_grad, qkvo_grad, d_mod, router_grad,
    bias, rows_t, d_heads, d_att, d_att_t, d_rows_t, d_rows, d_residual, d_proj,
):
    bf, f32 = jnp.bfloat16, jnp.float32
    upstream = cotangent[...].astype(f32)

    def image_sums(part, values):
        for j in range(2):
            d_mod[j : j + 1, 768 * part : 768 * part + 768] = jnp.sum(
                inside[:, j : j + 1] * values, axis=0, keepdims=True
            )

    share = [gates[:, k : k + 1] for k in range(2)]
    places = lax.broadcasted_iota(jnp.int32, (512, 1152), 1)
    hot = [(places == target[:, k : k + 1]).astype(f32).astype(bf) for k in range(2)]
    picked = [nn(each, returned[...]) for each in hot]
    mixed = shared_out[...] + (share[0] * picked[0] + share[1] * picked[1])
    gate_two = modulated(inside, mod, 5)
    output[...] = (residual[...] + gate_two * mixed).astype(bf)
    image_sums(5, upstream * mixed)
    mixed_grad = gate_two * upstream
    d_share = [jnp.sum(mixed_grad * each, axis=-1, keepdims=True) for each in picked]
    inner = share[0] * d_share[0] + share[1] * d_share[1]
    ids = lax.broadcasted_iota(jnp.int32, (512, 8), 1)
    d_logits = sum(
        jnp.where(ids == routes[:, k : k + 1], share[k] * (d_share[k] - inner), 0.0) for k in range(2)
    ).astype(bf)
    router_grad[...] = tn(d_logits, second[...])
    d_second = (
        d_shared[...] + nt(d_logits, router[...]) + (nn(hot[0], d_returned[...]) + nn(hot[1], d_returned[...]))
    )
    normed, inv_std = layer_stats(residual[...])
    image_sums(3, d_second)
    image_sums(4, d_second * normed)
    d_residual[...] = upstream + norm_grad(d_second * (1.0 + modulated(inside, mod, 4)), normed, inv_std)
    gate_one = modulated(inside, mod, 2)
    image_sums(2, d_residual[...] * projected[...])
    d_proj[...] = (gate_one * d_residual[...]).astype(bf)
    d_attended = jnp.zeros((512, 768), f32)
    for j in range(4):
        piece = jnp.concatenate(
            [jnp.zeros((512, 64), bf), d_proj[:, 192 * j : 192 * j + 192]], axis=1
        )
        d_attended += nt(piece, qkvo[:, 768 * j + 512 : 768 * j + 768])
    d_attended = d_attended.astype(bf)
    d_att_t[...] = d_attended.T
    for h in range(12):
        d_att[h] = d_attended[:, 64 * h : 64 * h + 64]
    for j in range(18):
        pair = jnp.concatenate([heads[2 * j], heads[2 * j + 1]], axis=1)
        rows_t[128 * j : 128 * j + 128] = pair.T
    bias[...] = jnp.where(seg_col[...] == seg_row[...], 0.0, -1e30)

    def head(h, carry):
        def at_head(g):
            return pl.ds(pl.multiple_of(64 * g, 64), 64)

        d_key, d_value = jnp.zeros((64, 512), f32), jnp.zeros((64, 512), f32)
        for part in range(512 // QUERY_ROWS):
            lines = slice(part * QUERY_ROWS, (part + 1) * QUERY_ROWS)
            scores = nn(heads[h, lines], rows_t[at_head(12 + h)]) * 0.125 + bias[lines]
            probability = jnp.exp(scores - totals[h, lines])
            d_prob = nn(d_att[h, lines], rows_t[at_head(24 + h)])
            inner = jnp.sum(probability * d_prob, axis=-1, keepdims=True)
            d_scores = (probability * (d_prob - inner)).astype(bf)
            d_heads[h, lines] = (nn(d_scores, heads[12 + h]) * 0.125).astype(bf)
            d_key += nn(rows_t[at_head(h), lines], d_scores)
            d_value += nn(d_att_t[at_head(h), lines], probability.astype(bf))
        d_rows_t[at_head(h)] = (d_key * 0.125).astype(bf)
        d_rows_t[at_head(12 + h)] = d_value.astype(bf)
        return carry

    lax.fori_loop(0, 12, head, 0)
    for g in range(12):
        column = head_column(g)
        d_rows[:, column : column + 64] = d_heads[g]
    for j in range(12):
        pair = d_rows_t[128 * j : 128 * j + 128].T
        for i in range(2):
            column = head_column(12 + 2 * j + i)
            d_rows[:, column : column + 64] = pair[:, 64 * i : 64 * i + 64]
    for j in range(4):
        d_rows[:, 768 * j + 576 : 768 * j + 768] = jnp.zeros((512, 192), bf)
    token_float = tokens[...].astype(f32)
    normed, inv_std = layer_stats(token_float)
    scale_one = 1.0 + modulated(inside, mod, 1)
    first_t = (normed * scale_one + modulated(inside, mod, 0)).astype(bf).T
    attended_t = attended[...].T
    for j in range(4):
        qkvo_grad[:, 768 * j : 768 * j + 640] = nn(first_t, d_rows[:, 768 * j : 768 * j + 640]).astype(bf)
        qkvo_grad[:, 768 * j + 576 : 768 * j + 768] = nn(
            attended_t, d_proj[:, 192 * j : 192 * j + 192]
        ).astype(bf)
    d_first = nt(d_rows[...], qkvo[...])
    image_sums(0, d_first)
    image_sums(1, d_first * normed)
    tokens_grad[...] = d_residual[...] + norm_grad(d_first * scale_one, normed, inv_std)


def rear(*operands):
    bf, f32 = jnp.bfloat16, jnp.float32
    return pl.pallas_call(
        rear_kernel,
        out_shape=(
            jax.ShapeDtypeStruct((512, 768), bf),
            jax.ShapeDtypeStruct((512, 768), f32),
            jax.ShapeDtypeStruct((768, 3072), bf),
            jax.ShapeDtypeStruct((2, 4608), f32),
            jax.ShapeDtypeStruct((8, 768), f32),
        ),
        in_specs=[ONCHIP] * len(operands),
        out_specs=(ONCHIP,) * 5,
        scratch_shapes=[
            pltpu.VMEM((512, 512), f32),
            pltpu.VMEM((2304, 512), bf),
            pltpu.VMEM((12, 512, 64), bf),
            pltpu.VMEM((12, 512, 64), bf),
            pltpu.VMEM((768, 512), bf),
            pltpu.VMEM((1536, 512), bf),
            pltpu.VMEM((512, 3072), bf),
            pltpu.VMEM((512, 768), f32),
            pltpu.VMEM((512, 768), bf),
        ],
        compiler_params=pltpu.CompilerParams(vmem_limit_bytes=67043328),
        cost_estimate=pl.CostEstimate(flops=60_000_000_000, bytes_accessed=30_000_000, transcendentals=0),
        name="rear",
    )(*operands)


def fitted_shards(
    tokens,
    condition,
    ada_weight,
    qkv_weight,
    out_weight,
    shared_up,
    shared_down,
    router_weight,
    expert_up,
    expert_down,
    routes,
    image_sizes,
    cotangent,
):
    bf = jnp.bfloat16
    d_index, f_index = lax.axis_index("dp"), lax.axis_index("fsdp")
    model_width = tokens.shape[1]
    head_size = model_width // HEADS
    inside, segment = owners(image_sizes)
    ids = jnp.arange(EXPERTS, dtype=jnp.int32)
    hot = routes[:, :, None] == ids[None, None, :]
    hot_any = jnp.any(hot, axis=1).astype(bf)
    order = jnp.arange(LONG, dtype=jnp.int32)
    earlier = (order[:, None] > order[None, :]).astype(bf)
    before = nn(earlier, hot_any)
    position = jnp.sum(jnp.where(hot, before[:, None, :], 0.0), axis=-1).astype(jnp.int32)
    target = routes * CAP + position
    live = (segment < IMG_DEV).astype(jnp.float32)
    counts = jnp.sum(live[:, None] * hot_any.astype(jnp.float32), axis=0)
    cond_float = condition.astype(jnp.float32)
    activated = jax.nn.silu(cond_float).astype(bf)
    act_slices = activated.astype(jnp.float32).reshape(IMG_DEV, 8, 96).transpose(1, 0, 2)
    act_slices = jnp.pad(act_slices, ((0, 0), (0, 6), (0, 32)))
    act_slices = act_slices.at[:, 2, :EXPERTS].set(counts)
    ada_pad = jnp.pad(ada_weight, ((0, 32), (0, 0)))
    router_pack = jnp.pad(router_weight.reshape(192), (0, 2048 - 192)).reshape(16, 128)
    qkvo_shard = jnp.concatenate([qkv_weight, out_weight], axis=1)
    qkvo, routers, seen, mod_rows, up_line, down_line, up_m, up_x0, up_y0, down_own, down_m = opening(
        qkvo_shard, router_pack, act_slices, ada_pad, shared_up, shared_down.T, expert_up, expert_down
    )
    hops = hop(up_m, 2), hop(up_m, 4), hop(down_own, 2), hop(down_own, 4)
    expert_counts = seen[66, :EXPERTS].astype(jnp.int32)
    modulation = lax.dynamic_slice(mod_rows, (0, 2 * d_index, 0), (4, 2, 1152))
    modulation = modulation.transpose(1, 0, 2).reshape(2, 4608)
    router_full = (
        routers.reshape(32, 2048)[:, :192]
        .reshape(4, 8, 96, 2)
        .transpose(1, 2, 0, 3)
        .reshape(model_width, EXPERTS)
    )
    segments = (segment[:, None], segment[None, :])
    heads, totals, attended, projected, residual, second_input, d_mixed, gates, rows, grads = front(
        tokens, modulation, inside, *segments, qkvo, router_full, cotangent, routes, target.T
    )
    rows = rows.reshape(EXPERTS, CAP, model_width)
    grads = grads.reshape(EXPERTS, CAP, model_width)
    rows, (up_x1, up_y1, down_x0, down_y0) = lax.optimization_barrier((rows, hops))
    rows_in, grads_in, up_corner, down_x1, down_y1, down_corner, shared_out, d_second, *shared_grads = (
        outbound(
            rows, grads, up_line, down_line, second_input, d_mixed, up_x0, up_y1, down_m, down_x0
        )
    )
    returned, d_returned, up_keep, *up_near, down_keep, down_x, down_y, first_part, second_part = experts(
        rows_in, grads_in, (expert_up, up_m, up_x0, up_x1, up_y0, up_y1, up_corner),
        (down_own, down_m, down_x0, down_x1, down_y0, down_y1, down_corner),
        *shared_grads,
    )
    up_next = square_next(up_keep, *up_near)
    down_near = hop(down_x, 2), hop(down_y, 4)
    returned = returned.reshape(EXPERTS * CAP, model_width)
    d_returned = d_returned.reshape(EXPERTS * CAP, model_width)
    output, tokens_grad, qkvo_grad, d_modulation, router_grad = rear(
        tokens, modulation, inside, *segments, qkvo, router_full, cotangent, routes, target,
        heads, totals, attended, projected, residual, second_input, gates,
        returned, d_returned, shared_out, d_second,
    )
    qkvo_grad, down_near, up_next = lax.optimization_barrier((qkvo_grad, down_near, up_next))
    d_modulation = d_modulation.astype(bf)
    d_mod_rows = d_modulation.astype(jnp.float32).reshape(2, 4, 1152).transpose(1, 0, 2)
    d_mod_rows = lax.dynamic_update_slice(
        jnp.zeros((4, 8, 1152), jnp.float32), d_mod_rows, (0, 2 * d_index, 0)
    )
    router_tiles = jnp.pad(
        router_grad.reshape(EXPERTS, 8, 96).transpose(1, 0, 2), ((0, 0), (0, 0), (0, 32))
    )
    (
        qkvo_sum, shared_first_sum, shared_second_sum, ada_grad, d_act_tiles, router_sum,
        expert_up_grad, expert_down_grad,
    ) = dense_sums(
        qkvo_grad, first_part, second_part,
        (d_mod_rows, router_tiles, seen[:64].astype(bf), ada_weight),
        (up_keep, *up_near, *up_next, down_keep, *down_near),
    )
    d_activated = lax.dynamic_slice(d_act_tiles, (0, 2 * d_index, 0), (8, 2, 96))
    d_activated = d_activated.transpose(1, 0, 2).reshape(2, model_width)
    condition_grad = jax.vjp(jax.nn.silu, cond_float)[1](d_activated)[0]
    router_out = lax.dynamic_slice(router_sum, (2 * d_index, 0), (2, 96)).T
    return (
        output,
        tokens_grad,
        condition_grad,
        ada_grad,
        qkvo_sum[:, :576],
        qkvo_sum[:, 576:],
        shared_first_sum,
        shared_second_sum.T,
        router_out,
        expert_up_grad,
        expert_down_grad,
        expert_counts,
    )


def solution(mesh):
    placed = (
        P(("dp", "fsdp"), None),
        P(("dp", "fsdp"), None),
        P("fsdp", "dp"),
        P("fsdp", "dp"),
        P("fsdp", "dp"),
        P("fsdp", "dp"),
        P("fsdp", "dp"),
        P("fsdp", "dp"),
        P("dp", "fsdp", None),
        P("dp", "fsdp", None),
        P(("dp", "fsdp"), None),
        P(("dp", "fsdp")),
        P(("dp", "fsdp"), None),
    )
    fitted = mesh.shape["dp"] == 4 and mesh.shape["fsdp"] == 8
    return jax.shard_map(
        fitted_shards if fitted else shards,
        mesh=mesh,
        in_specs=placed,
        out_specs=(
            P(("dp", "fsdp"), None),
            P(("dp", "fsdp"), None),
            P(("dp", "fsdp"), None),
            P("fsdp", "dp"),
            P("fsdp", "dp"),
            P("fsdp", "dp"),
            P("fsdp", "dp"),
            P("fsdp", "dp"),
            P("fsdp", "dp"),
            P("dp", "fsdp", None),
            P("dp", "fsdp", None),
            P(),
        ),
        check_vma=False,
    )
```

```python
import functools

import jax
import jax.numpy as jnp
from jax import lax
from jax.experimental import pallas as pl
from jax.experimental.pallas import tpu as pltpu
from jax.sharding import PartitionSpec as P

HEADS = 12
EXPERTS = 8
CAP = 144
IMG_DEV = 2
LONG = 512
MESH = pl.DeviceIdType.MESH


EXACT = lax.Precision.HIGHEST


def owners(image_sizes):
    starts = jnp.cumsum(image_sizes) - image_sizes
    position = jnp.arange(LONG, dtype=jnp.int32)[:, None]
    inside = (position >= starts[None, :]) & (position < (starts + image_sizes)[None, :])
    slot_ids = jnp.arange(IMG_DEV, dtype=jnp.int32)
    segment = jnp.sum(jnp.where(inside, slot_ids[None, :], 0), axis=1) + jnp.where(
        jnp.any(inside, axis=1), 0, IMG_DEV
    )
    return (inside.astype(jnp.float32), segment)


def dispatch_plan(routes):
    flat = routes.reshape(-1)
    onehot = (flat[:, None] == jnp.arange(EXPERTS, dtype=jnp.int32)[None, :]).astype(jnp.int32)
    before = jnp.cumsum(onehot, axis=0) - onehot
    position = jnp.sum(before * onehot, axis=1)
    target = flat * CAP + position
    assignment = jnp.arange(2 * LONG, dtype=jnp.int32)
    source = jnp.zeros((EXPERTS * CAP,), jnp.int32).at[target].set(assignment)
    filled = jnp.zeros((EXPERTS * CAP,), jnp.int32).at[target].set(1)
    return (target, source, filled)


def layer_norm(values_in):
    centred = values_in - jnp.mean(values_in, axis=-1, keepdims=True)
    inv_std = lax.rsqrt(jnp.mean(centred * centred, axis=-1, keepdims=True) + 1e-06)
    return (centred * inv_std, inv_std)


def norm_back(upstream, normed, inv_std):
    return (
        upstream
        - jnp.mean(upstream, axis=-1, keepdims=True)
        - normed * jnp.mean(upstream * normed, axis=-1, keepdims=True)
    ) * inv_std


def gelu_tanh(values_in):
    return jax.nn.gelu(values_in, approximate=True)


def gelu_back(values_in, upstream):
    return jax.vjp(gelu_tanh, values_in)[1](upstream)[0]


def collect(first, second, third):
    widened = (
        lax.all_gather(first, "dp", axis=1, tiled=True),
        lax.all_gather(second, "dp", axis=1, tiled=True),
        lax.all_gather(third, "dp", axis=1, tiled=True),
    )
    return (
        lax.all_gather(widened[0], "fsdp", axis=0, tiled=True),
        lax.all_gather(widened[1], "fsdp", axis=0, tiled=True),
        lax.all_gather(widened[2], "fsdp", axis=0, tiled=True),
    )


def spread(first, second, third):
    row_sums = (
        lax.psum_scatter(first, "fsdp", scatter_dimension=0, tiled=True),
        lax.psum_scatter(second, "fsdp", scatter_dimension=0, tiled=True),
        lax.psum_scatter(third, "fsdp", scatter_dimension=0, tiled=True),
    )
    return (
        lax.psum_scatter(row_sums[0], "dp", scatter_dimension=1, tiled=True),
        lax.psum_scatter(row_sums[1], "dp", scatter_dimension=1, tiled=True),
        lax.psum_scatter(row_sums[2], "dp", scatter_dimension=1, tiled=True),
    )


def gather_experts(up_shard, down_shard):
    return (
        lax.all_gather(up_shard, "fsdp", axis=1, tiled=True),
        lax.all_gather(down_shard, "fsdp", axis=1, tiled=True),
    )


def expert_forward(buffer_in, up_full, down_full):
    expert_pre = jnp.einsum(
        "secd,edf->secf", buffer_in, up_full, preferred_element_type=jnp.float32
    )
    expert_act = gelu_tanh(expert_pre).astype(jnp.bfloat16)
    expert_out = jnp.einsum(
        "secf,efd->secd", expert_act, down_full, preferred_element_type=jnp.float32
    ).astype(jnp.bfloat16)
    return (expert_pre, expert_act, expert_out)


def expert_backward(buffer_in, expert_pre, expert_act, d_out, up_full, down_full):
    d_act = jnp.einsum("secd,efd->secf", d_out, down_full, preferred_element_type=jnp.float32)
    d_pre = gelu_back(expert_pre, d_act).astype(jnp.bfloat16)
    d_rows = jnp.einsum(
        "secf,edf->secd", d_pre, up_full, preferred_element_type=jnp.float32
    ).astype(jnp.bfloat16)
    down_grad = jnp.einsum("secf,secd->efd", expert_act, d_out, preferred_element_type=jnp.float32)
    up_grad = jnp.einsum("secd,secf->edf", buffer_in, d_pre, preferred_element_type=jnp.float32)
    return (up_grad, down_grad, d_rows)


def attend(queries, keys_all, values_all, segment):
    row_count, head_count, head_size = queries.shape
    block_rows = min(512, row_count)
    block_count = row_count // block_rows
    score_scale = head_size ** (-0.5)

    def one_block(pieces):
        query_part, segment_part = pieces
        allowed = (segment_part[:, None] == segment[None, :])[None]
        scores = (
            jnp.einsum("qhd,khd->hqk", query_part, keys_all, preferred_element_type=jnp.float32)
            * score_scale
        )
        scores = jnp.where(allowed, scores, -1e30)
        row_max = jnp.max(scores, axis=-1, keepdims=True)
        weight = jnp.exp(scores - row_max)
        running = jnp.sum(weight, axis=-1, keepdims=True)
        probability = (weight / running).astype(jnp.bfloat16)
        attended = jnp.einsum(
            "hqk,khd->qhd", probability, values_all, preferred_element_type=jnp.float32
        )
        return (attended.astype(jnp.bfloat16), (row_max + jnp.log(running))[:, :, 0])

    return lax.map(
        one_block,
        (
            queries.reshape(block_count, block_rows, head_count, head_size),
            segment.reshape(block_count, block_rows),
        ),
    )


def attend_back(queries, keys_all, values_all, segment, log_totals, d_attended):
    row_count, head_count, head_size = queries.shape
    block_rows = min(512, row_count)
    block_count = row_count // block_rows
    score_scale = head_size ** (-0.5)

    def one_block(carry, pieces):
        key_sum, value_sum = carry
        query_part, segment_part, total_part, grad_part = pieces
        allowed = (segment_part[:, None] == segment[None, :])[None]
        scores = (
            jnp.einsum("qhd,khd->hqk", query_part, keys_all, preferred_element_type=jnp.float32)
            * score_scale
        )
        scores = jnp.where(allowed, scores, -1e30)
        probability = jnp.exp(scores - total_part[:, :, None])
        d_prob = jnp.einsum(
            "qhd,khd->hqk", grad_part, values_all, preferred_element_type=jnp.float32
        )
        d_scores = (
            probability * (d_prob - jnp.sum(probability * d_prob, axis=-1, keepdims=True))
        ).astype(jnp.bfloat16)
        query_grad = (
            jnp.einsum("hqk,khd->qhd", d_scores, keys_all, preferred_element_type=jnp.float32)
            * score_scale
        )
        key_sum = (
            key_sum
            + jnp.einsum("hqk,qhd->khd", d_scores, query_part, preferred_element_type=jnp.float32)
            * score_scale
        )
        value_sum = value_sum + jnp.einsum(
            "hqk,qhd->khd",
            probability.astype(jnp.bfloat16),
            grad_part,
            preferred_element_type=jnp.float32,
        )
        return ((key_sum, value_sum), query_grad)

    empty = jnp.zeros(keys_all.shape, jnp.float32)
    sums, query_grads = lax.scan(
        one_block,
        (empty, empty),
        (
            queries.reshape(block_count, block_rows, head_count, head_size),
            segment.reshape(block_count, block_rows),
            log_totals,
            d_attended.reshape(block_count, block_rows, head_count, head_size),
        ),
    )
    return (query_grads.reshape(row_count, head_count, head_size), sums[0], sums[1])


def shards(
    tokens,
    condition,
    ada_weight,
    qkv_weight,
    out_weight,
    shared_up,
    shared_down,
    router_weight,
    expert_up,
    expert_down,
    routes,
    image_sizes,
    cotangent,
):
    model_width = tokens.shape[1]
    head_size = model_width // HEADS
    inside, segment = owners(image_sizes)
    target, source, filled = dispatch_plan(routes)
    route_hot = (routes[:, :, None] == jnp.arange(EXPERTS, dtype=jnp.int32)[None, None, :]).astype(
        jnp.float32
    )
    live = (segment < IMG_DEV).astype(jnp.int32)
    local_counts = jnp.sum(live[:, None, None] * route_hot.astype(jnp.int32), axis=(0, 1))
    expert_counts = lax.psum(local_counts, ("dp", "fsdp"))
    ada_full, qkv_full, out_full = collect(ada_weight, qkv_weight, out_weight)
    cond_float = condition.astype(jnp.float32)
    activated = jax.nn.silu(cond_float).astype(jnp.bfloat16)
    modulation = jnp.dot(activated, ada_full, preferred_element_type=jnp.float32)
    per_row = jnp.dot(inside, modulation, precision=EXACT, preferred_element_type=jnp.float32)
    shift_one, scale_one, gate_one, shift_two, scale_two, gate_two = jnp.split(per_row, 6, axis=1)
    token_float = tokens.astype(jnp.float32)
    normed_one, inv_one = layer_norm(token_float)
    first_input = (normed_one * (1.0 + scale_one) + shift_one).astype(jnp.bfloat16)
    qkv_rows = jnp.dot(first_input, qkv_full, preferred_element_type=jnp.float32).astype(
        jnp.bfloat16
    )
    queries = qkv_rows[:, :model_width].reshape(-1, HEADS, head_size)
    keys_all = qkv_rows[:, model_width : 2 * model_width].reshape(-1, HEADS, head_size)
    values_all = qkv_rows[:, 2 * model_width :].reshape(-1, HEADS, head_size)
    attended_blocks, log_totals = attend(queries, keys_all, values_all, segment)
    attended = attended_blocks.reshape(-1, model_width)
    projected = jnp.dot(attended, out_full, preferred_element_type=jnp.float32)
    residual_one = token_float + gate_one * projected
    normed_two, inv_two = layer_norm(residual_one)
    second_input = (normed_two * (1.0 + scale_two) + shift_two).astype(jnp.bfloat16)
    shared_first, shared_second, router_full = collect(shared_up, shared_down, router_weight)
    shared_pre = jnp.dot(second_input, shared_first, preferred_element_type=jnp.float32)
    shared_act = gelu_tanh(shared_pre).astype(jnp.bfloat16)
    shared_out = jnp.dot(shared_act, shared_second, preferred_element_type=jnp.float32)
    logits = jnp.dot(second_input, router_full, preferred_element_type=jnp.float32)
    chosen = jnp.sum(logits[:, None, :] * route_hot, axis=-1)
    gate_share = jax.nn.softmax(chosen, axis=-1)
    buffer_rows = jnp.take(second_input, source // 2, axis=0).reshape(EXPERTS, CAP, model_width)
    up_full, down_full = gather_experts(expert_up, expert_down)
    groups = lax.axis_size("dp")
    expert_in = lax.all_to_all(
        buffer_rows.reshape(groups, EXPERTS // groups, CAP, model_width),
        "dp",
        split_axis=0,
        concat_axis=0,
        tiled=True,
    )
    expert_pre, expert_act, expert_out = expert_forward(expert_in, up_full, down_full)
    returned = lax.all_to_all(expert_out, "dp", split_axis=0, concat_axis=0, tiled=True).reshape(
        EXPERTS, CAP, model_width
    )
    picked = (
        jnp.take(returned.reshape(EXPERTS * CAP, model_width), target, axis=0)
        .reshape(-1, 2, model_width)
        .astype(jnp.float32)
    )
    mixed = shared_out + jnp.sum(gate_share[:, :, None] * picked, axis=1)
    output = (residual_one + gate_two * mixed).astype(jnp.bfloat16)
    upstream = cotangent.astype(jnp.float32)
    d_mixed = gate_two * upstream
    d_gate_two = upstream * mixed
    d_gate_share = jnp.sum(d_mixed[:, None, :] * picked, axis=-1)
    slot_gate = jnp.take(gate_share.reshape(-1), source) * filled.astype(jnp.float32)
    d_buffer = (
        (jnp.take(d_mixed, source // 2, axis=0) * slot_gate[:, None])
        .astype(jnp.bfloat16)
        .reshape(EXPERTS, CAP, model_width)
    )
    shared_first, shared_second, router_full = collect(shared_up, shared_down, router_weight)
    up_full, down_full = gather_experts(expert_up, expert_down)
    arrived = lax.all_to_all(
        d_buffer.reshape(groups, EXPERTS // groups, CAP, model_width),
        "dp",
        split_axis=0,
        concat_axis=0,
        tiled=True,
    )
    up_grad, down_grad, d_rows = expert_backward(
        expert_in, expert_pre, expert_act, arrived, up_full, down_full
    )
    d_returned = lax.all_to_all(d_rows, "dp", split_axis=0, concat_axis=0, tiled=True).reshape(
        EXPERTS, CAP, model_width
    )
    expert_sums = (
        lax.psum_scatter(up_grad, "fsdp", scatter_dimension=1, tiled=True),
        lax.psum_scatter(down_grad, "fsdp", scatter_dimension=1, tiled=True),
    )
    d_shared = d_mixed.astype(jnp.bfloat16)
    shared_second_grad = jnp.einsum(
        "tf,td->fd", shared_act, d_shared, preferred_element_type=jnp.float32
    )
    d_shared_act = jnp.einsum(
        "td,fd->tf", d_shared, shared_second, preferred_element_type=jnp.float32
    )
    d_shared_pre = gelu_back(shared_pre, d_shared_act).astype(jnp.bfloat16)
    shared_first_grad = jnp.einsum(
        "td,tf->df", second_input, d_shared_pre, preferred_element_type=jnp.float32
    )
    d_chosen = gate_share * (
        d_gate_share - jnp.sum(gate_share * d_gate_share, axis=-1, keepdims=True)
    )
    d_logits = jnp.sum(d_chosen[:, :, None] * route_hot, axis=1).astype(jnp.bfloat16)
    router_grad = jnp.einsum(
        "td,te->de", second_input, d_logits, preferred_element_type=jnp.float32
    )
    from_experts = (
        jnp.take(d_returned.reshape(EXPERTS * CAP, model_width), target, axis=0)
        .reshape(-1, 2, model_width)
        .astype(jnp.float32)
    )
    d_second = (
        jnp.einsum("tf,df->td", d_shared_pre, shared_first, preferred_element_type=jnp.float32)
        + jnp.einsum("te,de->td", d_logits, router_full, preferred_element_type=jnp.float32)
        + jnp.sum(from_experts, axis=1)
    )
    mlp_sums = spread(shared_first_grad, shared_second_grad, router_grad)
    d_scale_two = d_second * normed_two
    d_residual = upstream + norm_back(d_second * (1.0 + scale_two), normed_two, inv_two)
    ada_full, qkv_full, out_full = collect(ada_weight, qkv_weight, out_weight)
    d_projected = (gate_one * d_residual).astype(jnp.bfloat16)
    d_gate_one = d_residual * projected
    out_grad = jnp.einsum("td,te->de", attended, d_projected, preferred_element_type=jnp.float32)
    d_attended = jnp.einsum(
        "te,de->td", d_projected, out_full, preferred_element_type=jnp.float32
    ).astype(jnp.bfloat16)
    d_queries, d_keys, d_values = attend_back(
        queries, keys_all, values_all, segment, log_totals, d_attended.reshape(-1, HEADS, head_size)
    )
    d_qkv = jnp.concatenate(
        [
            d_queries.reshape(-1, model_width),
            d_keys.reshape(-1, model_width),
            d_values.reshape(-1, model_width),
        ],
        axis=1,
    ).astype(jnp.bfloat16)
    qkv_grad = jnp.einsum("td,te->de", first_input, d_qkv, preferred_element_type=jnp.float32)
    d_first = jnp.einsum("te,de->td", d_qkv, qkv_full, preferred_element_type=jnp.float32)
    d_scale_one = d_first * normed_one
    tokens_grad = d_residual + norm_back(d_first * (1.0 + scale_one), normed_one, inv_one)
    d_per_row = jnp.concatenate(
        [d_first, d_scale_one, d_gate_one, d_second, d_scale_two, d_gate_two], axis=1
    )
    d_modulation = jnp.einsum(
        "tj,te->je", inside, d_per_row, precision=EXACT, preferred_element_type=jnp.float32
    ).astype(jnp.bfloat16)
    ada_grad = jnp.einsum("jd,je->de", activated, d_modulation, preferred_element_type=jnp.float32)
    d_activated = jnp.einsum(
        "je,de->jd", d_modulation, ada_full, preferred_element_type=jnp.float32
    )
    condition_grad = jax.vjp(jax.nn.silu, cond_float)[1](d_activated)[0]
    attn_sums = spread(ada_grad, qkv_grad, out_grad)
    return (
        output,
        tokens_grad,
        condition_grad,
        attn_sums[0],
        attn_sums[1],
        attn_sums[2],
        mlp_sums[0],
        mlp_sums[1],
        mlp_sums[2],
        expert_sums[0],
        expert_sums[1],
        expert_counts,
    )


def at(d, s, c):
    return (d, 2 * s + c)


def slot(kind, f, d):
    if kind == "cols":
        return (pl.ds(pl.multiple_of(96 * f, 96), 96), pl.ds(pl.multiple_of(768 * d, 768), 768))
    return (pl.ds(pl.multiple_of(192 * d, 192), 192), pl.ds(pl.multiple_of(384 * f, 384), 384))


def half_slot(kind, f, d, h):
    if kind == "cols":
        return (
            pl.ds(pl.multiple_of(96 * f, 96), 96),
            pl.ds(pl.multiple_of(768 * d + 384 * h, 384), 384),
        )
    return (
        pl.ds(pl.multiple_of(192 * d + 96 * h, 96), 96),
        pl.ds(pl.multiple_of(384 * f, 384), 384),
    )


def place():
    d = lax.axis_index("dp")
    f = lax.axis_index("fsdp")
    return d, f // 2, lax.rem(f, 2)


def flip(v, bit):
    return v + bit - 2 * bit * lax.rem(v // bit, 2)


def greet(devices):
    barrier = pltpu.get_barrier_semaphore()
    for device in devices:
        pl.semaphore_signal(barrier, inc=1, device_id=device, device_id_type=MESH)
    pl.semaphore_wait(barrier, len(devices))


def push(src, dst, send_sem, recv_sem, device):
    return pltpu.make_async_remote_copy(
        src_ref=src,
        dst_ref=dst,
        send_sem=send_sem,
        recv_sem=recv_sem,
        device_id=device,
        device_id_type=MESH,
    )


GATHER_SEMS = 3 + 8 + 8 + 20


class Gather:
    def __init__(self, kind, shard, full, ssem, rsem, lsem):
        self.kind, self.shard, self.full = kind, shard, full
        self.ssem, self.rsem, self.lsem = ssem, rsem, lsem
        self.d, self.s, self.c = place()
        self.sent = []

    def f(self, s):
        return 2 * s + self.c

    def go(self, index, where, device, src=None):
        ref = self.full.at[where]
        copy = push(
            ref if src is None else src, ref, self.ssem.at[index], self.rsem.at[index], device
        )
        copy.start()
        self.sent.append(copy)

    def arrived(self, index, where):
        ref = self.full.at[where]
        push(ref, ref, self.ssem.at[index], self.rsem.at[index], at(self.d, self.s, self.c)).wait_recv()

    def start(self):
        d, s, c = self.d, self.s, self.c
        mine = slot(self.kind, self.f(s), d)
        self.own = pltpu.make_async_copy(self.shard, self.full.at[mine], self.lsem)
        self.own.start()
        self.go(1, mine, at(flip(d, 2), s, c), self.shard)
        self.go(0, mine, at(flip(d, 1), s, c), self.shard)
        self.go(3, mine, at(d, flip(s, 1), c), self.shard)
        self.go(4, mine, at(d, flip(s, 2), c), self.shard)
        self.go(19, mine, at(d, s, 1 - c), self.shard)

    def source(self, k):
        return (self.d, flip(self.d, 1), flip(self.d, 2), flip(flip(self.d, 1), 2))[k]

    def spread_z(self, k):
        d, s, c = self.d, self.s, self.c
        block = slot(self.kind, self.f(s), self.source(k))
        self.arrived(k - 1, block)
        if k == 2:
            self.go(2, block, at(flip(d, 1), s, c))
        self.go(3 + 2 * k, block, at(d, flip(s, 1), c))
        self.go(4 + 2 * k, block, at(d, flip(s, 2), c))
        self.go(19 + 5 * k, block, at(d, s, 1 - c))

    def relay(self, k):
        d, s, c = self.d, self.s, self.c
        source = self.source(k)
        sx, sy = flip(s, 1), flip(s, 2)
        from_x = slot(self.kind, self.f(sx), source)
        from_y = slot(self.kind, self.f(sy), source)
        self.arrived(3 + 2 * k, from_x)
        self.go(11 + 2 * k, half_slot(self.kind, self.f(sx), source, 0), at(d, sy, c))
        self.go(20 + 5 * k, from_x, at(d, s, 1 - c))
        self.arrived(4 + 2 * k, from_y)
        self.go(12 + 2 * k, half_slot(self.kind, self.f(sy), source, 1), at(d, sx, c))
        self.go(21 + 5 * k, from_y, at(d, s, 1 - c))

    def corner(self, k):
        d, s, c = self.d, self.s, self.c
        source = self.source(k)
        sd = flip(flip(s, 1), 2)
        for h in range(2):
            where = half_slot(self.kind, self.f(sd), source, h)
            self.arrived(11 + 2 * k + h, where)
            self.go(22 + 5 * k + h, where, at(d, s, 1 - c))

    def finish(self):
        d, s, c = self.d, self.s, self.c
        sx, sy = flip(s, 1), flip(s, 2)
        sd = flip(sx, 2)
        self.own.wait()
        for k in range(4):
            source = self.source(k)
            for j, position in enumerate((s, sx, sy)):
                self.arrived(19 + 5 * k + j, slot(self.kind, 2 * position + 1 - c, source))
            for h in range(2):
                self.arrived(22 + 5 * k + h, half_slot(self.kind, 2 * sd + 1 - c, source, h))
        for copy in self.sent:
            copy.wait_send()


class Line:
    def __init__(self, kind, shard, line, ssem, rsem, lsem):
        self.kind, self.shard, self.line = kind, shard, line
        self.ssem, self.rsem, self.lsem = ssem, rsem, lsem
        self.d, self.s, self.c = place()

    def block(self, d):
        if self.kind == "cols":
            return self.line.at[:, pl.ds(pl.multiple_of(768 * d, 768), 768)]
        return self.line.at[pl.ds(pl.multiple_of(192 * d, 192), 192)]

    def copy(self, index, src, source, target):
        return push(
            src, self.block(source), self.ssem.at[index], self.rsem.at[index], at(target, self.s, self.c)
        )

    def start(self):
        d = self.d
        self.own = pltpu.make_async_copy(self.shard, self.block(d), self.lsem)
        self.own.start()
        self.sent = [
            self.copy(0, self.shard, d, flip(d, 2)),
            self.copy(1, self.shard, d, flip(d, 1)),
        ]
        for copy in self.sent:
            copy.start()

    def relay(self):
        d2 = flip(self.d, 2)
        self.copy(0, self.shard, d2, d2).wait_recv()
        copy = self.copy(2, self.block(d2), d2, flip(self.d, 1))
        copy.start()
        self.sent.append(copy)

    def finish(self):
        d1 = flip(self.d, 1)
        self.own.wait()
        self.copy(1, self.shard, d1, d1).wait_recv()
        self.copy(2, self.shard, flip(d1, 2), d1).wait_recv()
        for copy in self.sent:
            copy.wait_send()


class Spread:
    def __init__(self, kind, line, full, ssem, rsem, lsem):
        self.kind, self.line, self.full = kind, line, full
        self.ssem, self.rsem, self.lsem = ssem, rsem, lsem
        self.d, self.s, self.c = place()
        self.sx, self.sy = flip(self.s, 1), flip(self.s, 2)
        self.sd = flip(self.sx, 2)
        self.mate = at(self.d, self.s, 1 - self.c)
        self.to_x, self.to_y = at(self.d, self.sx, self.c), at(self.d, self.sy, self.c)
        self.sent = []

    def block(self, position, c, h=None):
        f = 2 * position + c
        if self.kind == "cols":
            rows = pl.ds(pl.multiple_of(96 * f, 96), 96)
            return self.full.at[rows] if h is None else self.full.at[rows, pl.ds(1536 * h, 1536)]
        columns = pl.ds(pl.multiple_of(384 * f, 384), 384)
        rows = pl.ds(0, 768) if h is None else pl.ds(384 * h, 384)
        return self.full.at[rows, columns]

    def go(self, index, ref, device, src=None):
        copy = push(
            ref if src is None else src, ref, self.ssem.at[index], self.rsem.at[index], device
        )
        copy.start()
        self.sent.append(copy)

    def arrived(self, index, ref):
        push(ref, ref, self.ssem.at[index], self.rsem.at[index], self.mate).wait_recv()

    def start(self):
        mine = self.block(self.s, self.c)
        self.own = pltpu.make_async_copy(self.line, mine, self.lsem)
        self.own.start()
        self.go(0, mine, self.to_x, self.line)
        self.go(1, mine, self.to_y, self.line)
        self.go(2, mine, self.mate, self.line)

    def relay(self):
        c = self.c
        from_x, from_y = self.block(self.sx, c), self.block(self.sy, c)
        self.arrived(0, from_x)
        self.go(3, self.block(self.sx, c, 0), self.to_y)
        self.go(5, from_x, self.mate)
        self.arrived(1, from_y)
        self.go(4, self.block(self.sy, c, 1), self.to_x)
        self.go(6, from_y, self.mate)

    def corner(self):
        for h in range(2):
            ref = self.block(self.sd, self.c, h)
            self.arrived(3 + h, ref)
            self.go(7 + h, ref, self.mate)

    def finish(self):
        c = 1 - self.c
        self.own.wait()
        self.arrived(2, self.block(self.s, c))
        self.arrived(5, self.block(self.sx, c))
        self.arrived(6, self.block(self.sy, c))
        for h in range(2):
            self.arrived(7 + h, self.block(self.sd, c, h))
        for copy in self.sent:
            copy.wait_send()


class Near:
    def __init__(self, up_shard, down_shard, up_mate, up_x, up_y, down_own, down_mate, ssem, rsem, lsem):
        d, s, c = place()
        self.local = pltpu.make_async_copy(down_shard.at[c], down_own, lsem)
        plan = (
            (up_shard, c, up_x, flip(s, 1)),
            (up_shard, c, up_y, flip(s, 2)),
            (up_shard, 1 - c, up_mate, s),
            (down_shard, 1 - c, down_mate, s),
        )
        self.away = [
            push(shard.at[which], out, ssem.at[i], rsem.at[i], at(d, position, which))
            for i, (shard, which, out, position) in enumerate(plan)
        ]

    def start(self):
        for copy in self.away + [self.local]:
            copy.start()

    def finish(self):
        for copy in self.away + [self.local]:
            copy.wait()


class Pair:
    def __init__(self, over_x, into_x, over_y, into_y, ssem, rsem):
        d, s, c = place()
        self.copies = [
            push(over_x, into_x, ssem.at[0], rsem.at[0], at(d, flip(s, 1), c)),
            push(over_y, into_y, ssem.at[1], rsem.at[1], at(d, flip(s, 2), c)),
        ]

    def start(self):
        for copy in self.copies:
            copy.start()

    def finish(self):
        for copy in self.copies:
            copy.wait()


def everyone_else():
    me = lax.axis_index("dp") * 8 + lax.axis_index("fsdp")

    def other(k):
        device = lax.rem(me + k, 32)
        return (device // 8, lax.rem(device, 8))

    return me, other


def open_kernel(
    qkv_shard, out_shard, act_ref, ada_ref, up_shard, down_shard, expert_up, expert_down,
    full, router_t, seen, rows_out, up_line, down_line, up_mate, up_x, up_y, down_own, down_mate,
    shard, heard, part, got, mixed, ssem, rsem, lsem, asem, brsem, tssem, trsem, zssem, zrsem,
    us, ur, ds, dr, es, er, el,
):
    me, other = everyone_else()
    d, s, c = place()
    f = 2 * s + c
    shard[:, 0:576] = qkv_shard[...]
    shard[:, 576:768] = out_shard[...]
    barrier = pltpu.get_barrier_semaphore()

    def hello(k, carry):
        pl.semaphore_signal(barrier, inc=1, device_id=other(k), device_id_type=MESH)
        return carry

    lax.fori_loop(1, 32, hello, 0)
    pl.semaphore_wait(barrier, 31)

    def act_copy(k, source):
        device = other(k)
        return push(act_ref.at[device[1]], heard.at[source], asem.at[k], brsem.at[k], device)

    def send(k, carry):
        act_copy(k, me).start()
        return carry

    lax.fori_loop(1, 32, send, 0)
    gather = Gather("cols", shard, full, ssem, rsem, lsem.at[0])
    gather.start()
    near = Near(
        expert_up, expert_down, up_mate, up_x, up_y, down_own, down_mate, es, er, el.at[0]
    )
    lines = (
        Line("cols", up_shard, up_line, us, ur, lsem.at[3]),
        Line("rows", down_shard, down_line, ds, dr, lsem.at[4]),
    )
    gather.spread_z(1)
    gather.spread_z(2)
    heard[me] = act_ref[f]

    def take(k, carry):
        copy = act_copy(k, lax.rem(me + 32 - k, 32))
        copy.wait_recv()
        return carry

    lax.fori_loop(1, 32, take, 0)
    everything = heard[...].reshape(256, 128)
    row = lax.broadcasted_iota(jnp.int32, (64, 256), 0)
    column = lax.broadcasted_iota(jnp.int32, (64, 256), 1)
    source = lax.rem(row // 2, 4) * 8 + row // 8
    pick = (column == source * 8 + lax.rem(row, 2)).astype(jnp.bfloat16)
    compact = jnp.dot(
        pick, everything.astype(jnp.bfloat16), preferred_element_type=jnp.float32
    ).astype(jnp.bfloat16)
    seen[...] = jnp.concatenate(
        [compact.astype(jnp.float32), jnp.sum(heard[...], axis=0)], axis=0
    )
    for column_block in range(8):
        tiles = [heard[8 * j + column_block, 3:5, 0:96] for j in range(4)]
        router_t[:, 96 * column_block : 96 * column_block + 96] = jnp.concatenate(tiles, axis=0)
    part[...] = nn(compact[:, 0:96], ada_ref[...]).reshape(8, 8, 1152)

    def tile_copy(k):
        target = lax.rem(f + k, 8)
        return push(part.at[target], got.at[k], tssem.at[k], trsem.at[k], (d, target))

    for k in range(1, 8):
        tile_copy(k).start()
    gather.relay(0)
    gather.spread_z(3)
    near.start()
    gather.relay(1)
    gather.relay(2)
    for k in range(1, 8):
        tile_copy(k).wait_recv()
    total = part[f]
    for k in range(1, 8):
        total = total + got[k]
    mixed[...] = total
    zs = []
    for k in range(1, 4):
        copy = push(mixed, rows_out.at[d], zssem.at[k], zrsem.at[k], at(lax.rem(d + k, 4), s, c))
        copy.start()
        zs.append(copy)
    own_rows = pltpu.make_async_copy(mixed, rows_out.at[d], lsem.at[2])
    own_rows.start()
    for line in lines:
        line.start()
    gather.relay(3)
    gather.corner(0)
    gather.corner(1)
    gather.corner(2)
    for line in lines:
        line.relay()
    gather.corner(3)
    gather.finish()
    for line in lines:
        line.finish()
    near.finish()
    own_rows.wait()
    for k in range(1, 4):
        push(
            mixed, rows_out.at[lax.rem(d + 4 - k, 4)], zssem.at[k], zrsem.at[k],
            at(lax.rem(d + k, 4), s, c),
        ).wait_recv()
    for copy in zs:
        copy.wait_send()
    for k in range(1, 8):
        tile_copy(k).wait_send()

    def drain(k, carry):
        act_copy(k, me).wait_send()
        return carry

    lax.fori_loop(1, 32, drain, 0)


DMA = pltpu.SemaphoreType.DMA
ANYWHERE = pl.BlockSpec(memory_space=pl.ANY)
ONCHIP = pl.BlockSpec(memory_space=pltpu.VMEM)


def opening(*operands):
    return pl.pallas_call(
        open_kernel,
        out_shape=(
            jax.ShapeDtypeStruct((768, 3072), jnp.bfloat16),
            jax.ShapeDtypeStruct((8, 768), jnp.float32),
            jax.ShapeDtypeStruct((72, 128), jnp.float32),
            jax.ShapeDtypeStruct((4, 8, 1152), jnp.float32),
            jax.ShapeDtypeStruct((96, 3072), jnp.bfloat16),
            jax.ShapeDtypeStruct((768, 384), jnp.bfloat16),
        )
        + (jax.ShapeDtypeStruct((96, 3072), jnp.bfloat16),) * 3
        + (jax.ShapeDtypeStruct((384, 768), jnp.bfloat16),) * 2,
        in_specs=[ONCHIP] * 6 + [ANYWHERE] * 2,
        out_specs=(ANYWHERE, ONCHIP, ONCHIP) + (ANYWHERE,) * 8,
        scratch_shapes=[
            pltpu.VMEM((96, 768), jnp.bfloat16),
            pltpu.VMEM((32, 8, 128), jnp.float32),
            pltpu.VMEM((8, 8, 1152), jnp.float32),
            pltpu.VMEM((8, 8, 1152), jnp.float32),
            pltpu.VMEM((8, 1152), jnp.float32),
            DMA((GATHER_SEMS,)), DMA((GATHER_SEMS,)), DMA((5,)),
            DMA((32,)), DMA((32,)),
            DMA((8,)), DMA((8,)), DMA((4,)), DMA((4,)),
            DMA((3,)), DMA((3,)), DMA((3,)), DMA((3,)),
            DMA((4,)), DMA((4,)), DMA((1,)),
        ],
        compiler_params=pltpu.CompilerParams(collective_id=0, has_side_effects=True),
        name="opening",
    )(*operands)


def group_of(d, s, c):
    return [(j, at(lax.rem(d + j // 2, 4), s, lax.rem(c + j, 2))) for j in range(1, 8)]


class Swap:
    def __init__(self, blocks, out, ssem, rsem, lsem):
        self.blocks, self.out, self.ssem, self.rsem, self.lsem = blocks, out, ssem, rsem, lsem
        self.d, self.s, self.c = place()
        self.me = 2 * self.d + self.c

    def copy(self, j, landing):
        target_d = lax.rem(self.d + j // 2, 4)
        target_c = lax.rem(self.c + j, 2)
        return push(
            self.blocks.at[2 * target_d + target_c],
            self.out.at[landing],
            self.ssem.at[j],
            self.rsem.at[j],
            at(target_d, self.s, target_c),
        )

    def start(self):
        for j in (4, 5, 2, 3, 6, 7, 1):
            self.copy(j, self.me).start()
        self.own = pltpu.make_async_copy(
            self.blocks.at[self.me], self.out.at[self.me], self.lsem
        )
        self.own.start()

    def send(self, step):
        for j in (2 * step, 2 * step + 1):
            if j:
                self.copy(j, self.me).start()
            else:
                self.own = pltpu.make_async_copy(
                    self.blocks.at[self.me], self.out.at[self.me], self.lsem
                )
                self.own.start()

    def finish(self):
        self.own.wait()
        for j in range(1, 8):
            source_d = lax.rem(self.d + 4 - j // 2, 4)
            source_c = lax.rem(self.c + j, 2)
            copy = self.copy(j, 2 * source_d + source_c)
            copy.wait_recv()
            copy.wait_send()


def nt(left, right):
    return lax.dot_general(left, right, (((1,), (1,)), ((), ())), preferred_element_type=jnp.float32)


def tn(left, right):
    return lax.dot_general(left, right, (((0,), (0,)), ((), ())), preferred_element_type=jnp.float32)


def nn(left, right):
    return jnp.dot(left, right, preferred_element_type=jnp.float32)


GELU_SCALE = 0.7978845608028654


def gelu_pair(v):
    square = v * v
    bend = jnp.tanh(GELU_SCALE * (v + 0.044715 * (square * v)))
    half = 0.5 * (1.0 + bend)
    slope = half + 0.5 * v * (1.0 - bend * bend) * (
        GELU_SCALE * (1.0 + (3.0 * 0.044715) * square)
    )
    return v * half, slope


HIDDEN = 512


def out_kernel(
    rows, grads, up_line, down_line, tokens, d_tokens, up_x, up_y, down_mate, down_x,
    rows_in, grads_in, up_corner, down_x_mate, down_y_mate, down_corner, mixed_out, d_tokens_out, up_grad, down_grad,
    up_full, down_full, tokens_t, d_tokens_t, s1, r1, s2, r2, ssem, rsem, ssem2, rsem2, lsem,
    es, er, fs, fr, gs, gr,
):
    d, s, c = place()
    greet([device for _, device in group_of(d, s, c)] + [at(d, flip(s, 1), c), at(d, flip(s, 2), c)])
    both = (
        Spread("cols", up_line, up_full, ssem, rsem, lsem.at[0]),
        Spread("rows", down_line, down_full, ssem2, rsem2, lsem.at[1]),
    )
    swap_a = Swap(rows, rows_in, s1, r1, lsem.at[2])
    swap_b = Swap(grads, grads_in, s2, r2, lsem.at[3])
    for g in both:
        g.start()
    swap_a.start()
    swap_b.start()
    mates = Pair(down_mate, down_x_mate, down_mate, down_y_mate, gs, gr)
    up_corners = Pair(up_y, up_corner.at[1], up_x, up_corner.at[0], es, er)
    down_corners = Pair(down_y_mate, down_corner.at[1], down_x, down_corner.at[0], fs, fr)
    tokens_t[...] = tokens[...].T
    d_tokens_t[...] = d_tokens[...].T
    mixed_out[...] = jnp.zeros_like(mixed_out)
    d_tokens_out[...] = jnp.zeros_like(d_tokens_out)
    for g in both:
        g.relay()
    mates.start()
    up_corners.start()
    for g in both:
        g.corner()
    for g in both:
        g.finish()

    def block(b, carry):
        where = pl.ds(pl.multiple_of(b * HIDDEN, HIDDEN), HIDDEN)
        up, down = up_full[:, where], down_full[:, where]
        act, slope = gelu_pair(nn(tokens[...], up))
        act = act.astype(jnp.bfloat16)
        mixed_out[...] += nt(act, down)
        down_grad[:, where] = nn(d_tokens_t[...], act).astype(jnp.bfloat16)
        d_pre = (slope * nn(d_tokens[...], down)).astype(jnp.bfloat16)
        d_tokens_out[...] += nt(d_pre, up)
        up_grad[:, where] = nn(tokens_t[...], d_pre).astype(jnp.bfloat16)
        return carry

    lax.fori_loop(0, 1, block, 0)
    mates.finish()
    down_corners.start()
    lax.fori_loop(1, 3072 // HIDDEN, block, 0)
    swap_a.finish()
    swap_b.finish()
    up_corners.finish()
    down_corners.finish()


def outbound(*operands):
    bf, f32 = jnp.bfloat16, jnp.float32
    return pl.pallas_call(
        out_kernel,
        out_shape=(
            jax.ShapeDtypeStruct((8, 144, 768), bf),
            jax.ShapeDtypeStruct((8, 144, 768), bf),
            jax.ShapeDtypeStruct((2, 96, 3072), bf),
            jax.ShapeDtypeStruct((384, 768), bf),
            jax.ShapeDtypeStruct((384, 768), bf),
            jax.ShapeDtypeStruct((2, 384, 768), bf),
            jax.ShapeDtypeStruct((512, 768), f32),
            jax.ShapeDtypeStruct((512, 768), f32),
            jax.ShapeDtypeStruct((768, 3072), bf),
            jax.ShapeDtypeStruct((768, 3072), bf),
        ),
        in_specs=[ONCHIP] * 6 + [ANYWHERE] * 4,
        out_specs=(ANYWHERE,) * 6 + (ONCHIP,) * 4,
        scratch_shapes=[pltpu.VMEM((768, 3072), bf)] * 2
        + [pltpu.VMEM((768, 512), bf)] * 2
        + [DMA((8,))] * 4
        + [DMA((9,))] * 4
        + [DMA((4,))]
        + [DMA((2,))] * 6,
        compiler_params=pltpu.CompilerParams(
            collective_id=1, has_side_effects=True, vmem_limit_bytes=60 << 20
        ),
        name="outbound",
    )(*operands)


def widened(ref):
    return ref[...].astype(jnp.float32)


class Parts:
    def __init__(self, grad, keep, over_x, over_y, sem, rsem=None):
        d, s, c = place()
        sx, sy = flip(s, 1), flip(s, 2)
        sd = flip(sx, 2)
        rows = grad.shape[0] // 8
        slots = (
            (s, 0, keep.at[0, 0], s), (sy, 0, keep.at[0, 1], s),
            (s, 1, keep.at[1, 0], s), (sx, 1, keep.at[1, 1], s),
            (sx, 0, over_x.at[0], sx), (sd, 0, over_x.at[1], sx),
            (sy, 1, over_y.at[0], sy), (sd, 1, over_y.at[1], sy),
        )
        self.copies, self.away = [], []
        for i, (position, h, out, target) in enumerate(slots):
            part = grad.at[pl.ds(pl.multiple_of((2 * position + h) * rows, 32), rows)]
            if i < 4 or rsem is None:
                self.copies.append(pltpu.make_async_copy(part, out, sem.at[i]))
            else:
                self.away.append(push(part, out, sem.at[i], rsem.at[i], at(d, target, c)))

    def start(self):
        for copy in self.away + self.copies:
            copy.start()

    def finish(self):
        for copy in self.copies + self.away:
            copy.wait()


class Pieces:
    def __init__(self, parts, full, sem):
        d, s, c = place()
        rows = full.shape[0] // 8
        sx, sy = flip(s, 1), flip(s, 2)
        positions = [p for p in (s, sx, sy, flip(sx, 2)) for _ in range(2)]
        self.copies = [
            pltpu.make_async_copy(
                part,
                full.at[pl.ds(pl.multiple_of(rows * (2 * p + (c if i % 2 == 0 else 1 - c)), 32), rows)],
                sem.at[i],
            )
            for i, (p, part) in enumerate(zip(positions, parts))
        ]

    def start(self):
        for copy in self.copies:
            copy.start()

    def finish(self):
        for copy in self.copies:
            copy.wait()


def expert_kernel(
    rows, grads, expert_up, up_m, up_x0, up_x1, up_y0, up_y1, up_corner,
    down_own, down_m, down_x0, down_x1, down_y0, down_y1, down_corner, first_grad, second_grad,
    rows_back, grads_back, up_keep, up_x, up_y, down_keep, down_x, down_y, first_part, second_part,
    up, down, act, d_pre, made, d_made, total, d_total, up_grad, down_grad, rows_t,
    fo, fm, fn, ff, fs, fr, fl, so, sm, sn, sf, ss, sr, sl,
    s1, r1, s2, r2, lsem, wsem, vsem, psem, arsem, qsem,
):
    bf = jnp.bfloat16
    d, s, c = place()
    weights = (
        Pieces(
            (expert_up.at[c], up_m, up_x0, up_x1, up_y0, up_y1, up_corner.at[0], up_corner.at[1]), up, wsem
        ),
        Pieces(
            (down_own, down_m, down_x0, down_x1, down_y0, down_y1, down_corner.at[0], down_corner.at[1]),
            down, vsem,
        ),
    )
    for each in weights:
        each.start()
    greet([device for _, device in group_of(d, s, c)] + [at(d, flip(s, 1), c), at(d, flip(s, 2), c)])
    sums = (
        DenseSum("cols", first_grad, first_part, fo, fm, fn, ff, None, fs, fr, fl),
        DenseSum("rows", second_grad, second_part, so, sm, sn, sf, None, ss, sr, sl),
    )
    for each in sums:
        each.start()
    swap_a = Swap(made, rows_back, s1, r1, lsem.at[0])
    swap_b = Swap(d_made, grads_back, s2, r2, lsem.at[1])
    for each in weights:
        each.finish()
    for step in (2, 1, 3, 0):
        there = lax.rem(d + step, 4)
        chunk = pl.ds(2 * there, 2)
        lines = pl.ds(pl.multiple_of(288 * there, 288), 288)
        x = rows[chunk].reshape(288, 768)
        g = grads[chunk].reshape(288, 768)
        total[...] = jnp.zeros_like(total)
        d_total[...] = jnp.zeros_like(d_total)

        def block(b, carry):
            where = pl.ds(pl.multiple_of(b * HIDDEN, HIDDEN), HIDDEN)
            up_part, down_part = up[:, where], down[where]
            made_act, slope = gelu_pair(nn(x, up_part))
            made_act = made_act.astype(bf)
            act[lines, where] = made_act
            total[...] += nn(made_act, down_part)
            d_part = (slope * nt(g, down_part)).astype(bf)
            d_pre[lines, where] = d_part
            d_total[...] += nt(d_part, up_part)
            return carry

        lax.fori_loop(0, 3072 // HIDDEN, block, 0)
        made[chunk] = total[...].astype(bf).reshape(2, 144, 768)
        d_made[chunk] = d_total[...].astype(bf).reshape(2, 144, 768)
        swap_a.send(step)
        swap_b.send(step)
        if step == 2:
            for each in sums:
                each.merge()
        if step == 3:
            for each in sums:
                each.join()
    rows_t[...] = rows.reshape(1152, 768)[...].T
    g_all = grads.reshape(1152, 768)

    def up_block(b, carry):
        where = pl.ds(pl.multiple_of(b * HIDDEN, HIDDEN), HIDDEN)
        up_grad[:, where] = nn(rows_t[...], d_pre[:, where]).astype(bf)
        return carry

    def down_block(b, carry):
        where = pl.ds(pl.multiple_of(384 * b, 384), 384)
        down_grad[where] = tn(act[:, where], g_all[...]).astype(bf)
        return carry

    up_parts = Parts(up_grad, up_keep, up_x, up_y, psem, arsem)
    down_parts = Parts(down_grad, down_keep, down_x, down_y, qsem)
    lax.fori_loop(0, 3072 // HIDDEN, up_block, 0)
    up_parts.start()
    lax.fori_loop(0, 8, down_block, 0)
    down_parts.start()
    for each in sums:
        each.close()
    swap_a.finish()
    swap_b.finish()
    up_parts.finish()
    down_parts.finish()


def experts(rows, grads, up_pieces, down_pieces, first_grad, second_grad):
    bf, f32 = jnp.bfloat16, jnp.float32

    def rooms(piece, half):
        return [
            pltpu.VMEM((4,) + piece, bf),
            pltpu.VMEM((4,) + piece, bf),
            pltpu.VMEM((2,) + half, bf),
            pltpu.VMEM((2,) + piece, bf),
            DMA((8,)),
            DMA((8,)),
            DMA((4,)),
        ]

    def parts(r, n):
        return (
            jax.ShapeDtypeStruct((2, 2, r, n), bf),
            jax.ShapeDtypeStruct((2, r, n), bf),
            jax.ShapeDtypeStruct((2, r, n), bf),
        )

    return pl.pallas_call(
        expert_kernel,
        out_shape=(
            jax.ShapeDtypeStruct((8, 144, 768), bf),
            jax.ShapeDtypeStruct((8, 144, 768), bf),
        )
        + parts(96, 3072)
        + parts(384, 768)
        + (
            jax.ShapeDtypeStruct((96, 3072), bf),
            jax.ShapeDtypeStruct((768, 384), bf),
        ),
        in_specs=[ONCHIP, ONCHIP] + [ANYWHERE] * 16,
        out_specs=(ANYWHERE,) * 8 + (ONCHIP, ONCHIP),
        scratch_shapes=[
            pltpu.VMEM((768, 3072), bf),
            pltpu.VMEM((3072, 768), bf),
            pltpu.VMEM((1152, 3072), bf),
            pltpu.VMEM((1152, 3072), bf),
            pltpu.VMEM((8, 144, 768), bf),
            pltpu.VMEM((8, 144, 768), bf),
            pltpu.VMEM((288, 768), f32),
            pltpu.VMEM((288, 768), f32),
            pltpu.VMEM((768, 3072), bf),
            pltpu.VMEM((3072, 768), bf),
            pltpu.VMEM((768, 1152), bf),
        ]
        + rooms((96, 3072), (96, 1536))
        + rooms((768, 384), (384, 384))
        + [DMA((8,))] * 4
        + [DMA((2,)), DMA((8,)), DMA((8,)), DMA((8,)), DMA((8,)), DMA((8,))],
        compiler_params=pltpu.CompilerParams(
            collective_id=2, has_side_effects=True, vmem_limit_bytes=67043328
        ),
        name="experts",
    )(rows, grads, *up_pieces, *down_pieces, first_grad, second_grad)


def hop(values, bit):
    return lax.ppermute(values, "fsdp", [(f, f ^ bit) for f in range(8)])


def square_next(keep, from_x, from_y):
    f32, bf = jnp.float32, jnp.bfloat16
    return (
        hop((keep[0, 1].astype(f32) + from_x[1].astype(f32)).astype(bf), 4),
        hop((keep[1, 1].astype(f32) + from_y[1].astype(f32)).astype(bf), 2),
    )


class DenseSum:
    def __init__(self, kind, grad, out, own, mate, near, far, line, ssem, rsem, lsem):
        self.kind, self.grad, self.out = kind, grad, out
        self.own, self.mate, self.near, self.far, self.line = own, mate, near, far, line
        self.ssem, self.rsem, self.lsem = ssem, rsem, lsem
        self.d, self.s, self.c = place()
        self.order = (
            flip(flip(self.s, 1), 2),
            flip(self.s, 1),
            flip(self.s, 2),
            self.s,
        )

    def piece(self, f):
        if self.kind == "cols":
            return self.grad.at[pl.ds(pl.multiple_of(96 * f, 96), 96)]
        return self.grad.at[:, pl.ds(pl.multiple_of(384 * f, 384), 384)]

    def half(self, ref, h):
        if self.kind == "cols":
            return ref.at[:, pl.ds(1536 * h, 1536)]
        return ref.at[pl.ds(384 * h, 384)]

    def quarter(self, ref, q):
        if self.kind == "cols":
            return ref.at[:, pl.ds(pl.multiple_of(768 * q, 768), 768)]
        return ref.at[pl.ds(pl.multiple_of(192 * q, 192), 192)]

    def start(self):
        d, s, c = self.d, self.s, self.c
        self.zero, self.local = [], []
        for j, position in enumerate(self.order):
            copy = push(
                self.piece(2 * position + 1 - c), self.mate.at[j], self.ssem.at[j], self.rsem.at[j], at(d, s, 1 - c)
            )
            copy.start()
            self.zero.append(copy)
            copy = pltpu.make_async_copy(self.piece(2 * position + c), self.own.at[j], self.lsem.at[j])
            copy.start()
            self.local.append(copy)

    def merge(self):
        d, s, c = self.d, self.s, self.c
        sx, sy = flip(s, 1), flip(s, 2)
        self.one = []
        for j in range(4):
            self.zero[j].wait_recv()
            self.local[j].wait()
            self.own[j] = (widened(self.own.at[j]) + widened(self.mate.at[j])).astype(jnp.bfloat16)
            if j == 0:
                for h, target in enumerate((sx, sy)):
                    copy = push(
                        self.half(self.own.at[0], h), self.near.at[h], self.ssem.at[4 + h], self.rsem.at[4 + h],
                        at(d, target, c),
                    )
                    copy.start()
                    self.one.append(copy)

    def join(self):
        d, s, c = self.d, self.s, self.c
        sx, sy = flip(s, 1), flip(s, 2)
        for h, j in ((0, 2), (1, 1)):
            self.one[h].wait_recv()
            where = self.half(self.own.at[j], h)
            where[...] = (widened(where) + widened(self.near.at[h])).astype(jnp.bfloat16)
        self.two = []
        for h, target in enumerate((sx, sy)):
            copy = push(
                self.own.at[1 + h], self.far.at[h], self.ssem.at[6 + h], self.rsem.at[6 + h], at(d, target, c)
            )
            copy.start()
            self.two.append(copy)

    def square(self):
        for copy in self.two:
            copy.wait_recv()
        return (
            widened(self.own.at[3]) + widened(self.far.at[0]) + widened(self.far.at[1])
        ).astype(jnp.bfloat16)

    def along(self):
        d, s, c = self.d, self.s, self.c
        self.own[3] = self.square()
        self.three = []
        for k in range(1, 4):
            target = lax.rem(d + k, 4)
            copy = push(
                self.quarter(self.own.at[3], target), self.line.at[k - 1], self.ssem.at[7 + k], self.rsem.at[7 + k],
                at(target, s, c),
            )
            copy.start()
            self.three.append(copy)

    def finish(self):
        total = widened(self.quarter(self.own.at[3], self.d))
        for k in range(1, 4):
            self.three[k - 1].wait_recv()
            total = total + widened(self.line.at[k - 1])
        self.out[...] = total
        self.sent(self.three)

    def close(self):
        self.out[...] = self.square()
        self.sent([])

    def sent(self, more):
        for copy in self.zero + self.one + self.two + more:
            copy.wait_send()


class LineSum:
    def __init__(self, kind, part, out, landing, ssem, rsem):
        self.kind, self.part, self.out, self.landing = kind, part, out, landing
        self.ssem, self.rsem = ssem, rsem
        self.d, self.s, self.c = place()

    def quarter(self, q):
        if self.kind == "cols":
            return self.part.at[:, pl.ds(pl.multiple_of(768 * q, 768), 768)]
        return self.part.at[pl.ds(pl.multiple_of(192 * q, 192), 192)]

    def start(self):
        self.copies = []
        for k in range(1, 4):
            target = lax.rem(self.d + k, 4)
            copy = push(
                self.quarter(target), self.landing.at[k - 1], self.ssem.at[k - 1], self.rsem.at[k - 1],
                at(target, self.s, self.c),
            )
            copy.start()
            self.copies.append(copy)

    def finish(self):
        total = widened(self.quarter(self.d))
        for k in range(3):
            self.copies[k].wait_recv()
            total = total + widened(self.landing.at[k])
        self.out[...] = total
        for copy in self.copies:
            copy.wait_send()


class Ending:
    def __init__(self, keep, from_x, from_y, out, room, stage, landed, last, lsem, ssem, rsem, loaded=None):
        self.out, self.room, self.stage, self.landed, self.last = out, room, stage, landed, last
        self.ssem, self.rsem = ssem, rsem
        self.d, self.s, self.c = place()
        sources = [
            keep.at[0, 0], keep.at[0, 1], keep.at[1, 0], keep.at[1, 1],
            from_x.at[0], from_x.at[1], from_y.at[0], from_y.at[1],
        ]
        self.loads = [
            pltpu.make_async_copy(source, room.at[i], lsem.at[i]) for i, source in enumerate(sources)
        ]
        for i, source in enumerate(loaded or ()):
            self.loads.append(pltpu.make_async_copy(source, landed.at[i], lsem.at[8 + i]))
        self.sent = []

    def load(self):
        for copy in self.loads:
            copy.start()

    def loaded(self):
        for copy in self.loads:
            copy.wait()

    def go(self, index, target):
        dst = self.last if index == 2 else self.landed.at[index]
        copy = push(self.stage.at[index], dst, self.ssem.at[index], self.rsem.at[index], target)
        copy.start()
        self.sent.append(copy)

    def next(self):
        bf = jnp.bfloat16
        room = self.room
        self.stage[0] = (widened(room.at[1]) + widened(room.at[5])).astype(bf)
        self.go(0, at(self.d, flip(self.s, 2), self.c))
        self.stage[1] = (widened(room.at[3]) + widened(room.at[7])).astype(bf)
        self.go(1, at(self.d, flip(self.s, 1), self.c))

    def close(self):
        for copy in self.sent:
            copy.wait_recv()
        c = self.c
        mine, theirs = c, 1 - c

        def total(h):
            return (
                widened(self.room.at[2 * h]) + widened(self.room.at[4 + 2 * h]) + widened(self.landed.at[h])
            )

        self.stage[2] = total(theirs).astype(jnp.bfloat16)
        self.go(2, at(self.d, self.s, 1 - c))
        self.out[c] = total(mine)

    def finish(self):
        self.sent[-1].wait_recv()
        self.out[1 - self.c] = widened(self.last)
        for copy in self.sent:
            copy.wait_send()


class Tail:
    def __init__(self, d_rows, router, act, ada, ada_out, d_act_out, router_out, z1, plane, plane_in, z2, z2_in, sems):
        self.d_rows, self.router, self.act, self.ada = d_rows, router, act, ada
        self.ada_out, self.d_act_out, self.router_out = ada_out, d_act_out, router_out
        self.z1, self.plane, self.plane_in, self.z2, self.z2_in = z1, plane, plane_in, z2, z2_in
        self.sems = sems
        self.d, self.s, self.c = place()
        self.f = 2 * self.s + self.c

    def z_copy(self, k, src, dst, base):
        send, recv = self.sems[base], self.sems[base + 1]
        return push(src, dst, send.at[k], recv.at[k], at(lax.rem(self.d + k, 4), self.s, self.c))

    def f_copy(self, k, src, dst, base):
        send, recv = self.sems[base], self.sems[base + 1]
        return push(src, dst, send.at[k], recv.at[k], (self.d, lax.rem(self.f + k, 8)))

    def start(self):
        self.all = [
            self.z_copy(k, self.d_rows.at[lax.rem(self.d + k, 4)], self.z1.at[k], 0) for k in range(1, 4)
        ]
        for copy in self.all:
            copy.start()

    def second(self):
        total = self.d_rows[self.d]
        for k in range(1, 4):
            self.all[k - 1].wait_recv()
            total = total + self.z1[k]
        for target in range(8):
            self.plane[target, :, 0:1152] = total
            self.plane[target, :, 1152:1280] = self.router[target]
        copies = [
            self.f_copy(k, self.plane.at[lax.rem(self.f + k, 8)], self.plane_in.at[lax.rem(8 - k, 8)], 2)
            for k in range(1, 8)
        ]
        for copy in copies:
            copy.start()
        self.in_plane = copies
        self.all = self.all + copies

    def third(self):
        f = self.f
        self.plane_in[0] = self.plane[f]
        for copy in self.in_plane:
            copy.wait_recv()
        everything = self.plane_in[...]
        router = jnp.sum(everything[:, :, 1152:1280], axis=0)
        rows = everything[:, :, 0:1152].reshape(64, 1152)
        line = lax.broadcasted_iota(jnp.int32, (64, 64), 0)
        column = lax.broadcasted_iota(jnp.int32, (64, 64), 1)
        turn = (lax.rem(line // 8 + 8 - f, 8) * 8 + lax.rem(line, 8) == column).astype(jnp.bfloat16)
        d_mod = nn(turn, rows.astype(jnp.bfloat16)).astype(jnp.bfloat16)
        self.ada_out[...] = tn(self.act[...], d_mod)[0:96]
        part = nt(d_mod, self.ada[...])
        self.z2[0:64, 0:96] = part
        self.z2[0:64, 96:128] = jnp.zeros((64, 32), jnp.float32)
        self.z2[64:72, :] = router
        copies = [self.z_copy(k, self.z2, self.z2_in.at[k], 4) for k in range(1, 4)]
        for copy in copies:
            copy.start()
        self.along = copies
        self.all = self.all + copies

    def fourth(self):
        total = self.z2[...]
        for k in range(1, 4):
            self.along[k - 1].wait_recv()
            total = total + self.z2_in[k]
        self.router_out[...] = total[64:72]
        self.z2_in[0] = total
        copies = [
            self.f_copy(
                k,
                self.z2_in.at[0, pl.ds(pl.multiple_of(8 * lax.rem(self.f + k, 8), 8), 8)],
                self.d_act_out.at[self.f],
                6,
            )
            for k in range(1, 8)
        ]
        for copy in copies:
            copy.start()
        self.d_act_out[self.f] = self.z2_in[0, pl.ds(pl.multiple_of(8 * self.f, 8), 8)]
        self.last = copies
        self.all = self.all + copies

    def finish(self):
        for k in range(1, 8):
            self.f_copy(
                k, self.z2_in.at[0, pl.ds(0, 8)], self.d_act_out.at[lax.rem(self.f + 8 - k, 8)], 6
            ).wait_recv()
        for copy in self.all:
            copy.wait_send()


def dense_kernel(
    grad, first_part, second_part, d_rows, router, act, ada,
    up_keep, up_x, up_y, up_low, up_high, down_keep, down_x, down_y,
    out, first_out, second_out, ada_out, d_act_out, router_out, up_out, down_out,
    ur, us, ul, ue, ula, usa, ura, dr, ds, dl, de, dla, dsa, dra,
    own, mate, near, far, line, ssem, rsem, lsem,
    first_in, fs, fr, second_in, ss, sr, *rest,
):
    d, s, c = place()
    f = 2 * s + c
    greet(
        [at(lax.rem(d + k, 4), s, c) for k in range(1, 4)]
        + [(d, lax.rem(f + k, 8)) for k in range(1, 8)]
    )
    dense = DenseSum("cols", grad, out, own, mate, near, far, line, ssem, rsem, lsem)
    lines = (
        LineSum("cols", first_part, first_out, first_in, fs, fr),
        LineSum("rows", second_part, second_out, second_in, ss, sr),
    )
    tail = Tail(d_rows, router, act, ada, ada_out, d_act_out, router_out, *rest[:5], rest[5:])
    ups = Ending(up_keep, up_x, up_y, up_out, ur, us, ul, ue, ula, usa, ura, (up_low, up_high))
    downs = Ending(down_keep, down_x, down_y, down_out, dr, ds, dl, de, dla, dsa, dra)
    tail.start()
    dense.start()
    for each in lines:
        each.start()
    downs.load()
    ups.load()
    tail.second()
    dense.merge()
    tail.third()
    downs.loaded()
    ups.loaded()
    ups.close()
    dense.join()
    downs.next()
    tail.fourth()
    dense.along()
    downs.close()
    for each in lines:
        each.finish()
    ups.finish()
    dense.finish()
    downs.finish()
    tail.finish()


def dense_sums(grad, first_part, second_part, small, routed):
    bf, f32 = jnp.bfloat16, jnp.float32

    def rooms(r, n):
        return [
            pltpu.VMEM((8, r, n), bf),
            pltpu.VMEM((3, r, n), bf),
            pltpu.VMEM((2, r, n), bf),
            pltpu.VMEM((r, n), bf),
            DMA((10,)),
            DMA((3,)),
            DMA((3,)),
        ]

    return pl.pallas_call(
        dense_kernel,
        out_shape=(
            jax.ShapeDtypeStruct((96, 768), f32),
            jax.ShapeDtypeStruct((96, 768), f32),
            jax.ShapeDtypeStruct((192, 384), f32),
            jax.ShapeDtypeStruct((96, 1152), f32),
            jax.ShapeDtypeStruct((8, 8, 128), f32),
            jax.ShapeDtypeStruct((8, 128), f32),
            jax.ShapeDtypeStruct((2, 96, 3072), f32),
            jax.ShapeDtypeStruct((2, 384, 768), f32),
        ),
        in_specs=[ANYWHERE] + [ONCHIP] * 6 + [ANYWHERE] * 8,
        out_specs=(ONCHIP,) * 8,
        scratch_shapes=rooms(96, 3072) + rooms(384, 768) + [
            pltpu.VMEM((4, 96, 3072), bf),
            pltpu.VMEM((4, 96, 3072), bf),
            pltpu.VMEM((2, 96, 1536), bf),
            pltpu.VMEM((2, 96, 3072), bf),
            pltpu.VMEM((3, 96, 768), bf),
            DMA((11,)), DMA((11,)), DMA((4,)),
            pltpu.VMEM((3, 96, 768), bf),
            DMA((3,)), DMA((3,)),
            pltpu.VMEM((3, 192, 384), bf),
            DMA((3,)), DMA((3,)),
            pltpu.VMEM((4, 8, 1152), f32),
            pltpu.VMEM((8, 8, 1280), f32),
            pltpu.VMEM((8, 8, 1280), f32),
            pltpu.VMEM((72, 128), f32),
            pltpu.VMEM((4, 72, 128), f32),
            DMA((4,)), DMA((4,)), DMA((8,)), DMA((8,)), DMA((4,)), DMA((4,)), DMA((8,)), DMA((8,)),
        ],
        compiler_params=pltpu.CompilerParams(
            collective_id=3, has_side_effects=True, vmem_limit_bytes=60 << 20
        ),
        cost_estimate=pl.CostEstimate(flops=40_000_000_000, bytes_accessed=20_000_000, transcendentals=0),
        name="dense_sums",
    )(grad, first_part, second_part, *small, *routed)


def layer_stats(values_in):
    centred = values_in - jnp.mean(values_in, axis=-1, keepdims=True)
    inv_std = lax.rsqrt(jnp.mean(centred * centred, axis=-1, keepdims=True) + 1e-06)
    return centred * inv_std, inv_std


def lines_of(tile, first):
    row = lax.broadcasted_iota(jnp.int32, tile.shape, 0)
    picked = [
        jnp.sum(jnp.where(row == first + i, tile, 0.0), axis=0, keepdims=True) for i in range(2)
    ]
    return jnp.concatenate(picked, axis=0)


def modulated(inside, mod, part):
    columns = slice(768 * part, 768 * part + 768)
    return inside[:, 0:1] * mod[0:1, columns] + inside[:, 1:2] * mod[1:2, columns]


def head_column(g):
    return 768 * (g // 9) + 64 * (g % 9)


QUERY_ROWS = 256


def front_kernel(
    tokens, mod_rows, inside, seg_col, seg_row, qkvo, router_t, cotangent, routes, target,
    heads, totals, attended, projected, residual, second, d_mixed, gates, rows, grads, mod,
    bias, made, weighted,
):
    bf, f32 = jnp.bfloat16, jnp.float32
    d = lax.axis_index("dp")
    for j in range(4):
        mod[:, 1152 * j : 1152 * j + 1152] = lines_of(mod_rows[j], 2 * d)
    token_float = tokens[...].astype(f32)
    normed, _ = layer_stats(token_float)
    first = (normed * (1.0 + modulated(inside, mod, 1)) + modulated(inside, mod, 0)).astype(bf)
    for j in range(4):
        piece = nn(first, qkvo[:, 768 * j : 768 * j + 640]).astype(bf)
        for i in range(9):
            heads[9 * j + i] = piece[:, 64 * i : 64 * i + 64]
    bias[...] = jnp.where(seg_col[...] == seg_row[...], 0.0, -1e30)

    def block(n, carry):
        h, part = n // (512 // QUERY_ROWS), lax.rem(n, 512 // QUERY_ROWS)
        lines = pl.ds(pl.multiple_of(part * QUERY_ROWS, QUERY_ROWS), QUERY_ROWS)
        scores = nt(heads[h, lines], heads[12 + h]) * 0.125 + bias[lines]
        row_max = jnp.max(scores, axis=-1, keepdims=True)
        weight = jnp.exp(scores - row_max)
        running = jnp.sum(weight, axis=-1, keepdims=True)
        probability = (weight * (1.0 / running)).astype(bf)
        made[h, lines] = nn(probability, heads[24 + h]).astype(bf)
        totals[h, lines] = row_max + jnp.log(running)
        return carry

    lax.fori_loop(0, 12 * (512 // QUERY_ROWS), block, 0)
    for h in range(12):
        attended[:, 64 * h : 64 * h + 64] = made[h]
    for j in range(4):
        piece = nn(attended[...], qkvo[:, 768 * j + 512 : 768 * j + 768])
        projected[:, 192 * j : 192 * j + 192] = piece[:, 64:256]
    residual[...] = token_float + modulated(inside, mod, 2) * projected[...]
    normed, _ = layer_stats(residual[...])
    second[...] = (normed * (1.0 + modulated(inside, mod, 4)) + modulated(inside, mod, 3)).astype(bf)
    logits = nt(second[...], router_t[...].astype(bf))
    ids = lax.broadcasted_iota(jnp.int32, (512, 8), 1)
    chosen = [
        jnp.sum(jnp.where(ids == routes[:, k : k + 1], logits, 0.0), axis=-1, keepdims=True)
        for k in range(2)
    ]
    top = jnp.maximum(chosen[0], chosen[1])
    raised = [jnp.exp(each - top) for each in chosen]
    share = [each / (raised[0] + raised[1]) for each in raised]
    pair = lax.broadcasted_iota(jnp.int32, (512, 2), 1)
    gates[...] = jnp.where(pair == 0, share[0], share[1])
    mixed_grad = modulated(inside, mod, 5) * cotangent[...].astype(f32)
    d_mixed[...] = mixed_grad.astype(bf)
    for k in range(2):
        weighted[k] = (share[k] * mixed_grad).astype(bf)

    def send(b, carry):
        lines = pl.ds(pl.multiple_of(288 * b, 288), 288)
        places = lax.broadcasted_iota(jnp.int32, (288, 512), 0) + 288 * b
        first_hot = (places == target[0:1]).astype(f32)
        second_hot = (places == target[1:2]).astype(f32)
        rows[lines] = nn((first_hot + second_hot).astype(bf), second[...]).astype(bf)
        grads[lines] = (
            nn(first_hot.astype(bf), weighted[0]) + nn(second_hot.astype(bf), weighted[1])
        ).astype(bf)
        return carry

    lax.fori_loop(0, 4, send, 0)


def front(*operands):
    bf, f32 = jnp.bfloat16, jnp.float32
    return pl.pallas_call(
        front_kernel,
        out_shape=(
            jax.ShapeDtypeStruct((36, 512, 64), bf),
            jax.ShapeDtypeStruct((12, 512, 1), f32),
            jax.ShapeDtypeStruct((512, 768), bf),
            jax.ShapeDtypeStruct((512, 768), f32),
            jax.ShapeDtypeStruct((512, 768), f32),
            jax.ShapeDtypeStruct((512, 768), bf),
            jax.ShapeDtypeStruct((512, 768), bf),
            jax.ShapeDtypeStruct((512, 2), f32),
            jax.ShapeDtypeStruct((1152, 768), bf),
            jax.ShapeDtypeStruct((1152, 768), bf),
            jax.ShapeDtypeStruct((2, 4608), f32),
        ),
        in_specs=[ONCHIP] * 10,
        out_specs=(ONCHIP,) * 11,
        scratch_shapes=[
            pltpu.VMEM((512, 512), f32),
            pltpu.VMEM((12, 512, 64), bf),
            pltpu.VMEM((2, 512, 768), bf),
        ],
        compiler_params=pltpu.CompilerParams(vmem_limit_bytes=60 << 20),
        cost_estimate=pl.CostEstimate(flops=40_000_000_000, bytes_accessed=20_000_000, transcendentals=0),
        name="front",
    )(*operands)


def norm_grad(upstream, normed, inv_std):
    return (
        upstream
        - jnp.mean(upstream, axis=-1, keepdims=True)
        - normed * jnp.mean(upstream * normed, axis=-1, keepdims=True)
    ) * inv_std


def rear_kernel(
    tokens, mod, inside, seg_col, seg_row, qkvo, router_t, cotangent, routes, target,
    heads, totals, attended, projected, residual, second, gates,
    returned, d_returned, shared_out, d_shared,
    output, tokens_grad, qkvo_grad, d_mod, router_grad,
    bias, rows_t, d_heads, d_att, d_att_t, d_rows_t, d_rows, d_residual, d_proj,
):
    bf, f32 = jnp.bfloat16, jnp.float32
    upstream = cotangent[...].astype(f32)

    def image_sums(part, values):
        for j in range(2):
            d_mod[j : j + 1, 768 * part : 768 * part + 768] = jnp.sum(
                inside[:, j : j + 1] * values, axis=0, keepdims=True
            )

    share = [gates[:, k : k + 1] for k in range(2)]
    places = lax.broadcasted_iota(jnp.int32, (512, 1152), 1)
    hot = [(places == target[:, k : k + 1]).astype(f32).astype(bf) for k in range(2)]
    picked = [nn(each, returned[...]) for each in hot]
    mixed = shared_out[...] + (share[0] * picked[0] + share[1] * picked[1])
    gate_two = modulated(inside, mod, 5)
    output[...] = (residual[...] + gate_two * mixed).astype(bf)
    image_sums(5, upstream * mixed)
    mixed_grad = gate_two * upstream
    d_share = [jnp.sum(mixed_grad * each, axis=-1, keepdims=True) for each in picked]
    inner = share[0] * d_share[0] + share[1] * d_share[1]
    ids = lax.broadcasted_iota(jnp.int32, (512, 8), 1)
    d_logits = sum(
        jnp.where(ids == routes[:, k : k + 1], share[k] * (d_share[k] - inner), 0.0) for k in range(2)
    ).astype(bf)
    router_grad[...] = tn(d_logits, second[...])
    d_second = (
        d_shared[...] + nn(d_logits, router_t[...].astype(bf)) + (nn(hot[0], d_returned[...]) + nn(hot[1], d_returned[...]))
    )
    normed, inv_std = layer_stats(residual[...])
    image_sums(3, d_second)
    image_sums(4, d_second * normed)
    d_residual[...] = upstream + norm_grad(d_second * (1.0 + modulated(inside, mod, 4)), normed, inv_std)
    gate_one = modulated(inside, mod, 2)
    image_sums(2, d_residual[...] * projected[...])
    d_proj[...] = (gate_one * d_residual[...]).astype(bf)
    d_attended = jnp.zeros((512, 768), f32)
    for j in range(4):
        piece = jnp.concatenate(
            [jnp.zeros((512, 64), bf), d_proj[:, 192 * j : 192 * j + 192]], axis=1
        )
        d_attended += nt(piece, qkvo[:, 768 * j + 512 : 768 * j + 768])
    d_attended = d_attended.astype(bf)
    d_att_t[...] = d_attended.T
    for h in range(12):
        d_att[h] = d_attended[:, 64 * h : 64 * h + 64]
    for j in range(18):
        pair = jnp.concatenate([heads[2 * j], heads[2 * j + 1]], axis=1)
        rows_t[128 * j : 128 * j + 128] = pair.T
    bias[...] = jnp.where(seg_col[...] == seg_row[...], 0.0, -1e30)

    def head(h, carry):
        def at_head(g):
            return pl.ds(pl.multiple_of(64 * g, 64), 64)

        d_key, d_value = jnp.zeros((64, 512), f32), jnp.zeros((64, 512), f32)
        for part in range(512 // QUERY_ROWS):
            lines = slice(part * QUERY_ROWS, (part + 1) * QUERY_ROWS)
            scores = nn(heads[h, lines], rows_t[at_head(12 + h)]) * 0.125 + bias[lines]
            probability = jnp.exp(scores - totals[h, lines])
            d_prob = nn(d_att[h, lines], rows_t[at_head(24 + h)])
            inner = jnp.sum(probability * d_prob, axis=-1, keepdims=True)
            d_scores = (probability * (d_prob - inner)).astype(bf)
            d_heads[h, lines] = (nn(d_scores, heads[12 + h]) * 0.125).astype(bf)
            d_key += nn(rows_t[at_head(h), lines], d_scores)
            d_value += nn(d_att_t[at_head(h), lines], probability.astype(bf))
        d_rows_t[at_head(h)] = (d_key * 0.125).astype(bf)
        d_rows_t[at_head(12 + h)] = d_value.astype(bf)
        return carry

    lax.fori_loop(0, 12, head, 0)
    for g in range(12):
        column = head_column(g)
        d_rows[:, column : column + 64] = d_heads[g]
    for j in range(12):
        pair = d_rows_t[128 * j : 128 * j + 128].T
        for i in range(2):
            column = head_column(12 + 2 * j + i)
            d_rows[:, column : column + 64] = pair[:, 64 * i : 64 * i + 64]
    for j in range(4):
        d_rows[:, 768 * j + 576 : 768 * j + 768] = jnp.zeros((512, 192), bf)
    token_float = tokens[...].astype(f32)
    normed, inv_std = layer_stats(token_float)
    scale_one = 1.0 + modulated(inside, mod, 1)
    first_t = (normed * scale_one + modulated(inside, mod, 0)).astype(bf).T
    attended_t = attended[...].T
    for j in range(4):
        qkvo_grad[:, 768 * j : 768 * j + 640] = nn(first_t, d_rows[:, 768 * j : 768 * j + 640]).astype(bf)
        qkvo_grad[:, 768 * j + 576 : 768 * j + 768] = nn(
            attended_t, d_proj[:, 192 * j : 192 * j + 192]
        ).astype(bf)
    d_first = nt(d_rows[...], qkvo[...])
    image_sums(0, d_first)
    image_sums(1, d_first * normed)
    tokens_grad[...] = d_residual[...] + norm_grad(d_first * scale_one, normed, inv_std)


def rear(*operands):
    bf, f32 = jnp.bfloat16, jnp.float32
    return pl.pallas_call(
        rear_kernel,
        out_shape=(
            jax.ShapeDtypeStruct((512, 768), bf),
            jax.ShapeDtypeStruct((512, 768), f32),
            jax.ShapeDtypeStruct((768, 3072), bf),
            jax.ShapeDtypeStruct((2, 4608), f32),
            jax.ShapeDtypeStruct((8, 768), f32),
        ),
        in_specs=[ONCHIP] * len(operands),
        out_specs=(ONCHIP,) * 5,
        scratch_shapes=[
            pltpu.VMEM((512, 512), f32),
            pltpu.VMEM((2304, 512), bf),
            pltpu.VMEM((12, 512, 64), bf),
            pltpu.VMEM((12, 512, 64), bf),
            pltpu.VMEM((768, 512), bf),
            pltpu.VMEM((1536, 512), bf),
            pltpu.VMEM((512, 3072), bf),
            pltpu.VMEM((512, 768), f32),
            pltpu.VMEM((512, 768), bf),
        ],
        compiler_params=pltpu.CompilerParams(vmem_limit_bytes=67043328),
        cost_estimate=pl.CostEstimate(flops=60_000_000_000, bytes_accessed=30_000_000, transcendentals=0),
        name="rear",
    )(*operands)


def last_kernel(
    qkvo_sum, first, second, ada, up, down, d_act, router, condition,
    qkv_out, out_out, first_out, second_out, ada_out, up_out, down_out, condition_out, router_out,
):
    d = lax.axis_index("dp")
    qkv_out[...] = qkvo_sum[:, 0:576]
    out_out[...] = qkvo_sum[:, 576:768]
    first_out[...] = first[...]
    second_out[...] = second[...]
    ada_out[...] = ada[...]
    up_out[...] = up[...]
    down_out[...] = down[...]
    router_out[...] = lines_of(router[...], 2 * d)[:, 0:96]
    for f in range(8):
        columns = slice(96 * f, 96 * f + 96)
        v = condition[:, columns].astype(jnp.float32)
        sigmoid = jax.nn.sigmoid(v)
        condition_out[:, columns] = lines_of(d_act[f], 2 * d)[:, 0:96] * (
            sigmoid * (1.0 + v * (1.0 - sigmoid))
        )


def last(*operands):
    f32 = jnp.float32
    return pl.pallas_call(
        last_kernel,
        out_shape=tuple(
            jax.ShapeDtypeStruct(shape, f32)
            for shape in (
                (96, 576), (96, 192), (96, 768), (192, 384), (96, 1152), (2, 96, 3072), (2, 384, 768),
                (2, 768), (2, 96),
            )
        ),
        in_specs=[ONCHIP] * 9,
        out_specs=(ONCHIP,) * 9,
        compiler_params=pltpu.CompilerParams(vmem_limit_bytes=40 << 20),
        name="last",
    )(*operands)


def fitted_shards(
    tokens,
    condition,
    ada_weight,
    qkv_weight,
    out_weight,
    shared_up,
    shared_down,
    router_weight,
    expert_up,
    expert_down,
    routes,
    image_sizes,
    cotangent,
):
    bf = jnp.bfloat16
    d_index, f_index = lax.axis_index("dp"), lax.axis_index("fsdp")
    model_width = tokens.shape[1]
    head_size = model_width // HEADS
    inside, segment = owners(image_sizes)
    ids = jnp.arange(EXPERTS, dtype=jnp.int32)
    hot = routes[:, :, None] == ids[None, None, :]
    hot_any = jnp.any(hot, axis=1).astype(bf)
    order = jnp.arange(LONG, dtype=jnp.int32)
    earlier = (order[:, None] > order[None, :]).astype(bf)
    before = nn(earlier, hot_any)
    position = jnp.sum(jnp.where(hot, before[:, None, :], 0.0), axis=-1).astype(jnp.int32)
    target = routes * CAP + position
    live = (segment < IMG_DEV).astype(jnp.float32)
    counts = jnp.sum(live[:, None] * hot_any.astype(jnp.float32), axis=0)
    cond_float = condition.astype(jnp.float32)
    activated = jax.nn.silu(cond_float).astype(bf)
    act_slices = activated.astype(jnp.float32).reshape(IMG_DEV, 8, 96).transpose(1, 0, 2)
    act_slices = jnp.pad(act_slices, ((0, 0), (0, 6), (0, 32)))
    act_slices = act_slices.at[:, 2, :EXPERTS].set(counts)
    act_slices = act_slices.at[:, 3:5, :96].set(router_weight.T.astype(jnp.float32))
    qkvo, router_t, seen, mod_rows, up_line, down_line, up_m, up_x0, up_y0, down_own, down_m = opening(
        qkv_weight, out_weight, act_slices, ada_weight, shared_up, shared_down.T, expert_up, expert_down
    )
    hops = hop(up_m, 2), hop(up_m, 4), hop(down_own, 2), hop(down_own, 4)
    expert_counts = seen[66, :EXPERTS].astype(jnp.int32)
    segments = (segment[:, None], segment[None, :])
    (
        heads, totals, attended, projected, residual, second_input, d_mixed, gates, rows, grads, modulation,
    ) = front(tokens, mod_rows, inside, *segments, qkvo, router_t, cotangent, routes, target.T)
    rows = rows.reshape(EXPERTS, CAP, model_width)
    grads = grads.reshape(EXPERTS, CAP, model_width)
    rows, (up_x1, up_y1, down_x0, down_y0) = lax.optimization_barrier((rows, hops))
    rows_in, grads_in, up_corner, down_x1, down_y1, down_corner, shared_out, d_second, *shared_grads = (
        outbound(
            rows, grads, up_line, down_line, second_input, d_mixed, up_x0, up_y1, down_m, down_x0
        )
    )
    returned, d_returned, up_keep, *up_near, down_keep, down_x, down_y, first_part, second_part = experts(
        rows_in, grads_in, (expert_up, up_m, up_x0, up_x1, up_y0, up_y1, up_corner),
        (down_own, down_m, down_x0, down_x1, down_y0, down_y1, down_corner),
        *shared_grads,
    )
    up_next = square_next(up_keep, *up_near)
    down_near = hop(down_x, 2), hop(down_y, 4)
    returned = returned.reshape(EXPERTS * CAP, model_width)
    d_returned = d_returned.reshape(EXPERTS * CAP, model_width)
    output, tokens_grad, qkvo_grad, d_modulation, router_grad = rear(
        tokens, modulation, inside, *segments, qkvo, router_t, cotangent, routes, target,
        heads, totals, attended, projected, residual, second_input, gates,
        returned, d_returned, shared_out, d_second,
    )
    qkvo_grad, down_near, up_next = lax.optimization_barrier((qkvo_grad, down_near, up_next))
    d_modulation = d_modulation.astype(bf)
    d_mod_rows = d_modulation.astype(jnp.float32).reshape(2, 4, 1152).transpose(1, 0, 2)
    d_mod_rows = lax.dynamic_update_slice(
        jnp.zeros((4, 8, 1152), jnp.float32), d_mod_rows, (0, 2 * d_index, 0)
    )
    router_tiles = jnp.pad(
        router_grad.reshape(EXPERTS, 8, 96).transpose(1, 0, 2), ((0, 0), (0, 0), (0, 32))
    )
    (
        qkvo_sum, shared_first_sum, shared_second_sum, ada_grad, d_act_tiles, router_sum,
        expert_up_grad, expert_down_grad,
    ) = dense_sums(
        qkvo_grad, first_part, second_part,
        (d_mod_rows, router_tiles, seen[:64].astype(bf), ada_weight),
        (up_keep, *up_near, *up_next, down_keep, *down_near),
    )
    (
        qkv_grad, out_grad, shared_first_sum, shared_second_sum, ada_grad, expert_up_grad, expert_down_grad,
        condition_grad, router_out,
    ) = last(
        qkvo_sum, shared_first_sum, shared_second_sum, ada_grad, expert_up_grad, expert_down_grad,
        d_act_tiles, router_sum, condition,
    )
    return (
        output,
        tokens_grad,
        condition_grad,
        ada_grad,
        qkv_grad,
        out_grad,
        shared_first_sum,
        shared_second_sum.T,
        router_out.T,
        expert_up_grad,
        expert_down_grad,
        expert_counts,
    )


def solution(mesh):
    placed = (
        P(("dp", "fsdp"), None),
        P(("dp", "fsdp"), None),
        P("fsdp", "dp"),
        P("fsdp", "dp"),
        P("fsdp", "dp"),
        P("fsdp", "dp"),
        P("fsdp", "dp"),
        P("fsdp", "dp"),
        P("dp", "fsdp", None),
        P("dp", "fsdp", None),
        P(("dp", "fsdp"), None),
        P(("dp", "fsdp")),
        P(("dp", "fsdp"), None),
    )
    fitted = mesh.shape["dp"] == 4 and mesh.shape["fsdp"] == 8
    return jax.shard_map(
        fitted_shards if fitted else shards,
        mesh=mesh,
        in_specs=placed,
        out_specs=(
            P(("dp", "fsdp"), None),
            P(("dp", "fsdp"), None),
            P(("dp", "fsdp"), None),
            P("fsdp", "dp"),
            P("fsdp", "dp"),
            P("fsdp", "dp"),
            P("fsdp", "dp"),
            P("fsdp", "dp"),
            P("fsdp", "dp"),
            P("dp", "fsdp", None),
            P("dp", "fsdp", None),
            P(),
        ),
        check_vma=False,
    )
```

```python
import functools

import jax
import jax.numpy as jnp
from jax import lax
from jax.experimental import pallas as pl
from jax.experimental.pallas import tpu as pltpu
from jax.sharding import PartitionSpec as P

HEADS = 12
EXPERTS = 8
CAP = 144
IMG_DEV = 2
LONG = 512
MESH = pl.DeviceIdType.MESH


EXACT = lax.Precision.HIGHEST


def owners(image_sizes):
    starts = jnp.cumsum(image_sizes) - image_sizes
    position = jnp.arange(LONG, dtype=jnp.int32)[:, None]
    inside = (position >= starts[None, :]) & (position < (starts + image_sizes)[None, :])
    slot_ids = jnp.arange(IMG_DEV, dtype=jnp.int32)
    segment = jnp.sum(jnp.where(inside, slot_ids[None, :], 0), axis=1) + jnp.where(
        jnp.any(inside, axis=1), 0, IMG_DEV
    )
    return (inside.astype(jnp.float32), segment)


def dispatch_plan(routes):
    flat = routes.reshape(-1)
    onehot = (flat[:, None] == jnp.arange(EXPERTS, dtype=jnp.int32)[None, :]).astype(jnp.int32)
    before = jnp.cumsum(onehot, axis=0) - onehot
    position = jnp.sum(before * onehot, axis=1)
    target = flat * CAP + position
    assignment = jnp.arange(2 * LONG, dtype=jnp.int32)
    source = jnp.zeros((EXPERTS * CAP,), jnp.int32).at[target].set(assignment)
    filled = jnp.zeros((EXPERTS * CAP,), jnp.int32).at[target].set(1)
    return (target, source, filled)


def layer_norm(values_in):
    centred = values_in - jnp.mean(values_in, axis=-1, keepdims=True)
    inv_std = lax.rsqrt(jnp.mean(centred * centred, axis=-1, keepdims=True) + 1e-06)
    return (centred * inv_std, inv_std)


def norm_back(upstream, normed, inv_std):
    return (
        upstream
        - jnp.mean(upstream, axis=-1, keepdims=True)
        - normed * jnp.mean(upstream * normed, axis=-1, keepdims=True)
    ) * inv_std


def gelu_tanh(values_in):
    return jax.nn.gelu(values_in, approximate=True)


def gelu_back(values_in, upstream):
    return jax.vjp(gelu_tanh, values_in)[1](upstream)[0]


def collect(first, second, third):
    widened = (
        lax.all_gather(first, "dp", axis=1, tiled=True),
        lax.all_gather(second, "dp", axis=1, tiled=True),
        lax.all_gather(third, "dp", axis=1, tiled=True),
    )
    return (
        lax.all_gather(widened[0], "fsdp", axis=0, tiled=True),
        lax.all_gather(widened[1], "fsdp", axis=0, tiled=True),
        lax.all_gather(widened[2], "fsdp", axis=0, tiled=True),
    )


def spread(first, second, third):
    row_sums = (
        lax.psum_scatter(first, "fsdp", scatter_dimension=0, tiled=True),
        lax.psum_scatter(second, "fsdp", scatter_dimension=0, tiled=True),
        lax.psum_scatter(third, "fsdp", scatter_dimension=0, tiled=True),
    )
    return (
        lax.psum_scatter(row_sums[0], "dp", scatter_dimension=1, tiled=True),
        lax.psum_scatter(row_sums[1], "dp", scatter_dimension=1, tiled=True),
        lax.psum_scatter(row_sums[2], "dp", scatter_dimension=1, tiled=True),
    )


def gather_experts(up_shard, down_shard):
    return (
        lax.all_gather(up_shard, "fsdp", axis=1, tiled=True),
        lax.all_gather(down_shard, "fsdp", axis=1, tiled=True),
    )


def expert_forward(buffer_in, up_full, down_full):
    expert_pre = jnp.einsum(
        "secd,edf->secf", buffer_in, up_full, preferred_element_type=jnp.float32
    )
    expert_act = gelu_tanh(expert_pre).astype(jnp.bfloat16)
    expert_out = jnp.einsum(
        "secf,efd->secd", expert_act, down_full, preferred_element_type=jnp.float32
    ).astype(jnp.bfloat16)
    return (expert_pre, expert_act, expert_out)


def expert_backward(buffer_in, expert_pre, expert_act, d_out, up_full, down_full):
    d_act = jnp.einsum("secd,efd->secf", d_out, down_full, preferred_element_type=jnp.float32)
    d_pre = gelu_back(expert_pre, d_act).astype(jnp.bfloat16)
    d_rows = jnp.einsum(
        "secf,edf->secd", d_pre, up_full, preferred_element_type=jnp.float32
    ).astype(jnp.bfloat16)
    down_grad = jnp.einsum("secf,secd->efd", expert_act, d_out, preferred_element_type=jnp.float32)
    up_grad = jnp.einsum("secd,secf->edf", buffer_in, d_pre, preferred_element_type=jnp.float32)
    return (up_grad, down_grad, d_rows)


def attend(queries, keys_all, values_all, segment):
    row_count, head_count, head_size = queries.shape
    block_rows = min(512, row_count)
    block_count = row_count // block_rows
    score_scale = head_size ** (-0.5)

    def one_block(pieces):
        query_part, segment_part = pieces
        allowed = (segment_part[:, None] == segment[None, :])[None]
        scores = (
            jnp.einsum("qhd,khd->hqk", query_part, keys_all, preferred_element_type=jnp.float32)
            * score_scale
        )
        scores = jnp.where(allowed, scores, -1e30)
        row_max = jnp.max(scores, axis=-1, keepdims=True)
        weight = jnp.exp(scores - row_max)
        running = jnp.sum(weight, axis=-1, keepdims=True)
        probability = (weight / running).astype(jnp.bfloat16)
        attended = jnp.einsum(
            "hqk,khd->qhd", probability, values_all, preferred_element_type=jnp.float32
        )
        return (attended.astype(jnp.bfloat16), (row_max + jnp.log(running))[:, :, 0])

    return lax.map(
        one_block,
        (
            queries.reshape(block_count, block_rows, head_count, head_size),
            segment.reshape(block_count, block_rows),
        ),
    )


def attend_back(queries, keys_all, values_all, segment, log_totals, d_attended):
    row_count, head_count, head_size = queries.shape
    block_rows = min(512, row_count)
    block_count = row_count // block_rows
    score_scale = head_size ** (-0.5)

    def one_block(carry, pieces):
        key_sum, value_sum = carry
        query_part, segment_part, total_part, grad_part = pieces
        allowed = (segment_part[:, None] == segment[None, :])[None]
        scores = (
            jnp.einsum("qhd,khd->hqk", query_part, keys_all, preferred_element_type=jnp.float32)
            * score_scale
        )
        scores = jnp.where(allowed, scores, -1e30)
        probability = jnp.exp(scores - total_part[:, :, None])
        d_prob = jnp.einsum(
            "qhd,khd->hqk", grad_part, values_all, preferred_element_type=jnp.float32
        )
        d_scores = (
            probability * (d_prob - jnp.sum(probability * d_prob, axis=-1, keepdims=True))
        ).astype(jnp.bfloat16)
        query_grad = (
            jnp.einsum("hqk,khd->qhd", d_scores, keys_all, preferred_element_type=jnp.float32)
            * score_scale
        )
        key_sum = (
            key_sum
            + jnp.einsum("hqk,qhd->khd", d_scores, query_part, preferred_element_type=jnp.float32)
            * score_scale
        )
        value_sum = value_sum + jnp.einsum(
            "hqk,qhd->khd",
            probability.astype(jnp.bfloat16),
            grad_part,
            preferred_element_type=jnp.float32,
        )
        return ((key_sum, value_sum), query_grad)

    empty = jnp.zeros(keys_all.shape, jnp.float32)
    sums, query_grads = lax.scan(
        one_block,
        (empty, empty),
        (
            queries.reshape(block_count, block_rows, head_count, head_size),
            segment.reshape(block_count, block_rows),
            log_totals,
            d_attended.reshape(block_count, block_rows, head_count, head_size),
        ),
    )
    return (query_grads.reshape(row_count, head_count, head_size), sums[0], sums[1])


def shards(
    tokens,
    condition,
    ada_weight,
    qkv_weight,
    out_weight,
    shared_up,
    shared_down,
    router_weight,
    expert_up,
    expert_down,
    routes,
    image_sizes,
    cotangent,
):
    model_width = tokens.shape[1]
    head_size = model_width // HEADS
    inside, segment = owners(image_sizes)
    target, source, filled = dispatch_plan(routes)
    route_hot = (routes[:, :, None] == jnp.arange(EXPERTS, dtype=jnp.int32)[None, None, :]).astype(
        jnp.float32
    )
    live = (segment < IMG_DEV).astype(jnp.int32)
    local_counts = jnp.sum(live[:, None, None] * route_hot.astype(jnp.int32), axis=(0, 1))
    expert_counts = lax.psum(local_counts, ("dp", "fsdp"))
    ada_full, qkv_full, out_full = collect(ada_weight, qkv_weight, out_weight)
    cond_float = condition.astype(jnp.float32)
    activated = jax.nn.silu(cond_float).astype(jnp.bfloat16)
    modulation = jnp.dot(activated, ada_full, preferred_element_type=jnp.float32)
    per_row = jnp.dot(inside, modulation, precision=EXACT, preferred_element_type=jnp.float32)
    shift_one, scale_one, gate_one, shift_two, scale_two, gate_two = jnp.split(per_row, 6, axis=1)
    token_float = tokens.astype(jnp.float32)
    normed_one, inv_one = layer_norm(token_float)
    first_input = (normed_one * (1.0 + scale_one) + shift_one).astype(jnp.bfloat16)
    qkv_rows = jnp.dot(first_input, qkv_full, preferred_element_type=jnp.float32).astype(
        jnp.bfloat16
    )
    queries = qkv_rows[:, :model_width].reshape(-1, HEADS, head_size)
    keys_all = qkv_rows[:, model_width : 2 * model_width].reshape(-1, HEADS, head_size)
    values_all = qkv_rows[:, 2 * model_width :].reshape(-1, HEADS, head_size)
    attended_blocks, log_totals = attend(queries, keys_all, values_all, segment)
    attended = attended_blocks.reshape(-1, model_width)
    projected = jnp.dot(attended, out_full, preferred_element_type=jnp.float32)
    residual_one = token_float + gate_one * projected
    normed_two, inv_two = layer_norm(residual_one)
    second_input = (normed_two * (1.0 + scale_two) + shift_two).astype(jnp.bfloat16)
    shared_first, shared_second, router_full = collect(shared_up, shared_down, router_weight)
    shared_pre = jnp.dot(second_input, shared_first, preferred_element_type=jnp.float32)
    shared_act = gelu_tanh(shared_pre).astype(jnp.bfloat16)
    shared_out = jnp.dot(shared_act, shared_second, preferred_element_type=jnp.float32)
    logits = jnp.dot(second_input, router_full, preferred_element_type=jnp.float32)
    chosen = jnp.sum(logits[:, None, :] * route_hot, axis=-1)
    gate_share = jax.nn.softmax(chosen, axis=-1)
    buffer_rows = jnp.take(second_input, source // 2, axis=0).reshape(EXPERTS, CAP, model_width)
    up_full, down_full = gather_experts(expert_up, expert_down)
    groups = lax.axis_size("dp")
    expert_in = lax.all_to_all(
        buffer_rows.reshape(groups, EXPERTS // groups, CAP, model_width),
        "dp",
        split_axis=0,
        concat_axis=0,
        tiled=True,
    )
    expert_pre, expert_act, expert_out = expert_forward(expert_in, up_full, down_full)
    returned = lax.all_to_all(expert_out, "dp", split_axis=0, concat_axis=0, tiled=True).reshape(
        EXPERTS, CAP, model_width
    )
    picked = (
        jnp.take(returned.reshape(EXPERTS * CAP, model_width), target, axis=0)
        .reshape(-1, 2, model_width)
        .astype(jnp.float32)
    )
    mixed = shared_out + jnp.sum(gate_share[:, :, None] * picked, axis=1)
    output = (residual_one + gate_two * mixed).astype(jnp.bfloat16)
    upstream = cotangent.astype(jnp.float32)
    d_mixed = gate_two * upstream
    d_gate_two = upstream * mixed
    d_gate_share = jnp.sum(d_mixed[:, None, :] * picked, axis=-1)
    slot_gate = jnp.take(gate_share.reshape(-1), source) * filled.astype(jnp.float32)
    d_buffer = (
        (jnp.take(d_mixed, source // 2, axis=0) * slot_gate[:, None])
        .astype(jnp.bfloat16)
        .reshape(EXPERTS, CAP, model_width)
    )
    shared_first, shared_second, router_full = collect(shared_up, shared_down, router_weight)
    up_full, down_full = gather_experts(expert_up, expert_down)
    arrived = lax.all_to_all(
        d_buffer.reshape(groups, EXPERTS // groups, CAP, model_width),
        "dp",
        split_axis=0,
        concat_axis=0,
        tiled=True,
    )
    up_grad, down_grad, d_rows = expert_backward(
        expert_in, expert_pre, expert_act, arrived, up_full, down_full
    )
    d_returned = lax.all_to_all(d_rows, "dp", split_axis=0, concat_axis=0, tiled=True).reshape(
        EXPERTS, CAP, model_width
    )
    expert_sums = (
        lax.psum_scatter(up_grad, "fsdp", scatter_dimension=1, tiled=True),
        lax.psum_scatter(down_grad, "fsdp", scatter_dimension=1, tiled=True),
    )
    d_shared = d_mixed.astype(jnp.bfloat16)
    shared_second_grad = jnp.einsum(
        "tf,td->fd", shared_act, d_shared, preferred_element_type=jnp.float32
    )
    d_shared_act = jnp.einsum(
        "td,fd->tf", d_shared, shared_second, preferred_element_type=jnp.float32
    )
    d_shared_pre = gelu_back(shared_pre, d_shared_act).astype(jnp.bfloat16)
    shared_first_grad = jnp.einsum(
        "td,tf->df", second_input, d_shared_pre, preferred_element_type=jnp.float32
    )
    d_chosen = gate_share * (
        d_gate_share - jnp.sum(gate_share * d_gate_share, axis=-1, keepdims=True)
    )
    d_logits = jnp.sum(d_chosen[:, :, None] * route_hot, axis=1).astype(jnp.bfloat16)
    router_grad = jnp.einsum(
        "td,te->de", second_input, d_logits, preferred_element_type=jnp.float32
    )
    from_experts = (
        jnp.take(d_returned.reshape(EXPERTS * CAP, model_width), target, axis=0)
        .reshape(-1, 2, model_width)
        .astype(jnp.float32)
    )
    d_second = (
        jnp.einsum("tf,df->td", d_shared_pre, shared_first, preferred_element_type=jnp.float32)
        + jnp.einsum("te,de->td", d_logits, router_full, preferred_element_type=jnp.float32)
        + jnp.sum(from_experts, axis=1)
    )
    mlp_sums = spread(shared_first_grad, shared_second_grad, router_grad)
    d_scale_two = d_second * normed_two
    d_residual = upstream + norm_back(d_second * (1.0 + scale_two), normed_two, inv_two)
    ada_full, qkv_full, out_full = collect(ada_weight, qkv_weight, out_weight)
    d_projected = (gate_one * d_residual).astype(jnp.bfloat16)
    d_gate_one = d_residual * projected
    out_grad = jnp.einsum("td,te->de", attended, d_projected, preferred_element_type=jnp.float32)
    d_attended = jnp.einsum(
        "te,de->td", d_projected, out_full, preferred_element_type=jnp.float32
    ).astype(jnp.bfloat16)
    d_queries, d_keys, d_values = attend_back(
        queries, keys_all, values_all, segment, log_totals, d_attended.reshape(-1, HEADS, head_size)
    )
    d_qkv = jnp.concatenate(
        [
            d_queries.reshape(-1, model_width),
            d_keys.reshape(-1, model_width),
            d_values.reshape(-1, model_width),
        ],
        axis=1,
    ).astype(jnp.bfloat16)
    qkv_grad = jnp.einsum("td,te->de", first_input, d_qkv, preferred_element_type=jnp.float32)
    d_first = jnp.einsum("te,de->td", d_qkv, qkv_full, preferred_element_type=jnp.float32)
    d_scale_one = d_first * normed_one
    tokens_grad = d_residual + norm_back(d_first * (1.0 + scale_one), normed_one, inv_one)
    d_per_row = jnp.concatenate(
        [d_first, d_scale_one, d_gate_one, d_second, d_scale_two, d_gate_two], axis=1
    )
    d_modulation = jnp.einsum(
        "tj,te->je", inside, d_per_row, precision=EXACT, preferred_element_type=jnp.float32
    ).astype(jnp.bfloat16)
    ada_grad = jnp.einsum("jd,je->de", activated, d_modulation, preferred_element_type=jnp.float32)
    d_activated = jnp.einsum(
        "je,de->jd", d_modulation, ada_full, preferred_element_type=jnp.float32
    )
    condition_grad = jax.vjp(jax.nn.silu, cond_float)[1](d_activated)[0]
    attn_sums = spread(ada_grad, qkv_grad, out_grad)
    return (
        output,
        tokens_grad,
        condition_grad,
        attn_sums[0],
        attn_sums[1],
        attn_sums[2],
        mlp_sums[0],
        mlp_sums[1],
        mlp_sums[2],
        expert_sums[0],
        expert_sums[1],
        expert_counts,
    )


def at(d, s, c):
    return (d, 2 * s + c)


def slot(kind, f, d):
    if kind == "cols":
        return (pl.ds(pl.multiple_of(96 * f, 96), 96), pl.ds(pl.multiple_of(768 * d, 768), 768))
    return (pl.ds(pl.multiple_of(192 * d, 192), 192), pl.ds(pl.multiple_of(384 * f, 384), 384))


def half_slot(kind, f, d, h):
    if kind == "cols":
        return (
            pl.ds(pl.multiple_of(96 * f, 96), 96),
            pl.ds(pl.multiple_of(768 * d + 384 * h, 384), 384),
        )
    return (
        pl.ds(pl.multiple_of(192 * d + 96 * h, 96), 96),
        pl.ds(pl.multiple_of(384 * f, 384), 384),
    )


def place():
    d = lax.axis_index("dp")
    f = lax.axis_index("fsdp")
    return d, f // 2, lax.rem(f, 2)


def flip(v, bit):
    return v + bit - 2 * bit * lax.rem(v // bit, 2)


def greet(devices):
    barrier = pltpu.get_barrier_semaphore()
    for device in devices:
        pl.semaphore_signal(barrier, inc=1, device_id=device, device_id_type=MESH)
    pl.semaphore_wait(barrier, len(devices))


def push(src, dst, send_sem, recv_sem, device):
    return pltpu.make_async_remote_copy(
        src_ref=src,
        dst_ref=dst,
        send_sem=send_sem,
        recv_sem=recv_sem,
        device_id=device,
        device_id_type=MESH,
    )


GATHER_SEMS = 3 + 8 + 8 + 20


class Gather:
    def __init__(self, kind, shard, full, ssem, rsem, lsem):
        self.kind, self.shard, self.full = kind, shard, full
        self.ssem, self.rsem, self.lsem = ssem, rsem, lsem
        self.d, self.s, self.c = place()
        self.sent = []

    def f(self, s):
        return 2 * s + self.c

    def go(self, index, where, device, src=None):
        ref = self.full.at[where]
        copy = push(
            ref if src is None else src, ref, self.ssem.at[index], self.rsem.at[index], device
        )
        copy.start()
        self.sent.append(copy)

    def arrived(self, index, where):
        ref = self.full.at[where]
        push(ref, ref, self.ssem.at[index], self.rsem.at[index], at(self.d, self.s, self.c)).wait_recv()

    def start(self):
        d, s, c = self.d, self.s, self.c
        mine = slot(self.kind, self.f(s), d)
        self.own = pltpu.make_async_copy(self.shard, self.full.at[mine], self.lsem)
        self.own.start()
        self.go(1, mine, at(flip(d, 2), s, c), self.shard)
        self.go(0, mine, at(flip(d, 1), s, c), self.shard)
        self.go(3, mine, at(d, flip(s, 1), c), self.shard)
        self.go(4, mine, at(d, flip(s, 2), c), self.shard)
        self.go(19, mine, at(d, s, 1 - c), self.shard)

    def source(self, k):
        return (self.d, flip(self.d, 1), flip(self.d, 2), flip(flip(self.d, 1), 2))[k]

    def spread_z(self, k):
        d, s, c = self.d, self.s, self.c
        block = slot(self.kind, self.f(s), self.source(k))
        self.arrived(k - 1, block)
        if k == 2:
            self.go(2, block, at(flip(d, 1), s, c))
        self.go(3 + 2 * k, block, at(d, flip(s, 1), c))
        self.go(4 + 2 * k, block, at(d, flip(s, 2), c))
        self.go(19 + 5 * k, block, at(d, s, 1 - c))

    def relay(self, k):
        d, s, c = self.d, self.s, self.c
        source = self.source(k)
        sx, sy = flip(s, 1), flip(s, 2)
        from_x = slot(self.kind, self.f(sx), source)
        from_y = slot(self.kind, self.f(sy), source)
        self.arrived(3 + 2 * k, from_x)
        self.go(11 + 2 * k, half_slot(self.kind, self.f(sx), source, 0), at(d, sy, c))
        self.go(20 + 5 * k, from_x, at(d, s, 1 - c))
        self.arrived(4 + 2 * k, from_y)
        self.go(12 + 2 * k, half_slot(self.kind, self.f(sy), source, 1), at(d, sx, c))
        self.go(21 + 5 * k, from_y, at(d, s, 1 - c))

    def corner(self, k):
        d, s, c = self.d, self.s, self.c
        source = self.source(k)
        sd = flip(flip(s, 1), 2)
        for h in range(2):
            where = half_slot(self.kind, self.f(sd), source, h)
            self.arrived(11 + 2 * k + h, where)
            self.go(22 + 5 * k + h, where, at(d, s, 1 - c))

    def finish(self):
        d, s, c = self.d, self.s, self.c
        sx, sy = flip(s, 1), flip(s, 2)
        sd = flip(sx, 2)
        self.own.wait()
        for k in range(4):
            source = self.source(k)
            for j, position in enumerate((s, sx, sy)):
                self.arrived(19 + 5 * k + j, slot(self.kind, 2 * position + 1 - c, source))
            for h in range(2):
                self.arrived(22 + 5 * k + h, half_slot(self.kind, 2 * sd + 1 - c, source, h))
        for copy in self.sent:
            copy.wait_send()


class Line:
    def __init__(self, kind, shard, line, ssem, rsem, lsem):
        self.kind, self.shard, self.line = kind, shard, line
        self.ssem, self.rsem, self.lsem = ssem, rsem, lsem
        self.d, self.s, self.c = place()

    def block(self, d):
        if self.kind == "cols":
            return self.line.at[:, pl.ds(pl.multiple_of(768 * d, 768), 768)]
        return self.line.at[pl.ds(pl.multiple_of(192 * d, 192), 192)]

    def copy(self, index, src, source, target):
        return push(
            src, self.block(source), self.ssem.at[index], self.rsem.at[index], at(target, self.s, self.c)
        )

    def start(self):
        d = self.d
        self.own = pltpu.make_async_copy(self.shard, self.block(d), self.lsem)
        self.own.start()
        self.sent = [
            self.copy(0, self.shard, d, flip(d, 2)),
            self.copy(1, self.shard, d, flip(d, 1)),
        ]
        for copy in self.sent:
            copy.start()

    def relay(self):
        d2 = flip(self.d, 2)
        self.copy(0, self.shard, d2, d2).wait_recv()
        copy = self.copy(2, self.block(d2), d2, flip(self.d, 1))
        copy.start()
        self.sent.append(copy)

    def finish(self):
        d1 = flip(self.d, 1)
        self.own.wait()
        self.copy(1, self.shard, d1, d1).wait_recv()
        self.copy(2, self.shard, flip(d1, 2), d1).wait_recv()
        for copy in self.sent:
            copy.wait_send()


class Spread:
    def __init__(self, kind, line, full, ssem, rsem, lsem):
        self.kind, self.line, self.full = kind, line, full
        self.ssem, self.rsem, self.lsem = ssem, rsem, lsem
        self.d, self.s, self.c = place()
        self.sx, self.sy = flip(self.s, 1), flip(self.s, 2)
        self.sd = flip(self.sx, 2)
        self.mate = at(self.d, self.s, 1 - self.c)
        self.to_x, self.to_y = at(self.d, self.sx, self.c), at(self.d, self.sy, self.c)
        self.sent = []

    def block(self, position, c, h=None):
        f = 2 * position + c
        if self.kind == "cols":
            rows = pl.ds(pl.multiple_of(96 * f, 96), 96)
            return self.full.at[rows] if h is None else self.full.at[rows, pl.ds(1536 * h, 1536)]
        columns = pl.ds(pl.multiple_of(384 * f, 384), 384)
        rows = pl.ds(0, 768) if h is None else pl.ds(384 * h, 384)
        return self.full.at[rows, columns]

    def go(self, index, ref, device, src=None):
        copy = push(
            ref if src is None else src, ref, self.ssem.at[index], self.rsem.at[index], device
        )
        copy.start()
        self.sent.append(copy)

    def arrived(self, index, ref):
        push(ref, ref, self.ssem.at[index], self.rsem.at[index], self.mate).wait_recv()

    def start(self):
        mine = self.block(self.s, self.c)
        self.own = pltpu.make_async_copy(self.line, mine, self.lsem)
        self.own.start()
        self.go(0, mine, self.to_x, self.line)
        self.go(1, mine, self.to_y, self.line)
        self.go(2, mine, self.mate, self.line)

    def relay(self):
        c = self.c
        from_x, from_y = self.block(self.sx, c), self.block(self.sy, c)
        self.arrived(0, from_x)
        self.go(3, self.block(self.sx, c, 0), self.to_y)
        self.go(5, from_x, self.mate)
        self.arrived(1, from_y)
        self.go(4, self.block(self.sy, c, 1), self.to_x)
        self.go(6, from_y, self.mate)

    def corner(self):
        for h in range(2):
            ref = self.block(self.sd, self.c, h)
            self.arrived(3 + h, ref)
            self.go(7 + h, ref, self.mate)

    def finish(self):
        c = 1 - self.c
        self.own.wait()
        self.arrived(2, self.block(self.s, c))
        self.arrived(5, self.block(self.sx, c))
        self.arrived(6, self.block(self.sy, c))
        for h in range(2):
            self.arrived(7 + h, self.block(self.sd, c, h))
        for copy in self.sent:
            copy.wait_send()


class Near:
    def __init__(self, up_shard, down_shard, up_mate, up_x, up_y, down_own, down_mate, ssem, rsem, lsem):
        d, s, c = place()
        self.local = pltpu.make_async_copy(down_shard.at[c], down_own, lsem)
        plan = (
            (up_shard, c, up_x, flip(s, 1)),
            (up_shard, c, up_y, flip(s, 2)),
            (up_shard, 1 - c, up_mate, s),
            (down_shard, 1 - c, down_mate, s),
        )
        self.away = [
            push(shard.at[which], out, ssem.at[i], rsem.at[i], at(d, position, which))
            for i, (shard, which, out, position) in enumerate(plan)
        ]

    def start(self):
        for copy in self.away + [self.local]:
            copy.start()

    def finish(self):
        for copy in self.away + [self.local]:
            copy.wait()


class Pair:
    def __init__(self, over_x, into_x, over_y, into_y, ssem, rsem):
        d, s, c = place()
        self.copies = [
            push(over_x, into_x, ssem.at[0], rsem.at[0], at(d, flip(s, 1), c)),
            push(over_y, into_y, ssem.at[1], rsem.at[1], at(d, flip(s, 2), c)),
        ]

    def start(self):
        for copy in self.copies:
            copy.start()

    def finish(self):
        for copy in self.copies:
            copy.wait()


def everyone_else():
    me = lax.axis_index("dp") * 8 + lax.axis_index("fsdp")

    def other(k):
        device = lax.rem(me + k, 32)
        return (device // 8, lax.rem(device, 8))

    return me, other


def open_kernel(
    qkv_shard, out_shard, act_ref, ada_ref, up_shard, down_shard, expert_up, expert_down,
    full, router_t, seen, rows_out, up_line, down_line, up_mate, up_x, up_y, down_own, down_mate,
    shard, heard, part, got, mixed, ssem, rsem, lsem, asem, brsem, tssem, trsem, zssem, zrsem,
    us, ur, ds, dr, es, er, el,
):
    me, other = everyone_else()
    d, s, c = place()
    f = 2 * s + c
    shard[:, 0:576] = qkv_shard[...]
    shard[:, 576:768] = out_shard[...]
    barrier = pltpu.get_barrier_semaphore()

    def hello(k, carry):
        pl.semaphore_signal(barrier, inc=1, device_id=other(k), device_id_type=MESH)
        return carry

    lax.fori_loop(1, 32, hello, 0)
    pl.semaphore_wait(barrier, 31)

    def act_copy(k, source):
        device = other(k)
        return push(act_ref.at[device[1]], heard.at[source], asem.at[k], brsem.at[k], device)

    def send(k, carry):
        act_copy(k, me).start()
        return carry

    lax.fori_loop(1, 32, send, 0)
    gather = Gather("cols", shard, full, ssem, rsem, lsem.at[0])
    gather.start()
    near = Near(
        expert_up, expert_down, up_mate, up_x, up_y, down_own, down_mate, es, er, el.at[0]
    )
    lines = (
        Line("cols", up_shard, up_line, us, ur, lsem.at[3]),
        Line("rows", down_shard, down_line, ds, dr, lsem.at[4]),
    )
    gather.spread_z(1)
    gather.spread_z(2)
    for line in lines:
        line.start()
    heard[me] = act_ref[f]

    def take(k, carry):
        copy = act_copy(k, lax.rem(me + 32 - k, 32))
        copy.wait_recv()
        return carry

    lax.fori_loop(1, 32, take, 0)
    everything = heard[...].reshape(256, 128)
    row = lax.broadcasted_iota(jnp.int32, (64, 256), 0)
    column = lax.broadcasted_iota(jnp.int32, (64, 256), 1)
    source = lax.rem(row // 2, 4) * 8 + row // 8
    pick = (column == source * 8 + lax.rem(row, 2)).astype(jnp.bfloat16)
    compact = jnp.dot(
        pick, everything.astype(jnp.bfloat16), preferred_element_type=jnp.float32
    ).astype(jnp.bfloat16)
    seen[...] = jnp.concatenate(
        [compact.astype(jnp.float32), jnp.sum(heard[...], axis=0)], axis=0
    )
    for column_block in range(8):
        tiles = [heard[8 * j + column_block, 3:5, 0:96] for j in range(4)]
        router_t[:, 96 * column_block : 96 * column_block + 96] = jnp.concatenate(tiles, axis=0)
    part[...] = nn(compact[:, 0:96], ada_ref[...]).reshape(8, 8, 1152)

    def tile_copy(k):
        target = lax.rem(f + k, 8)
        return push(part.at[target], got.at[k], tssem.at[k], trsem.at[k], (d, target))

    for k in range(1, 8):
        tile_copy(k).start()
    gather.relay(0)
    gather.spread_z(3)
    near.start()
    gather.relay(1)
    gather.relay(2)
    for k in range(1, 8):
        tile_copy(k).wait_recv()
    total = part[f]
    for k in range(1, 8):
        total = total + got[k]
    mixed[...] = total
    zs = []
    for k in range(1, 4):
        copy = push(mixed, rows_out.at[d], zssem.at[k], zrsem.at[k], at(lax.rem(d + k, 4), s, c))
        copy.start()
        zs.append(copy)
    own_rows = pltpu.make_async_copy(mixed, rows_out.at[d], lsem.at[2])
    own_rows.start()
    for line in lines:
        line.relay()
    gather.relay(3)
    gather.corner(0)
    gather.corner(1)
    gather.corner(2)
    gather.corner(3)
    gather.finish()
    for line in lines:
        line.finish()
    near.finish()
    own_rows.wait()
    for k in range(1, 4):
        push(
            mixed, rows_out.at[lax.rem(d + 4 - k, 4)], zssem.at[k], zrsem.at[k],
            at(lax.rem(d + k, 4), s, c),
        ).wait_recv()
    for copy in zs:
        copy.wait_send()
    for k in range(1, 8):
        tile_copy(k).wait_send()

    def drain(k, carry):
        act_copy(k, me).wait_send()
        return carry

    lax.fori_loop(1, 32, drain, 0)


DMA = pltpu.SemaphoreType.DMA
ANYWHERE = pl.BlockSpec(memory_space=pl.ANY)
ONCHIP = pl.BlockSpec(memory_space=pltpu.VMEM)


def opening(*operands):
    return pl.pallas_call(
        open_kernel,
        out_shape=(
            jax.ShapeDtypeStruct((768, 3072), jnp.bfloat16),
            jax.ShapeDtypeStruct((8, 768), jnp.float32),
            jax.ShapeDtypeStruct((72, 128), jnp.float32),
            jax.ShapeDtypeStruct((4, 8, 1152), jnp.float32),
            jax.ShapeDtypeStruct((96, 3072), jnp.bfloat16),
            jax.ShapeDtypeStruct((768, 384), jnp.bfloat16),
        )
        + (jax.ShapeDtypeStruct((96, 3072), jnp.bfloat16),) * 3
        + (jax.ShapeDtypeStruct((384, 768), jnp.bfloat16),) * 2,
        in_specs=[ONCHIP] * 6 + [ANYWHERE] * 2,
        out_specs=(ANYWHERE, ONCHIP, ONCHIP) + (ANYWHERE,) * 8,
        scratch_shapes=[
            pltpu.VMEM((96, 768), jnp.bfloat16),
            pltpu.VMEM((32, 8, 128), jnp.float32),
            pltpu.VMEM((8, 8, 1152), jnp.float32),
            pltpu.VMEM((8, 8, 1152), jnp.float32),
            pltpu.VMEM((8, 1152), jnp.float32),
            DMA((GATHER_SEMS,)), DMA((GATHER_SEMS,)), DMA((5,)),
            DMA((32,)), DMA((32,)),
            DMA((8,)), DMA((8,)), DMA((4,)), DMA((4,)),
            DMA((3,)), DMA((3,)), DMA((3,)), DMA((3,)),
            DMA((4,)), DMA((4,)), DMA((1,)),
        ],
        compiler_params=pltpu.CompilerParams(collective_id=0, has_side_effects=True),
        name="opening",
    )(*operands)


def group_of(d, s, c):
    return [(j, at(lax.rem(d + j // 2, 4), s, lax.rem(c + j, 2))) for j in range(1, 8)]


class Swap:
    def __init__(self, blocks, out, ssem, rsem, lsem):
        self.blocks, self.out, self.ssem, self.rsem, self.lsem = blocks, out, ssem, rsem, lsem
        self.d, self.s, self.c = place()
        self.me = 2 * self.d + self.c

    def copy(self, j, landing):
        target_d = lax.rem(self.d + j // 2, 4)
        target_c = lax.rem(self.c + j, 2)
        return push(
            self.blocks.at[2 * target_d + target_c],
            self.out.at[landing],
            self.ssem.at[j],
            self.rsem.at[j],
            at(target_d, self.s, target_c),
        )

    def start(self):
        for j in (4, 5, 2, 3, 6, 7, 1):
            self.copy(j, self.me).start()
        self.own = pltpu.make_async_copy(
            self.blocks.at[self.me], self.out.at[self.me], self.lsem
        )
        self.own.start()

    def send(self, step):
        for j in (2 * step, 2 * step + 1):
            if j:
                self.copy(j, self.me).start()
            else:
                self.own = pltpu.make_async_copy(
                    self.blocks.at[self.me], self.out.at[self.me], self.lsem
                )
                self.own.start()

    def finish(self):
        self.own.wait()
        for j in range(1, 8):
            source_d = lax.rem(self.d + 4 - j // 2, 4)
            source_c = lax.rem(self.c + j, 2)
            copy = self.copy(j, 2 * source_d + source_c)
            copy.wait_recv()
            copy.wait_send()


def nt(left, right):
    return lax.dot_general(left, right, (((1,), (1,)), ((), ())), preferred_element_type=jnp.float32)


def tn(left, right):
    return lax.dot_general(left, right, (((0,), (0,)), ((), ())), preferred_element_type=jnp.float32)


def nn(left, right):
    return jnp.dot(left, right, preferred_element_type=jnp.float32)


GELU_SCALE = 0.7978845608028654


def gelu_pair(v):
    square = v * v
    bend = jnp.tanh(GELU_SCALE * (v + 0.044715 * (square * v)))
    half = 0.5 * (1.0 + bend)
    slope = half + 0.5 * v * (1.0 - bend * bend) * (
        GELU_SCALE * (1.0 + (3.0 * 0.044715) * square)
    )
    return v * half, slope


HIDDEN = 512


def out_kernel(
    rows, grads, up_line, down_line, tokens, d_tokens, up_x, up_y, down_mate, down_x,
    rows_in, grads_in, up_corner, down_x_mate, down_y_mate, down_corner, mixed_out, d_tokens_out, up_grad, down_grad,
    up_full, down_full, tokens_t, d_tokens_t, s1, r1, s2, r2, ssem, rsem, ssem2, rsem2, lsem,
    es, er, fs, fr, gs, gr,
):
    d, s, c = place()
    greet([device for _, device in group_of(d, s, c)] + [at(d, flip(s, 1), c), at(d, flip(s, 2), c)])
    both = (
        Spread("cols", up_line, up_full, ssem, rsem, lsem.at[0]),
        Spread("rows", down_line, down_full, ssem2, rsem2, lsem.at[1]),
    )
    swap_a = Swap(rows, rows_in, s1, r1, lsem.at[2])
    swap_b = Swap(grads, grads_in, s2, r2, lsem.at[3])
    for g in both:
        g.start()
    swap_a.start()
    swap_b.start()
    mates = Pair(down_mate, down_x_mate, down_mate, down_y_mate, gs, gr)
    up_corners = Pair(up_y, up_corner.at[1], up_x, up_corner.at[0], es, er)
    down_corners = Pair(down_y_mate, down_corner.at[1], down_x, down_corner.at[0], fs, fr)
    tokens_t[...] = tokens[...].T
    d_tokens_t[...] = d_tokens[...].T
    mixed_out[...] = jnp.zeros_like(mixed_out)
    d_tokens_out[...] = jnp.zeros_like(d_tokens_out)
    for g in both:
        g.relay()
    mates.start()
    up_corners.start()
    for g in both:
        g.corner()
    for g in both:
        g.finish()

    def block(b, carry):
        where = pl.ds(pl.multiple_of(b * HIDDEN, HIDDEN), HIDDEN)
        up, down = up_full[:, where], down_full[:, where]
        act, slope = gelu_pair(nn(tokens[...], up))
        act = act.astype(jnp.bfloat16)
        mixed_out[...] += nt(act, down)
        down_grad[:, where] = nn(d_tokens_t[...], act).astype(jnp.bfloat16)
        d_pre = (slope * nn(d_tokens[...], down)).astype(jnp.bfloat16)
        d_tokens_out[...] += nt(d_pre, up)
        up_grad[:, where] = nn(tokens_t[...], d_pre).astype(jnp.bfloat16)
        return carry

    lax.fori_loop(0, 1, block, 0)
    mates.finish()
    down_corners.start()
    lax.fori_loop(1, 3072 // HIDDEN, block, 0)
    swap_a.finish()
    swap_b.finish()
    up_corners.finish()
    down_corners.finish()


def outbound(*operands):
    bf, f32 = jnp.bfloat16, jnp.float32
    return pl.pallas_call(
        out_kernel,
        out_shape=(
            jax.ShapeDtypeStruct((8, 144, 768), bf),
            jax.ShapeDtypeStruct((8, 144, 768), bf),
            jax.ShapeDtypeStruct((2, 96, 3072), bf),
            jax.ShapeDtypeStruct((384, 768), bf),
            jax.ShapeDtypeStruct((384, 768), bf),
            jax.ShapeDtypeStruct((2, 384, 768), bf),
            jax.ShapeDtypeStruct((512, 768), f32),
            jax.ShapeDtypeStruct((512, 768), f32),
            jax.ShapeDtypeStruct((768, 3072), bf),
            jax.ShapeDtypeStruct((768, 3072), bf),
        ),
        in_specs=[ONCHIP] * 6 + [ANYWHERE] * 4,
        out_specs=(ANYWHERE,) * 6 + (ONCHIP,) * 4,
        scratch_shapes=[pltpu.VMEM((768, 3072), bf)] * 2
        + [pltpu.VMEM((768, 512), bf)] * 2
        + [DMA((8,))] * 4
        + [DMA((9,))] * 4
        + [DMA((4,))]
        + [DMA((2,))] * 6,
        compiler_params=pltpu.CompilerParams(
            collective_id=1, has_side_effects=True, vmem_limit_bytes=60 << 20
        ),
        name="outbound",
    )(*operands)


def widened(ref):
    return ref[...].astype(jnp.float32)


class Parts:
    def __init__(self, grad, keep, over_x, over_y, sem, rsem=None):
        d, s, c = place()
        sx, sy = flip(s, 1), flip(s, 2)
        sd = flip(sx, 2)
        rows = grad.shape[0] // 8
        slots = (
            (s, 0, keep.at[0, 0], s), (sy, 0, keep.at[0, 1], s),
            (s, 1, keep.at[1, 0], s), (sx, 1, keep.at[1, 1], s),
            (sx, 0, over_x.at[0], sx), (sd, 0, over_x.at[1], sx),
            (sy, 1, over_y.at[0], sy), (sd, 1, over_y.at[1], sy),
        )
        self.copies, self.away = [], []
        for i, (position, h, out, target) in enumerate(slots):
            part = grad.at[pl.ds(pl.multiple_of((2 * position + h) * rows, 32), rows)]
            if i < 4 or rsem is None:
                self.copies.append(pltpu.make_async_copy(part, out, sem.at[i]))
            else:
                self.away.append(push(part, out, sem.at[i], rsem.at[i], at(d, target, c)))

    def start(self):
        for copy in self.away + self.copies:
            copy.start()

    def finish(self):
        for copy in self.copies + self.away:
            copy.wait()


class Pieces:
    def __init__(self, parts, full, sem):
        d, s, c = place()
        rows = full.shape[0] // 8
        sx, sy = flip(s, 1), flip(s, 2)
        positions = [p for p in (s, sx, sy, flip(sx, 2)) for _ in range(2)]
        self.copies = [
            pltpu.make_async_copy(
                part,
                full.at[pl.ds(pl.multiple_of(rows * (2 * p + (c if i % 2 == 0 else 1 - c)), 32), rows)],
                sem.at[i],
            )
            for i, (p, part) in enumerate(zip(positions, parts))
        ]

    def start(self):
        for copy in self.copies:
            copy.start()

    def finish(self):
        for copy in self.copies:
            copy.wait()


def expert_kernel(
    rows, grads, expert_up, up_m, up_x0, up_x1, up_y0, up_y1, up_corner,
    down_own, down_m, down_x0, down_x1, down_y0, down_y1, down_corner, first_grad, second_grad,
    rows_back, grads_back, up_keep, up_x, up_y, down_keep, down_x, down_y, first_part, second_part,
    up, down, act, d_pre, made, d_made, total, d_total, up_grad, down_grad, rows_t,
    fo, fm, fn, ff, fs, fr, fl, so, sm, sn, sf, ss, sr, sl,
    s1, r1, s2, r2, lsem, wsem, vsem, psem, arsem, qsem,
):
    bf = jnp.bfloat16
    d, s, c = place()
    weights = (
        Pieces(
            (expert_up.at[c], up_m, up_x0, up_x1, up_y0, up_y1, up_corner.at[0], up_corner.at[1]), up, wsem
        ),
        Pieces(
            (down_own, down_m, down_x0, down_x1, down_y0, down_y1, down_corner.at[0], down_corner.at[1]),
            down, vsem,
        ),
    )
    for each in weights:
        each.start()
    greet([device for _, device in group_of(d, s, c)] + [at(d, flip(s, 1), c), at(d, flip(s, 2), c)])
    sums = (
        DenseSum("cols", first_grad, first_part, fo, fm, fn, ff, None, fs, fr, fl),
        DenseSum("rows", second_grad, second_part, so, sm, sn, sf, None, ss, sr, sl),
    )
    for each in sums:
        each.start()
    swap_a = Swap(made, rows_back, s1, r1, lsem.at[0])
    swap_b = Swap(d_made, grads_back, s2, r2, lsem.at[1])
    for each in weights:
        each.finish()
    for step in (2, 1, 3, 0):
        there = lax.rem(d + step, 4)
        chunk = pl.ds(2 * there, 2)
        lines = pl.ds(pl.multiple_of(288 * there, 288), 288)
        x = rows[chunk].reshape(288, 768)
        g = grads[chunk].reshape(288, 768)
        total[...] = jnp.zeros_like(total)
        d_total[...] = jnp.zeros_like(d_total)

        def block(b, carry):
            where = pl.ds(pl.multiple_of(b * HIDDEN, HIDDEN), HIDDEN)
            up_part, down_part = up[:, where], down[where]
            made_act, slope = gelu_pair(nn(x, up_part))
            made_act = made_act.astype(bf)
            act[lines, where] = made_act
            total[...] += nn(made_act, down_part)
            d_part = (slope * nt(g, down_part)).astype(bf)
            d_pre[lines, where] = d_part
            d_total[...] += nt(d_part, up_part)
            return carry

        lax.fori_loop(0, 3072 // HIDDEN, block, 0)
        made[chunk] = total[...].astype(bf).reshape(2, 144, 768)
        d_made[chunk] = d_total[...].astype(bf).reshape(2, 144, 768)
        swap_a.send(step)
        swap_b.send(step)
        if step == 2:
            for each in sums:
                each.merge()
        if step == 3:
            for each in sums:
                each.join()
    rows_t[...] = rows.reshape(1152, 768)[...].T
    g_all = grads.reshape(1152, 768)

    def up_block(b, carry):
        where = pl.ds(pl.multiple_of(b * HIDDEN, HIDDEN), HIDDEN)
        up_grad[:, where] = nn(rows_t[...], d_pre[:, where]).astype(bf)
        return carry

    def down_block(b, carry):
        where = pl.ds(pl.multiple_of(384 * b, 384), 384)
        down_grad[where] = tn(act[:, where], g_all[...]).astype(bf)
        return carry

    up_parts = Parts(up_grad, up_keep, up_x, up_y, psem, arsem)
    down_parts = Parts(down_grad, down_keep, down_x, down_y, qsem)
    lax.fori_loop(0, 3072 // HIDDEN, up_block, 0)
    up_parts.start()
    lax.fori_loop(0, 8, down_block, 0)
    down_parts.start()
    for each in sums:
        each.close()
    swap_a.finish()
    swap_b.finish()
    up_parts.finish()
    down_parts.finish()


def experts(rows, grads, up_pieces, down_pieces, first_grad, second_grad):
    bf, f32 = jnp.bfloat16, jnp.float32

    def rooms(piece, half):
        return [
            pltpu.VMEM((4,) + piece, bf),
            pltpu.VMEM((4,) + piece, bf),
            pltpu.VMEM((2,) + half, bf),
            pltpu.VMEM((2,) + piece, bf),
            DMA((8,)),
            DMA((8,)),
            DMA((4,)),
        ]

    def parts(r, n):
        return (
            jax.ShapeDtypeStruct((2, 2, r, n), bf),
            jax.ShapeDtypeStruct((2, r, n), bf),
            jax.ShapeDtypeStruct((2, r, n), bf),
        )

    return pl.pallas_call(
        expert_kernel,
        out_shape=(
            jax.ShapeDtypeStruct((8, 144, 768), bf),
            jax.ShapeDtypeStruct((8, 144, 768), bf),
        )
        + parts(96, 3072)
        + parts(384, 768)
        + (
            jax.ShapeDtypeStruct((96, 3072), bf),
            jax.ShapeDtypeStruct((768, 384), bf),
        ),
        in_specs=[ONCHIP, ONCHIP] + [ANYWHERE] * 16,
        out_specs=(ANYWHERE,) * 8 + (ONCHIP, ONCHIP),
        scratch_shapes=[
            pltpu.VMEM((768, 3072), bf),
            pltpu.VMEM((3072, 768), bf),
            pltpu.VMEM((1152, 3072), bf),
            pltpu.VMEM((1152, 3072), bf),
            pltpu.VMEM((8, 144, 768), bf),
            pltpu.VMEM((8, 144, 768), bf),
            pltpu.VMEM((288, 768), f32),
            pltpu.VMEM((288, 768), f32),
            pltpu.VMEM((768, 3072), bf),
            pltpu.VMEM((3072, 768), bf),
            pltpu.VMEM((768, 1152), bf),
        ]
        + rooms((96, 3072), (96, 1536))
        + rooms((768, 384), (384, 384))
        + [DMA((8,))] * 4
        + [DMA((2,)), DMA((8,)), DMA((8,)), DMA((8,)), DMA((8,)), DMA((8,))],
        compiler_params=pltpu.CompilerParams(
            collective_id=2, has_side_effects=True, vmem_limit_bytes=67043328
        ),
        name="experts",
    )(rows, grads, *up_pieces, *down_pieces, first_grad, second_grad)


def hop(values, bit):
    return lax.ppermute(values, "fsdp", [(f, f ^ bit) for f in range(8)])


def square_next(keep, from_x, from_y):
    f32, bf = jnp.float32, jnp.bfloat16
    return (
        hop((keep[0, 1].astype(f32) + from_x[1].astype(f32)).astype(bf), 4),
        hop((keep[1, 1].astype(f32) + from_y[1].astype(f32)).astype(bf), 2),
    )


class DenseSum:
    def __init__(self, kind, grad, out, own, mate, near, far, line, ssem, rsem, lsem, part=None):
        self.kind, self.grad, self.out, self.part = kind, grad, out, part
        self.own, self.mate, self.near, self.far, self.line = own, mate, near, far, line
        self.ssem, self.rsem, self.lsem = ssem, rsem, lsem
        self.d, self.s, self.c = place()
        self.order = (
            flip(flip(self.s, 1), 2),
            flip(self.s, 1),
            flip(self.s, 2),
            self.s,
        )

    def piece(self, f):
        if self.part is not None:
            return self.grad.at[pl.ds(pl.multiple_of(96 * f + 48 * self.part, 48), 48)]
        if self.kind == "cols":
            return self.grad.at[pl.ds(pl.multiple_of(96 * f, 96), 96)]
        return self.grad.at[:, pl.ds(pl.multiple_of(384 * f, 384), 384)]

    def half(self, ref, h):
        if self.kind == "cols":
            return ref.at[:, pl.ds(1536 * h, 1536)]
        return ref.at[pl.ds(384 * h, 384)]

    def quarter(self, ref, q):
        if self.kind == "cols":
            return ref.at[:, pl.ds(pl.multiple_of(768 * q, 768), 768)]
        return ref.at[pl.ds(pl.multiple_of(192 * q, 192), 192)]

    def start(self):
        d, s, c = self.d, self.s, self.c
        self.zero, self.local = [], []
        for j, position in enumerate(self.order):
            copy = push(
                self.piece(2 * position + 1 - c), self.mate.at[j], self.ssem.at[j], self.rsem.at[j], at(d, s, 1 - c)
            )
            copy.start()
            self.zero.append(copy)
            copy = pltpu.make_async_copy(self.piece(2 * position + c), self.own.at[j], self.lsem.at[j])
            copy.start()
            self.local.append(copy)

    def merge(self):
        d, s, c = self.d, self.s, self.c
        sx, sy = flip(s, 1), flip(s, 2)
        self.one = []
        for j in range(4):
            self.zero[j].wait_recv()
            self.local[j].wait()
            self.own[j] = (widened(self.own.at[j]) + widened(self.mate.at[j])).astype(jnp.bfloat16)
            if j == 0:
                for h, target in enumerate((sx, sy)):
                    copy = push(
                        self.half(self.own.at[0], h), self.near.at[h], self.ssem.at[4 + h], self.rsem.at[4 + h],
                        at(d, target, c),
                    )
                    copy.start()
                    self.one.append(copy)

    def join(self):
        d, s, c = self.d, self.s, self.c
        sx, sy = flip(s, 1), flip(s, 2)
        for h, j in ((0, 2), (1, 1)):
            self.one[h].wait_recv()
            where = self.half(self.own.at[j], h)
            where[...] = (widened(where) + widened(self.near.at[h])).astype(jnp.bfloat16)
        self.two = []
        for h, target in enumerate((sx, sy)):
            copy = push(
                self.own.at[1 + h], self.far.at[h], self.ssem.at[6 + h], self.rsem.at[6 + h], at(d, target, c)
            )
            copy.start()
            self.two.append(copy)

    def square(self):
        for copy in self.two:
            copy.wait_recv()
        return (
            widened(self.own.at[3]) + widened(self.far.at[0]) + widened(self.far.at[1])
        ).astype(jnp.bfloat16)

    def along(self):
        d, s, c = self.d, self.s, self.c
        self.own[3] = self.square()
        self.three = []
        for k in range(1, 4):
            target = lax.rem(d + k, 4)
            copy = push(
                self.quarter(self.own.at[3], target), self.line.at[k - 1], self.ssem.at[7 + k], self.rsem.at[7 + k],
                at(target, s, c),
            )
            copy.start()
            self.three.append(copy)

    def finish(self):
        total = widened(self.quarter(self.own.at[3], self.d))
        for k in range(1, 4):
            self.three[k - 1].wait_recv()
            total = total + widened(self.line.at[k - 1])
        self.out[...] = total
        self.sent(self.three)

    def close(self):
        self.out[...] = self.square()
        self.sent([])

    def sent(self, more):
        for copy in self.zero + self.one + self.two + more:
            copy.wait_send()


class LineSum:
    def __init__(self, kind, part, out, landing, ssem, rsem):
        self.kind, self.part, self.out, self.landing = kind, part, out, landing
        self.ssem, self.rsem = ssem, rsem
        self.d, self.s, self.c = place()

    def quarter(self, q):
        if self.kind == "cols":
            return self.part.at[:, pl.ds(pl.multiple_of(768 * q, 768), 768)]
        return self.part.at[pl.ds(pl.multiple_of(192 * q, 192), 192)]

    def start(self):
        self.copies = []
        for k in range(1, 4):
            target = lax.rem(self.d + k, 4)
            copy = push(
                self.quarter(target), self.landing.at[k - 1], self.ssem.at[k - 1], self.rsem.at[k - 1],
                at(target, self.s, self.c),
            )
            copy.start()
            self.copies.append(copy)

    def finish(self):
        total = widened(self.quarter(self.d))
        for k in range(3):
            self.copies[k].wait_recv()
            total = total + widened(self.landing.at[k])
        self.out[...] = total
        for copy in self.copies:
            copy.wait_send()


class Ending:
    def __init__(self, keep, from_x, from_y, out, room, stage, landed, last, lsem, ssem, rsem, loaded=None):
        self.out, self.room, self.stage, self.landed, self.last = out, room, stage, landed, last
        self.ssem, self.rsem = ssem, rsem
        self.d, self.s, self.c = place()
        sources = [
            keep.at[0, 0], keep.at[0, 1], keep.at[1, 0], keep.at[1, 1],
            from_x.at[0], from_x.at[1], from_y.at[0], from_y.at[1],
        ]
        self.loads = [
            pltpu.make_async_copy(source, room.at[i], lsem.at[i]) for i, source in enumerate(sources)
        ]
        for i, source in enumerate(loaded or ()):
            self.loads.append(pltpu.make_async_copy(source, landed.at[i], lsem.at[8 + i]))
        self.sent = []

    def load(self):
        for copy in self.loads:
            copy.start()

    def loaded(self):
        for copy in self.loads:
            copy.wait()

    def go(self, index, target):
        dst = self.last if index == 2 else self.landed.at[index]
        copy = push(self.stage.at[index], dst, self.ssem.at[index], self.rsem.at[index], target)
        copy.start()
        self.sent.append(copy)

    def next(self):
        bf = jnp.bfloat16
        room = self.room
        self.stage[0] = (widened(room.at[1]) + widened(room.at[5])).astype(bf)
        self.go(0, at(self.d, flip(self.s, 2), self.c))
        self.stage[1] = (widened(room.at[3]) + widened(room.at[7])).astype(bf)
        self.go(1, at(self.d, flip(self.s, 1), self.c))

    def close(self):
        for copy in self.sent:
            copy.wait_recv()
        c = self.c
        mine, theirs = c, 1 - c

        def total(h):
            return (
                widened(self.room.at[2 * h]) + widened(self.room.at[4 + 2 * h]) + widened(self.landed.at[h])
            )

        self.stage[2] = total(theirs).astype(jnp.bfloat16)
        self.go(2, at(self.d, self.s, 1 - c))
        self.out[c] = total(mine)

    def finish(self):
        self.sent[-1].wait_recv()
        self.out[1 - self.c] = widened(self.last)
        for copy in self.sent:
            copy.wait_send()


class Tail:
    def __init__(self, d_rows, router, act, ada, ada_out, d_act_out, router_out, z1, plane, plane_in, z2, z2_in, sems):
        self.d_rows, self.router, self.act, self.ada = d_rows, router, act, ada
        self.ada_out, self.d_act_out, self.router_out = ada_out, d_act_out, router_out
        self.z1, self.plane, self.plane_in, self.z2, self.z2_in = z1, plane, plane_in, z2, z2_in
        self.sems = sems
        self.d, self.s, self.c = place()
        self.f = 2 * self.s + self.c

    def z_copy(self, k, src, dst, base):
        send, recv = self.sems[base], self.sems[base + 1]
        return push(src, dst, send.at[k], recv.at[k], at(lax.rem(self.d + k, 4), self.s, self.c))

    def f_copy(self, k, src, dst, base):
        send, recv = self.sems[base], self.sems[base + 1]
        return push(src, dst, send.at[k], recv.at[k], (self.d, lax.rem(self.f + k, 8)))

    def start(self):
        self.all = [
            self.z_copy(k, self.d_rows.at[lax.rem(self.d + k, 4)], self.z1.at[k], 0) for k in range(1, 4)
        ]
        for copy in self.all:
            copy.start()

    def second(self):
        total = self.d_rows[self.d]
        for k in range(1, 4):
            self.all[k - 1].wait_recv()
            total = total + self.z1[k]
        for target in range(8):
            self.plane[target, :, 0:1152] = total
            self.plane[target, :, 1152:1280] = self.router[target]
        copies = [
            self.f_copy(k, self.plane.at[lax.rem(self.f + k, 8)], self.plane_in.at[lax.rem(8 - k, 8)], 2)
            for k in range(1, 8)
        ]
        for copy in copies:
            copy.start()
        self.in_plane = copies
        self.all = self.all + copies

    def third(self):
        f = self.f
        self.plane_in[0] = self.plane[f]
        for copy in self.in_plane:
            copy.wait_recv()
        everything = self.plane_in[...]
        router = jnp.sum(everything[:, :, 1152:1280], axis=0)
        rows = everything[:, :, 0:1152].reshape(64, 1152)
        line = lax.broadcasted_iota(jnp.int32, (64, 64), 0)
        column = lax.broadcasted_iota(jnp.int32, (64, 64), 1)
        turn = (lax.rem(line // 8 + 8 - f, 8) * 8 + lax.rem(line, 8) == column).astype(jnp.bfloat16)
        d_mod = nn(turn, rows.astype(jnp.bfloat16)).astype(jnp.bfloat16)
        self.ada_out[...] = tn(self.act[...], d_mod)[0:96]
        part = nt(d_mod, self.ada[...])
        self.z2[0:64, 0:96] = part
        self.z2[0:64, 96:128] = jnp.zeros((64, 32), jnp.float32)
        self.z2[64:72, :] = router
        copies = [self.z_copy(k, self.z2, self.z2_in.at[k], 4) for k in range(1, 4)]
        for copy in copies:
            copy.start()
        self.along = copies
        self.all = self.all + copies

    def fourth(self):
        total = self.z2[...]
        for k in range(1, 4):
            self.along[k - 1].wait_recv()
            total = total + self.z2_in[k]
        self.router_out[...] = total[64:72]
        self.z2_in[0] = total
        copies = [
            self.f_copy(
                k,
                self.z2_in.at[0, pl.ds(pl.multiple_of(8 * lax.rem(self.f + k, 8), 8), 8)],
                self.d_act_out.at[self.f],
                6,
            )
            for k in range(1, 8)
        ]
        for copy in copies:
            copy.start()
        self.d_act_out[self.f] = self.z2_in[0, pl.ds(pl.multiple_of(8 * self.f, 8), 8)]
        self.last = copies
        self.all = self.all + copies

    def finish(self):
        for k in range(1, 8):
            self.f_copy(
                k, self.z2_in.at[0, pl.ds(0, 8)], self.d_act_out.at[lax.rem(self.f + 8 - k, 8)], 6
            ).wait_recv()
        for copy in self.all:
            copy.wait_send()


def dense_kernel(
    grad, first_part, second_part, d_rows, router, act, ada,
    up_keep, up_x, up_y, up_low, up_high, down_keep, down_x, down_y,
    out, first_out, second_out, ada_out, d_act_out, router_out, up_out, down_out,
    ur, us, ul, ue, ula, usa, ura, dr, ds, dl, de, dla, dsa, dra,
    own, mate, near, far, line, ssem, rsem, lsem,
    own_2, mate_2, near_2, far_2, line_2, ssem_2, rsem_2, lsem_2,
    first_in, fs, fr, second_in, ss, sr, *rest,
):
    d, s, c = place()
    f = 2 * s + c
    greet(
        [at(lax.rem(d + k, 4), s, c) for k in range(1, 4)]
        + [(d, lax.rem(f + k, 8)) for k in range(1, 8)]
    )
    both = (
        DenseSum("cols", grad, out.at[pl.ds(0, 48)], own, mate, near, far, line, ssem, rsem, lsem, 0),
        DenseSum(
            "cols", grad, out.at[pl.ds(48, 48)], own_2, mate_2, near_2, far_2, line_2, ssem_2, rsem_2, lsem_2, 1
        ),
    )
    lines = (
        LineSum("cols", first_part, first_out, first_in, fs, fr),
        LineSum("rows", second_part, second_out, second_in, ss, sr),
    )
    tail = Tail(d_rows, router, act, ada, ada_out, d_act_out, router_out, *rest[:5], rest[5:])
    ups = Ending(up_keep, up_x, up_y, up_out, ur, us, ul, ue, ula, usa, ura, (up_low, up_high))
    downs = Ending(down_keep, down_x, down_y, down_out, dr, ds, dl, de, dla, dsa, dra)
    tail.start()
    for each in both:
        each.start()
    for each in lines:
        each.start()
    downs.load()
    ups.load()
    for each in both:
        each.merge()
    tail.second()
    for each in both:
        each.join()
    downs.loaded()
    downs.next()
    tail.third()
    for each in both:
        each.along()
    ups.loaded()
    ups.close()
    tail.fourth()
    downs.close()
    for each in lines:
        each.finish()
    ups.finish()
    for each in both:
        each.finish()
    downs.finish()
    tail.finish()


def dense_sums(grad, first_part, second_part, small, routed):
    bf, f32 = jnp.bfloat16, jnp.float32

    def rooms(r, n):
        return [
            pltpu.VMEM((8, r, n), bf),
            pltpu.VMEM((3, r, n), bf),
            pltpu.VMEM((2, r, n), bf),
            pltpu.VMEM((r, n), bf),
            DMA((10,)),
            DMA((3,)),
            DMA((3,)),
        ]

    return pl.pallas_call(
        dense_kernel,
        out_shape=(
            jax.ShapeDtypeStruct((96, 768), f32),
            jax.ShapeDtypeStruct((96, 768), f32),
            jax.ShapeDtypeStruct((192, 384), f32),
            jax.ShapeDtypeStruct((96, 1152), f32),
            jax.ShapeDtypeStruct((8, 8, 128), f32),
            jax.ShapeDtypeStruct((8, 128), f32),
            jax.ShapeDtypeStruct((2, 96, 3072), f32),
            jax.ShapeDtypeStruct((2, 384, 768), f32),
        ),
        in_specs=[ANYWHERE] + [ONCHIP] * 6 + [ANYWHERE] * 8,
        out_specs=(ONCHIP,) * 8,
        scratch_shapes=rooms(96, 3072) + rooms(384, 768) + [
            pltpu.VMEM((4, 48, 3072), bf),
            pltpu.VMEM((4, 48, 3072), bf),
            pltpu.VMEM((2, 48, 1536), bf),
            pltpu.VMEM((2, 48, 3072), bf),
            pltpu.VMEM((3, 48, 768), bf),
            DMA((11,)), DMA((11,)), DMA((4,)),
        ] * 2 + [
            pltpu.VMEM((3, 96, 768), bf),
            DMA((3,)), DMA((3,)),
            pltpu.VMEM((3, 192, 384), bf),
            DMA((3,)), DMA((3,)),
            pltpu.VMEM((4, 8, 1152), f32),
            pltpu.VMEM((8, 8, 1280), f32),
            pltpu.VMEM((8, 8, 1280), f32),
            pltpu.VMEM((72, 128), f32),
            pltpu.VMEM((4, 72, 128), f32),
            DMA((4,)), DMA((4,)), DMA((8,)), DMA((8,)), DMA((4,)), DMA((4,)), DMA((8,)), DMA((8,)),
        ],
        compiler_params=pltpu.CompilerParams(
            collective_id=3, has_side_effects=True, vmem_limit_bytes=60 << 20
        ),
        cost_estimate=pl.CostEstimate(flops=40_000_000_000, bytes_accessed=20_000_000, transcendentals=0),
        name="dense_sums",
    )(grad, first_part, second_part, *small, *routed)


def layer_stats(values_in):
    centred = values_in - jnp.mean(values_in, axis=-1, keepdims=True)
    inv_std = lax.rsqrt(jnp.mean(centred * centred, axis=-1, keepdims=True) + 1e-06)
    return centred * inv_std, inv_std


def lines_of(tile, first):
    row = lax.broadcasted_iota(jnp.int32, tile.shape, 0)
    picked = [
        jnp.sum(jnp.where(row == first + i, tile, 0.0), axis=0, keepdims=True) for i in range(2)
    ]
    return jnp.concatenate(picked, axis=0)


def modulated(inside, mod, part):
    columns = slice(768 * part, 768 * part + 768)
    return inside[:, 0:1] * mod[0:1, columns] + inside[:, 1:2] * mod[1:2, columns]


def head_column(g):
    return 768 * (g // 9) + 64 * (g % 9)


QUERY_ROWS = 512


def front_kernel(
    tokens, mod_rows, inside, seg_col, seg_row, qkvo, router_t, cotangent, routes, target,
    heads, totals, attended, projected, residual, second, d_mixed, gates, rows, grads, mod,
    bias, made, weighted,
):
    bf, f32 = jnp.bfloat16, jnp.float32
    d = lax.axis_index("dp")
    for j in range(4):
        mod[:, 1152 * j : 1152 * j + 1152] = lines_of(mod_rows[j], 2 * d)
    token_float = tokens[...].astype(f32)
    normed, _ = layer_stats(token_float)
    first = (normed * (1.0 + modulated(inside, mod, 1)) + modulated(inside, mod, 0)).astype(bf)
    for j in range(4):
        piece = nn(first, qkvo[:, 768 * j : 768 * j + 640]).astype(bf)
        for i in range(9):
            heads[9 * j + i] = piece[:, 64 * i : 64 * i + 64]
    bias[...] = jnp.where(seg_col[...] == seg_row[...], 0.0, -1e30)

    def block(n, carry):
        h, part = n // (512 // QUERY_ROWS), lax.rem(n, 512 // QUERY_ROWS)
        lines = pl.ds(pl.multiple_of(part * QUERY_ROWS, QUERY_ROWS), QUERY_ROWS)
        scores = nt(heads[h, lines], heads[12 + h]) * 0.125 + bias[lines]
        row_max = jnp.max(scores, axis=-1, keepdims=True)
        weight = jnp.exp(scores - row_max)
        running = jnp.sum(weight, axis=-1, keepdims=True)
        probability = (weight * (1.0 / running)).astype(bf)
        made[h, lines] = nn(probability, heads[24 + h]).astype(bf)
        totals[h, lines] = row_max + jnp.log(running)
        return carry

    lax.fori_loop(0, 12 * (512 // QUERY_ROWS), block, 0)
    for h in range(12):
        attended[:, 64 * h : 64 * h + 64] = made[h]
    for j in range(4):
        piece = nn(attended[...], qkvo[:, 768 * j + 512 : 768 * j + 768])
        projected[:, 192 * j : 192 * j + 192] = piece[:, 64:256]
    residual[...] = token_float + modulated(inside, mod, 2) * projected[...]
    normed, _ = layer_stats(residual[...])
    second[...] = (normed * (1.0 + modulated(inside, mod, 4)) + modulated(inside, mod, 3)).astype(bf)
    logits = nt(second[...], router_t[...].astype(bf))
    ids = lax.broadcasted_iota(jnp.int32, (512, 8), 1)
    chosen = [
        jnp.sum(jnp.where(ids == routes[:, k : k + 1], logits, 0.0), axis=-1, keepdims=True)
        for k in range(2)
    ]
    top = jnp.maximum(chosen[0], chosen[1])
    raised = [jnp.exp(each - top) for each in chosen]
    share = [each / (raised[0] + raised[1]) for each in raised]
    pair = lax.broadcasted_iota(jnp.int32, (512, 2), 1)
    gates[...] = jnp.where(pair == 0, share[0], share[1])
    mixed_grad = modulated(inside, mod, 5) * cotangent[...].astype(f32)
    d_mixed[...] = mixed_grad.astype(bf)
    for k in range(2):
        weighted[k] = (share[k] * mixed_grad).astype(bf)

    def send(b, carry):
        lines = pl.ds(pl.multiple_of(288 * b, 288), 288)
        places = lax.broadcasted_iota(jnp.int32, (288, 512), 0) + 288 * b
        first_hot = (places == target[0:1]).astype(f32)
        second_hot = (places == target[1:2]).astype(f32)
        rows[lines] = nn((first_hot + second_hot).astype(bf), second[...]).astype(bf)
        grads[lines] = (
            nn(first_hot.astype(bf), weighted[0]) + nn(second_hot.astype(bf), weighted[1])
        ).astype(bf)
        return carry

    lax.fori_loop(0, 4, send, 0)


def front(*operands):
    bf, f32 = jnp.bfloat16, jnp.float32
    return pl.pallas_call(
        front_kernel,
        out_shape=(
            jax.ShapeDtypeStruct((36, 512, 64), bf),
            jax.ShapeDtypeStruct((12, 512, 1), f32),
            jax.ShapeDtypeStruct((512, 768), bf),
            jax.ShapeDtypeStruct((512, 768), f32),
            jax.ShapeDtypeStruct((512, 768), f32),
            jax.ShapeDtypeStruct((512, 768), bf),
            jax.ShapeDtypeStruct((512, 768), bf),
            jax.ShapeDtypeStruct((512, 2), f32),
            jax.ShapeDtypeStruct((1152, 768), bf),
            jax.ShapeDtypeStruct((1152, 768), bf),
            jax.ShapeDtypeStruct((2, 4608), f32),
        ),
        in_specs=[ONCHIP] * 10,
        out_specs=(ONCHIP,) * 11,
        scratch_shapes=[
            pltpu.VMEM((512, 512), f32),
            pltpu.VMEM((12, 512, 64), bf),
            pltpu.VMEM((2, 512, 768), bf),
        ],
        compiler_params=pltpu.CompilerParams(vmem_limit_bytes=60 << 20),
        cost_estimate=pl.CostEstimate(flops=40_000_000_000, bytes_accessed=20_000_000, transcendentals=0),
        name="front",
    )(*operands)


def norm_grad(upstream, normed, inv_std):
    return (
        upstream
        - jnp.mean(upstream, axis=-1, keepdims=True)
        - normed * jnp.mean(upstream * normed, axis=-1, keepdims=True)
    ) * inv_std


def rear_kernel(
    tokens, mod, inside, seg_col, seg_row, qkvo_in, router_t, cotangent, routes, target,
    heads_in, totals_in, attended_in, projected, residual, second, gates,
    returned, d_returned, shared_out, d_shared,
    output, tokens_grad, qkvo_grad, d_mod, router_grad,
    bias, rows_t, d_heads, d_att, d_att_t, d_rows_t, d_rows, d_residual, d_proj,
    qkvo, heads, totals, attended, sem,
):
    bf, f32 = jnp.bfloat16, jnp.float32
    pairs = ((heads_in, heads), (qkvo_in, qkvo), (totals_in, totals), (attended_in, attended))
    loads = [pltpu.make_async_copy(src, dst, sem.at[i]) for i, (src, dst) in enumerate(pairs)]
    for copy in loads:
        copy.start()
    upstream = cotangent[...].astype(f32)

    def image_sums(part, values):
        for j in range(2):
            d_mod[j : j + 1, 768 * part : 768 * part + 768] = jnp.sum(
                inside[:, j : j + 1] * values, axis=0, keepdims=True
            )

    share = [gates[:, k : k + 1] for k in range(2)]
    places = lax.broadcasted_iota(jnp.int32, (512, 1152), 1)
    hot = [(places == target[:, k : k + 1]).astype(f32).astype(bf) for k in range(2)]
    picked = [nn(each, returned[...]) for each in hot]
    mixed = shared_out[...] + (share[0] * picked[0] + share[1] * picked[1])
    gate_two = modulated(inside, mod, 5)
    output[...] = (residual[...] + gate_two * mixed).astype(bf)
    image_sums(5, upstream * mixed)
    mixed_grad = gate_two * upstream
    d_share = [jnp.sum(mixed_grad * each, axis=-1, keepdims=True) for each in picked]
    inner = share[0] * d_share[0] + share[1] * d_share[1]
    ids = lax.broadcasted_iota(jnp.int32, (512, 8), 1)
    d_logits = sum(
        jnp.where(ids == routes[:, k : k + 1], share[k] * (d_share[k] - inner), 0.0) for k in range(2)
    ).astype(bf)
    router_grad[...] = tn(d_logits, second[...])
    d_second = (
        d_shared[...] + nn(d_logits, router_t[...].astype(bf)) + (nn(hot[0], d_returned[...]) + nn(hot[1], d_returned[...]))
    )
    normed, inv_std = layer_stats(residual[...])
    image_sums(3, d_second)
    image_sums(4, d_second * normed)
    d_residual[...] = upstream + norm_grad(d_second * (1.0 + modulated(inside, mod, 4)), normed, inv_std)
    gate_one = modulated(inside, mod, 2)
    image_sums(2, d_residual[...] * projected[...])
    d_proj[...] = (gate_one * d_residual[...]).astype(bf)
    for copy in loads:
        copy.wait()
    d_attended = jnp.zeros((512, 768), f32)
    for j in range(4):
        piece = jnp.concatenate(
            [jnp.zeros((512, 64), bf), d_proj[:, 192 * j : 192 * j + 192]], axis=1
        )
        d_attended += nt(piece, qkvo[:, 768 * j + 512 : 768 * j + 768])
    d_attended = d_attended.astype(bf)
    d_att_t[...] = d_attended.T
    for h in range(12):
        d_att[h] = d_attended[:, 64 * h : 64 * h + 64]
    for j in range(18):
        pair = jnp.concatenate([heads[2 * j], heads[2 * j + 1]], axis=1)
        rows_t[128 * j : 128 * j + 128] = pair.T
    bias[...] = jnp.where(seg_col[...] == seg_row[...], 0.0, -1e30)

    def head(h, carry):
        def at_head(g):
            return pl.ds(pl.multiple_of(64 * g, 64), 64)

        d_key, d_value = jnp.zeros((64, 512), f32), jnp.zeros((64, 512), f32)
        for part in range(512 // QUERY_ROWS):
            lines = slice(part * QUERY_ROWS, (part + 1) * QUERY_ROWS)
            scores = nn(heads[h, lines], rows_t[at_head(12 + h)]) * 0.125 + bias[lines]
            probability = jnp.exp(scores - totals[h, lines])
            d_prob = nn(d_att[h, lines], rows_t[at_head(24 + h)])
            inner = jnp.sum(probability * d_prob, axis=-1, keepdims=True)
            d_scores = (probability * (d_prob - inner)).astype(bf)
            d_heads[h, lines] = (nn(d_scores, heads[12 + h]) * 0.125).astype(bf)
            d_key += nn(rows_t[at_head(h), lines], d_scores)
            d_value += nn(d_att_t[at_head(h), lines], probability.astype(bf))
        d_rows_t[at_head(h)] = (d_key * 0.125).astype(bf)
        d_rows_t[at_head(12 + h)] = d_value.astype(bf)
        return carry

    lax.fori_loop(0, 12, head, 0)
    for g in range(12):
        column = head_column(g)
        d_rows[:, column : column + 64] = d_heads[g]
    for j in range(12):
        pair = d_rows_t[128 * j : 128 * j + 128].T
        for i in range(2):
            column = head_column(12 + 2 * j + i)
            d_rows[:, column : column + 64] = pair[:, 64 * i : 64 * i + 64]
    for j in range(4):
        d_rows[:, 768 * j + 576 : 768 * j + 768] = jnp.zeros((512, 192), bf)
    token_float = tokens[...].astype(f32)
    normed, inv_std = layer_stats(token_float)
    scale_one = 1.0 + modulated(inside, mod, 1)
    first_t = (normed * scale_one + modulated(inside, mod, 0)).astype(bf).T
    attended_t = attended[...].T
    for j in range(4):
        qkvo_grad[:, 768 * j : 768 * j + 640] = nn(first_t, d_rows[:, 768 * j : 768 * j + 640]).astype(bf)
        qkvo_grad[:, 768 * j + 576 : 768 * j + 768] = nn(
            attended_t, d_proj[:, 192 * j : 192 * j + 192]
        ).astype(bf)
    d_first = nt(d_rows[...], qkvo[...])
    image_sums(0, d_first)
    image_sums(1, d_first * normed)
    tokens_grad[...] = d_residual[...] + norm_grad(d_first * scale_one, normed, inv_std)


def rear(*operands):
    bf, f32 = jnp.bfloat16, jnp.float32
    return pl.pallas_call(
        rear_kernel,
        out_shape=(
            jax.ShapeDtypeStruct((512, 768), bf),
            jax.ShapeDtypeStruct((512, 768), f32),
            jax.ShapeDtypeStruct((768, 3072), bf),
            jax.ShapeDtypeStruct((2, 4608), f32),
            jax.ShapeDtypeStruct((8, 768), f32),
        ),
        in_specs=[ANYWHERE if i in (5, 10, 11, 12) else ONCHIP for i in range(len(operands))],
        out_specs=(ONCHIP,) * 5,
        scratch_shapes=[
            pltpu.VMEM((512, 512), f32),
            pltpu.VMEM((2304, 512), bf),
            pltpu.VMEM((12, 512, 64), bf),
            pltpu.VMEM((12, 512, 64), bf),
            pltpu.VMEM((768, 512), bf),
            pltpu.VMEM((1536, 512), bf),
            pltpu.VMEM((512, 3072), bf),
            pltpu.VMEM((512, 768), f32),
            pltpu.VMEM((512, 768), bf),
            pltpu.VMEM((768, 3072), bf),
            pltpu.VMEM((36, 512, 64), bf),
            pltpu.VMEM((12, 512, 1), f32),
            pltpu.VMEM((512, 768), bf),
            DMA((4,)),
        ],
        compiler_params=pltpu.CompilerParams(vmem_limit_bytes=67043328),
        cost_estimate=pl.CostEstimate(flops=60_000_000_000, bytes_accessed=30_000_000, transcendentals=0),
        name="rear",
    )(*operands)


def last_kernel(
    qkvo_in, first_in, second_in, ada_in, up_in, down_in, d_act_in, router_in, condition,
    qkv_out, out_out, first_out, second_out, ada_out, up_out, down_out, condition_out, router_out,
    qkvo_sum, first, second, ada, up, down, d_act, router, sem,
):
    d = lax.axis_index("dp")
    pairs = (
        (up_in, up), (down_in, down), (ada_in, ada), (qkvo_in, qkvo_sum), (first_in, first),
        (second_in, second), (d_act_in, d_act), (router_in, router),
    )
    loads = [pltpu.make_async_copy(src, dst, sem.at[i]) for i, (src, dst) in enumerate(pairs)]
    for copy in loads:
        copy.start()
    for copy in loads:
        copy.wait()
    qkv_out[...] = qkvo_sum[:, 0:576]
    out_out[...] = qkvo_sum[:, 576:768]
    first_out[...] = first[...]
    second_out[...] = second[...]
    ada_out[...] = ada[...]
    up_out[...] = up[...]
    down_out[...] = down[...]
    router_out[...] = lines_of(router[...], 2 * d)[:, 0:96]
    for f in range(8):
        columns = slice(96 * f, 96 * f + 96)
        v = condition[:, columns].astype(jnp.float32)
        sigmoid = jax.nn.sigmoid(v)
        condition_out[:, columns] = lines_of(d_act[f], 2 * d)[:, 0:96] * (
            sigmoid * (1.0 + v * (1.0 - sigmoid))
        )


def last(*operands):
    f32 = jnp.float32
    return pl.pallas_call(
        last_kernel,
        out_shape=tuple(
            jax.ShapeDtypeStruct(shape, f32)
            for shape in (
                (96, 576), (96, 192), (96, 768), (192, 384), (96, 1152), (2, 96, 3072), (2, 384, 768),
                (2, 768), (2, 96),
            )
        ),
        in_specs=[ANYWHERE] * 8 + [ONCHIP],
        out_specs=(ONCHIP,) * 9,
        scratch_shapes=[
            pltpu.VMEM(shape, f32)
            for shape in (
                (96, 768), (96, 768), (192, 384), (96, 1152), (2, 96, 3072), (2, 384, 768), (8, 8, 128), (8, 128),
            )
        ]
        + [DMA((8,))],
        compiler_params=pltpu.CompilerParams(vmem_limit_bytes=40 << 20),
        name="last",
    )(*operands)


def fitted_shards(
    tokens,
    condition,
    ada_weight,
    qkv_weight,
    out_weight,
    shared_up,
    shared_down,
    router_weight,
    expert_up,
    expert_down,
    routes,
    image_sizes,
    cotangent,
):
    bf = jnp.bfloat16
    d_index, f_index = lax.axis_index("dp"), lax.axis_index("fsdp")
    model_width = tokens.shape[1]
    head_size = model_width // HEADS
    inside, segment = owners(image_sizes)
    ids = jnp.arange(EXPERTS, dtype=jnp.int32)
    hot = routes[:, :, None] == ids[None, None, :]
    hot_any = jnp.any(hot, axis=1).astype(bf)
    order = jnp.arange(LONG, dtype=jnp.int32)
    earlier = (order[:, None] > order[None, :]).astype(bf)
    before = nn(earlier, hot_any)
    position = jnp.sum(jnp.where(hot, before[:, None, :], 0.0), axis=-1).astype(jnp.int32)
    target = routes * CAP + position
    live = (segment < IMG_DEV).astype(jnp.float32)
    counts = jnp.sum(live[:, None] * hot_any.astype(jnp.float32), axis=0)
    cond_float = condition.astype(jnp.float32)
    activated = jax.nn.silu(cond_float).astype(bf)
    act_slices = activated.astype(jnp.float32).reshape(IMG_DEV, 8, 96).transpose(1, 0, 2)
    act_slices = jnp.pad(act_slices, ((0, 0), (0, 6), (0, 32)))
    act_slices = act_slices.at[:, 2, :EXPERTS].set(counts)
    act_slices = act_slices.at[:, 3:5, :96].set(router_weight.T.astype(jnp.float32))
    qkvo, router_t, seen, mod_rows, up_line, down_line, up_m, up_x0, up_y0, down_own, down_m = opening(
        qkv_weight, out_weight, act_slices, ada_weight, shared_up, shared_down.T, expert_up, expert_down
    )
    hops = hop(up_m, 2), hop(up_m, 4), hop(down_own, 2), hop(down_own, 4)
    expert_counts = seen[66, :EXPERTS].astype(jnp.int32)
    segments = (segment[:, None], segment[None, :])
    (
        heads, totals, attended, projected, residual, second_input, d_mixed, gates, rows, grads, modulation,
    ) = front(tokens, mod_rows, inside, *segments, qkvo, router_t, cotangent, routes, target.T)
    rows = rows.reshape(EXPERTS, CAP, model_width)
    grads = grads.reshape(EXPERTS, CAP, model_width)
    rows, (up_x1, up_y1, down_x0, down_y0) = lax.optimization_barrier((rows, hops))
    rows_in, grads_in, up_corner, down_x1, down_y1, down_corner, shared_out, d_second, *shared_grads = (
        outbound(
            rows, grads, up_line, down_line, second_input, d_mixed, up_x0, up_y1, down_m, down_x0
        )
    )
    returned, d_returned, up_keep, *up_near, down_keep, down_x, down_y, first_part, second_part = experts(
        rows_in, grads_in, (expert_up, up_m, up_x0, up_x1, up_y0, up_y1, up_corner),
        (down_own, down_m, down_x0, down_x1, down_y0, down_y1, down_corner),
        *shared_grads,
    )
    up_next = square_next(up_keep, *up_near)
    down_near = hop(down_x, 2), hop(down_y, 4)
    returned = returned.reshape(EXPERTS * CAP, model_width)
    d_returned = d_returned.reshape(EXPERTS * CAP, model_width)
    output, tokens_grad, qkvo_grad, d_modulation, router_grad = rear(
        tokens, modulation, inside, *segments, qkvo, router_t, cotangent, routes, target,
        heads, totals, attended, projected, residual, second_input, gates,
        returned, d_returned, shared_out, d_second,
    )
    qkvo_grad, down_near, up_next = lax.optimization_barrier((qkvo_grad, down_near, up_next))
    d_modulation = d_modulation.astype(bf)
    d_mod_rows = d_modulation.astype(jnp.float32).reshape(2, 4, 1152).transpose(1, 0, 2)
    d_mod_rows = lax.dynamic_update_slice(
        jnp.zeros((4, 8, 1152), jnp.float32), d_mod_rows, (0, 2 * d_index, 0)
    )
    router_tiles = jnp.pad(
        router_grad.reshape(EXPERTS, 8, 96).transpose(1, 0, 2), ((0, 0), (0, 0), (0, 32))
    )
    (
        qkvo_sum, shared_first_sum, shared_second_sum, ada_grad, d_act_tiles, router_sum,
        expert_up_grad, expert_down_grad,
    ) = dense_sums(
        qkvo_grad, first_part, second_part,
        (d_mod_rows, router_tiles, seen[:64].astype(bf), ada_weight),
        (up_keep, *up_near, *up_next, down_keep, *down_near),
    )
    (
        qkv_grad, out_grad, shared_first_sum, shared_second_sum, ada_grad, expert_up_grad, expert_down_grad,
        condition_grad, router_out,
    ) = last(
        qkvo_sum, shared_first_sum, shared_second_sum, ada_grad, expert_up_grad, expert_down_grad,
        d_act_tiles, router_sum, condition,
    )
    return (
        output,
        tokens_grad,
        condition_grad,
        ada_grad,
        qkv_grad,
        out_grad,
        shared_first_sum,
        shared_second_sum.T,
        router_out.T,
        expert_up_grad,
        expert_down_grad,
        expert_counts,
    )


def solution(mesh):
    placed = (
        P(("dp", "fsdp"), None),
        P(("dp", "fsdp"), None),
        P("fsdp", "dp"),
        P("fsdp", "dp"),
        P("fsdp", "dp"),
        P("fsdp", "dp"),
        P("fsdp", "dp"),
        P("fsdp", "dp"),
        P("dp", "fsdp", None),
        P("dp", "fsdp", None),
        P(("dp", "fsdp"), None),
        P(("dp", "fsdp")),
        P(("dp", "fsdp"), None),
    )
    fitted = mesh.shape["dp"] == 4 and mesh.shape["fsdp"] == 8
    return jax.shard_map(
        fitted_shards if fitted else shards,
        mesh=mesh,
        in_specs=placed,
        out_specs=(
            P(("dp", "fsdp"), None),
            P(("dp", "fsdp"), None),
            P(("dp", "fsdp"), None),
            P("fsdp", "dp"),
            P("fsdp", "dp"),
            P("fsdp", "dp"),
            P("fsdp", "dp"),
            P("fsdp", "dp"),
            P("fsdp", "dp"),
            P("dp", "fsdp", None),
            P("dp", "fsdp", None),
            P(),
        ),
        check_vma=False,
    )
```

```python
import functools

import jax
import jax.numpy as jnp
from jax import lax
from jax.experimental import pallas as pl
from jax.experimental.pallas import tpu as pltpu
from jax.sharding import PartitionSpec as P

HEADS = 12
EXPERTS = 8
CAP = 144
IMG_DEV = 2
LONG = 512
MESH = pl.DeviceIdType.MESH


EXACT = lax.Precision.HIGHEST


def owners(image_sizes):
    starts = jnp.cumsum(image_sizes) - image_sizes
    position = jnp.arange(LONG, dtype=jnp.int32)[:, None]
    inside = (position >= starts[None, :]) & (position < (starts + image_sizes)[None, :])
    slot_ids = jnp.arange(IMG_DEV, dtype=jnp.int32)
    segment = jnp.sum(jnp.where(inside, slot_ids[None, :], 0), axis=1) + jnp.where(
        jnp.any(inside, axis=1), 0, IMG_DEV
    )
    return (inside.astype(jnp.float32), segment)


def dispatch_plan(routes):
    flat = routes.reshape(-1)
    onehot = (flat[:, None] == jnp.arange(EXPERTS, dtype=jnp.int32)[None, :]).astype(jnp.int32)
    before = jnp.cumsum(onehot, axis=0) - onehot
    position = jnp.sum(before * onehot, axis=1)
    target = flat * CAP + position
    assignment = jnp.arange(2 * LONG, dtype=jnp.int32)
    source = jnp.zeros((EXPERTS * CAP,), jnp.int32).at[target].set(assignment)
    filled = jnp.zeros((EXPERTS * CAP,), jnp.int32).at[target].set(1)
    return (target, source, filled)


def layer_norm(values_in):
    centred = values_in - jnp.mean(values_in, axis=-1, keepdims=True)
    inv_std = lax.rsqrt(jnp.mean(centred * centred, axis=-1, keepdims=True) + 1e-06)
    return (centred * inv_std, inv_std)


def norm_back(upstream, normed, inv_std):
    return (
        upstream
        - jnp.mean(upstream, axis=-1, keepdims=True)
        - normed * jnp.mean(upstream * normed, axis=-1, keepdims=True)
    ) * inv_std


def gelu_tanh(values_in):
    return jax.nn.gelu(values_in, approximate=True)


def gelu_back(values_in, upstream):
    return jax.vjp(gelu_tanh, values_in)[1](upstream)[0]


def collect(first, second, third):
    widened = (
        lax.all_gather(first, "dp", axis=1, tiled=True),
        lax.all_gather(second, "dp", axis=1, tiled=True),
        lax.all_gather(third, "dp", axis=1, tiled=True),
    )
    return (
        lax.all_gather(widened[0], "fsdp", axis=0, tiled=True),
        lax.all_gather(widened[1], "fsdp", axis=0, tiled=True),
        lax.all_gather(widened[2], "fsdp", axis=0, tiled=True),
    )


def spread(first, second, third):
    row_sums = (
        lax.psum_scatter(first, "fsdp", scatter_dimension=0, tiled=True),
        lax.psum_scatter(second, "fsdp", scatter_dimension=0, tiled=True),
        lax.psum_scatter(third, "fsdp", scatter_dimension=0, tiled=True),
    )
    return (
        lax.psum_scatter(row_sums[0], "dp", scatter_dimension=1, tiled=True),
        lax.psum_scatter(row_sums[1], "dp", scatter_dimension=1, tiled=True),
        lax.psum_scatter(row_sums[2], "dp", scatter_dimension=1, tiled=True),
    )


def gather_experts(up_shard, down_shard):
    return (
        lax.all_gather(up_shard, "fsdp", axis=1, tiled=True),
        lax.all_gather(down_shard, "fsdp", axis=1, tiled=True),
    )


def expert_forward(buffer_in, up_full, down_full):
    expert_pre = jnp.einsum(
        "secd,edf->secf", buffer_in, up_full, preferred_element_type=jnp.float32
    )
    expert_act = gelu_tanh(expert_pre).astype(jnp.bfloat16)
    expert_out = jnp.einsum(
        "secf,efd->secd", expert_act, down_full, preferred_element_type=jnp.float32
    ).astype(jnp.bfloat16)
    return (expert_pre, expert_act, expert_out)


def expert_backward(buffer_in, expert_pre, expert_act, d_out, up_full, down_full):
    d_act = jnp.einsum("secd,efd->secf", d_out, down_full, preferred_element_type=jnp.float32)
    d_pre = gelu_back(expert_pre, d_act).astype(jnp.bfloat16)
    d_rows = jnp.einsum(
        "secf,edf->secd", d_pre, up_full, preferred_element_type=jnp.float32
    ).astype(jnp.bfloat16)
    down_grad = jnp.einsum("secf,secd->efd", expert_act, d_out, preferred_element_type=jnp.float32)
    up_grad = jnp.einsum("secd,secf->edf", buffer_in, d_pre, preferred_element_type=jnp.float32)
    return (up_grad, down_grad, d_rows)


def attend(queries, keys_all, values_all, segment):
    row_count, head_count, head_size = queries.shape
    block_rows = min(512, row_count)
    block_count = row_count // block_rows
    score_scale = head_size ** (-0.5)

    def one_block(pieces):
        query_part, segment_part = pieces
        allowed = (segment_part[:, None] == segment[None, :])[None]
        scores = (
            jnp.einsum("qhd,khd->hqk", query_part, keys_all, preferred_element_type=jnp.float32)
            * score_scale
        )
        scores = jnp.where(allowed, scores, -1e30)
        row_max = jnp.max(scores, axis=-1, keepdims=True)
        weight = jnp.exp(scores - row_max)
        running = jnp.sum(weight, axis=-1, keepdims=True)
        probability = (weight / running).astype(jnp.bfloat16)
        attended = jnp.einsum(
            "hqk,khd->qhd", probability, values_all, preferred_element_type=jnp.float32
        )
        return (attended.astype(jnp.bfloat16), (row_max + jnp.log(running))[:, :, 0])

    return lax.map(
        one_block,
        (
            queries.reshape(block_count, block_rows, head_count, head_size),
            segment.reshape(block_count, block_rows),
        ),
    )


def attend_back(queries, keys_all, values_all, segment, log_totals, d_attended):
    row_count, head_count, head_size = queries.shape
    block_rows = min(512, row_count)
    block_count = row_count // block_rows
    score_scale = head_size ** (-0.5)

    def one_block(carry, pieces):
        key_sum, value_sum = carry
        query_part, segment_part, total_part, grad_part = pieces
        allowed = (segment_part[:, None] == segment[None, :])[None]
        scores = (
            jnp.einsum("qhd,khd->hqk", query_part, keys_all, preferred_element_type=jnp.float32)
            * score_scale
        )
        scores = jnp.where(allowed, scores, -1e30)
        probability = jnp.exp(scores - total_part[:, :, None])
        d_prob = jnp.einsum(
            "qhd,khd->hqk", grad_part, values_all, preferred_element_type=jnp.float32
        )
        d_scores = (
            probability * (d_prob - jnp.sum(probability * d_prob, axis=-1, keepdims=True))
        ).astype(jnp.bfloat16)
        query_grad = (
            jnp.einsum("hqk,khd->qhd", d_scores, keys_all, preferred_element_type=jnp.float32)
            * score_scale
        )
        key_sum = (
            key_sum
            + jnp.einsum("hqk,qhd->khd", d_scores, query_part, preferred_element_type=jnp.float32)
            * score_scale
        )
        value_sum = value_sum + jnp.einsum(
            "hqk,qhd->khd",
            probability.astype(jnp.bfloat16),
            grad_part,
            preferred_element_type=jnp.float32,
        )
        return ((key_sum, value_sum), query_grad)

    empty = jnp.zeros(keys_all.shape, jnp.float32)
    sums, query_grads = lax.scan(
        one_block,
        (empty, empty),
        (
            queries.reshape(block_count, block_rows, head_count, head_size),
            segment.reshape(block_count, block_rows),
            log_totals,
            d_attended.reshape(block_count, block_rows, head_count, head_size),
        ),
    )
    return (query_grads.reshape(row_count, head_count, head_size), sums[0], sums[1])


def shards(
    tokens,
    condition,
    ada_weight,
    qkv_weight,
    out_weight,
    shared_up,
    shared_down,
    router_weight,
    expert_up,
    expert_down,
    routes,
    image_sizes,
    cotangent,
):
    model_width = tokens.shape[1]
    head_size = model_width // HEADS
    inside, segment = owners(image_sizes)
    target, source, filled = dispatch_plan(routes)
    route_hot = (routes[:, :, None] == jnp.arange(EXPERTS, dtype=jnp.int32)[None, None, :]).astype(
        jnp.float32
    )
    live = (segment < IMG_DEV).astype(jnp.int32)
    local_counts = jnp.sum(live[:, None, None] * route_hot.astype(jnp.int32), axis=(0, 1))
    expert_counts = lax.psum(local_counts, ("dp", "fsdp"))
    ada_full, qkv_full, out_full = collect(ada_weight, qkv_weight, out_weight)
    cond_float = condition.astype(jnp.float32)
    activated = jax.nn.silu(cond_float).astype(jnp.bfloat16)
    modulation = jnp.dot(activated, ada_full, preferred_element_type=jnp.float32)
    per_row = jnp.dot(inside, modulation, precision=EXACT, preferred_element_type=jnp.float32)
    shift_one, scale_one, gate_one, shift_two, scale_two, gate_two = jnp.split(per_row, 6, axis=1)
    token_float = tokens.astype(jnp.float32)
    normed_one, inv_one = layer_norm(token_float)
    first_input = (normed_one * (1.0 + scale_one) + shift_one).astype(jnp.bfloat16)
    qkv_rows = jnp.dot(first_input, qkv_full, preferred_element_type=jnp.float32).astype(
        jnp.bfloat16
    )
    queries = qkv_rows[:, :model_width].reshape(-1, HEADS, head_size)
    keys_all = qkv_rows[:, model_width : 2 * model_width].reshape(-1, HEADS, head_size)
    values_all = qkv_rows[:, 2 * model_width :].reshape(-1, HEADS, head_size)
    attended_blocks, log_totals = attend(queries, keys_all, values_all, segment)
    attended = attended_blocks.reshape(-1, model_width)
    projected = jnp.dot(attended, out_full, preferred_element_type=jnp.float32)
    residual_one = token_float + gate_one * projected
    normed_two, inv_two = layer_norm(residual_one)
    second_input = (normed_two * (1.0 + scale_two) + shift_two).astype(jnp.bfloat16)
    shared_first, shared_second, router_full = collect(shared_up, shared_down, router_weight)
    shared_pre = jnp.dot(second_input, shared_first, preferred_element_type=jnp.float32)
    shared_act = gelu_tanh(shared_pre).astype(jnp.bfloat16)
    shared_out = jnp.dot(shared_act, shared_second, preferred_element_type=jnp.float32)
    logits = jnp.dot(second_input, router_full, preferred_element_type=jnp.float32)
    chosen = jnp.sum(logits[:, None, :] * route_hot, axis=-1)
    gate_share = jax.nn.softmax(chosen, axis=-1)
    buffer_rows = jnp.take(second_input, source // 2, axis=0).reshape(EXPERTS, CAP, model_width)
    up_full, down_full = gather_experts(expert_up, expert_down)
    groups = lax.axis_size("dp")
    expert_in = lax.all_to_all(
        buffer_rows.reshape(groups, EXPERTS // groups, CAP, model_width),
        "dp",
        split_axis=0,
        concat_axis=0,
        tiled=True,
    )
    expert_pre, expert_act, expert_out = expert_forward(expert_in, up_full, down_full)
    returned = lax.all_to_all(expert_out, "dp", split_axis=0, concat_axis=0, tiled=True).reshape(
        EXPERTS, CAP, model_width
    )
    picked = (
        jnp.take(returned.reshape(EXPERTS * CAP, model_width), target, axis=0)
        .reshape(-1, 2, model_width)
        .astype(jnp.float32)
    )
    mixed = shared_out + jnp.sum(gate_share[:, :, None] * picked, axis=1)
    output = (residual_one + gate_two * mixed).astype(jnp.bfloat16)
    upstream = cotangent.astype(jnp.float32)
    d_mixed = gate_two * upstream
    d_gate_two = upstream * mixed
    d_gate_share = jnp.sum(d_mixed[:, None, :] * picked, axis=-1)
    slot_gate = jnp.take(gate_share.reshape(-1), source) * filled.astype(jnp.float32)
    d_buffer = (
        (jnp.take(d_mixed, source // 2, axis=0) * slot_gate[:, None])
        .astype(jnp.bfloat16)
        .reshape(EXPERTS, CAP, model_width)
    )
    shared_first, shared_second, router_full = collect(shared_up, shared_down, router_weight)
    up_full, down_full = gather_experts(expert_up, expert_down)
    arrived = lax.all_to_all(
        d_buffer.reshape(groups, EXPERTS // groups, CAP, model_width),
        "dp",
        split_axis=0,
        concat_axis=0,
        tiled=True,
    )
    up_grad, down_grad, d_rows = expert_backward(
        expert_in, expert_pre, expert_act, arrived, up_full, down_full
    )
    d_returned = lax.all_to_all(d_rows, "dp", split_axis=0, concat_axis=0, tiled=True).reshape(
        EXPERTS, CAP, model_width
    )
    expert_sums = (
        lax.psum_scatter(up_grad, "fsdp", scatter_dimension=1, tiled=True),
        lax.psum_scatter(down_grad, "fsdp", scatter_dimension=1, tiled=True),
    )
    d_shared = d_mixed.astype(jnp.bfloat16)
    shared_second_grad = jnp.einsum(
        "tf,td->fd", shared_act, d_shared, preferred_element_type=jnp.float32
    )
    d_shared_act = jnp.einsum(
        "td,fd->tf", d_shared, shared_second, preferred_element_type=jnp.float32
    )
    d_shared_pre = gelu_back(shared_pre, d_shared_act).astype(jnp.bfloat16)
    shared_first_grad = jnp.einsum(
        "td,tf->df", second_input, d_shared_pre, preferred_element_type=jnp.float32
    )
    d_chosen = gate_share * (
        d_gate_share - jnp.sum(gate_share * d_gate_share, axis=-1, keepdims=True)
    )
    d_logits = jnp.sum(d_chosen[:, :, None] * route_hot, axis=1).astype(jnp.bfloat16)
    router_grad = jnp.einsum(
        "td,te->de", second_input, d_logits, preferred_element_type=jnp.float32
    )
    from_experts = (
        jnp.take(d_returned.reshape(EXPERTS * CAP, model_width), target, axis=0)
        .reshape(-1, 2, model_width)
        .astype(jnp.float32)
    )
    d_second = (
        jnp.einsum("tf,df->td", d_shared_pre, shared_first, preferred_element_type=jnp.float32)
        + jnp.einsum("te,de->td", d_logits, router_full, preferred_element_type=jnp.float32)
        + jnp.sum(from_experts, axis=1)
    )
    mlp_sums = spread(shared_first_grad, shared_second_grad, router_grad)
    d_scale_two = d_second * normed_two
    d_residual = upstream + norm_back(d_second * (1.0 + scale_two), normed_two, inv_two)
    ada_full, qkv_full, out_full = collect(ada_weight, qkv_weight, out_weight)
    d_projected = (gate_one * d_residual).astype(jnp.bfloat16)
    d_gate_one = d_residual * projected
    out_grad = jnp.einsum("td,te->de", attended, d_projected, preferred_element_type=jnp.float32)
    d_attended = jnp.einsum(
        "te,de->td", d_projected, out_full, preferred_element_type=jnp.float32
    ).astype(jnp.bfloat16)
    d_queries, d_keys, d_values = attend_back(
        queries, keys_all, values_all, segment, log_totals, d_attended.reshape(-1, HEADS, head_size)
    )
    d_qkv = jnp.concatenate(
        [
            d_queries.reshape(-1, model_width),
            d_keys.reshape(-1, model_width),
            d_values.reshape(-1, model_width),
        ],
        axis=1,
    ).astype(jnp.bfloat16)
    qkv_grad = jnp.einsum("td,te->de", first_input, d_qkv, preferred_element_type=jnp.float32)
    d_first = jnp.einsum("te,de->td", d_qkv, qkv_full, preferred_element_type=jnp.float32)
    d_scale_one = d_first * normed_one
    tokens_grad = d_residual + norm_back(d_first * (1.0 + scale_one), normed_one, inv_one)
    d_per_row = jnp.concatenate(
        [d_first, d_scale_one, d_gate_one, d_second, d_scale_two, d_gate_two], axis=1
    )
    d_modulation = jnp.einsum(
        "tj,te->je", inside, d_per_row, precision=EXACT, preferred_element_type=jnp.float32
    ).astype(jnp.bfloat16)
    ada_grad = jnp.einsum("jd,je->de", activated, d_modulation, preferred_element_type=jnp.float32)
    d_activated = jnp.einsum(
        "je,de->jd", d_modulation, ada_full, preferred_element_type=jnp.float32
    )
    condition_grad = jax.vjp(jax.nn.silu, cond_float)[1](d_activated)[0]
    attn_sums = spread(ada_grad, qkv_grad, out_grad)
    return (
        output,
        tokens_grad,
        condition_grad,
        attn_sums[0],
        attn_sums[1],
        attn_sums[2],
        mlp_sums[0],
        mlp_sums[1],
        mlp_sums[2],
        expert_sums[0],
        expert_sums[1],
        expert_counts,
    )


def at(d, s, c):
    return (d, 2 * s + c)


def slot(kind, f, d):
    if kind == "cols":
        return (pl.ds(pl.multiple_of(96 * f, 96), 96), pl.ds(pl.multiple_of(768 * d, 768), 768))
    return (pl.ds(pl.multiple_of(192 * d, 192), 192), pl.ds(pl.multiple_of(384 * f, 384), 384))


def half_slot(kind, f, d, h):
    if kind == "cols":
        return (
            pl.ds(pl.multiple_of(96 * f, 96), 96),
            pl.ds(pl.multiple_of(768 * d + 384 * h, 384), 384),
        )
    return (
        pl.ds(pl.multiple_of(192 * d + 96 * h, 96), 96),
        pl.ds(pl.multiple_of(384 * f, 384), 384),
    )


def place():
    d = lax.axis_index("dp")
    f = lax.axis_index("fsdp")
    return d, f // 2, lax.rem(f, 2)


def flip(v, bit):
    return v + bit - 2 * bit * lax.rem(v // bit, 2)


def greet(devices):
    barrier = pltpu.get_barrier_semaphore()
    for device in devices:
        pl.semaphore_signal(barrier, inc=1, device_id=device, device_id_type=MESH)
    pl.semaphore_wait(barrier, len(devices))


def push(src, dst, send_sem, recv_sem, device):
    return pltpu.make_async_remote_copy(
        src_ref=src,
        dst_ref=dst,
        send_sem=send_sem,
        recv_sem=recv_sem,
        device_id=device,
        device_id_type=MESH,
    )


GATHER_SEMS = 3 + 8 + 8 + 20


class Gather:
    def __init__(self, kind, shard, full, ssem, rsem, lsem):
        self.kind, self.shard, self.full = kind, shard, full
        self.ssem, self.rsem, self.lsem = ssem, rsem, lsem
        self.d, self.s, self.c = place()
        self.sent = []

    def f(self, s):
        return 2 * s + self.c

    def go(self, index, where, device, src=None):
        ref = self.full.at[where]
        copy = push(
            ref if src is None else src, ref, self.ssem.at[index], self.rsem.at[index], device
        )
        copy.start()
        self.sent.append(copy)

    def arrived(self, index, where):
        ref = self.full.at[where]
        push(ref, ref, self.ssem.at[index], self.rsem.at[index], at(self.d, self.s, self.c)).wait_recv()

    def start(self):
        d, s, c = self.d, self.s, self.c
        mine = slot(self.kind, self.f(s), d)
        self.own = pltpu.make_async_copy(self.shard, self.full.at[mine], self.lsem)
        self.own.start()
        self.go(1, mine, at(flip(d, 2), s, c), self.shard)
        self.go(0, mine, at(flip(d, 1), s, c), self.shard)
        self.go(3, mine, at(d, flip(s, 1), c), self.shard)
        self.go(4, mine, at(d, flip(s, 2), c), self.shard)
        self.go(19, mine, at(d, s, 1 - c), self.shard)

    def source(self, k):
        return (self.d, flip(self.d, 1), flip(self.d, 2), flip(flip(self.d, 1), 2))[k]

    def spread_z(self, k):
        d, s, c = self.d, self.s, self.c
        block = slot(self.kind, self.f(s), self.source(k))
        self.arrived(k - 1, block)
        if k == 2:
            self.go(2, block, at(flip(d, 1), s, c))
        self.go(3 + 2 * k, block, at(d, flip(s, 1), c))
        self.go(4 + 2 * k, block, at(d, flip(s, 2), c))
        self.go(19 + 5 * k, block, at(d, s, 1 - c))

    def relay(self, k):
        d, s, c = self.d, self.s, self.c
        source = self.source(k)
        sx, sy = flip(s, 1), flip(s, 2)
        from_x = slot(self.kind, self.f(sx), source)
        from_y = slot(self.kind, self.f(sy), source)
        self.arrived(3 + 2 * k, from_x)
        self.go(11 + 2 * k, half_slot(self.kind, self.f(sx), source, 0), at(d, sy, c))
        self.go(20 + 5 * k, from_x, at(d, s, 1 - c))
        self.arrived(4 + 2 * k, from_y)
        self.go(12 + 2 * k, half_slot(self.kind, self.f(sy), source, 1), at(d, sx, c))
        self.go(21 + 5 * k, from_y, at(d, s, 1 - c))

    def corner(self, k):
        d, s, c = self.d, self.s, self.c
        source = self.source(k)
        sd = flip(flip(s, 1), 2)
        for h in range(2):
            where = half_slot(self.kind, self.f(sd), source, h)
            self.arrived(11 + 2 * k + h, where)
            self.go(22 + 5 * k + h, where, at(d, s, 1 - c))

    def finish(self):
        d, s, c = self.d, self.s, self.c
        sx, sy = flip(s, 1), flip(s, 2)
        sd = flip(sx, 2)
        self.own.wait()
        for k in range(4):
            source = self.source(k)
            for j, position in enumerate((s, sx, sy)):
                self.arrived(19 + 5 * k + j, slot(self.kind, 2 * position + 1 - c, source))
            for h in range(2):
                self.arrived(22 + 5 * k + h, half_slot(self.kind, 2 * sd + 1 - c, source, h))
        for copy in self.sent:
            copy.wait_send()


class Line:
    def __init__(self, kind, shard, line, ssem, rsem, lsem):
        self.kind, self.shard, self.line = kind, shard, line
        self.ssem, self.rsem, self.lsem = ssem, rsem, lsem
        self.d, self.s, self.c = place()

    def block(self, d):
        if self.kind == "cols":
            return self.line.at[:, pl.ds(pl.multiple_of(768 * d, 768), 768)]
        return self.line.at[pl.ds(pl.multiple_of(192 * d, 192), 192)]

    def copy(self, index, src, source, target):
        return push(
            src, self.block(source), self.ssem.at[index], self.rsem.at[index], at(target, self.s, self.c)
        )

    def start(self):
        d = self.d
        self.own = pltpu.make_async_copy(self.shard, self.block(d), self.lsem)
        self.own.start()
        self.sent = [
            self.copy(0, self.shard, d, flip(d, 2)),
            self.copy(1, self.shard, d, flip(d, 1)),
        ]
        for copy in self.sent:
            copy.start()

    def relay(self):
        d2 = flip(self.d, 2)
        self.copy(0, self.shard, d2, d2).wait_recv()
        copy = self.copy(2, self.block(d2), d2, flip(self.d, 1))
        copy.start()
        self.sent.append(copy)

    def finish(self):
        d1 = flip(self.d, 1)
        self.own.wait()
        self.copy(1, self.shard, d1, d1).wait_recv()
        self.copy(2, self.shard, flip(d1, 2), d1).wait_recv()
        for copy in self.sent:
            copy.wait_send()


class Spread:
    def __init__(self, kind, line, full, ssem, rsem, lsem):
        self.kind, self.line, self.full = kind, line, full
        self.ssem, self.rsem, self.lsem = ssem, rsem, lsem
        self.d, self.s, self.c = place()
        self.sx, self.sy = flip(self.s, 1), flip(self.s, 2)
        self.sd = flip(self.sx, 2)
        self.mate = at(self.d, self.s, 1 - self.c)
        self.to_x, self.to_y = at(self.d, self.sx, self.c), at(self.d, self.sy, self.c)
        self.sent = []

    def block(self, position, c, h=None):
        f = 2 * position + c
        if self.kind == "cols":
            rows = pl.ds(pl.multiple_of(96 * f, 96), 96)
            return self.full.at[rows] if h is None else self.full.at[rows, pl.ds(1536 * h, 1536)]
        columns = pl.ds(pl.multiple_of(384 * f, 384), 384)
        rows = pl.ds(0, 768) if h is None else pl.ds(384 * h, 384)
        return self.full.at[rows, columns]

    def go(self, index, ref, device, src=None):
        copy = push(
            ref if src is None else src, ref, self.ssem.at[index], self.rsem.at[index], device
        )
        copy.start()
        self.sent.append(copy)

    def arrived(self, index, ref):
        push(ref, ref, self.ssem.at[index], self.rsem.at[index], self.mate).wait_recv()

    def start(self):
        mine = self.block(self.s, self.c)
        self.own = pltpu.make_async_copy(self.line, mine, self.lsem)
        self.own.start()
        self.go(0, mine, self.to_x, self.line)
        self.go(1, mine, self.to_y, self.line)
        self.go(2, mine, self.mate, self.line)

    def relay(self):
        c = self.c
        from_x, from_y = self.block(self.sx, c), self.block(self.sy, c)
        self.arrived(0, from_x)
        self.go(3, self.block(self.sx, c, 0), self.to_y)
        self.go(5, from_x, self.mate)
        self.arrived(1, from_y)
        self.go(4, self.block(self.sy, c, 1), self.to_x)
        self.go(6, from_y, self.mate)

    def corner(self):
        for h in range(2):
            ref = self.block(self.sd, self.c, h)
            self.arrived(3 + h, ref)
            self.go(7 + h, ref, self.mate)

    def finish(self):
        c = 1 - self.c
        self.own.wait()
        self.arrived(2, self.block(self.s, c))
        self.arrived(5, self.block(self.sx, c))
        self.arrived(6, self.block(self.sy, c))
        for h in range(2):
            self.arrived(7 + h, self.block(self.sd, c, h))
        for copy in self.sent:
            copy.wait_send()


class Near:
    def __init__(self, up_shard, down_shard, up_mate, up_x, up_y, down_own, down_mate, ssem, rsem, lsem):
        d, s, c = place()
        self.local = pltpu.make_async_copy(down_shard.at[c], down_own, lsem)
        plan = (
            (up_shard, c, up_x, flip(s, 1)),
            (up_shard, c, up_y, flip(s, 2)),
            (up_shard, 1 - c, up_mate, s),
            (down_shard, 1 - c, down_mate, s),
        )
        self.away = [
            push(shard.at[which], out, ssem.at[i], rsem.at[i], at(d, position, which))
            for i, (shard, which, out, position) in enumerate(plan)
        ]

    def start(self):
        for copy in self.away + [self.local]:
            copy.start()

    def finish(self):
        for copy in self.away + [self.local]:
            copy.wait()


class Pair:
    def __init__(self, over_x, into_x, over_y, into_y, ssem, rsem):
        d, s, c = place()
        self.copies = [
            push(over_x, into_x, ssem.at[0], rsem.at[0], at(d, flip(s, 1), c)),
            push(over_y, into_y, ssem.at[1], rsem.at[1], at(d, flip(s, 2), c)),
        ]

    def start(self):
        for copy in self.copies:
            copy.start()

    def finish(self):
        for copy in self.copies:
            copy.wait()


def everyone_else():
    me = lax.axis_index("dp") * 8 + lax.axis_index("fsdp")

    def other(k):
        device = lax.rem(me + k, 32)
        return (device // 8, lax.rem(device, 8))

    return me, other


def open_kernel(
    qkv_shard, out_shard, act_ref, ada_ref, up_shard, down_shard, expert_up, expert_down,
    full, router_t, seen, rows_out, up_line, down_line, up_mate, up_x, up_y, down_own, down_mate,
    shard, heard, part, got, mixed, ssem, rsem, lsem, asem, brsem, tssem, trsem, zssem, zrsem,
    us, ur, ds, dr, es, er, el,
):
    me, other = everyone_else()
    d, s, c = place()
    f = 2 * s + c
    shard[:, 0:576] = qkv_shard[...]
    shard[:, 576:768] = out_shard[...]
    barrier = pltpu.get_barrier_semaphore()

    def hello(k, carry):
        pl.semaphore_signal(barrier, inc=1, device_id=other(k), device_id_type=MESH)
        return carry

    lax.fori_loop(1, 32, hello, 0)
    pl.semaphore_wait(barrier, 31)

    def act_copy(k, source):
        device = other(k)
        return push(act_ref.at[device[1]], heard.at[source], asem.at[k], brsem.at[k], device)

    def send(k, carry):
        act_copy(k, me).start()
        return carry

    lax.fori_loop(1, 32, send, 0)
    gather = Gather("cols", shard, full, ssem, rsem, lsem.at[0])
    gather.start()
    near = Near(
        expert_up, expert_down, up_mate, up_x, up_y, down_own, down_mate, es, er, el.at[0]
    )
    lines = (
        Line("cols", up_shard, up_line, us, ur, lsem.at[3]),
        Line("rows", down_shard, down_line, ds, dr, lsem.at[4]),
    )
    gather.spread_z(1)
    gather.spread_z(2)
    for line in lines:
        line.start()
    heard[me] = act_ref[f]

    def take(k, carry):
        copy = act_copy(k, lax.rem(me + 32 - k, 32))
        copy.wait_recv()
        return carry

    lax.fori_loop(1, 32, take, 0)
    everything = heard[...].reshape(256, 128)
    row = lax.broadcasted_iota(jnp.int32, (64, 256), 0)
    column = lax.broadcasted_iota(jnp.int32, (64, 256), 1)
    source = lax.rem(row // 2, 4) * 8 + row // 8
    pick = (column == source * 8 + lax.rem(row, 2)).astype(jnp.bfloat16)
    compact = jnp.dot(
        pick, everything.astype(jnp.bfloat16), preferred_element_type=jnp.float32
    ).astype(jnp.bfloat16)
    seen[...] = jnp.concatenate(
        [compact.astype(jnp.float32), jnp.sum(heard[...], axis=0)], axis=0
    )
    for column_block in range(8):
        tiles = [heard[8 * j + column_block, 3:5, 0:96] for j in range(4)]
        router_t[:, 96 * column_block : 96 * column_block + 96] = jnp.concatenate(tiles, axis=0)
    part[...] = nn(compact[:, 0:96], ada_ref[...]).reshape(8, 8, 1152)

    def tile_copy(k):
        target = lax.rem(f + k, 8)
        return push(part.at[target], got.at[k], tssem.at[k], trsem.at[k], (d, target))

    for k in range(1, 8):
        tile_copy(k).start()
    gather.relay(0)
    gather.spread_z(3)
    near.start()
    gather.relay(1)
    gather.relay(2)
    for k in range(1, 8):
        tile_copy(k).wait_recv()
    total = part[f]
    for k in range(1, 8):
        total = total + got[k]
    mixed[...] = total
    zs = []
    for k in range(1, 4):
        copy = push(mixed, rows_out.at[d], zssem.at[k], zrsem.at[k], at(lax.rem(d + k, 4), s, c))
        copy.start()
        zs.append(copy)
    own_rows = pltpu.make_async_copy(mixed, rows_out.at[d], lsem.at[2])
    own_rows.start()
    for line in lines:
        line.relay()
    gather.relay(3)
    gather.corner(0)
    gather.corner(1)
    gather.corner(2)
    gather.corner(3)
    gather.finish()
    for line in lines:
        line.finish()
    near.finish()
    own_rows.wait()
    for k in range(1, 4):
        push(
            mixed, rows_out.at[lax.rem(d + 4 - k, 4)], zssem.at[k], zrsem.at[k],
            at(lax.rem(d + k, 4), s, c),
        ).wait_recv()
    for copy in zs:
        copy.wait_send()
    for k in range(1, 8):
        tile_copy(k).wait_send()

    def drain(k, carry):
        act_copy(k, me).wait_send()
        return carry

    lax.fori_loop(1, 32, drain, 0)


DMA = pltpu.SemaphoreType.DMA
ANYWHERE = pl.BlockSpec(memory_space=pl.ANY)
ONCHIP = pl.BlockSpec(memory_space=pltpu.VMEM)


def opening(*operands):
    return pl.pallas_call(
        open_kernel,
        out_shape=(
            jax.ShapeDtypeStruct((768, 3072), jnp.bfloat16),
            jax.ShapeDtypeStruct((8, 768), jnp.float32),
            jax.ShapeDtypeStruct((72, 128), jnp.float32),
            jax.ShapeDtypeStruct((4, 8, 1152), jnp.float32),
            jax.ShapeDtypeStruct((96, 3072), jnp.bfloat16),
            jax.ShapeDtypeStruct((768, 384), jnp.bfloat16),
        )
        + (jax.ShapeDtypeStruct((96, 3072), jnp.bfloat16),) * 3
        + (jax.ShapeDtypeStruct((384, 768), jnp.bfloat16),) * 2,
        in_specs=[ONCHIP] * 6 + [ANYWHERE] * 2,
        out_specs=(ANYWHERE, ONCHIP, ONCHIP) + (ANYWHERE,) * 8,
        scratch_shapes=[
            pltpu.VMEM((96, 768), jnp.bfloat16),
            pltpu.VMEM((32, 8, 128), jnp.float32),
            pltpu.VMEM((8, 8, 1152), jnp.float32),
            pltpu.VMEM((8, 8, 1152), jnp.float32),
            pltpu.VMEM((8, 1152), jnp.float32),
            DMA((GATHER_SEMS,)), DMA((GATHER_SEMS,)), DMA((5,)),
            DMA((32,)), DMA((32,)),
            DMA((8,)), DMA((8,)), DMA((4,)), DMA((4,)),
            DMA((3,)), DMA((3,)), DMA((3,)), DMA((3,)),
            DMA((4,)), DMA((4,)), DMA((1,)),
        ],
        compiler_params=pltpu.CompilerParams(collective_id=0, has_side_effects=True),
        name="opening",
    )(*operands)


def group_of(d, s, c):
    return [(j, at(lax.rem(d + j // 2, 4), s, lax.rem(c + j, 2))) for j in range(1, 8)]


class Swap:
    def __init__(self, blocks, out, ssem, rsem, lsem):
        self.blocks, self.out, self.ssem, self.rsem, self.lsem = blocks, out, ssem, rsem, lsem
        self.d, self.s, self.c = place()
        self.me = 2 * self.d + self.c

    def copy(self, j, landing):
        target_d = lax.rem(self.d + j // 2, 4)
        target_c = lax.rem(self.c + j, 2)
        return push(
            self.blocks.at[2 * target_d + target_c],
            self.out.at[landing],
            self.ssem.at[j],
            self.rsem.at[j],
            at(target_d, self.s, target_c),
        )

    def start(self):
        for j in (4, 5, 2, 3, 6, 7, 1):
            self.copy(j, self.me).start()
        self.own = pltpu.make_async_copy(
            self.blocks.at[self.me], self.out.at[self.me], self.lsem
        )
        self.own.start()

    def send(self, step, half=None):
        for j in (2 * step, 2 * step + 1) if half is None else (2 * step + half,):
            if j:
                self.copy(j, self.me).start()
            else:
                self.own = pltpu.make_async_copy(
                    self.blocks.at[self.me], self.out.at[self.me], self.lsem
                )
                self.own.start()

    def finish(self):
        self.own.wait()
        for j in range(1, 8):
            source_d = lax.rem(self.d + 4 - j // 2, 4)
            source_c = lax.rem(self.c + j, 2)
            copy = self.copy(j, 2 * source_d + source_c)
            copy.wait_recv()
            copy.wait_send()


def nt(left, right):
    return lax.dot_general(left, right, (((1,), (1,)), ((), ())), preferred_element_type=jnp.float32)


def tn(left, right):
    return lax.dot_general(left, right, (((0,), (0,)), ((), ())), preferred_element_type=jnp.float32)


def nn(left, right):
    return jnp.dot(left, right, preferred_element_type=jnp.float32)


GELU_SCALE = 0.7978845608028654


def gelu_pair(v):
    square = v * v
    bend = jnp.tanh(GELU_SCALE * (v + 0.044715 * (square * v)))
    half = 0.5 * (1.0 + bend)
    slope = half + 0.5 * v * (1.0 - bend * bend) * (
        GELU_SCALE * (1.0 + (3.0 * 0.044715) * square)
    )
    return v * half, slope


HIDDEN = 512


def out_kernel(
    rows, grads, up_line, down_line, tokens, d_tokens, up_x, up_y, down_mate, down_x,
    rows_in, grads_in, up_corner, down_x_mate, down_y_mate, down_corner, mixed_out, d_tokens_out, up_grad, down_grad,
    up_full, down_full, tokens_t, d_tokens_t, s1, r1, s2, r2, ssem, rsem, ssem2, rsem2, lsem,
    es, er, fs, fr, gs, gr,
):
    d, s, c = place()
    greet([device for _, device in group_of(d, s, c)] + [at(d, flip(s, 1), c), at(d, flip(s, 2), c)])
    both = (
        Spread("cols", up_line, up_full, ssem, rsem, lsem.at[0]),
        Spread("rows", down_line, down_full, ssem2, rsem2, lsem.at[1]),
    )
    swap_a = Swap(rows, rows_in, s1, r1, lsem.at[2])
    swap_b = Swap(grads, grads_in, s2, r2, lsem.at[3])
    for g in both:
        g.start()
    swap_a.start()
    swap_b.start()
    mates = Pair(down_mate, down_x_mate, down_mate, down_y_mate, gs, gr)
    up_corners = Pair(up_y, up_corner.at[1], up_x, up_corner.at[0], es, er)
    down_corners = Pair(down_y_mate, down_corner.at[1], down_x, down_corner.at[0], fs, fr)
    tokens_t[...] = tokens[...].T
    d_tokens_t[...] = d_tokens[...].T
    mixed_out[...] = jnp.zeros_like(mixed_out)
    d_tokens_out[...] = jnp.zeros_like(d_tokens_out)
    for g in both:
        g.relay()
    mates.start()
    up_corners.start()
    for g in both:
        g.corner()
    for g in both:
        g.finish()

    def block(b, carry):
        where = pl.ds(pl.multiple_of(b * HIDDEN, HIDDEN), HIDDEN)
        up, down = up_full[:, where], down_full[:, where]
        act, slope = gelu_pair(nn(tokens[...], up))
        act = act.astype(jnp.bfloat16)
        mixed_out[...] += nt(act, down)
        down_grad[:, where] = nn(d_tokens_t[...], act).astype(jnp.bfloat16)
        d_pre = (slope * nn(d_tokens[...], down)).astype(jnp.bfloat16)
        d_tokens_out[...] += nt(d_pre, up)
        up_grad[:, where] = nn(tokens_t[...], d_pre).astype(jnp.bfloat16)
        return carry

    lax.fori_loop(0, 1, block, 0)
    mates.finish()
    down_corners.start()
    lax.fori_loop(1, 3072 // HIDDEN, block, 0)
    swap_a.finish()
    swap_b.finish()
    up_corners.finish()
    down_corners.finish()


def outbound(*operands):
    bf, f32 = jnp.bfloat16, jnp.float32
    return pl.pallas_call(
        out_kernel,
        out_shape=(
            jax.ShapeDtypeStruct((8, 144, 768), bf),
            jax.ShapeDtypeStruct((8, 144, 768), bf),
            jax.ShapeDtypeStruct((2, 96, 3072), bf),
            jax.ShapeDtypeStruct((384, 768), bf),
            jax.ShapeDtypeStruct((384, 768), bf),
            jax.ShapeDtypeStruct((2, 384, 768), bf),
            jax.ShapeDtypeStruct((512, 768), f32),
            jax.ShapeDtypeStruct((512, 768), f32),
            jax.ShapeDtypeStruct((768, 3072), bf),
            jax.ShapeDtypeStruct((768, 3072), bf),
        ),
        in_specs=[ONCHIP] * 6 + [ANYWHERE] * 4,
        out_specs=(ANYWHERE,) * 6 + (ONCHIP,) * 4,
        scratch_shapes=[pltpu.VMEM((768, 3072), bf)] * 2
        + [pltpu.VMEM((768, 512), bf)] * 2
        + [DMA((8,))] * 4
        + [DMA((9,))] * 4
        + [DMA((4,))]
        + [DMA((2,))] * 6,
        compiler_params=pltpu.CompilerParams(
            collective_id=1, has_side_effects=True, vmem_limit_bytes=60 << 20
        ),
        name="outbound",
    )(*operands)


def widened(ref):
    return ref[...].astype(jnp.float32)


class Parts:
    def __init__(self, grad, keep, over_x, over_y, sem, rsem=None):
        d, s, c = place()
        sx, sy = flip(s, 1), flip(s, 2)
        sd = flip(sx, 2)
        rows = grad.shape[0] // 8
        slots = (
            (s, 0, keep.at[0, 0], s), (sy, 0, keep.at[0, 1], s),
            (s, 1, keep.at[1, 0], s), (sx, 1, keep.at[1, 1], s),
            (sx, 0, over_x.at[0], sx), (sd, 0, over_x.at[1], sx),
            (sy, 1, over_y.at[0], sy), (sd, 1, over_y.at[1], sy),
        )
        self.copies, self.away = [], []
        for i, (position, h, out, target) in enumerate(slots):
            part = grad.at[pl.ds(pl.multiple_of((2 * position + h) * rows, 32), rows)]
            if i < 4 or rsem is None:
                self.copies.append(pltpu.make_async_copy(part, out, sem.at[i]))
            else:
                self.away.append(push(part, out, sem.at[i], rsem.at[i], at(d, target, c)))

    def start(self):
        for copy in self.away + self.copies:
            copy.start()

    def finish(self):
        for copy in self.copies + self.away:
            copy.wait()


class Pieces:
    def __init__(self, parts, full, sem):
        d, s, c = place()
        rows = full.shape[0] // 8
        sx, sy = flip(s, 1), flip(s, 2)
        positions = [p for p in (s, sx, sy, flip(sx, 2)) for _ in range(2)]
        self.copies = [
            pltpu.make_async_copy(
                part,
                full.at[pl.ds(pl.multiple_of(rows * (2 * p + (c if i % 2 == 0 else 1 - c)), 32), rows)],
                sem.at[i],
            )
            for i, (p, part) in enumerate(zip(positions, parts))
        ]

    def start(self):
        for copy in self.copies:
            copy.start()

    def finish(self):
        for copy in self.copies:
            copy.wait()


def expert_kernel(
    rows, grads, expert_up, up_m, up_x0, up_x1, up_y0, up_y1, up_corner,
    down_own, down_m, down_x0, down_x1, down_y0, down_y1, down_corner, first_grad, second_grad,
    rows_back, grads_back, up_keep, up_x, up_y, down_keep, down_x, down_y, first_part, second_part,
    up, down, act, d_pre, made, d_made, total, d_total, up_grad, down_grad, rows_t,
    fo, fm, fn, ff, fs, fr, fl, so, sm, sn, sf, ss, sr, sl,
    s1, r1, s2, r2, lsem, wsem, vsem, psem, arsem, qsem,
):
    bf = jnp.bfloat16
    d, s, c = place()
    weights = (
        Pieces(
            (expert_up.at[c], up_m, up_x0, up_x1, up_y0, up_y1, up_corner.at[0], up_corner.at[1]), up, wsem
        ),
        Pieces(
            (down_own, down_m, down_x0, down_x1, down_y0, down_y1, down_corner.at[0], down_corner.at[1]),
            down, vsem,
        ),
    )
    for each in weights:
        each.start()
    greet([device for _, device in group_of(d, s, c)] + [at(d, flip(s, 1), c), at(d, flip(s, 2), c)])
    sums = (
        DenseSum("cols", first_grad, first_part, fo, fm, fn, ff, None, fs, fr, fl),
        DenseSum("rows", second_grad, second_part, so, sm, sn, sf, None, ss, sr, sl),
    )
    for each in sums:
        each.start()
    swap_a = Swap(made, rows_back, s1, r1, lsem.at[0])
    swap_b = Swap(d_made, grads_back, s2, r2, lsem.at[1])
    for each in weights:
        each.finish()
    for step, half in ((2, 0), (2, 1), (1, None), (3, None), (0, None)):
        there = lax.rem(d + step, 4)
        count = 2 if half is None else 1
        size = 144 * count
        start = 2 * there if half is None else 2 * there + lax.rem(c + half, 2)
        chunk = pl.ds(start, count)
        lines = pl.ds(pl.multiple_of(144 * start, 144), size)
        kept = pl.ds(0, size)
        x = rows[chunk].reshape(size, 768)
        g = grads[chunk].reshape(size, 768)
        total[kept] = jnp.zeros((size, 768), jnp.float32)
        d_total[kept] = jnp.zeros((size, 768), jnp.float32)

        def block(b, carry):
            where = pl.ds(pl.multiple_of(b * HIDDEN, HIDDEN), HIDDEN)
            up_part, down_part = up[:, where], down[where]
            made_act, slope = gelu_pair(nn(x, up_part))
            made_act = made_act.astype(bf)
            act[lines, where] = made_act
            total[kept] += nn(made_act, down_part)
            d_part = (slope * nt(g, down_part)).astype(bf)
            d_pre[lines, where] = d_part
            d_total[kept] += nt(d_part, up_part)
            return carry

        lax.fori_loop(0, 3072 // HIDDEN, block, 0)
        made[chunk] = total[kept].astype(bf).reshape(count, 144, 768)
        d_made[chunk] = d_total[kept].astype(bf).reshape(count, 144, 768)
        swap_a.send(step, half)
        swap_b.send(step, half)
        if half == 1:
            for each in sums:
                each.merge()
        if step == 3:
            for each in sums:
                each.join()
    rows_t[...] = rows.reshape(1152, 768)[...].T
    g_all = grads.reshape(1152, 768)

    def up_block(b, carry):
        where = pl.ds(pl.multiple_of(b * HIDDEN, HIDDEN), HIDDEN)
        up_grad[:, where] = nn(rows_t[...], d_pre[:, where]).astype(bf)
        return carry

    def down_block(b, carry):
        where = pl.ds(pl.multiple_of(384 * b, 384), 384)
        down_grad[where] = tn(act[:, where], g_all[...]).astype(bf)
        return carry

    up_parts = Parts(up_grad, up_keep, up_x, up_y, psem, arsem)
    down_parts = Parts(down_grad, down_keep, down_x, down_y, qsem)
    lax.fori_loop(0, 3072 // HIDDEN, up_block, 0)
    up_parts.start()
    lax.fori_loop(0, 8, down_block, 0)
    down_parts.start()
    for each in sums:
        each.close()
    swap_a.finish()
    swap_b.finish()
    up_parts.finish()
    down_parts.finish()


def experts(rows, grads, up_pieces, down_pieces, first_grad, second_grad):
    bf, f32 = jnp.bfloat16, jnp.float32

    def rooms(piece, half):
        return [
            pltpu.VMEM((4,) + piece, bf),
            pltpu.VMEM((4,) + piece, bf),
            pltpu.VMEM((2,) + half, bf),
            pltpu.VMEM((2,) + piece, bf),
            DMA((8,)),
            DMA((8,)),
            DMA((4,)),
        ]

    def parts(r, n):
        return (
            jax.ShapeDtypeStruct((2, 2, r, n), bf),
            jax.ShapeDtypeStruct((2, r, n), bf),
            jax.ShapeDtypeStruct((2, r, n), bf),
        )

    return pl.pallas_call(
        expert_kernel,
        out_shape=(
            jax.ShapeDtypeStruct((8, 144, 768), bf),
            jax.ShapeDtypeStruct((8, 144, 768), bf),
        )
        + parts(96, 3072)
        + parts(384, 768)
        + (
            jax.ShapeDtypeStruct((96, 3072), bf),
            jax.ShapeDtypeStruct((768, 384), bf),
        ),
        in_specs=[ONCHIP, ONCHIP] + [ANYWHERE] * 16,
        out_specs=(ANYWHERE,) * 8 + (ONCHIP, ONCHIP),
        scratch_shapes=[
            pltpu.VMEM((768, 3072), bf),
            pltpu.VMEM((3072, 768), bf),
            pltpu.VMEM((1152, 3072), bf),
            pltpu.VMEM((1152, 3072), bf),
            pltpu.VMEM((8, 144, 768), bf),
            pltpu.VMEM((8, 144, 768), bf),
            pltpu.VMEM((288, 768), f32),
            pltpu.VMEM((288, 768), f32),
            pltpu.VMEM((768, 3072), bf),
            pltpu.VMEM((3072, 768), bf),
            pltpu.VMEM((768, 1152), bf),
        ]
        + rooms((96, 3072), (96, 1536))
        + rooms((768, 384), (384, 384))
        + [DMA((8,))] * 4
        + [DMA((2,)), DMA((8,)), DMA((8,)), DMA((8,)), DMA((8,)), DMA((8,))],
        compiler_params=pltpu.CompilerParams(
            collective_id=2, has_side_effects=True, vmem_limit_bytes=67043328
        ),
        name="experts",
    )(rows, grads, *up_pieces, *down_pieces, first_grad, second_grad)


def hop(values, bit):
    return lax.ppermute(values, "fsdp", [(f, f ^ bit) for f in range(8)])


def square_next(keep, from_x, from_y):
    f32, bf = jnp.float32, jnp.bfloat16
    return (
        hop((keep[0, 1].astype(f32) + from_x[1].astype(f32)).astype(bf), 4),
        hop((keep[1, 1].astype(f32) + from_y[1].astype(f32)).astype(bf), 2),
    )


class DenseSum:
    def __init__(self, kind, grad, out, own, mate, near, far, line, ssem, rsem, lsem, part=None):
        self.kind, self.grad, self.out, self.part = kind, grad, out, part
        self.own, self.mate, self.near, self.far, self.line = own, mate, near, far, line
        self.ssem, self.rsem, self.lsem = ssem, rsem, lsem
        self.d, self.s, self.c = place()
        self.order = (
            flip(flip(self.s, 1), 2),
            flip(self.s, 1),
            flip(self.s, 2),
            self.s,
        )

    def piece(self, f):
        if self.part is not None:
            return self.grad.at[pl.ds(pl.multiple_of(96 * f + 48 * self.part, 48), 48)]
        if self.kind == "cols":
            return self.grad.at[pl.ds(pl.multiple_of(96 * f, 96), 96)]
        return self.grad.at[:, pl.ds(pl.multiple_of(384 * f, 384), 384)]

    def half(self, ref, h):
        if self.kind == "cols":
            return ref.at[:, pl.ds(1536 * h, 1536)]
        return ref.at[pl.ds(384 * h, 384)]

    def quarter(self, ref, q):
        if self.kind == "cols":
            return ref.at[:, pl.ds(pl.multiple_of(768 * q, 768), 768)]
        return ref.at[pl.ds(pl.multiple_of(192 * q, 192), 192)]

    def start(self):
        d, s, c = self.d, self.s, self.c
        self.zero, self.local = [], []
        for j, position in enumerate(self.order):
            copy = push(
                self.piece(2 * position + 1 - c), self.mate.at[j], self.ssem.at[j], self.rsem.at[j], at(d, s, 1 - c)
            )
            copy.start()
            self.zero.append(copy)
            copy = pltpu.make_async_copy(self.piece(2 * position + c), self.own.at[j], self.lsem.at[j])
            copy.start()
            self.local.append(copy)

    def merge(self):
        d, s, c = self.d, self.s, self.c
        sx, sy = flip(s, 1), flip(s, 2)
        self.one = []
        for j in range(4):
            self.zero[j].wait_recv()
            self.local[j].wait()
            self.own[j] = (widened(self.own.at[j]) + widened(self.mate.at[j])).astype(jnp.bfloat16)
            if j == 0:
                for h, target in enumerate((sx, sy)):
                    copy = push(
                        self.half(self.own.at[0], h), self.near.at[h], self.ssem.at[4 + h], self.rsem.at[4 + h],
                        at(d, target, c),
                    )
                    copy.start()
                    self.one.append(copy)

    def join(self):
        d, s, c = self.d, self.s, self.c
        sx, sy = flip(s, 1), flip(s, 2)
        for h, j in ((0, 2), (1, 1)):
            self.one[h].wait_recv()
            where = self.half(self.own.at[j], h)
            where[...] = (widened(where) + widened(self.near.at[h])).astype(jnp.bfloat16)
        self.two = []
        for h, target in enumerate((sx, sy)):
            copy = push(
                self.own.at[1 + h], self.far.at[h], self.ssem.at[6 + h], self.rsem.at[6 + h], at(d, target, c)
            )
            copy.start()
            self.two.append(copy)

    def square(self):
        for copy in self.two:
            copy.wait_recv()
        return (
            widened(self.own.at[3]) + widened(self.far.at[0]) + widened(self.far.at[1])
        ).astype(jnp.bfloat16)

    def along(self):
        d, s, c = self.d, self.s, self.c
        self.own[3] = self.square()
        self.three = []
        for k in range(1, 4):
            target = lax.rem(d + k, 4)
            copy = push(
                self.quarter(self.own.at[3], target), self.line.at[k - 1], self.ssem.at[7 + k], self.rsem.at[7 + k],
                at(target, s, c),
            )
            copy.start()
            self.three.append(copy)

    def finish(self):
        total = widened(self.quarter(self.own.at[3], self.d))
        for k in range(1, 4):
            self.three[k - 1].wait_recv()
            total = total + widened(self.line.at[k - 1])
        self.out[...] = total
        self.sent(self.three)

    def close(self):
        self.out[...] = self.square()
        self.sent([])

    def sent(self, more):
        for copy in self.zero + self.one + self.two + more:
            copy.wait_send()


class LineSum:
    def __init__(self, kind, part, out, landing, ssem, rsem):
        self.kind, self.part, self.out, self.landing = kind, part, out, landing
        self.ssem, self.rsem = ssem, rsem
        self.d, self.s, self.c = place()

    def quarter(self, q):
        if self.kind == "cols":
            return self.part.at[:, pl.ds(pl.multiple_of(768 * q, 768), 768)]
        return self.part.at[pl.ds(pl.multiple_of(192 * q, 192), 192)]

    def start(self):
        self.copies = []
        for k in range(1, 4):
            target = lax.rem(self.d + k, 4)
            copy = push(
                self.quarter(target), self.landing.at[k - 1], self.ssem.at[k - 1], self.rsem.at[k - 1],
                at(target, self.s, self.c),
            )
            copy.start()
            self.copies.append(copy)

    def finish(self):
        total = widened(self.quarter(self.d))
        for k in range(3):
            self.copies[k].wait_recv()
            total = total + widened(self.landing.at[k])
        self.out[...] = total
        for copy in self.copies:
            copy.wait_send()


class Ending:
    def __init__(self, keep, from_x, from_y, out, room, stage, landed, last, lsem, ssem, rsem, loaded=None):
        self.out, self.room, self.stage, self.landed, self.last = out, room, stage, landed, last
        self.ssem, self.rsem = ssem, rsem
        self.d, self.s, self.c = place()
        sources = [
            keep.at[0, 0], keep.at[0, 1], keep.at[1, 0], keep.at[1, 1],
            from_x.at[0], from_x.at[1], from_y.at[0], from_y.at[1],
        ]
        self.loads = [
            pltpu.make_async_copy(source, room.at[i], lsem.at[i]) for i, source in enumerate(sources)
        ]
        for i, source in enumerate(loaded or ()):
            self.loads.append(pltpu.make_async_copy(source, landed.at[i], lsem.at[8 + i]))
        self.sent = []

    def load(self):
        for copy in self.loads:
            copy.start()

    def loaded(self):
        for copy in self.loads:
            copy.wait()

    def go(self, index, target):
        dst = self.last if index == 2 else self.landed.at[index]
        copy = push(self.stage.at[index], dst, self.ssem.at[index], self.rsem.at[index], target)
        copy.start()
        self.sent.append(copy)

    def next(self):
        bf = jnp.bfloat16
        room = self.room
        self.stage[0] = (widened(room.at[1]) + widened(room.at[5])).astype(bf)
        self.go(0, at(self.d, flip(self.s, 2), self.c))
        self.stage[1] = (widened(room.at[3]) + widened(room.at[7])).astype(bf)
        self.go(1, at(self.d, flip(self.s, 1), self.c))

    def close(self):
        for copy in self.sent:
            copy.wait_recv()
        c = self.c
        mine, theirs = c, 1 - c

        def total(h):
            return (
                widened(self.room.at[2 * h]) + widened(self.room.at[4 + 2 * h]) + widened(self.landed.at[h])
            )

        self.stage[2] = total(theirs).astype(jnp.bfloat16)
        self.go(2, at(self.d, self.s, 1 - c))
        self.out[c] = total(mine)

    def finish(self):
        self.sent[-1].wait_recv()
        self.out[1 - self.c] = widened(self.last)
        for copy in self.sent:
            copy.wait_send()


class Tail:
    def __init__(self, d_rows, router, act, ada, ada_out, d_act_out, router_out, z1, plane, plane_in, z2, z2_in, sems):
        self.d_rows, self.router, self.act, self.ada = d_rows, router, act, ada
        self.ada_out, self.d_act_out, self.router_out = ada_out, d_act_out, router_out
        self.z1, self.plane, self.plane_in, self.z2, self.z2_in = z1, plane, plane_in, z2, z2_in
        self.sems = sems
        self.d, self.s, self.c = place()
        self.f = 2 * self.s + self.c

    def z_copy(self, k, src, dst, base):
        send, recv = self.sems[base], self.sems[base + 1]
        return push(src, dst, send.at[k], recv.at[k], at(lax.rem(self.d + k, 4), self.s, self.c))

    def f_copy(self, k, src, dst, base):
        send, recv = self.sems[base], self.sems[base + 1]
        return push(src, dst, send.at[k], recv.at[k], (self.d, lax.rem(self.f + k, 8)))

    def start(self):
        self.all = [
            self.z_copy(k, self.d_rows.at[lax.rem(self.d + k, 4)], self.z1.at[k], 0) for k in range(1, 4)
        ]
        for copy in self.all:
            copy.start()

    def second(self):
        total = self.d_rows[self.d]
        for k in range(1, 4):
            self.all[k - 1].wait_recv()
            total = total + self.z1[k]
        for target in range(8):
            self.plane[target, :, 0:1152] = total
            self.plane[target, :, 1152:1280] = self.router[target]
        copies = [
            self.f_copy(k, self.plane.at[lax.rem(self.f + k, 8)], self.plane_in.at[lax.rem(8 - k, 8)], 2)
            for k in range(1, 8)
        ]
        for copy in copies:
            copy.start()
        self.in_plane = copies
        self.all = self.all + copies

    def third(self):
        f = self.f
        self.plane_in[0] = self.plane[f]
        for copy in self.in_plane:
            copy.wait_recv()
        everything = self.plane_in[...]
        router = jnp.sum(everything[:, :, 1152:1280], axis=0)
        rows = everything[:, :, 0:1152].reshape(64, 1152)
        line = lax.broadcasted_iota(jnp.int32, (64, 64), 0)
        column = lax.broadcasted_iota(jnp.int32, (64, 64), 1)
        turn = (lax.rem(line // 8 + 8 - f, 8) * 8 + lax.rem(line, 8) == column).astype(jnp.bfloat16)
        d_mod = nn(turn, rows.astype(jnp.bfloat16)).astype(jnp.bfloat16)
        self.ada_out[...] = tn(self.act[...], d_mod)[0:96]
        part = nt(d_mod, self.ada[...])
        self.z2[0:64, 0:96] = part
        self.z2[0:64, 96:128] = jnp.zeros((64, 32), jnp.float32)
        self.z2[64:72, :] = router
        copies = [self.z_copy(k, self.z2, self.z2_in.at[k], 4) for k in range(1, 4)]
        for copy in copies:
            copy.start()
        self.along = copies
        self.all = self.all + copies

    def fourth(self):
        total = self.z2[...]
        for k in range(1, 4):
            self.along[k - 1].wait_recv()
            total = total + self.z2_in[k]
        self.router_out[...] = total[64:72]
        self.z2_in[0] = total
        copies = [
            self.f_copy(
                k,
                self.z2_in.at[0, pl.ds(pl.multiple_of(8 * lax.rem(self.f + k, 8), 8), 8)],
                self.d_act_out.at[self.f],
                6,
            )
            for k in range(1, 8)
        ]
        for copy in copies:
            copy.start()
        self.d_act_out[self.f] = self.z2_in[0, pl.ds(pl.multiple_of(8 * self.f, 8), 8)]
        self.last = copies
        self.all = self.all + copies

    def finish(self):
        for k in range(1, 8):
            self.f_copy(
                k, self.z2_in.at[0, pl.ds(0, 8)], self.d_act_out.at[lax.rem(self.f + 8 - k, 8)], 6
            ).wait_recv()
        for copy in self.all:
            copy.wait_send()


def dense_kernel(
    grad, first_part, second_part, d_rows, router, act, ada,
    up_keep, up_x, up_y, up_low, up_high, down_keep, down_x, down_y,
    out, first_out, second_out, ada_out, d_act_out, router_out, up_out, down_out,
    ur, us, ul, ue, ula, usa, ura, dr, ds, dl, de, dla, dsa, dra,
    own, mate, near, far, line, ssem, rsem, lsem,
    own_2, mate_2, near_2, far_2, line_2, ssem_2, rsem_2, lsem_2,
    first_in, fs, fr, second_in, ss, sr, *rest,
):
    d, s, c = place()
    f = 2 * s + c
    greet(
        [at(lax.rem(d + k, 4), s, c) for k in range(1, 4)]
        + [(d, lax.rem(f + k, 8)) for k in range(1, 8)]
    )
    both = (
        DenseSum("cols", grad, out.at[pl.ds(0, 48)], own, mate, near, far, line, ssem, rsem, lsem, 0),
        DenseSum(
            "cols", grad, out.at[pl.ds(48, 48)], own_2, mate_2, near_2, far_2, line_2, ssem_2, rsem_2, lsem_2, 1
        ),
    )
    lines = (
        LineSum("cols", first_part, first_out, first_in, fs, fr),
        LineSum("rows", second_part, second_out, second_in, ss, sr),
    )
    tail = Tail(d_rows, router, act, ada, ada_out, d_act_out, router_out, *rest[:5], rest[5:])
    ups = Ending(up_keep, up_x, up_y, up_out, ur, us, ul, ue, ula, usa, ura, (up_low, up_high))
    downs = Ending(down_keep, down_x, down_y, down_out, dr, ds, dl, de, dla, dsa, dra)
    tail.start()
    for each in both:
        each.start()
    for each in lines:
        each.start()
    downs.load()
    ups.load()
    for each in both:
        each.merge()
    tail.second()
    for each in both:
        each.join()
    downs.loaded()
    downs.next()
    ups.loaded()
    ups.close()
    tail.third()
    for each in both:
        each.along()
    tail.fourth()
    downs.close()
    for each in lines:
        each.finish()
    ups.finish()
    for each in both:
        each.finish()
    downs.finish()
    tail.finish()


def dense_sums(grad, first_part, second_part, small, routed):
    bf, f32 = jnp.bfloat16, jnp.float32

    def rooms(r, n):
        return [
            pltpu.VMEM((8, r, n), bf),
            pltpu.VMEM((3, r, n), bf),
            pltpu.VMEM((2, r, n), bf),
            pltpu.VMEM((r, n), bf),
            DMA((10,)),
            DMA((3,)),
            DMA((3,)),
        ]

    return pl.pallas_call(
        dense_kernel,
        out_shape=(
            jax.ShapeDtypeStruct((96, 768), f32),
            jax.ShapeDtypeStruct((96, 768), f32),
            jax.ShapeDtypeStruct((192, 384), f32),
            jax.ShapeDtypeStruct((96, 1152), f32),
            jax.ShapeDtypeStruct((8, 8, 128), f32),
            jax.ShapeDtypeStruct((8, 128), f32),
            jax.ShapeDtypeStruct((2, 96, 3072), f32),
            jax.ShapeDtypeStruct((2, 384, 768), f32),
        ),
        in_specs=[ANYWHERE] + [ONCHIP] * 6 + [ANYWHERE] * 8,
        out_specs=(ONCHIP,) * 8,
        scratch_shapes=rooms(96, 3072) + rooms(384, 768) + [
            pltpu.VMEM((4, 48, 3072), bf),
            pltpu.VMEM((4, 48, 3072), bf),
            pltpu.VMEM((2, 48, 1536), bf),
            pltpu.VMEM((2, 48, 3072), bf),
            pltpu.VMEM((3, 48, 768), bf),
            DMA((11,)), DMA((11,)), DMA((4,)),
        ] * 2 + [
            pltpu.VMEM((3, 96, 768), bf),
            DMA((3,)), DMA((3,)),
            pltpu.VMEM((3, 192, 384), bf),
            DMA((3,)), DMA((3,)),
            pltpu.VMEM((4, 8, 1152), f32),
            pltpu.VMEM((8, 8, 1280), f32),
            pltpu.VMEM((8, 8, 1280), f32),
            pltpu.VMEM((72, 128), f32),
            pltpu.VMEM((4, 72, 128), f32),
            DMA((4,)), DMA((4,)), DMA((8,)), DMA((8,)), DMA((4,)), DMA((4,)), DMA((8,)), DMA((8,)),
        ],
        compiler_params=pltpu.CompilerParams(
            collective_id=3, has_side_effects=True, vmem_limit_bytes=60 << 20
        ),
        cost_estimate=pl.CostEstimate(flops=40_000_000_000, bytes_accessed=20_000_000, transcendentals=0),
        name="dense_sums",
    )(grad, first_part, second_part, *small, *routed)


def layer_stats(values_in):
    centred = values_in - jnp.mean(values_in, axis=-1, keepdims=True)
    inv_std = lax.rsqrt(jnp.mean(centred * centred, axis=-1, keepdims=True) + 1e-06)
    return centred * inv_std, inv_std


def lines_of(tile, first):
    row = lax.broadcasted_iota(jnp.int32, tile.shape, 0)
    picked = [
        jnp.sum(jnp.where(row == first + i, tile, 0.0), axis=0, keepdims=True) for i in range(2)
    ]
    return jnp.concatenate(picked, axis=0)


def modulated(inside, mod, part):
    columns = slice(768 * part, 768 * part + 768)
    return inside[:, 0:1] * mod[0:1, columns] + inside[:, 1:2] * mod[1:2, columns]


def head_column(g):
    return 768 * (g // 9) + 64 * (g % 9)


QUERY_ROWS = 512


def front_kernel(
    tokens, mod_rows, inside, seg_col, seg_row, qkvo, router_t, cotangent, routes, target,
    heads, totals, attended, projected, residual, second, d_mixed, gates, rows, grads, mod,
    bias, made, weighted,
):
    bf, f32 = jnp.bfloat16, jnp.float32
    d = lax.axis_index("dp")
    for j in range(4):
        mod[:, 1152 * j : 1152 * j + 1152] = lines_of(mod_rows[j], 2 * d)
    token_float = tokens[...].astype(f32)
    normed, _ = layer_stats(token_float)
    first = (normed * (1.0 + modulated(inside, mod, 1)) + modulated(inside, mod, 0)).astype(bf)
    for j in range(4):
        piece = nn(first, qkvo[:, 768 * j : 768 * j + 640]).astype(bf)
        for i in range(9):
            heads[9 * j + i] = piece[:, 64 * i : 64 * i + 64]
    bias[...] = jnp.where(seg_col[...] == seg_row[...], 0.0, -1e30)

    def block(n, carry):
        h, part = n // (512 // QUERY_ROWS), lax.rem(n, 512 // QUERY_ROWS)
        lines = pl.ds(pl.multiple_of(part * QUERY_ROWS, QUERY_ROWS), QUERY_ROWS)
        scores = nt(heads[h, lines], heads[12 + h]) * 0.125 + bias[lines]
        row_max = jnp.max(scores, axis=-1, keepdims=True)
        weight = jnp.exp(scores - row_max)
        running = jnp.sum(weight, axis=-1, keepdims=True)
        probability = (weight * (1.0 / running)).astype(bf)
        made[h, lines] = nn(probability, heads[24 + h]).astype(bf)
        totals[h, lines] = row_max + jnp.log(running)
        return carry

    lax.fori_loop(0, 12 * (512 // QUERY_ROWS), block, 0)
    for h in range(12):
        attended[:, 64 * h : 64 * h + 64] = made[h]
    for j in range(4):
        piece = nn(attended[...], qkvo[:, 768 * j + 512 : 768 * j + 768])
        projected[:, 192 * j : 192 * j + 192] = piece[:, 64:256]
    residual[...] = token_float + modulated(inside, mod, 2) * projected[...]
    normed, _ = layer_stats(residual[...])
    second[...] = (normed * (1.0 + modulated(inside, mod, 4)) + modulated(inside, mod, 3)).astype(bf)
    logits = nt(second[...], router_t[...].astype(bf))
    ids = lax.broadcasted_iota(jnp.int32, (512, 8), 1)
    chosen = [
        jnp.sum(jnp.where(ids == routes[:, k : k + 1], logits, 0.0), axis=-1, keepdims=True)
        for k in range(2)
    ]
    top = jnp.maximum(chosen[0], chosen[1])
    raised = [jnp.exp(each - top) for each in chosen]
    share = [each / (raised[0] + raised[1]) for each in raised]
    pair = lax.broadcasted_iota(jnp.int32, (512, 2), 1)
    gates[...] = jnp.where(pair == 0, share[0], share[1])
    mixed_grad = modulated(inside, mod, 5) * cotangent[...].astype(f32)
    d_mixed[...] = mixed_grad.astype(bf)
    for k in range(2):
        weighted[k] = (share[k] * mixed_grad).astype(bf)

    def send(b, carry):
        lines = pl.ds(pl.multiple_of(288 * b, 288), 288)
        places = lax.broadcasted_iota(jnp.int32, (288, 512), 0) + 288 * b
        first_hot = (places == target[0:1]).astype(f32)
        second_hot = (places == target[1:2]).astype(f32)
        rows[lines] = nn((first_hot + second_hot).astype(bf), second[...]).astype(bf)
        grads[lines] = (
            nn(first_hot.astype(bf), weighted[0]) + nn(second_hot.astype(bf), weighted[1])
        ).astype(bf)
        return carry

    lax.fori_loop(0, 4, send, 0)


def front(*operands):
    bf, f32 = jnp.bfloat16, jnp.float32
    return pl.pallas_call(
        front_kernel,
        out_shape=(
            jax.ShapeDtypeStruct((36, 512, 64), bf),
            jax.ShapeDtypeStruct((12, 512, 1), f32),
            jax.ShapeDtypeStruct((512, 768), bf),
            jax.ShapeDtypeStruct((512, 768), f32),
            jax.ShapeDtypeStruct((512, 768), f32),
            jax.ShapeDtypeStruct((512, 768), bf),
            jax.ShapeDtypeStruct((512, 768), bf),
            jax.ShapeDtypeStruct((512, 2), f32),
            jax.ShapeDtypeStruct((1152, 768), bf),
            jax.ShapeDtypeStruct((1152, 768), bf),
            jax.ShapeDtypeStruct((2, 4608), f32),
        ),
        in_specs=[ONCHIP] * 10,
        out_specs=(ONCHIP,) * 11,
        scratch_shapes=[
            pltpu.VMEM((512, 512), f32),
            pltpu.VMEM((12, 512, 64), bf),
            pltpu.VMEM((2, 512, 768), bf),
        ],
        compiler_params=pltpu.CompilerParams(vmem_limit_bytes=60 << 20),
        cost_estimate=pl.CostEstimate(flops=40_000_000_000, bytes_accessed=20_000_000, transcendentals=0),
        name="front",
    )(*operands)


def norm_grad(upstream, normed, inv_std):
    return (
        upstream
        - jnp.mean(upstream, axis=-1, keepdims=True)
        - normed * jnp.mean(upstream * normed, axis=-1, keepdims=True)
    ) * inv_std


def rear_kernel(
    tokens, mod, inside, seg_col, seg_row, qkvo_in, router_t, cotangent, routes, target,
    heads_in, totals_in, attended_in, projected, residual, second, gates,
    returned, d_returned, shared_out, d_shared,
    output, tokens_grad, qkvo_grad, d_mod, router_grad,
    bias, rows_t, d_heads, d_att, d_att_t, d_rows_t, d_rows, d_residual, d_proj,
    qkvo, heads, totals, attended, sem,
):
    bf, f32 = jnp.bfloat16, jnp.float32
    pairs = ((heads_in, heads), (qkvo_in, qkvo), (totals_in, totals), (attended_in, attended))
    loads = [pltpu.make_async_copy(src, dst, sem.at[i]) for i, (src, dst) in enumerate(pairs)]
    for copy in loads:
        copy.start()
    upstream = cotangent[...].astype(f32)

    def image_sums(part, values):
        for j in range(2):
            d_mod[j : j + 1, 768 * part : 768 * part + 768] = jnp.sum(
                inside[:, j : j + 1] * values, axis=0, keepdims=True
            )

    share = [gates[:, k : k + 1] for k in range(2)]
    places = lax.broadcasted_iota(jnp.int32, (512, 1152), 1)
    hot = [(places == target[:, k : k + 1]).astype(f32).astype(bf) for k in range(2)]
    picked = [nn(each, returned[...]) for each in hot]
    mixed = shared_out[...] + (share[0] * picked[0] + share[1] * picked[1])
    gate_two = modulated(inside, mod, 5)
    output[...] = (residual[...] + gate_two * mixed).astype(bf)
    image_sums(5, upstream * mixed)
    mixed_grad = gate_two * upstream
    d_share = [jnp.sum(mixed_grad * each, axis=-1, keepdims=True) for each in picked]
    inner = share[0] * d_share[0] + share[1] * d_share[1]
    ids = lax.broadcasted_iota(jnp.int32, (512, 8), 1)
    d_logits = sum(
        jnp.where(ids == routes[:, k : k + 1], share[k] * (d_share[k] - inner), 0.0) for k in range(2)
    ).astype(bf)
    router_grad[...] = tn(d_logits, second[...])
    d_second = (
        d_shared[...] + nn(d_logits, router_t[...].astype(bf)) + nn(hot[0] + hot[1], d_returned[...])
    )
    normed, inv_std = layer_stats(residual[...])
    image_sums(3, d_second)
    image_sums(4, d_second * normed)
    d_residual[...] = upstream + norm_grad(d_second * (1.0 + modulated(inside, mod, 4)), normed, inv_std)
    gate_one = modulated(inside, mod, 2)
    image_sums(2, d_residual[...] * projected[...])
    d_proj[...] = (gate_one * d_residual[...]).astype(bf)
    for copy in loads:
        copy.wait()
    d_attended = jnp.zeros((512, 768), f32)
    for j in range(4):
        piece = jnp.concatenate(
            [jnp.zeros((512, 64), bf), d_proj[:, 192 * j : 192 * j + 192]], axis=1
        )
        d_attended += nt(piece, qkvo[:, 768 * j + 512 : 768 * j + 768])
    d_attended = d_attended.astype(bf)
    d_att_t[...] = d_attended.T
    for h in range(12):
        d_att[h] = d_attended[:, 64 * h : 64 * h + 64]
    for j in range(18):
        pair = jnp.concatenate([heads[2 * j], heads[2 * j + 1]], axis=1)
        rows_t[128 * j : 128 * j + 128] = pair.T
    bias[...] = jnp.where(seg_col[...] == seg_row[...], 0.0, -1e30)

    def head(h, carry):
        def at_head(g):
            return pl.ds(pl.multiple_of(64 * g, 64), 64)

        d_key, d_value = jnp.zeros((64, 512), f32), jnp.zeros((64, 512), f32)
        for part in range(512 // QUERY_ROWS):
            lines = slice(part * QUERY_ROWS, (part + 1) * QUERY_ROWS)
            scores = nn(heads[h, lines], rows_t[at_head(12 + h)]) * 0.125 + bias[lines]
            probability = jnp.exp(scores - totals[h, lines])
            d_prob = nn(d_att[h, lines], rows_t[at_head(24 + h)])
            inner = jnp.sum(probability * d_prob, axis=-1, keepdims=True)
            d_scores = (probability * (d_prob - inner)).astype(bf)
            d_heads[h, lines] = (nn(d_scores, heads[12 + h]) * 0.125).astype(bf)
            d_key += nn(rows_t[at_head(h), lines], d_scores)
            d_value += nn(d_att_t[at_head(h), lines], probability.astype(bf))
        d_rows_t[at_head(h)] = (d_key * 0.125).astype(bf)
        d_rows_t[at_head(12 + h)] = d_value.astype(bf)
        return carry

    lax.fori_loop(0, 12, head, 0)
    for g in range(12):
        column = head_column(g)
        d_rows[:, column : column + 64] = d_heads[g]
    for j in range(12):
        pair = d_rows_t[128 * j : 128 * j + 128].T
        for i in range(2):
            column = head_column(12 + 2 * j + i)
            d_rows[:, column : column + 64] = pair[:, 64 * i : 64 * i + 64]
    for j in range(4):
        d_rows[:, 768 * j + 576 : 768 * j + 768] = jnp.zeros((512, 192), bf)
    token_float = tokens[...].astype(f32)
    normed, inv_std = layer_stats(token_float)
    scale_one = 1.0 + modulated(inside, mod, 1)
    first_t = (normed * scale_one + modulated(inside, mod, 0)).astype(bf).T
    attended_t = attended[...].T
    for j in range(4):
        qkvo_grad[:, 768 * j : 768 * j + 640] = nn(first_t, d_rows[:, 768 * j : 768 * j + 640]).astype(bf)
        qkvo_grad[:, 768 * j + 576 : 768 * j + 768] = nn(
            attended_t, d_proj[:, 192 * j : 192 * j + 192]
        ).astype(bf)
    d_first = nt(d_rows[...], qkvo[...])
    image_sums(0, d_first)
    image_sums(1, d_first * normed)
    tokens_grad[...] = d_residual[...] + norm_grad(d_first * scale_one, normed, inv_std)


def rear(*operands):
    bf, f32 = jnp.bfloat16, jnp.float32
    return pl.pallas_call(
        rear_kernel,
        out_shape=(
            jax.ShapeDtypeStruct((512, 768), bf),
            jax.ShapeDtypeStruct((512, 768), f32),
            jax.ShapeDtypeStruct((768, 3072), bf),
            jax.ShapeDtypeStruct((2, 4608), f32),
            jax.ShapeDtypeStruct((8, 768), f32),
        ),
        in_specs=[ANYWHERE if i in (5, 10, 11, 12) else ONCHIP for i in range(len(operands))],
        out_specs=(ONCHIP,) * 5,
        scratch_shapes=[
            pltpu.VMEM((512, 512), f32),
            pltpu.VMEM((2304, 512), bf),
            pltpu.VMEM((12, 512, 64), bf),
            pltpu.VMEM((12, 512, 64), bf),
            pltpu.VMEM((768, 512), bf),
            pltpu.VMEM((1536, 512), bf),
            pltpu.VMEM((512, 3072), bf),
            pltpu.VMEM((512, 768), f32),
            pltpu.VMEM((512, 768), bf),
            pltpu.VMEM((768, 3072), bf),
            pltpu.VMEM((36, 512, 64), bf),
            pltpu.VMEM((12, 512, 1), f32),
            pltpu.VMEM((512, 768), bf),
            DMA((4,)),
        ],
        compiler_params=pltpu.CompilerParams(vmem_limit_bytes=67043328),
        cost_estimate=pl.CostEstimate(flops=60_000_000_000, bytes_accessed=30_000_000, transcendentals=0),
        name="rear",
    )(*operands)


def last_kernel(
    qkvo_in, first_in, second_in, ada_in, up_in, down_in, d_act_in, router_in, condition,
    qkv_out, out_out, first_out, second_out, ada_out, up_out, down_out, condition_out, router_out,
    qkvo_sum, first, second, ada, up, down, d_act, router, sem,
):
    d = lax.axis_index("dp")
    pairs = (
        (up_in, up), (down_in, down), (ada_in, ada), (qkvo_in, qkvo_sum), (first_in, first),
        (second_in, second), (d_act_in, d_act), (router_in, router),
    )
    loads = [pltpu.make_async_copy(src, dst, sem.at[i]) for i, (src, dst) in enumerate(pairs)]
    for copy in loads:
        copy.start()
    for copy in loads:
        copy.wait()
    qkv_out[...] = qkvo_sum[:, 0:576]
    out_out[...] = qkvo_sum[:, 576:768]
    first_out[...] = first[...]
    second_out[...] = second[...]
    ada_out[...] = ada[...]
    up_out[...] = up[...]
    down_out[...] = down[...]
    router_out[...] = lines_of(router[...], 2 * d)[:, 0:96]
    for f in range(8):
        columns = slice(96 * f, 96 * f + 96)
        v = condition[:, columns].astype(jnp.float32)
        sigmoid = jax.nn.sigmoid(v)
        condition_out[:, columns] = lines_of(d_act[f], 2 * d)[:, 0:96] * (
            sigmoid * (1.0 + v * (1.0 - sigmoid))
        )


def last(*operands):
    f32 = jnp.float32
    return pl.pallas_call(
        last_kernel,
        out_shape=tuple(
            jax.ShapeDtypeStruct(shape, f32)
            for shape in (
                (96, 576), (96, 192), (96, 768), (192, 384), (96, 1152), (2, 96, 3072), (2, 384, 768),
                (2, 768), (2, 96),
            )
        ),
        in_specs=[ANYWHERE] * 8 + [ONCHIP],
        out_specs=(ONCHIP,) * 9,
        scratch_shapes=[
            pltpu.VMEM(shape, f32)
            for shape in (
                (96, 768), (96, 768), (192, 384), (96, 1152), (2, 96, 3072), (2, 384, 768), (8, 8, 128), (8, 128),
            )
        ]
        + [DMA((8,))],
        compiler_params=pltpu.CompilerParams(vmem_limit_bytes=67043328),
        name="last",
    )(*operands)


def fitted_shards(
    tokens,
    condition,
    ada_weight,
    qkv_weight,
    out_weight,
    shared_up,
    shared_down,
    router_weight,
    expert_up,
    expert_down,
    routes,
    image_sizes,
    cotangent,
):
    bf = jnp.bfloat16
    d_index, f_index = lax.axis_index("dp"), lax.axis_index("fsdp")
    model_width = tokens.shape[1]
    head_size = model_width // HEADS
    inside, segment = owners(image_sizes)
    ids = jnp.arange(EXPERTS, dtype=jnp.int32)
    hot = routes[:, :, None] == ids[None, None, :]
    hot_any = jnp.any(hot, axis=1).astype(bf)
    order = jnp.arange(LONG, dtype=jnp.int32)
    earlier = (order[:, None] > order[None, :]).astype(bf)
    before = nn(earlier, hot_any)
    position = jnp.sum(jnp.where(hot, before[:, None, :], 0.0), axis=-1).astype(jnp.int32)
    target = routes * CAP + position
    live = (segment < IMG_DEV).astype(jnp.float32)
    counts = jnp.sum(live[:, None] * hot_any.astype(jnp.float32), axis=0)
    cond_float = condition.astype(jnp.float32)
    activated = jax.nn.silu(cond_float).astype(bf)
    act_slices = activated.astype(jnp.float32).reshape(IMG_DEV, 8, 96).transpose(1, 0, 2)
    act_slices = jnp.pad(act_slices, ((0, 0), (0, 6), (0, 32)))
    act_slices = act_slices.at[:, 2, :EXPERTS].set(counts)
    act_slices = act_slices.at[:, 3:5, :96].set(router_weight.T.astype(jnp.float32))
    qkvo, router_t, seen, mod_rows, up_line, down_line, up_m, up_x0, up_y0, down_own, down_m = opening(
        qkv_weight, out_weight, act_slices, ada_weight, shared_up, shared_down.T, expert_up, expert_down
    )
    hops = hop(up_m, 2), hop(up_m, 4), hop(down_own, 2), hop(down_own, 4)
    expert_counts = seen[66, :EXPERTS].astype(jnp.int32)
    segments = (segment[:, None], segment[None, :])
    (
        heads, totals, attended, projected, residual, second_input, d_mixed, gates, rows, grads, modulation,
    ) = front(tokens, mod_rows, inside, *segments, qkvo, router_t, cotangent, routes, target.T)
    rows = rows.reshape(EXPERTS, CAP, model_width)
    grads = grads.reshape(EXPERTS, CAP, model_width)
    rows, (up_x1, up_y1, down_x0, down_y0) = lax.optimization_barrier((rows, hops))
    rows_in, grads_in, up_corner, down_x1, down_y1, down_corner, shared_out, d_second, *shared_grads = (
        outbound(
            rows, grads, up_line, down_line, second_input, d_mixed, up_x0, up_y1, down_m, down_x0
        )
    )
    returned, d_returned, up_keep, *up_near, down_keep, down_x, down_y, first_part, second_part = experts(
        rows_in, grads_in, (expert_up, up_m, up_x0, up_x1, up_y0, up_y1, up_corner),
        (down_own, down_m, down_x0, down_x1, down_y0, down_y1, down_corner),
        *shared_grads,
    )
    up_next = square_next(up_keep, *up_near)
    down_near = hop(down_x, 2), hop(down_y, 4)
    returned = returned.reshape(EXPERTS * CAP, model_width)
    d_returned = d_returned.reshape(EXPERTS * CAP, model_width)
    output, tokens_grad, qkvo_grad, d_modulation, router_grad = rear(
        tokens, modulation, inside, *segments, qkvo, router_t, cotangent, routes, target,
        heads, totals, attended, projected, residual, second_input, gates,
        returned, d_returned, shared_out, d_second,
    )
    qkvo_grad, down_near, up_next = lax.optimization_barrier((qkvo_grad, down_near, up_next))
    d_modulation = d_modulation.astype(bf)
    d_mod_rows = d_modulation.astype(jnp.float32).reshape(2, 4, 1152).transpose(1, 0, 2)
    d_mod_rows = lax.dynamic_update_slice(
        jnp.zeros((4, 8, 1152), jnp.float32), d_mod_rows, (0, 2 * d_index, 0)
    )
    router_tiles = jnp.pad(
        router_grad.reshape(EXPERTS, 8, 96).transpose(1, 0, 2), ((0, 0), (0, 0), (0, 32))
    )
    (
        qkvo_sum, shared_first_sum, shared_second_sum, ada_grad, d_act_tiles, router_sum,
        expert_up_grad, expert_down_grad,
    ) = dense_sums(
        qkvo_grad, first_part, second_part,
        (d_mod_rows, router_tiles, seen[:64].astype(bf), ada_weight),
        (up_keep, *up_near, *up_next, down_keep, *down_near),
    )
    (
        qkv_grad, out_grad, shared_first_sum, shared_second_sum, ada_grad, expert_up_grad, expert_down_grad,
        condition_grad, router_out,
    ) = last(
        qkvo_sum, shared_first_sum, shared_second_sum, ada_grad, expert_up_grad, expert_down_grad,
        d_act_tiles, router_sum, condition,
    )
    return (
        output,
        tokens_grad,
        condition_grad,
        ada_grad,
        qkv_grad,
        out_grad,
        shared_first_sum,
        shared_second_sum.T,
        router_out.T,
        expert_up_grad,
        expert_down_grad,
        expert_counts,
    )


def solution(mesh):
    placed = (
        P(("dp", "fsdp"), None),
        P(("dp", "fsdp"), None),
        P("fsdp", "dp"),
        P("fsdp", "dp"),
        P("fsdp", "dp"),
        P("fsdp", "dp"),
        P("fsdp", "dp"),
        P("fsdp", "dp"),
        P("dp", "fsdp", None),
        P("dp", "fsdp", None),
        P(("dp", "fsdp"), None),
        P(("dp", "fsdp")),
        P(("dp", "fsdp"), None),
    )
    fitted = mesh.shape["dp"] == 4 and mesh.shape["fsdp"] == 8
    return jax.shard_map(
        fitted_shards if fitted else shards,
        mesh=mesh,
        in_specs=placed,
        out_specs=(
            P(("dp", "fsdp"), None),
            P(("dp", "fsdp"), None),
            P(("dp", "fsdp"), None),
            P("fsdp", "dp"),
            P("fsdp", "dp"),
            P("fsdp", "dp"),
            P("fsdp", "dp"),
            P("fsdp", "dp"),
            P("fsdp", "dp"),
            P("dp", "fsdp", None),
            P("dp", "fsdp", None),
            P(),
        ),
        check_vma=False,
    )
```

```python
import functools

import jax
import jax.numpy as jnp
from jax import lax
from jax.experimental import pallas as pl
from jax.experimental.pallas import tpu as pltpu
from jax.sharding import PartitionSpec as P

HEADS = 12
EXPERTS = 8
CAP = 144
IMG_DEV = 2
LONG = 512
MESH = pl.DeviceIdType.MESH


EXACT = lax.Precision.HIGHEST


def owners(image_sizes):
    starts = jnp.cumsum(image_sizes) - image_sizes
    position = jnp.arange(LONG, dtype=jnp.int32)[:, None]
    inside = (position >= starts[None, :]) & (position < (starts + image_sizes)[None, :])
    slot_ids = jnp.arange(IMG_DEV, dtype=jnp.int32)
    segment = jnp.sum(jnp.where(inside, slot_ids[None, :], 0), axis=1) + jnp.where(
        jnp.any(inside, axis=1), 0, IMG_DEV
    )
    return (inside.astype(jnp.float32), segment)


def dispatch_plan(routes):
    flat = routes.reshape(-1)
    onehot = (flat[:, None] == jnp.arange(EXPERTS, dtype=jnp.int32)[None, :]).astype(jnp.int32)
    before = jnp.cumsum(onehot, axis=0) - onehot
    position = jnp.sum(before * onehot, axis=1)
    target = flat * CAP + position
    assignment = jnp.arange(2 * LONG, dtype=jnp.int32)
    source = jnp.zeros((EXPERTS * CAP,), jnp.int32).at[target].set(assignment)
    filled = jnp.zeros((EXPERTS * CAP,), jnp.int32).at[target].set(1)
    return (target, source, filled)


def layer_norm(values_in):
    centred = values_in - jnp.mean(values_in, axis=-1, keepdims=True)
    inv_std = lax.rsqrt(jnp.mean(centred * centred, axis=-1, keepdims=True) + 1e-06)
    return (centred * inv_std, inv_std)


def norm_back(upstream, normed, inv_std):
    return (
        upstream
        - jnp.mean(upstream, axis=-1, keepdims=True)
        - normed * jnp.mean(upstream * normed, axis=-1, keepdims=True)
    ) * inv_std


def gelu_tanh(values_in):
    return jax.nn.gelu(values_in, approximate=True)


def gelu_back(values_in, upstream):
    return jax.vjp(gelu_tanh, values_in)[1](upstream)[0]


def collect(first, second, third):
    widened = (
        lax.all_gather(first, "dp", axis=1, tiled=True),
        lax.all_gather(second, "dp", axis=1, tiled=True),
        lax.all_gather(third, "dp", axis=1, tiled=True),
    )
    return (
        lax.all_gather(widened[0], "fsdp", axis=0, tiled=True),
        lax.all_gather(widened[1], "fsdp", axis=0, tiled=True),
        lax.all_gather(widened[2], "fsdp", axis=0, tiled=True),
    )


def spread(first, second, third):
    row_sums = (
        lax.psum_scatter(first, "fsdp", scatter_dimension=0, tiled=True),
        lax.psum_scatter(second, "fsdp", scatter_dimension=0, tiled=True),
        lax.psum_scatter(third, "fsdp", scatter_dimension=0, tiled=True),
    )
    return (
        lax.psum_scatter(row_sums[0], "dp", scatter_dimension=1, tiled=True),
        lax.psum_scatter(row_sums[1], "dp", scatter_dimension=1, tiled=True),
        lax.psum_scatter(row_sums[2], "dp", scatter_dimension=1, tiled=True),
    )


def gather_experts(up_shard, down_shard):
    return (
        lax.all_gather(up_shard, "fsdp", axis=1, tiled=True),
        lax.all_gather(down_shard, "fsdp", axis=1, tiled=True),
    )


def expert_forward(buffer_in, up_full, down_full):
    expert_pre = jnp.einsum(
        "secd,edf->secf", buffer_in, up_full, preferred_element_type=jnp.float32
    )
    expert_act = gelu_tanh(expert_pre).astype(jnp.bfloat16)
    expert_out = jnp.einsum(
        "secf,efd->secd", expert_act, down_full, preferred_element_type=jnp.float32
    ).astype(jnp.bfloat16)
    return (expert_pre, expert_act, expert_out)


def expert_backward(buffer_in, expert_pre, expert_act, d_out, up_full, down_full):
    d_act = jnp.einsum("secd,efd->secf", d_out, down_full, preferred_element_type=jnp.float32)
    d_pre = gelu_back(expert_pre, d_act).astype(jnp.bfloat16)
    d_rows = jnp.einsum(
        "secf,edf->secd", d_pre, up_full, preferred_element_type=jnp.float32
    ).astype(jnp.bfloat16)
    down_grad = jnp.einsum("secf,secd->efd", expert_act, d_out, preferred_element_type=jnp.float32)
    up_grad = jnp.einsum("secd,secf->edf", buffer_in, d_pre, preferred_element_type=jnp.float32)
    return (up_grad, down_grad, d_rows)


def attend(queries, keys_all, values_all, segment):
    row_count, head_count, head_size = queries.shape
    block_rows = min(512, row_count)
    block_count = row_count // block_rows
    score_scale = head_size ** (-0.5)

    def one_block(pieces):
        query_part, segment_part = pieces
        allowed = (segment_part[:, None] == segment[None, :])[None]
        scores = (
            jnp.einsum("qhd,khd->hqk", query_part, keys_all, preferred_element_type=jnp.float32)
            * score_scale
        )
        scores = jnp.where(allowed, scores, -1e30)
        row_max = jnp.max(scores, axis=-1, keepdims=True)
        weight = jnp.exp(scores - row_max)
        running = jnp.sum(weight, axis=-1, keepdims=True)
        probability = (weight / running).astype(jnp.bfloat16)
        attended = jnp.einsum(
            "hqk,khd->qhd", probability, values_all, preferred_element_type=jnp.float32
        )
        return (attended.astype(jnp.bfloat16), (row_max + jnp.log(running))[:, :, 0])

    return lax.map(
        one_block,
        (
            queries.reshape(block_count, block_rows, head_count, head_size),
            segment.reshape(block_count, block_rows),
        ),
    )


def attend_back(queries, keys_all, values_all, segment, log_totals, d_attended):
    row_count, head_count, head_size = queries.shape
    block_rows = min(512, row_count)
    block_count = row_count // block_rows
    score_scale = head_size ** (-0.5)

    def one_block(carry, pieces):
        key_sum, value_sum = carry
        query_part, segment_part, total_part, grad_part = pieces
        allowed = (segment_part[:, None] == segment[None, :])[None]
        scores = (
            jnp.einsum("qhd,khd->hqk", query_part, keys_all, preferred_element_type=jnp.float32)
            * score_scale
        )
        scores = jnp.where(allowed, scores, -1e30)
        probability = jnp.exp(scores - total_part[:, :, None])
        d_prob = jnp.einsum(
            "qhd,khd->hqk", grad_part, values_all, preferred_element_type=jnp.float32
        )
        d_scores = (
            probability * (d_prob - jnp.sum(probability * d_prob, axis=-1, keepdims=True))
        ).astype(jnp.bfloat16)
        query_grad = (
            jnp.einsum("hqk,khd->qhd", d_scores, keys_all, preferred_element_type=jnp.float32)
            * score_scale
        )
        key_sum = (
            key_sum
            + jnp.einsum("hqk,qhd->khd", d_scores, query_part, preferred_element_type=jnp.float32)
            * score_scale
        )
        value_sum = value_sum + jnp.einsum(
            "hqk,qhd->khd",
            probability.astype(jnp.bfloat16),
            grad_part,
            preferred_element_type=jnp.float32,
        )
        return ((key_sum, value_sum), query_grad)

    empty = jnp.zeros(keys_all.shape, jnp.float32)
    sums, query_grads = lax.scan(
        one_block,
        (empty, empty),
        (
            queries.reshape(block_count, block_rows, head_count, head_size),
            segment.reshape(block_count, block_rows),
            log_totals,
            d_attended.reshape(block_count, block_rows, head_count, head_size),
        ),
    )
    return (query_grads.reshape(row_count, head_count, head_size), sums[0], sums[1])


def shards(
    tokens,
    condition,
    ada_weight,
    qkv_weight,
    out_weight,
    shared_up,
    shared_down,
    router_weight,
    expert_up,
    expert_down,
    routes,
    image_sizes,
    cotangent,
):
    model_width = tokens.shape[1]
    head_size = model_width // HEADS
    inside, segment = owners(image_sizes)
    target, source, filled = dispatch_plan(routes)
    route_hot = (routes[:, :, None] == jnp.arange(EXPERTS, dtype=jnp.int32)[None, None, :]).astype(
        jnp.float32
    )
    live = (segment < IMG_DEV).astype(jnp.int32)
    local_counts = jnp.sum(live[:, None, None] * route_hot.astype(jnp.int32), axis=(0, 1))
    expert_counts = lax.psum(local_counts, ("dp", "fsdp"))
    ada_full, qkv_full, out_full = collect(ada_weight, qkv_weight, out_weight)
    cond_float = condition.astype(jnp.float32)
    activated = jax.nn.silu(cond_float).astype(jnp.bfloat16)
    modulation = jnp.dot(activated, ada_full, preferred_element_type=jnp.float32)
    per_row = jnp.dot(inside, modulation, precision=EXACT, preferred_element_type=jnp.float32)
    shift_one, scale_one, gate_one, shift_two, scale_two, gate_two = jnp.split(per_row, 6, axis=1)
    token_float = tokens.astype(jnp.float32)
    normed_one, inv_one = layer_norm(token_float)
    first_input = (normed_one * (1.0 + scale_one) + shift_one).astype(jnp.bfloat16)
    qkv_rows = jnp.dot(first_input, qkv_full, preferred_element_type=jnp.float32).astype(
        jnp.bfloat16
    )
    queries = qkv_rows[:, :model_width].reshape(-1, HEADS, head_size)
    keys_all = qkv_rows[:, model_width : 2 * model_width].reshape(-1, HEADS, head_size)
    values_all = qkv_rows[:, 2 * model_width :].reshape(-1, HEADS, head_size)
    attended_blocks, log_totals = attend(queries, keys_all, values_all, segment)
    attended = attended_blocks.reshape(-1, model_width)
    projected = jnp.dot(attended, out_full, preferred_element_type=jnp.float32)
    residual_one = token_float + gate_one * projected
    normed_two, inv_two = layer_norm(residual_one)
    second_input = (normed_two * (1.0 + scale_two) + shift_two).astype(jnp.bfloat16)
    shared_first, shared_second, router_full = collect(shared_up, shared_down, router_weight)
    shared_pre = jnp.dot(second_input, shared_first, preferred_element_type=jnp.float32)
    shared_act = gelu_tanh(shared_pre).astype(jnp.bfloat16)
    shared_out = jnp.dot(shared_act, shared_second, preferred_element_type=jnp.float32)
    logits = jnp.dot(second_input, router_full, preferred_element_type=jnp.float32)
    chosen = jnp.sum(logits[:, None, :] * route_hot, axis=-1)
    gate_share = jax.nn.softmax(chosen, axis=-1)
    buffer_rows = jnp.take(second_input, source // 2, axis=0).reshape(EXPERTS, CAP, model_width)
    up_full, down_full = gather_experts(expert_up, expert_down)
    groups = lax.axis_size("dp")
    expert_in = lax.all_to_all(
        buffer_rows.reshape(groups, EXPERTS // groups, CAP, model_width),
        "dp",
        split_axis=0,
        concat_axis=0,
        tiled=True,
    )
    expert_pre, expert_act, expert_out = expert_forward(expert_in, up_full, down_full)
    returned = lax.all_to_all(expert_out, "dp", split_axis=0, concat_axis=0, tiled=True).reshape(
        EXPERTS, CAP, model_width
    )
    picked = (
        jnp.take(returned.reshape(EXPERTS * CAP, model_width), target, axis=0)
        .reshape(-1, 2, model_width)
        .astype(jnp.float32)
    )
    mixed = shared_out + jnp.sum(gate_share[:, :, None] * picked, axis=1)
    output = (residual_one + gate_two * mixed).astype(jnp.bfloat16)
    upstream = cotangent.astype(jnp.float32)
    d_mixed = gate_two * upstream
    d_gate_two = upstream * mixed
    d_gate_share = jnp.sum(d_mixed[:, None, :] * picked, axis=-1)
    slot_gate = jnp.take(gate_share.reshape(-1), source) * filled.astype(jnp.float32)
    d_buffer = (
        (jnp.take(d_mixed, source // 2, axis=0) * slot_gate[:, None])
        .astype(jnp.bfloat16)
        .reshape(EXPERTS, CAP, model_width)
    )
    shared_first, shared_second, router_full = collect(shared_up, shared_down, router_weight)
    up_full, down_full = gather_experts(expert_up, expert_down)
    arrived = lax.all_to_all(
        d_buffer.reshape(groups, EXPERTS // groups, CAP, model_width),
        "dp",
        split_axis=0,
        concat_axis=0,
        tiled=True,
    )
    up_grad, down_grad, d_rows = expert_backward(
        expert_in, expert_pre, expert_act, arrived, up_full, down_full
    )
    d_returned = lax.all_to_all(d_rows, "dp", split_axis=0, concat_axis=0, tiled=True).reshape(
        EXPERTS, CAP, model_width
    )
    expert_sums = (
        lax.psum_scatter(up_grad, "fsdp", scatter_dimension=1, tiled=True),
        lax.psum_scatter(down_grad, "fsdp", scatter_dimension=1, tiled=True),
    )
    d_shared = d_mixed.astype(jnp.bfloat16)
    shared_second_grad = jnp.einsum(
        "tf,td->fd", shared_act, d_shared, preferred_element_type=jnp.float32
    )
    d_shared_act = jnp.einsum(
        "td,fd->tf", d_shared, shared_second, preferred_element_type=jnp.float32
    )
    d_shared_pre = gelu_back(shared_pre, d_shared_act).astype(jnp.bfloat16)
    shared_first_grad = jnp.einsum(
        "td,tf->df", second_input, d_shared_pre, preferred_element_type=jnp.float32
    )
    d_chosen = gate_share * (
        d_gate_share - jnp.sum(gate_share * d_gate_share, axis=-1, keepdims=True)
    )
    d_logits = jnp.sum(d_chosen[:, :, None] * route_hot, axis=1).astype(jnp.bfloat16)
    router_grad = jnp.einsum(
        "td,te->de", second_input, d_logits, preferred_element_type=jnp.float32
    )
    from_experts = (
        jnp.take(d_returned.reshape(EXPERTS * CAP, model_width), target, axis=0)
        .reshape(-1, 2, model_width)
        .astype(jnp.float32)
    )
    d_second = (
        jnp.einsum("tf,df->td", d_shared_pre, shared_first, preferred_element_type=jnp.float32)
        + jnp.einsum("te,de->td", d_logits, router_full, preferred_element_type=jnp.float32)
        + jnp.sum(from_experts, axis=1)
    )
    mlp_sums = spread(shared_first_grad, shared_second_grad, router_grad)
    d_scale_two = d_second * normed_two
    d_residual = upstream + norm_back(d_second * (1.0 + scale_two), normed_two, inv_two)
    ada_full, qkv_full, out_full = collect(ada_weight, qkv_weight, out_weight)
    d_projected = (gate_one * d_residual).astype(jnp.bfloat16)
    d_gate_one = d_residual * projected
    out_grad = jnp.einsum("td,te->de", attended, d_projected, preferred_element_type=jnp.float32)
    d_attended = jnp.einsum(
        "te,de->td", d_projected, out_full, preferred_element_type=jnp.float32
    ).astype(jnp.bfloat16)
    d_queries, d_keys, d_values = attend_back(
        queries, keys_all, values_all, segment, log_totals, d_attended.reshape(-1, HEADS, head_size)
    )
    d_qkv = jnp.concatenate(
        [
            d_queries.reshape(-1, model_width),
            d_keys.reshape(-1, model_width),
            d_values.reshape(-1, model_width),
        ],
        axis=1,
    ).astype(jnp.bfloat16)
    qkv_grad = jnp.einsum("td,te->de", first_input, d_qkv, preferred_element_type=jnp.float32)
    d_first = jnp.einsum("te,de->td", d_qkv, qkv_full, preferred_element_type=jnp.float32)
    d_scale_one = d_first * normed_one
    tokens_grad = d_residual + norm_back(d_first * (1.0 + scale_one), normed_one, inv_one)
    d_per_row = jnp.concatenate(
        [d_first, d_scale_one, d_gate_one, d_second, d_scale_two, d_gate_two], axis=1
    )
    d_modulation = jnp.einsum(
        "tj,te->je", inside, d_per_row, precision=EXACT, preferred_element_type=jnp.float32
    ).astype(jnp.bfloat16)
    ada_grad = jnp.einsum("jd,je->de", activated, d_modulation, preferred_element_type=jnp.float32)
    d_activated = jnp.einsum(
        "je,de->jd", d_modulation, ada_full, preferred_element_type=jnp.float32
    )
    condition_grad = jax.vjp(jax.nn.silu, cond_float)[1](d_activated)[0]
    attn_sums = spread(ada_grad, qkv_grad, out_grad)
    return (
        output,
        tokens_grad,
        condition_grad,
        attn_sums[0],
        attn_sums[1],
        attn_sums[2],
        mlp_sums[0],
        mlp_sums[1],
        mlp_sums[2],
        expert_sums[0],
        expert_sums[1],
        expert_counts,
    )


def at(d, s, c):
    return (d, 2 * s + c)


def slot(kind, f, d):
    if kind == "cols":
        return (pl.ds(pl.multiple_of(96 * f, 96), 96), pl.ds(pl.multiple_of(768 * d, 768), 768))
    return (pl.ds(pl.multiple_of(192 * d, 192), 192), pl.ds(pl.multiple_of(384 * f, 384), 384))


def half_slot(kind, f, d, h):
    if kind == "cols":
        return (
            pl.ds(pl.multiple_of(96 * f, 96), 96),
            pl.ds(pl.multiple_of(768 * d + 384 * h, 384), 384),
        )
    return (
        pl.ds(pl.multiple_of(192 * d + 96 * h, 96), 96),
        pl.ds(pl.multiple_of(384 * f, 384), 384),
    )


def place():
    d = lax.axis_index("dp")
    f = lax.axis_index("fsdp")
    return d, f // 2, lax.rem(f, 2)


def flip(v, bit):
    return v + bit - 2 * bit * lax.rem(v // bit, 2)


def greet(devices):
    barrier = pltpu.get_barrier_semaphore()
    for device in devices:
        pl.semaphore_signal(barrier, inc=1, device_id=device, device_id_type=MESH)
    pl.semaphore_wait(barrier, len(devices))


def push(src, dst, send_sem, recv_sem, device):
    return pltpu.make_async_remote_copy(
        src_ref=src,
        dst_ref=dst,
        send_sem=send_sem,
        recv_sem=recv_sem,
        device_id=device,
        device_id_type=MESH,
    )


GATHER_SEMS = 3 + 8 + 8 + 20


class Gather:
    def __init__(self, kind, shard, full, ssem, rsem, lsem):
        self.kind, self.shard, self.full = kind, shard, full
        self.ssem, self.rsem, self.lsem = ssem, rsem, lsem
        self.d, self.s, self.c = place()
        self.sent = []

    def f(self, s):
        return 2 * s + self.c

    def go(self, index, where, device, src=None):
        ref = self.full.at[where]
        copy = push(
            ref if src is None else src, ref, self.ssem.at[index], self.rsem.at[index], device
        )
        copy.start()
        self.sent.append(copy)

    def arrived(self, index, where):
        ref = self.full.at[where]
        push(ref, ref, self.ssem.at[index], self.rsem.at[index], at(self.d, self.s, self.c)).wait_recv()

    def start(self):
        d, s, c = self.d, self.s, self.c
        mine = slot(self.kind, self.f(s), d)
        self.own = pltpu.make_async_copy(self.shard, self.full.at[mine], self.lsem)
        self.own.start()
        self.go(1, mine, at(flip(d, 2), s, c), self.shard)
        self.go(0, mine, at(flip(d, 1), s, c), self.shard)
        self.go(3, mine, at(d, flip(s, 1), c), self.shard)
        self.go(4, mine, at(d, flip(s, 2), c), self.shard)
        self.go(19, mine, at(d, s, 1 - c), self.shard)

    def source(self, k):
        return (self.d, flip(self.d, 1), flip(self.d, 2), flip(flip(self.d, 1), 2))[k]

    def spread_z(self, k):
        d, s, c = self.d, self.s, self.c
        block = slot(self.kind, self.f(s), self.source(k))
        self.arrived(k - 1, block)
        if k == 2:
            self.go(2, block, at(flip(d, 1), s, c))
        self.go(3 + 2 * k, block, at(d, flip(s, 1), c))
        self.go(4 + 2 * k, block, at(d, flip(s, 2), c))
        self.go(19 + 5 * k, block, at(d, s, 1 - c))

    def relay(self, k):
        d, s, c = self.d, self.s, self.c
        source = self.source(k)
        sx, sy = flip(s, 1), flip(s, 2)
        from_x = slot(self.kind, self.f(sx), source)
        from_y = slot(self.kind, self.f(sy), source)
        self.arrived(3 + 2 * k, from_x)
        self.go(11 + 2 * k, half_slot(self.kind, self.f(sx), source, 0), at(d, sy, c))
        self.go(20 + 5 * k, from_x, at(d, s, 1 - c))
        self.arrived(4 + 2 * k, from_y)
        self.go(12 + 2 * k, half_slot(self.kind, self.f(sy), source, 1), at(d, sx, c))
        self.go(21 + 5 * k, from_y, at(d, s, 1 - c))

    def corner(self, k):
        d, s, c = self.d, self.s, self.c
        source = self.source(k)
        sd = flip(flip(s, 1), 2)
        for h in range(2):
            where = half_slot(self.kind, self.f(sd), source, h)
            self.arrived(11 + 2 * k + h, where)
            self.go(22 + 5 * k + h, where, at(d, s, 1 - c))

    def finish(self):
        d, s, c = self.d, self.s, self.c
        sx, sy = flip(s, 1), flip(s, 2)
        sd = flip(sx, 2)
        self.own.wait()
        for k in range(4):
            source = self.source(k)
            for j, position in enumerate((s, sx, sy)):
                self.arrived(19 + 5 * k + j, slot(self.kind, 2 * position + 1 - c, source))
            for h in range(2):
                self.arrived(22 + 5 * k + h, half_slot(self.kind, 2 * sd + 1 - c, source, h))
        for copy in self.sent:
            copy.wait_send()


class Line:
    def __init__(self, kind, shard, line, ssem, rsem, lsem):
        self.kind, self.shard, self.line = kind, shard, line
        self.ssem, self.rsem, self.lsem = ssem, rsem, lsem
        self.d, self.s, self.c = place()

    def block(self, d):
        if self.kind == "cols":
            return self.line.at[:, pl.ds(pl.multiple_of(768 * d, 768), 768)]
        return self.line.at[pl.ds(pl.multiple_of(192 * d, 192), 192)]

    def copy(self, index, src, source, target):
        return push(
            src, self.block(source), self.ssem.at[index], self.rsem.at[index], at(target, self.s, self.c)
        )

    def start(self):
        d = self.d
        self.own = pltpu.make_async_copy(self.shard, self.block(d), self.lsem)
        self.own.start()
        self.sent = [
            self.copy(0, self.shard, d, flip(d, 2)),
            self.copy(1, self.shard, d, flip(d, 1)),
        ]
        for copy in self.sent:
            copy.start()

    def relay(self):
        d2 = flip(self.d, 2)
        self.copy(0, self.shard, d2, d2).wait_recv()
        copy = self.copy(2, self.block(d2), d2, flip(self.d, 1))
        copy.start()
        self.sent.append(copy)

    def finish(self):
        d1 = flip(self.d, 1)
        self.own.wait()
        self.copy(1, self.shard, d1, d1).wait_recv()
        self.copy(2, self.shard, flip(d1, 2), d1).wait_recv()
        for copy in self.sent:
            copy.wait_send()


class Spread:
    def __init__(self, kind, line, full, ssem, rsem, lsem):
        self.kind, self.line, self.full = kind, line, full
        self.ssem, self.rsem, self.lsem = ssem, rsem, lsem
        self.d, self.s, self.c = place()
        self.sx, self.sy = flip(self.s, 1), flip(self.s, 2)
        self.sd = flip(self.sx, 2)
        self.mate = at(self.d, self.s, 1 - self.c)
        self.to_x, self.to_y = at(self.d, self.sx, self.c), at(self.d, self.sy, self.c)
        self.sent = []

    def block(self, position, c, h=None):
        f = 2 * position + c
        if self.kind == "cols":
            rows = pl.ds(pl.multiple_of(96 * f, 96), 96)
            return self.full.at[rows] if h is None else self.full.at[rows, pl.ds(1536 * h, 1536)]
        columns = pl.ds(pl.multiple_of(384 * f, 384), 384)
        rows = pl.ds(0, 768) if h is None else pl.ds(384 * h, 384)
        return self.full.at[rows, columns]

    def go(self, index, ref, device, src=None):
        copy = push(
            ref if src is None else src, ref, self.ssem.at[index], self.rsem.at[index], device
        )
        copy.start()
        self.sent.append(copy)

    def arrived(self, index, ref):
        push(ref, ref, self.ssem.at[index], self.rsem.at[index], self.mate).wait_recv()

    def start(self):
        mine = self.block(self.s, self.c)
        self.own = pltpu.make_async_copy(self.line, mine, self.lsem)
        self.own.start()
        self.go(0, mine, self.to_x, self.line)
        self.go(1, mine, self.to_y, self.line)
        self.go(2, mine, self.mate, self.line)

    def relay(self):
        c = self.c
        from_x, from_y = self.block(self.sx, c), self.block(self.sy, c)
        self.arrived(0, from_x)
        self.go(3, self.block(self.sx, c, 0), self.to_y)
        self.go(5, from_x, self.mate)
        self.arrived(1, from_y)
        self.go(4, self.block(self.sy, c, 1), self.to_x)
        self.go(6, from_y, self.mate)

    def corner(self):
        for h in range(2):
            ref = self.block(self.sd, self.c, h)
            self.arrived(3 + h, ref)
            self.go(7 + h, ref, self.mate)

    def finish(self):
        c = 1 - self.c
        self.own.wait()
        self.arrived(2, self.block(self.s, c))
        self.arrived(5, self.block(self.sx, c))
        self.arrived(6, self.block(self.sy, c))
        for h in range(2):
            self.arrived(7 + h, self.block(self.sd, c, h))
        for copy in self.sent:
            copy.wait_send()


class Near:
    def __init__(self, up_shard, down_shard, up_mate, up_x, up_y, down_own, down_mate, ssem, rsem, lsem):
        d, s, c = place()
        self.local = pltpu.make_async_copy(down_shard.at[c], down_own, lsem)
        plan = (
            (up_shard, c, up_x, flip(s, 1)),
            (up_shard, c, up_y, flip(s, 2)),
            (up_shard, 1 - c, up_mate, s),
            (down_shard, 1 - c, down_mate, s),
        )
        self.away = [
            push(shard.at[which], out, ssem.at[i], rsem.at[i], at(d, position, which))
            for i, (shard, which, out, position) in enumerate(plan)
        ]

    def start(self):
        for copy in self.away + [self.local]:
            copy.start()

    def finish(self):
        for copy in self.away + [self.local]:
            copy.wait()


class Pair:
    def __init__(self, over_x, into_x, over_y, into_y, ssem, rsem):
        d, s, c = place()
        self.copies = [
            push(over_x, into_x, ssem.at[0], rsem.at[0], at(d, flip(s, 1), c)),
            push(over_y, into_y, ssem.at[1], rsem.at[1], at(d, flip(s, 2), c)),
        ]

    def start(self):
        for copy in self.copies:
            copy.start()

    def finish(self):
        for copy in self.copies:
            copy.wait()


def everyone_else():
    me = lax.axis_index("dp") * 8 + lax.axis_index("fsdp")

    def other(k):
        device = lax.rem(me + k, 32)
        return (device // 8, lax.rem(device, 8))

    return me, other


def open_kernel(
    qkv_shard, out_shard, act_ref, ada_ref, up_shard, down_shard, expert_up, expert_down,
    full, router_t, seen, rows_out, up_line, down_line, up_mate, up_x, up_y, down_own, down_mate,
    shard, heard, part, got, mixed, ssem, rsem, lsem, asem, brsem, tssem, trsem, zssem, zrsem,
    us, ur, ds, dr, es, er, el,
):
    me, other = everyone_else()
    d, s, c = place()
    f = 2 * s + c
    shard[:, 0:576] = qkv_shard[...]
    shard[:, 576:768] = out_shard[...]
    barrier = pltpu.get_barrier_semaphore()

    def hello(k, carry):
        pl.semaphore_signal(barrier, inc=1, device_id=other(k), device_id_type=MESH)
        return carry

    lax.fori_loop(1, 32, hello, 0)
    pl.semaphore_wait(barrier, 31)

    def act_copy(k, source):
        device = other(k)
        return push(act_ref.at[device[1]], heard.at[source], asem.at[k], brsem.at[k], device)

    def send(k, carry):
        act_copy(k, me).start()
        return carry

    lax.fori_loop(1, 32, send, 0)
    gather = Gather("cols", shard, full, ssem, rsem, lsem.at[0])
    gather.start()
    near = Near(
        expert_up, expert_down, up_mate, up_x, up_y, down_own, down_mate, es, er, el.at[0]
    )
    lines = (
        Line("cols", up_shard, up_line, us, ur, lsem.at[3]),
        Line("rows", down_shard, down_line, ds, dr, lsem.at[4]),
    )
    gather.spread_z(1)
    gather.spread_z(2)
    for line in lines:
        line.start()
    heard[me] = act_ref[f]

    def take(k, carry):
        copy = act_copy(k, lax.rem(me + 32 - k, 32))
        copy.wait_recv()
        return carry

    lax.fori_loop(1, 32, take, 0)
    everything = heard[...].reshape(256, 128)
    row = lax.broadcasted_iota(jnp.int32, (64, 256), 0)
    column = lax.broadcasted_iota(jnp.int32, (64, 256), 1)
    source = lax.rem(row // 2, 4) * 8 + row // 8
    pick = (column == source * 8 + lax.rem(row, 2)).astype(jnp.bfloat16)
    compact = jnp.dot(
        pick, everything.astype(jnp.bfloat16), preferred_element_type=jnp.float32
    ).astype(jnp.bfloat16)
    seen[...] = jnp.concatenate(
        [compact.astype(jnp.float32), jnp.sum(heard[...], axis=0)], axis=0
    )
    for column_block in range(8):
        tiles = [heard[8 * j + column_block, 3:5, 0:96] for j in range(4)]
        router_t[:, 96 * column_block : 96 * column_block + 96] = jnp.concatenate(tiles, axis=0)
    part[...] = nn(compact[:, 0:96], ada_ref[...]).reshape(8, 8, 1152)

    def tile_copy(k):
        target = lax.rem(f + k, 8)
        return push(part.at[target], got.at[k], tssem.at[k], trsem.at[k], (d, target))

    for k in range(1, 8):
        tile_copy(k).start()
    gather.relay(0)
    gather.spread_z(3)
    near.start()
    gather.relay(1)
    gather.relay(2)
    for k in range(1, 8):
        tile_copy(k).wait_recv()
    total = part[f]
    for k in range(1, 8):
        total = total + got[k]
    mixed[...] = total
    zs = []
    for k in range(1, 4):
        copy = push(mixed, rows_out.at[d], zssem.at[k], zrsem.at[k], at(lax.rem(d + k, 4), s, c))
        copy.start()
        zs.append(copy)
    own_rows = pltpu.make_async_copy(mixed, rows_out.at[d], lsem.at[2])
    own_rows.start()
    for line in lines:
        line.relay()
    gather.relay(3)
    gather.corner(0)
    gather.corner(1)
    gather.corner(2)
    gather.corner(3)
    gather.finish()
    for line in lines:
        line.finish()
    near.finish()
    own_rows.wait()
    for k in range(1, 4):
        push(
            mixed, rows_out.at[lax.rem(d + 4 - k, 4)], zssem.at[k], zrsem.at[k],
            at(lax.rem(d + k, 4), s, c),
        ).wait_recv()
    for copy in zs:
        copy.wait_send()
    for k in range(1, 8):
        tile_copy(k).wait_send()

    def drain(k, carry):
        act_copy(k, me).wait_send()
        return carry

    lax.fori_loop(1, 32, drain, 0)


DMA = pltpu.SemaphoreType.DMA
ANYWHERE = pl.BlockSpec(memory_space=pl.ANY)
ONCHIP = pl.BlockSpec(memory_space=pltpu.VMEM)
SCALARS = pl.BlockSpec(memory_space=pltpu.SMEM)


def opening(*operands):
    return pl.pallas_call(
        open_kernel,
        out_shape=(
            jax.ShapeDtypeStruct((768, 3072), jnp.bfloat16),
            jax.ShapeDtypeStruct((8, 768), jnp.float32),
            jax.ShapeDtypeStruct((72, 128), jnp.float32),
            jax.ShapeDtypeStruct((4, 8, 1152), jnp.float32),
            jax.ShapeDtypeStruct((96, 3072), jnp.bfloat16),
            jax.ShapeDtypeStruct((768, 384), jnp.bfloat16),
        )
        + (jax.ShapeDtypeStruct((96, 3072), jnp.bfloat16),) * 3
        + (jax.ShapeDtypeStruct((384, 768), jnp.bfloat16),) * 2,
        in_specs=[ONCHIP] * 6 + [ANYWHERE] * 2,
        out_specs=(ANYWHERE, ONCHIP, ONCHIP) + (ANYWHERE,) * 8,
        scratch_shapes=[
            pltpu.VMEM((96, 768), jnp.bfloat16),
            pltpu.VMEM((32, 8, 128), jnp.float32),
            pltpu.VMEM((8, 8, 1152), jnp.float32),
            pltpu.VMEM((8, 8, 1152), jnp.float32),
            pltpu.VMEM((8, 1152), jnp.float32),
            DMA((GATHER_SEMS,)), DMA((GATHER_SEMS,)), DMA((5,)),
            DMA((32,)), DMA((32,)),
            DMA((8,)), DMA((8,)), DMA((4,)), DMA((4,)),
            DMA((3,)), DMA((3,)), DMA((3,)), DMA((3,)),
            DMA((4,)), DMA((4,)), DMA((1,)),
        ],
        compiler_params=pltpu.CompilerParams(collective_id=0, has_side_effects=True),
        name="opening",
    )(*operands)


def group_of(d, s, c):
    return [(j, at(lax.rem(d + j // 2, 4), s, lax.rem(c + j, 2))) for j in range(1, 8)]


class Swap:
    def __init__(self, blocks, out, ssem, rsem, lsem):
        self.blocks, self.out, self.ssem, self.rsem, self.lsem = blocks, out, ssem, rsem, lsem
        self.d, self.s, self.c = place()
        self.me = 2 * self.d + self.c

    def copy(self, j, landing):
        target_d = lax.rem(self.d + j // 2, 4)
        target_c = lax.rem(self.c + j, 2)
        return push(
            self.blocks.at[2 * target_d + target_c],
            self.out.at[landing],
            self.ssem.at[j],
            self.rsem.at[j],
            at(target_d, self.s, target_c),
        )

    def start(self):
        for j in (4, 5, 2, 3, 6, 7, 1):
            self.copy(j, self.me).start()
        self.own = pltpu.make_async_copy(
            self.blocks.at[self.me], self.out.at[self.me], self.lsem
        )
        self.own.start()

    def send(self, step, half=None):
        for j in (2 * step, 2 * step + 1) if half is None else (2 * step + half,):
            if j:
                self.copy(j, self.me).start()
            else:
                self.own = pltpu.make_async_copy(
                    self.blocks.at[self.me], self.out.at[self.me], self.lsem
                )
                self.own.start()

    def finish(self):
        self.own.wait()
        for j in range(1, 8):
            source_d = lax.rem(self.d + 4 - j // 2, 4)
            source_c = lax.rem(self.c + j, 2)
            copy = self.copy(j, 2 * source_d + source_c)
            copy.wait_recv()
            copy.wait_send()


def nt(left, right):
    return lax.dot_general(left, right, (((1,), (1,)), ((), ())), preferred_element_type=jnp.float32)


def tn(left, right):
    return lax.dot_general(left, right, (((0,), (0,)), ((), ())), preferred_element_type=jnp.float32)


def nn(left, right):
    return jnp.dot(left, right, preferred_element_type=jnp.float32)


GELU_SCALE = 0.7978845608028654


def gelu_pair(v):
    square = v * v
    bend = jnp.tanh(GELU_SCALE * (v + 0.044715 * (square * v)))
    half = 0.5 * (1.0 + bend)
    slope = half + 0.5 * v * (1.0 - bend * bend) * (
        GELU_SCALE * (1.0 + (3.0 * 0.044715) * square)
    )
    return v * half, slope


HIDDEN = 512


def out_kernel(
    rows, grads, up_line, down_line, tokens, d_tokens, up_x, up_y, down_mate, down_x,
    rows_in, grads_in, up_corner, down_x_mate, down_y_mate, down_corner, mixed_out, d_tokens_out, up_grad, down_grad,
    up_full, down_full, tokens_t, d_tokens_t, s1, r1, s2, r2, ssem, rsem, ssem2, rsem2, lsem,
    es, er, fs, fr, gs, gr,
):
    d, s, c = place()
    greet([device for _, device in group_of(d, s, c)] + [at(d, flip(s, 1), c), at(d, flip(s, 2), c)])
    both = (
        Spread("cols", up_line, up_full, ssem, rsem, lsem.at[0]),
        Spread("rows", down_line, down_full, ssem2, rsem2, lsem.at[1]),
    )
    swap_a = Swap(rows, rows_in, s1, r1, lsem.at[2])
    swap_b = Swap(grads, grads_in, s2, r2, lsem.at[3])
    for g in both:
        g.start()
    swap_a.start()
    swap_b.start()
    mates = Pair(down_mate, down_x_mate, down_mate, down_y_mate, gs, gr)
    up_corners = Pair(up_y, up_corner.at[1], up_x, up_corner.at[0], es, er)
    down_corners = Pair(down_y_mate, down_corner.at[1], down_x, down_corner.at[0], fs, fr)
    tokens_t[...] = tokens[...].T
    d_tokens_t[...] = d_tokens[...].T
    mixed_out[...] = jnp.zeros_like(mixed_out)
    d_tokens_out[...] = jnp.zeros_like(d_tokens_out)
    for g in both:
        g.relay()
    mates.start()
    up_corners.start()
    for g in both:
        g.corner()
    for g in both:
        g.finish()

    def block(b, carry):
        where = pl.ds(pl.multiple_of(b * HIDDEN, HIDDEN), HIDDEN)
        up, down = up_full[:, where], down_full[:, where]
        act, slope = gelu_pair(nn(tokens[...], up))
        act = act.astype(jnp.bfloat16)
        mixed_out[...] += nt(act, down)
        down_grad[:, where] = nn(d_tokens_t[...], act).astype(jnp.bfloat16)
        d_pre = (slope * nn(d_tokens[...], down)).astype(jnp.bfloat16)
        d_tokens_out[...] += nt(d_pre, up)
        up_grad[:, where] = nn(tokens_t[...], d_pre).astype(jnp.bfloat16)
        return carry

    lax.fori_loop(0, 1, block, 0)
    mates.finish()
    down_corners.start()
    lax.fori_loop(1, 3072 // HIDDEN, block, 0)
    swap_a.finish()
    swap_b.finish()
    up_corners.finish()
    down_corners.finish()


def outbound(*operands):
    bf, f32 = jnp.bfloat16, jnp.float32
    return pl.pallas_call(
        out_kernel,
        out_shape=(
            jax.ShapeDtypeStruct((8, 144, 768), bf),
            jax.ShapeDtypeStruct((8, 144, 768), bf),
            jax.ShapeDtypeStruct((2, 96, 3072), bf),
            jax.ShapeDtypeStruct((384, 768), bf),
            jax.ShapeDtypeStruct((384, 768), bf),
            jax.ShapeDtypeStruct((2, 384, 768), bf),
            jax.ShapeDtypeStruct((512, 768), f32),
            jax.ShapeDtypeStruct((512, 768), f32),
            jax.ShapeDtypeStruct((768, 3072), bf),
            jax.ShapeDtypeStruct((768, 3072), bf),
        ),
        in_specs=[ONCHIP] * 6 + [ANYWHERE] * 4,
        out_specs=(ANYWHERE,) * 6 + (ONCHIP,) * 4,
        scratch_shapes=[pltpu.VMEM((768, 3072), bf)] * 2
        + [pltpu.VMEM((768, 512), bf)] * 2
        + [DMA((8,))] * 4
        + [DMA((9,))] * 4
        + [DMA((4,))]
        + [DMA((2,))] * 6,
        compiler_params=pltpu.CompilerParams(
            collective_id=1, has_side_effects=True, vmem_limit_bytes=60 << 20
        ),
        name="outbound",
    )(*operands)


def widened(ref):
    return ref[...].astype(jnp.float32)


class Parts:
    def __init__(self, grad, keep, over_x, over_y, sem, rsem=None):
        d, s, c = place()
        sx, sy = flip(s, 1), flip(s, 2)
        sd = flip(sx, 2)
        rows = grad.shape[0] // 8
        slots = (
            (s, 0, keep.at[0, 0], s), (sy, 0, keep.at[0, 1], s),
            (s, 1, keep.at[1, 0], s), (sx, 1, keep.at[1, 1], s),
            (sx, 0, over_x.at[0], sx), (sd, 0, over_x.at[1], sx),
            (sy, 1, over_y.at[0], sy), (sd, 1, over_y.at[1], sy),
        )
        self.copies, self.away = [], []
        for i, (position, h, out, target) in enumerate(slots):
            part = grad.at[pl.ds(pl.multiple_of((2 * position + h) * rows, 32), rows)]
            if i < 4 or rsem is None:
                self.copies.append(pltpu.make_async_copy(part, out, sem.at[i]))
            else:
                self.away.append(push(part, out, sem.at[i], rsem.at[i], at(d, target, c)))

    def start(self):
        for copy in self.away + self.copies:
            copy.start()

    def finish(self):
        for copy in self.copies + self.away:
            copy.wait()


class Pieces:
    def __init__(self, parts, full, sem):
        d, s, c = place()
        rows = full.shape[0] // 8
        sx, sy = flip(s, 1), flip(s, 2)
        positions = [p for p in (s, sx, sy, flip(sx, 2)) for _ in range(2)]
        self.copies = [
            pltpu.make_async_copy(
                part,
                full.at[pl.ds(pl.multiple_of(rows * (2 * p + (c if i % 2 == 0 else 1 - c)), 32), rows)],
                sem.at[i],
            )
            for i, (p, part) in enumerate(zip(positions, parts))
        ]

    def start(self):
        for copy in self.copies:
            copy.start()

    def finish(self):
        for copy in self.copies:
            copy.wait()


def expert_kernel(
    rows, grads, expert_up, up_m, up_x0, up_x1, up_y0, up_y1, up_corner,
    down_own, down_m, down_x0, down_x1, down_y0, down_y1, down_corner, first_grad, second_grad,
    rows_back, grads_back, up_keep, up_x, up_y, down_keep, down_x, down_y, first_part, second_part,
    up, down, act, d_pre, made, d_made, total, d_total, up_grad, down_grad, rows_t,
    fo, fm, fn, ff, fs, fr, fl, so, sm, sn, sf, ss, sr, sl,
    s1, r1, s2, r2, lsem, wsem, vsem, psem, arsem, qsem,
):
    bf = jnp.bfloat16
    d, s, c = place()
    weights = (
        Pieces(
            (expert_up.at[c], up_m, up_x0, up_x1, up_y0, up_y1, up_corner.at[0], up_corner.at[1]), up, wsem
        ),
        Pieces(
            (down_own, down_m, down_x0, down_x1, down_y0, down_y1, down_corner.at[0], down_corner.at[1]),
            down, vsem,
        ),
    )
    for each in weights:
        each.start()
    greet([device for _, device in group_of(d, s, c)] + [at(d, flip(s, 1), c), at(d, flip(s, 2), c)])
    sums = (
        DenseSum("cols", first_grad, first_part, fo, fm, fn, ff, None, fs, fr, fl),
        DenseSum("rows", second_grad, second_part, so, sm, sn, sf, None, ss, sr, sl),
    )
    for each in sums:
        each.start()
    swap_a = Swap(made, rows_back, s1, r1, lsem.at[0])
    swap_b = Swap(d_made, grads_back, s2, r2, lsem.at[1])
    for each in weights:
        each.finish()
    for step, half in ((2, 0), (2, 1), (1, None), (3, None), (0, None)):
        there = lax.rem(d + step, 4)
        count = 2 if half is None else 1
        size = 144 * count
        start = 2 * there if half is None else 2 * there + lax.rem(c + half, 2)
        chunk = pl.ds(start, count)
        lines = pl.ds(pl.multiple_of(144 * start, 144), size)
        kept = pl.ds(0, size)
        x = rows[chunk].reshape(size, 768)
        g = grads[chunk].reshape(size, 768)
        total[kept] = jnp.zeros((size, 768), jnp.float32)
        d_total[kept] = jnp.zeros((size, 768), jnp.float32)

        def block(b, carry):
            where = pl.ds(pl.multiple_of(b * HIDDEN, HIDDEN), HIDDEN)
            up_part, down_part = up[:, where], down[where]
            made_act, slope = gelu_pair(nn(x, up_part))
            made_act = made_act.astype(bf)
            act[lines, where] = made_act
            total[kept] += nn(made_act, down_part)
            d_part = (slope * nt(g, down_part)).astype(bf)
            d_pre[lines, where] = d_part
            d_total[kept] += nt(d_part, up_part)
            return carry

        lax.fori_loop(0, 3072 // HIDDEN, block, 0)
        made[chunk] = total[kept].astype(bf).reshape(count, 144, 768)
        d_made[chunk] = d_total[kept].astype(bf).reshape(count, 144, 768)
        swap_a.send(step, half)
        swap_b.send(step, half)
        if half == 1:
            for each in sums:
                each.merge()
        if step == 3:
            for each in sums:
                each.join()
    rows_t[...] = rows.reshape(1152, 768)[...].T
    g_all = grads.reshape(1152, 768)

    def up_block(b, carry):
        where = pl.ds(pl.multiple_of(b * HIDDEN, HIDDEN), HIDDEN)
        up_grad[:, where] = nn(rows_t[...], d_pre[:, where]).astype(bf)
        return carry

    def down_block(b, carry):
        where = pl.ds(pl.multiple_of(384 * b, 384), 384)
        down_grad[where] = tn(act[:, where], g_all[...]).astype(bf)
        return carry

    up_parts = Parts(up_grad, up_keep, up_x, up_y, psem, arsem)
    down_parts = Parts(down_grad, down_keep, down_x, down_y, qsem)
    lax.fori_loop(0, 3072 // HIDDEN, up_block, 0)
    up_parts.start()
    lax.fori_loop(0, 8, down_block, 0)
    down_parts.start()
    for each in sums:
        each.close()
    swap_a.finish()
    swap_b.finish()
    up_parts.finish()
    down_parts.finish()


def experts(rows, grads, up_pieces, down_pieces, first_grad, second_grad):
    bf, f32 = jnp.bfloat16, jnp.float32

    def rooms(piece, half):
        return [
            pltpu.VMEM((4,) + piece, bf),
            pltpu.VMEM((4,) + piece, bf),
            pltpu.VMEM((2,) + half, bf),
            pltpu.VMEM((2,) + piece, bf),
            DMA((8,)),
            DMA((8,)),
            DMA((4,)),
        ]

    def parts(r, n):
        return (
            jax.ShapeDtypeStruct((2, 2, r, n), bf),
            jax.ShapeDtypeStruct((2, r, n), bf),
            jax.ShapeDtypeStruct((2, r, n), bf),
        )

    return pl.pallas_call(
        expert_kernel,
        out_shape=(
            jax.ShapeDtypeStruct((8, 144, 768), bf),
            jax.ShapeDtypeStruct((8, 144, 768), bf),
        )
        + parts(96, 3072)
        + parts(384, 768)
        + (
            jax.ShapeDtypeStruct((96, 3072), bf),
            jax.ShapeDtypeStruct((768, 384), bf),
        ),
        in_specs=[ONCHIP, ONCHIP] + [ANYWHERE] * 16,
        out_specs=(ANYWHERE,) * 8 + (ONCHIP, ONCHIP),
        scratch_shapes=[
            pltpu.VMEM((768, 3072), bf),
            pltpu.VMEM((3072, 768), bf),
            pltpu.VMEM((1152, 3072), bf),
            pltpu.VMEM((1152, 3072), bf),
            pltpu.VMEM((8, 144, 768), bf),
            pltpu.VMEM((8, 144, 768), bf),
            pltpu.VMEM((288, 768), f32),
            pltpu.VMEM((288, 768), f32),
            pltpu.VMEM((768, 3072), bf),
            pltpu.VMEM((3072, 768), bf),
            pltpu.VMEM((768, 1152), bf),
        ]
        + rooms((96, 3072), (96, 1536))
        + rooms((768, 384), (384, 384))
        + [DMA((8,))] * 4
        + [DMA((2,)), DMA((8,)), DMA((8,)), DMA((8,)), DMA((8,)), DMA((8,))],
        compiler_params=pltpu.CompilerParams(
            collective_id=2, has_side_effects=True, vmem_limit_bytes=67043328
        ),
        name="experts",
    )(rows, grads, *up_pieces, *down_pieces, first_grad, second_grad)


def hop(values, bit):
    return lax.ppermute(values, "fsdp", [(f, f ^ bit) for f in range(8)])


def square_next(keep, from_x, from_y):
    f32, bf = jnp.float32, jnp.bfloat16
    return (
        hop((keep[0, 1].astype(f32) + from_x[1].astype(f32)).astype(bf), 4),
        hop((keep[1, 1].astype(f32) + from_y[1].astype(f32)).astype(bf), 2),
    )


class DenseSum:
    def __init__(self, kind, grad, out, own, mate, near, far, line, ssem, rsem, lsem, part=None):
        self.kind, self.grad, self.out, self.part = kind, grad, out, part
        self.own, self.mate, self.near, self.far, self.line = own, mate, near, far, line
        self.ssem, self.rsem, self.lsem = ssem, rsem, lsem
        self.d, self.s, self.c = place()
        self.order = (
            flip(flip(self.s, 1), 2),
            flip(self.s, 1),
            flip(self.s, 2),
            self.s,
        )

    def piece(self, f):
        if self.part is not None:
            return self.grad.at[pl.ds(pl.multiple_of(96 * f + 48 * self.part, 48), 48)]
        if self.kind == "cols":
            return self.grad.at[pl.ds(pl.multiple_of(96 * f, 96), 96)]
        return self.grad.at[:, pl.ds(pl.multiple_of(384 * f, 384), 384)]

    def half(self, ref, h):
        if self.kind == "cols":
            return ref.at[:, pl.ds(1536 * h, 1536)]
        return ref.at[pl.ds(384 * h, 384)]

    def quarter(self, ref, q):
        if self.kind == "cols":
            return ref.at[:, pl.ds(pl.multiple_of(768 * q, 768), 768)]
        return ref.at[pl.ds(pl.multiple_of(192 * q, 192), 192)]

    def start(self):
        d, s, c = self.d, self.s, self.c
        self.zero, self.local = [], []
        for j, position in enumerate(self.order):
            copy = push(
                self.piece(2 * position + 1 - c), self.mate.at[j], self.ssem.at[j], self.rsem.at[j], at(d, s, 1 - c)
            )
            copy.start()
            self.zero.append(copy)
            copy = pltpu.make_async_copy(self.piece(2 * position + c), self.own.at[j], self.lsem.at[j])
            copy.start()
            self.local.append(copy)

    def merge(self):
        d, s, c = self.d, self.s, self.c
        sx, sy = flip(s, 1), flip(s, 2)
        self.one = []
        for j in range(4):
            self.zero[j].wait_recv()
            self.local[j].wait()
            self.own[j] = (widened(self.own.at[j]) + widened(self.mate.at[j])).astype(jnp.bfloat16)
            if j == 0:
                for h, target in enumerate((sx, sy)):
                    copy = push(
                        self.half(self.own.at[0], h), self.near.at[h], self.ssem.at[4 + h], self.rsem.at[4 + h],
                        at(d, target, c),
                    )
                    copy.start()
                    self.one.append(copy)

    def join(self):
        d, s, c = self.d, self.s, self.c
        sx, sy = flip(s, 1), flip(s, 2)
        for h, j in ((0, 2), (1, 1)):
            self.one[h].wait_recv()
            where = self.half(self.own.at[j], h)
            where[...] = (widened(where) + widened(self.near.at[h])).astype(jnp.bfloat16)
        self.two = []
        for h, target in enumerate((sx, sy)):
            copy = push(
                self.own.at[1 + h], self.far.at[h], self.ssem.at[6 + h], self.rsem.at[6 + h], at(d, target, c)
            )
            copy.start()
            self.two.append(copy)

    def square(self):
        for copy in self.two:
            copy.wait_recv()
        return (
            widened(self.own.at[3]) + widened(self.far.at[0]) + widened(self.far.at[1])
        ).astype(jnp.bfloat16)

    def along(self):
        d, s, c = self.d, self.s, self.c
        self.own[3] = self.square()
        self.three = []
        for k in range(1, 4):
            target = lax.rem(d + k, 4)
            copy = push(
                self.quarter(self.own.at[3], target), self.line.at[k - 1], self.ssem.at[7 + k], self.rsem.at[7 + k],
                at(target, s, c),
            )
            copy.start()
            self.three.append(copy)

    def finish(self):
        total = widened(self.quarter(self.own.at[3], self.d))
        for k in range(1, 4):
            self.three[k - 1].wait_recv()
            total = total + widened(self.line.at[k - 1])
        self.out[...] = total
        self.sent(self.three)

    def close(self):
        self.out[...] = self.square()
        self.sent([])

    def sent(self, more):
        for copy in self.zero + self.one + self.two + more:
            copy.wait_send()


class LineSum:
    def __init__(self, kind, part, out, landing, ssem, rsem):
        self.kind, self.part, self.out, self.landing = kind, part, out, landing
        self.ssem, self.rsem = ssem, rsem
        self.d, self.s, self.c = place()

    def quarter(self, q):
        if self.kind == "cols":
            return self.part.at[:, pl.ds(pl.multiple_of(768 * q, 768), 768)]
        return self.part.at[pl.ds(pl.multiple_of(192 * q, 192), 192)]

    def start(self):
        self.copies = []
        for k in range(1, 4):
            target = lax.rem(self.d + k, 4)
            copy = push(
                self.quarter(target), self.landing.at[k - 1], self.ssem.at[k - 1], self.rsem.at[k - 1],
                at(target, self.s, self.c),
            )
            copy.start()
            self.copies.append(copy)

    def finish(self):
        total = widened(self.quarter(self.d))
        for k in range(3):
            self.copies[k].wait_recv()
            total = total + widened(self.landing.at[k])
        self.out[...] = total
        for copy in self.copies:
            copy.wait_send()


class Ending:
    def __init__(self, keep, from_x, from_y, out, room, stage, landed, last, lsem, ssem, rsem, loaded=None):
        self.out, self.room, self.stage, self.landed, self.last = out, room, stage, landed, last
        self.ssem, self.rsem = ssem, rsem
        self.d, self.s, self.c = place()
        sources = [
            keep.at[0, 0], keep.at[0, 1], keep.at[1, 0], keep.at[1, 1],
            from_x.at[0], from_x.at[1], from_y.at[0], from_y.at[1],
        ]
        self.loads = [
            pltpu.make_async_copy(source, room.at[i], lsem.at[i]) for i, source in enumerate(sources)
        ]
        for i, source in enumerate(loaded or ()):
            self.loads.append(pltpu.make_async_copy(source, landed.at[i], lsem.at[8 + i]))
        self.sent = []

    def load(self):
        for copy in self.loads:
            copy.start()

    def loaded(self):
        for copy in self.loads:
            copy.wait()

    def go(self, index, target):
        dst = self.last if index == 2 else self.landed.at[index]
        copy = push(self.stage.at[index], dst, self.ssem.at[index], self.rsem.at[index], target)
        copy.start()
        self.sent.append(copy)

    def next(self):
        bf = jnp.bfloat16
        room = self.room
        self.stage[0] = (widened(room.at[1]) + widened(room.at[5])).astype(bf)
        self.go(0, at(self.d, flip(self.s, 2), self.c))
        self.stage[1] = (widened(room.at[3]) + widened(room.at[7])).astype(bf)
        self.go(1, at(self.d, flip(self.s, 1), self.c))

    def close(self):
        for copy in self.sent:
            copy.wait_recv()
        c = self.c
        mine, theirs = c, 1 - c

        def total(h):
            return (
                widened(self.room.at[2 * h]) + widened(self.room.at[4 + 2 * h]) + widened(self.landed.at[h])
            )

        self.stage[2] = total(theirs).astype(jnp.bfloat16)
        self.go(2, at(self.d, self.s, 1 - c))
        self.out[c] = total(mine)

    def finish(self):
        self.sent[-1].wait_recv()
        self.out[1 - self.c] = widened(self.last)
        for copy in self.sent:
            copy.wait_send()


class Tail:
    def __init__(self, d_rows, router, act, ada, ada_out, d_act_out, router_out, z1, plane, plane_in, z2, z2_in, sems):
        self.d_rows, self.router, self.act, self.ada = d_rows, router, act, ada
        self.ada_out, self.d_act_out, self.router_out = ada_out, d_act_out, router_out
        self.z1, self.plane, self.plane_in, self.z2, self.z2_in = z1, plane, plane_in, z2, z2_in
        self.sems = sems
        self.d, self.s, self.c = place()
        self.f = 2 * self.s + self.c

    def z_copy(self, k, src, dst, base):
        send, recv = self.sems[base], self.sems[base + 1]
        return push(src, dst, send.at[k], recv.at[k], at(lax.rem(self.d + k, 4), self.s, self.c))

    def f_copy(self, k, src, dst, base):
        send, recv = self.sems[base], self.sems[base + 1]
        return push(src, dst, send.at[k], recv.at[k], (self.d, lax.rem(self.f + k, 8)))

    def start(self):
        self.all = [
            self.z_copy(k, self.d_rows.at[lax.rem(self.d + k, 4)], self.z1.at[k], 0) for k in range(1, 4)
        ]
        for copy in self.all:
            copy.start()

    def second(self):
        total = self.d_rows[self.d]
        for k in range(1, 4):
            self.all[k - 1].wait_recv()
            total = total + self.z1[k]
        for target in range(8):
            self.plane[target, :, 0:1152] = total
            self.plane[target, :, 1152:1280] = self.router[target]
        copies = [
            self.f_copy(k, self.plane.at[lax.rem(self.f + k, 8)], self.plane_in.at[lax.rem(8 - k, 8)], 2)
            for k in range(1, 8)
        ]
        for copy in copies:
            copy.start()
        self.in_plane = copies
        self.all = self.all + copies

    def third(self):
        f = self.f
        self.plane_in[0] = self.plane[f]
        for copy in self.in_plane:
            copy.wait_recv()
        everything = self.plane_in[...]
        router = jnp.sum(everything[:, :, 1152:1280], axis=0)
        rows = everything[:, :, 0:1152].reshape(64, 1152)
        line = lax.broadcasted_iota(jnp.int32, (64, 64), 0)
        column = lax.broadcasted_iota(jnp.int32, (64, 64), 1)
        turn = (lax.rem(line // 8 + 8 - f, 8) * 8 + lax.rem(line, 8) == column).astype(jnp.bfloat16)
        d_mod = nn(turn, rows.astype(jnp.bfloat16)).astype(jnp.bfloat16)
        self.ada_out[...] = tn(self.act[...], d_mod)[0:96]
        part = nt(d_mod, self.ada[...])
        self.z2[0:64, 0:96] = part
        self.z2[0:64, 96:128] = jnp.zeros((64, 32), jnp.float32)
        self.z2[64:72, :] = router
        copies = [self.z_copy(k, self.z2, self.z2_in.at[k], 4) for k in range(1, 4)]
        for copy in copies:
            copy.start()
        self.along = copies
        self.all = self.all + copies

    def fourth(self):
        total = self.z2[...]
        for k in range(1, 4):
            self.along[k - 1].wait_recv()
            total = total + self.z2_in[k]
        self.router_out[...] = total[64:72]
        self.z2_in[0] = total
        copies = [
            self.f_copy(
                k,
                self.z2_in.at[0, pl.ds(pl.multiple_of(8 * lax.rem(self.f + k, 8), 8), 8)],
                self.d_act_out.at[self.f],
                6,
            )
            for k in range(1, 8)
        ]
        for copy in copies:
            copy.start()
        self.d_act_out[self.f] = self.z2_in[0, pl.ds(pl.multiple_of(8 * self.f, 8), 8)]
        self.last = copies
        self.all = self.all + copies

    def finish(self):
        for k in range(1, 8):
            self.f_copy(
                k, self.z2_in.at[0, pl.ds(0, 8)], self.d_act_out.at[lax.rem(self.f + 8 - k, 8)], 6
            ).wait_recv()
        for copy in self.all:
            copy.wait_send()


def dense_kernel(
    grad, first_part, second_part, d_rows, router, act, ada,
    up_keep, up_x, up_y, up_low, up_high, down_keep, down_x, down_y,
    out, first_out, second_out, ada_out, d_act_out, router_out, up_out, down_out,
    ur, us, ul, ue, ula, usa, ura, dr, ds, dl, de, dla, dsa, dra,
    own, mate, near, far, line, ssem, rsem, lsem,
    own_2, mate_2, near_2, far_2, line_2, ssem_2, rsem_2, lsem_2,
    first_in, fs, fr, second_in, ss, sr, *rest,
):
    d, s, c = place()
    f = 2 * s + c
    greet(
        [at(lax.rem(d + k, 4), s, c) for k in range(1, 4)]
        + [(d, lax.rem(f + k, 8)) for k in range(1, 8)]
    )
    both = (
        DenseSum("cols", grad, out.at[pl.ds(0, 48)], own, mate, near, far, line, ssem, rsem, lsem, 0),
        DenseSum(
            "cols", grad, out.at[pl.ds(48, 48)], own_2, mate_2, near_2, far_2, line_2, ssem_2, rsem_2, lsem_2, 1
        ),
    )
    lines = (
        LineSum("cols", first_part, first_out, first_in, fs, fr),
        LineSum("rows", second_part, second_out, second_in, ss, sr),
    )
    tail = Tail(d_rows, router, act, ada, ada_out, d_act_out, router_out, *rest[:5], rest[5:])
    ups = Ending(up_keep, up_x, up_y, up_out, ur, us, ul, ue, ula, usa, ura, (up_low, up_high))
    downs = Ending(down_keep, down_x, down_y, down_out, dr, ds, dl, de, dla, dsa, dra)
    tail.start()
    for each in both:
        each.start()
    for each in lines:
        each.start()
    downs.load()
    ups.load()
    for each in both:
        each.merge()
    tail.second()
    for each in both:
        each.join()
    downs.loaded()
    downs.next()
    ups.loaded()
    ups.close()
    tail.third()
    for each in both:
        each.along()
    tail.fourth()
    downs.close()
    for each in lines:
        each.finish()
    ups.finish()
    for each in both:
        each.finish()
    downs.finish()
    tail.finish()


def dense_sums(grad, first_part, second_part, small, routed):
    bf, f32 = jnp.bfloat16, jnp.float32

    def rooms(r, n):
        return [
            pltpu.VMEM((8, r, n), bf),
            pltpu.VMEM((3, r, n), bf),
            pltpu.VMEM((2, r, n), bf),
            pltpu.VMEM((r, n), bf),
            DMA((10,)),
            DMA((3,)),
            DMA((3,)),
        ]

    return pl.pallas_call(
        dense_kernel,
        out_shape=(
            jax.ShapeDtypeStruct((96, 768), f32),
            jax.ShapeDtypeStruct((96, 768), f32),
            jax.ShapeDtypeStruct((192, 384), f32),
            jax.ShapeDtypeStruct((96, 1152), f32),
            jax.ShapeDtypeStruct((8, 8, 128), f32),
            jax.ShapeDtypeStruct((8, 128), f32),
            jax.ShapeDtypeStruct((2, 96, 3072), f32),
            jax.ShapeDtypeStruct((2, 384, 768), f32),
        ),
        in_specs=[ANYWHERE] + [ONCHIP] * 6 + [ANYWHERE] * 8,
        out_specs=(ONCHIP,) * 8,
        scratch_shapes=rooms(96, 3072) + rooms(384, 768) + [
            pltpu.VMEM((4, 48, 3072), bf),
            pltpu.VMEM((4, 48, 3072), bf),
            pltpu.VMEM((2, 48, 1536), bf),
            pltpu.VMEM((2, 48, 3072), bf),
            pltpu.VMEM((3, 48, 768), bf),
            DMA((11,)), DMA((11,)), DMA((4,)),
        ] * 2 + [
            pltpu.VMEM((3, 96, 768), bf),
            DMA((3,)), DMA((3,)),
            pltpu.VMEM((3, 192, 384), bf),
            DMA((3,)), DMA((3,)),
            pltpu.VMEM((4, 8, 1152), f32),
            pltpu.VMEM((8, 8, 1280), f32),
            pltpu.VMEM((8, 8, 1280), f32),
            pltpu.VMEM((72, 128), f32),
            pltpu.VMEM((4, 72, 128), f32),
            DMA((4,)), DMA((4,)), DMA((8,)), DMA((8,)), DMA((4,)), DMA((4,)), DMA((8,)), DMA((8,)),
        ],
        compiler_params=pltpu.CompilerParams(
            collective_id=3, has_side_effects=True, vmem_limit_bytes=60 << 20
        ),
        cost_estimate=pl.CostEstimate(flops=40_000_000_000, bytes_accessed=20_000_000, transcendentals=0),
        name="dense_sums",
    )(grad, first_part, second_part, *small, *routed)


def layer_stats(values_in):
    centred = values_in - jnp.mean(values_in, axis=-1, keepdims=True)
    inv_std = lax.rsqrt(jnp.mean(centred * centred, axis=-1, keepdims=True) + 1e-06)
    return centred * inv_std, inv_std


def lines_of(tile, first):
    row = lax.broadcasted_iota(jnp.int32, tile.shape, 0)
    picked = [
        jnp.sum(jnp.where(row == first + i, tile, 0.0), axis=0, keepdims=True) for i in range(2)
    ]
    return jnp.concatenate(picked, axis=0)


def modulated(inside, mod, part):
    columns = slice(768 * part, 768 * part + 768)
    return inside[0] * mod[0:1, columns] + inside[1] * mod[1:2, columns]


def segment_along(sizes, axis):
    slots = lax.broadcasted_iota(jnp.int32, (LONG, 1) if axis == 0 else (1, LONG), axis)
    return (slots >= sizes[0]).astype(jnp.int32) + (slots >= sizes[0] + sizes[1]).astype(jnp.int32)


def head_column(g):
    return 768 * (g // 9) + 64 * (g % 9)


QUERY_ROWS = 512


def front_kernel(
    tokens, mod_rows, sizes, qkvo_in, router_t, cotangent, routes, target,
    heads_out, totals_out, attended_out, projected_out, residual, second, d_mixed, gates, rows, grads, mod,
    bias, made, weighted, qkvo, heads, totals, attended, projected, sem,
):
    bf, f32 = jnp.bfloat16, jnp.float32
    seg_col, seg_row = segment_along(sizes, 0), segment_along(sizes, 1)
    inside = [(seg_col == j).astype(f32) for j in range(2)]
    load = pltpu.make_async_copy(qkvo_in, qkvo, sem.at[0])
    load.start()
    pairs = ((heads, heads_out), (totals, totals_out), (attended, attended_out), (projected, projected_out))
    stores = [pltpu.make_async_copy(src, dst, sem.at[1 + i]) for i, (src, dst) in enumerate(pairs)]
    d = lax.axis_index("dp")
    for j in range(4):
        mod[:, 1152 * j : 1152 * j + 1152] = lines_of(mod_rows[j], 2 * d)
    token_float = tokens[...].astype(f32)
    normed, _ = layer_stats(token_float)
    first = (normed * (1.0 + modulated(inside, mod, 1)) + modulated(inside, mod, 0)).astype(bf)
    load.wait()
    for j in range(4):
        piece = nn(first, qkvo[:, 768 * j : 768 * j + 640]).astype(bf)
        for i in range(9):
            heads[9 * j + i] = piece[:, 64 * i : 64 * i + 64]
    stores[0].start()
    bias[...] = jnp.where(seg_col == seg_row, 0.0, -1e30)

    def block(n, carry):
        h, part = n // (512 // QUERY_ROWS), lax.rem(n, 512 // QUERY_ROWS)
        lines = pl.ds(pl.multiple_of(part * QUERY_ROWS, QUERY_ROWS), QUERY_ROWS)
        scores = nt(heads[h, lines], heads[12 + h]) * 0.125 + bias[lines]
        row_max = jnp.max(scores, axis=-1, keepdims=True)
        weight = jnp.exp(scores - row_max)
        running = jnp.sum(weight, axis=-1, keepdims=True)
        probability = (weight * (1.0 / running)).astype(bf)
        made[h, lines] = nn(probability, heads[24 + h]).astype(bf)
        totals[h, lines] = row_max + jnp.log(running)
        return carry

    lax.fori_loop(0, 12 * (512 // QUERY_ROWS), block, 0)
    stores[1].start()
    for h in range(12):
        attended[:, 64 * h : 64 * h + 64] = made[h]
    stores[2].start()
    for j in range(4):
        piece = nn(attended[...], qkvo[:, 768 * j + 512 : 768 * j + 768])
        projected[:, 192 * j : 192 * j + 192] = piece[:, 64:256]
    stores[3].start()
    residual[...] = token_float + modulated(inside, mod, 2) * projected[...]
    normed, _ = layer_stats(residual[...])
    second[...] = (normed * (1.0 + modulated(inside, mod, 4)) + modulated(inside, mod, 3)).astype(bf)
    logits = nt(second[...], router_t[...].astype(bf))
    ids = lax.broadcasted_iota(jnp.int32, (512, 8), 1)
    chosen = [
        jnp.sum(jnp.where(ids == routes[:, k : k + 1], logits, 0.0), axis=-1, keepdims=True)
        for k in range(2)
    ]
    top = jnp.maximum(chosen[0], chosen[1])
    raised = [jnp.exp(each - top) for each in chosen]
    share = [each / (raised[0] + raised[1]) for each in raised]
    pair = lax.broadcasted_iota(jnp.int32, (512, 2), 1)
    gates[...] = jnp.where(pair == 0, share[0], share[1])
    mixed_grad = modulated(inside, mod, 5) * cotangent[...].astype(f32)
    d_mixed[...] = mixed_grad.astype(bf)
    for k in range(2):
        weighted[k] = (share[k] * mixed_grad).astype(bf)

    def send(b, carry):
        lines = pl.ds(pl.multiple_of(288 * b, 288), 288)
        places = lax.broadcasted_iota(jnp.int32, (288, 512), 0) + 288 * b
        first_hot = (places == target[0:1]).astype(f32)
        second_hot = (places == target[1:2]).astype(f32)
        rows[lines] = nn((first_hot + second_hot).astype(bf), second[...]).astype(bf)
        grads[lines] = (
            nn(first_hot.astype(bf), weighted[0]) + nn(second_hot.astype(bf), weighted[1])
        ).astype(bf)
        return carry

    lax.fori_loop(0, 4, send, 0)
    for copy in stores:
        copy.wait()


def front(*operands):
    bf, f32 = jnp.bfloat16, jnp.float32
    return pl.pallas_call(
        front_kernel,
        out_shape=(
            jax.ShapeDtypeStruct((36, 512, 64), bf),
            jax.ShapeDtypeStruct((12, 512, 1), f32),
            jax.ShapeDtypeStruct((512, 768), bf),
            jax.ShapeDtypeStruct((512, 768), f32),
            jax.ShapeDtypeStruct((512, 768), f32),
            jax.ShapeDtypeStruct((512, 768), bf),
            jax.ShapeDtypeStruct((512, 768), bf),
            jax.ShapeDtypeStruct((512, 2), f32),
            jax.ShapeDtypeStruct((1152, 768), bf),
            jax.ShapeDtypeStruct((1152, 768), bf),
            jax.ShapeDtypeStruct((2, 4608), f32),
        ),
        in_specs=[SCALARS if i == 2 else ANYWHERE if i == 3 else ONCHIP for i in range(8)],
        out_specs=(ANYWHERE,) * 4 + (ONCHIP,) * 7,
        scratch_shapes=[
            pltpu.VMEM((512, 512), f32),
            pltpu.VMEM((12, 512, 64), bf),
            pltpu.VMEM((2, 512, 768), bf),
            pltpu.VMEM((768, 3072), bf),
            pltpu.VMEM((36, 512, 64), bf),
            pltpu.VMEM((12, 512, 1), f32),
            pltpu.VMEM((512, 768), bf),
            pltpu.VMEM((512, 768), f32),
            DMA((5,)),
        ],
        compiler_params=pltpu.CompilerParams(vmem_limit_bytes=67043328),
        cost_estimate=pl.CostEstimate(flops=40_000_000_000, bytes_accessed=20_000_000, transcendentals=0),
        name="front",
    )(*operands)


def norm_grad(upstream, normed, inv_std):
    return (
        upstream
        - jnp.mean(upstream, axis=-1, keepdims=True)
        - normed * jnp.mean(upstream * normed, axis=-1, keepdims=True)
    ) * inv_std


def rear_kernel(
    tokens, mod, sizes, qkvo_in, router_t, cotangent, routes, target,
    heads_in, totals_in, attended_in, projected_in, residual, second, gates,
    returned, d_returned_in, shared_out, d_shared_in,
    output, tokens_grad, qkvo_grad, d_mod, router_grad,
    bias, rows_t, d_heads, d_att, d_att_t, d_rows_t, d_rows, d_residual, d_proj,
    qkvo, heads, totals, attended, projected, d_returned, d_shared, sem,
):
    bf, f32 = jnp.bfloat16, jnp.float32
    pairs = (
        (d_returned_in, d_returned), (d_shared_in, d_shared), (projected_in, projected),
        (heads_in, heads), (qkvo_in, qkvo), (totals_in, totals), (attended_in, attended),
    )
    loads = [pltpu.make_async_copy(src, dst, sem.at[i]) for i, (src, dst) in enumerate(pairs)]
    for copy in loads:
        copy.start()
    upstream = cotangent[...].astype(f32)
    seg_col, seg_row = segment_along(sizes, 0), segment_along(sizes, 1)
    inside = [(seg_col == j).astype(f32) for j in range(2)]

    def image_sums(part, values):
        for j in range(2):
            d_mod[j : j + 1, 768 * part : 768 * part + 768] = jnp.sum(
                inside[j] * values, axis=0, keepdims=True
            )

    share = [gates[:, k : k + 1] for k in range(2)]
    places = lax.broadcasted_iota(jnp.int32, (512, 1152), 1)
    hot = [(places == target[:, k : k + 1]).astype(f32).astype(bf) for k in range(2)]
    picked = [nn(each, returned[...]) for each in hot]
    mixed = shared_out[...] + (share[0] * picked[0] + share[1] * picked[1])
    gate_two = modulated(inside, mod, 5)
    output[...] = (residual[...] + gate_two * mixed).astype(bf)
    image_sums(5, upstream * mixed)
    mixed_grad = gate_two * upstream
    d_share = [jnp.sum(mixed_grad * each, axis=-1, keepdims=True) for each in picked]
    inner = share[0] * d_share[0] + share[1] * d_share[1]
    ids = lax.broadcasted_iota(jnp.int32, (512, 8), 1)
    d_logits = sum(
        jnp.where(ids == routes[:, k : k + 1], share[k] * (d_share[k] - inner), 0.0) for k in range(2)
    ).astype(bf)
    router_grad[...] = tn(d_logits, second[...])
    for copy in loads[:3]:
        copy.wait()
    d_second = (
        d_shared[...] + nn(d_logits, router_t[...].astype(bf)) + nn(hot[0] + hot[1], d_returned[...])
    )
    normed, inv_std = layer_stats(residual[...])
    image_sums(3, d_second)
    image_sums(4, d_second * normed)
    d_residual[...] = upstream + norm_grad(d_second * (1.0 + modulated(inside, mod, 4)), normed, inv_std)
    gate_one = modulated(inside, mod, 2)
    image_sums(2, d_residual[...] * projected[...])
    d_proj[...] = (gate_one * d_residual[...]).astype(bf)
    for copy in loads[3:]:
        copy.wait()
    d_attended = jnp.zeros((512, 768), f32)
    for j in range(4):
        piece = jnp.concatenate(
            [jnp.zeros((512, 64), bf), d_proj[:, 192 * j : 192 * j + 192]], axis=1
        )
        d_attended += nt(piece, qkvo[:, 768 * j + 512 : 768 * j + 768])
    d_attended = d_attended.astype(bf)
    d_att_t[...] = d_attended.T
    for h in range(12):
        d_att[h] = d_attended[:, 64 * h : 64 * h + 64]
    for j in range(18):
        pair = jnp.concatenate([heads[2 * j], heads[2 * j + 1]], axis=1)
        rows_t[128 * j : 128 * j + 128] = pair.T
    bias[...] = jnp.where(seg_col == seg_row, 0.0, -1e30)

    def head(h, carry):
        def at_head(g):
            return pl.ds(pl.multiple_of(64 * g, 64), 64)

        d_key, d_value = jnp.zeros((64, 512), f32), jnp.zeros((64, 512), f32)
        for part in range(512 // QUERY_ROWS):
            lines = slice(part * QUERY_ROWS, (part + 1) * QUERY_ROWS)
            scores = nn(heads[h, lines], rows_t[at_head(12 + h)]) * 0.125 + bias[lines]
            probability = jnp.exp(scores - totals[h, lines])
            d_prob = nn(d_att[h, lines], rows_t[at_head(24 + h)])
            inner = jnp.sum(probability * d_prob, axis=-1, keepdims=True)
            d_scores = (probability * (d_prob - inner)).astype(bf)
            d_heads[h, lines] = (nn(d_scores, heads[12 + h]) * 0.125).astype(bf)
            d_key += nn(rows_t[at_head(h), lines], d_scores)
            d_value += nn(d_att_t[at_head(h), lines], probability.astype(bf))
        d_rows_t[at_head(h)] = (d_key * 0.125).astype(bf)
        d_rows_t[at_head(12 + h)] = d_value.astype(bf)
        return carry

    lax.fori_loop(0, 12, head, 0)
    for g in range(12):
        column = head_column(g)
        d_rows[:, column : column + 64] = d_heads[g]
    for j in range(12):
        pair = d_rows_t[128 * j : 128 * j + 128].T
        for i in range(2):
            column = head_column(12 + 2 * j + i)
            d_rows[:, column : column + 64] = pair[:, 64 * i : 64 * i + 64]
    for j in range(4):
        d_rows[:, 768 * j + 576 : 768 * j + 768] = jnp.zeros((512, 192), bf)
    token_float = tokens[...].astype(f32)
    normed, inv_std = layer_stats(token_float)
    scale_one = 1.0 + modulated(inside, mod, 1)
    first_t = (normed * scale_one + modulated(inside, mod, 0)).astype(bf).T
    attended_t = attended[...].T
    for j in range(4):
        qkvo_grad[:, 768 * j : 768 * j + 640] = nn(first_t, d_rows[:, 768 * j : 768 * j + 640]).astype(bf)
        qkvo_grad[:, 768 * j + 576 : 768 * j + 768] = nn(
            attended_t, d_proj[:, 192 * j : 192 * j + 192]
        ).astype(bf)
    d_first = nt(d_rows[...], qkvo[...])
    image_sums(0, d_first)
    image_sums(1, d_first * normed)
    tokens_grad[...] = d_residual[...] + norm_grad(d_first * scale_one, normed, inv_std)


def rear(*operands):
    bf, f32 = jnp.bfloat16, jnp.float32
    return pl.pallas_call(
        rear_kernel,
        out_shape=(
            jax.ShapeDtypeStruct((512, 768), bf),
            jax.ShapeDtypeStruct((512, 768), f32),
            jax.ShapeDtypeStruct((768, 3072), bf),
            jax.ShapeDtypeStruct((2, 4608), f32),
            jax.ShapeDtypeStruct((8, 768), f32),
        ),
        in_specs=[
            SCALARS if i == 2 else ANYWHERE if i in (3, 8, 9, 10, 11, 16, 18) else ONCHIP
            for i in range(len(operands))
        ],
        out_specs=(ONCHIP,) * 5,
        scratch_shapes=[
            pltpu.VMEM((512, 512), f32),
            pltpu.VMEM((2304, 512), bf),
            pltpu.VMEM((12, 512, 64), bf),
            pltpu.VMEM((12, 512, 64), bf),
            pltpu.VMEM((768, 512), bf),
            pltpu.VMEM((1536, 512), bf),
            pltpu.VMEM((512, 3072), bf),
            pltpu.VMEM((512, 768), f32),
            pltpu.VMEM((512, 768), bf),
            pltpu.VMEM((768, 3072), bf),
            pltpu.VMEM((36, 512, 64), bf),
            pltpu.VMEM((12, 512, 1), f32),
            pltpu.VMEM((512, 768), bf),
            pltpu.VMEM((512, 768), f32),
            pltpu.VMEM((1152, 768), bf),
            pltpu.VMEM((512, 768), f32),
            DMA((7,)),
        ],
        compiler_params=pltpu.CompilerParams(vmem_limit_bytes=67043328),
        cost_estimate=pl.CostEstimate(flops=60_000_000_000, bytes_accessed=30_000_000, transcendentals=0),
        name="rear",
    )(*operands)


def last_kernel(
    qkvo_in, first_in, second_in, ada_in, up_in, down_in, d_act_in, router_in, condition,
    qkv_out, out_out, first_out, second_out, ada_out, up_out, down_out, condition_out, router_out,
    qkvo_sum, first, second, ada, up, down, d_act, router, sem,
):
    d = lax.axis_index("dp")
    pairs = (
        (up_in, up), (down_in, down), (ada_in, ada), (qkvo_in, qkvo_sum), (first_in, first),
        (second_in, second), (d_act_in, d_act), (router_in, router),
    )
    loads = [pltpu.make_async_copy(src, dst, sem.at[i]) for i, (src, dst) in enumerate(pairs)]
    for copy in loads:
        copy.start()
    for copy in loads:
        copy.wait()
    qkv_out[...] = qkvo_sum[:, 0:576]
    out_out[...] = qkvo_sum[:, 576:768]
    first_out[...] = first[...]
    second_out[...] = second[...]
    ada_out[...] = ada[...]
    up_out[...] = up[...]
    down_out[...] = down[...]
    router_out[...] = lines_of(router[...], 2 * d)[:, 0:96]
    for f in range(8):
        columns = slice(96 * f, 96 * f + 96)
        v = condition[:, columns].astype(jnp.float32)
        sigmoid = jax.nn.sigmoid(v)
        condition_out[:, columns] = lines_of(d_act[f], 2 * d)[:, 0:96] * (
            sigmoid * (1.0 + v * (1.0 - sigmoid))
        )


def last(*operands):
    f32 = jnp.float32
    return pl.pallas_call(
        last_kernel,
        out_shape=tuple(
            jax.ShapeDtypeStruct(shape, f32)
            for shape in (
                (96, 576), (96, 192), (96, 768), (192, 384), (96, 1152), (2, 96, 3072), (2, 384, 768),
                (2, 768), (2, 96),
            )
        ),
        in_specs=[ANYWHERE] * 8 + [ONCHIP],
        out_specs=(ONCHIP,) * 9,
        scratch_shapes=[
            pltpu.VMEM(shape, f32)
            for shape in (
                (96, 768), (96, 768), (192, 384), (96, 1152), (2, 96, 3072), (2, 384, 768), (8, 8, 128), (8, 128),
            )
        ]
        + [DMA((8,))],
        compiler_params=pltpu.CompilerParams(vmem_limit_bytes=67043328),
        name="last",
    )(*operands)


def fitted_shards(
    tokens,
    condition,
    ada_weight,
    qkv_weight,
    out_weight,
    shared_up,
    shared_down,
    router_weight,
    expert_up,
    expert_down,
    routes,
    image_sizes,
    cotangent,
):
    bf = jnp.bfloat16
    d_index, f_index = lax.axis_index("dp"), lax.axis_index("fsdp")
    model_width = tokens.shape[1]
    head_size = model_width // HEADS
    ids = jnp.arange(EXPERTS, dtype=jnp.int32)
    hot = routes[:, :, None] == ids[None, None, :]
    hot_any = jnp.any(hot, axis=1).astype(bf)
    order = jnp.arange(LONG, dtype=jnp.int32)
    earlier = (order[:, None] > order[None, :]).astype(bf)
    before = nn(earlier, hot_any)
    position = jnp.sum(jnp.where(hot, before[:, None, :], 0.0), axis=-1).astype(jnp.int32)
    target = routes * CAP + position
    live = (order < jnp.sum(image_sizes)).astype(jnp.float32)
    counts = jnp.sum(live[:, None] * hot_any.astype(jnp.float32), axis=0)
    cond_float = condition.astype(jnp.float32)
    activated = jax.nn.silu(cond_float).astype(bf)
    act_slices = activated.astype(jnp.float32).reshape(IMG_DEV, 8, 96).transpose(1, 0, 2)
    act_slices = jnp.pad(act_slices, ((0, 0), (0, 6), (0, 32)))
    act_slices = act_slices.at[:, 2, :EXPERTS].set(counts)
    act_slices = act_slices.at[:, 3:5, :96].set(router_weight.T.astype(jnp.float32))
    qkvo, router_t, seen, mod_rows, up_line, down_line, up_m, up_x0, up_y0, down_own, down_m = opening(
        qkv_weight, out_weight, act_slices, ada_weight, shared_up, shared_down.T, expert_up, expert_down
    )
    hops = hop(up_m, 2), hop(up_m, 4), hop(down_own, 2), hop(down_own, 4)
    expert_counts = seen[66, :EXPERTS].astype(jnp.int32)
    (
        heads, totals, attended, projected, residual, second_input, d_mixed, gates, rows, grads, modulation,
    ) = front(tokens, mod_rows, image_sizes, qkvo, router_t, cotangent, routes, target.T)
    rows = rows.reshape(EXPERTS, CAP, model_width)
    grads = grads.reshape(EXPERTS, CAP, model_width)
    rows, (up_x1, up_y1, down_x0, down_y0) = lax.optimization_barrier((rows, hops))
    rows_in, grads_in, up_corner, down_x1, down_y1, down_corner, shared_out, d_second, *shared_grads = (
        outbound(
            rows, grads, up_line, down_line, second_input, d_mixed, up_x0, up_y1, down_m, down_x0
        )
    )
    returned, d_returned, up_keep, *up_near, down_keep, down_x, down_y, first_part, second_part = experts(
        rows_in, grads_in, (expert_up, up_m, up_x0, up_x1, up_y0, up_y1, up_corner),
        (down_own, down_m, down_x0, down_x1, down_y0, down_y1, down_corner),
        *shared_grads,
    )
    up_next = square_next(up_keep, *up_near)
    down_near = hop(down_x, 2), hop(down_y, 4)
    returned = returned.reshape(EXPERTS * CAP, model_width)
    d_returned = d_returned.reshape(EXPERTS * CAP, model_width)
    output, tokens_grad, qkvo_grad, d_modulation, router_grad = rear(
        tokens, modulation, image_sizes, qkvo, router_t, cotangent, routes, target,
        heads, totals, attended, projected, residual, second_input, gates,
        returned, d_returned, shared_out, d_second,
    )
    qkvo_grad, down_near, up_next = lax.optimization_barrier((qkvo_grad, down_near, up_next))
    d_modulation = d_modulation.astype(bf)
    d_mod_rows = d_modulation.astype(jnp.float32).reshape(2, 4, 1152).transpose(1, 0, 2)
    d_mod_rows = lax.dynamic_update_slice(
        jnp.zeros((4, 8, 1152), jnp.float32), d_mod_rows, (0, 2 * d_index, 0)
    )
    router_tiles = jnp.pad(
        router_grad.reshape(EXPERTS, 8, 96).transpose(1, 0, 2), ((0, 0), (0, 0), (0, 32))
    )
    (
        qkvo_sum, shared_first_sum, shared_second_sum, ada_grad, d_act_tiles, router_sum,
        expert_up_grad, expert_down_grad,
    ) = dense_sums(
        qkvo_grad, first_part, second_part,
        (d_mod_rows, router_tiles, seen[:64].astype(bf), ada_weight),
        (up_keep, *up_near, *up_next, down_keep, *down_near),
    )
    (
        qkv_grad, out_grad, shared_first_sum, shared_second_sum, ada_grad, expert_up_grad, expert_down_grad,
        condition_grad, router_out,
    ) = last(
        qkvo_sum, shared_first_sum, shared_second_sum, ada_grad, expert_up_grad, expert_down_grad,
        d_act_tiles, router_sum, condition,
    )
    return (
        output,
        tokens_grad,
        condition_grad,
        ada_grad,
        qkv_grad,
        out_grad,
        shared_first_sum,
        shared_second_sum.T,
        router_out.T,
        expert_up_grad,
        expert_down_grad,
        expert_counts,
    )


def solution(mesh):
    placed = (
        P(("dp", "fsdp"), None),
        P(("dp", "fsdp"), None),
        P("fsdp", "dp"),
        P("fsdp", "dp"),
        P("fsdp", "dp"),
        P("fsdp", "dp"),
        P("fsdp", "dp"),
        P("fsdp", "dp"),
        P("dp", "fsdp", None),
        P("dp", "fsdp", None),
        P(("dp", "fsdp"), None),
        P(("dp", "fsdp")),
        P(("dp", "fsdp"), None),
    )
    fitted = mesh.shape["dp"] == 4 and mesh.shape["fsdp"] == 8
    return jax.shard_map(
        fitted_shards if fitted else shards,
        mesh=mesh,
        in_specs=placed,
        out_specs=(
            P(("dp", "fsdp"), None),
            P(("dp", "fsdp"), None),
            P(("dp", "fsdp"), None),
            P("fsdp", "dp"),
            P("fsdp", "dp"),
            P("fsdp", "dp"),
            P("fsdp", "dp"),
            P("fsdp", "dp"),
            P("fsdp", "dp"),
            P("dp", "fsdp", None),
            P("dp", "fsdp", None),
            P(),
        ),
        check_vma=False,
    )
```
